32 devices in a mesh: shard: 2 (over core), context: 4 (over y, x), tensor: 4 (over z).
Axes of the slice: x: 2, y: 2, z: 4, core: 2. Of those that a mesh axis runs over, the one named last changes fastest.
Arguments:
- tokens: bfloat16 [2, 4096, 1536], P('shard', 'context'), may hold values from -6 to 6
- w_query: bfloat16 [1536, 1536], P('shard', 'tensor'), may hold values from -0.15625 to 0.15625
- key_weight: bfloat16 [1536, 768], P('shard', 'tensor'), may hold values from -0.15625 to 0.15625
- value_weight: bfloat16 [1536, 768], P('shard', 'tensor'), may hold values from -0.15625 to 0.15625
- w_out: bfloat16 [1536, 1536], P('tensor', 'shard'), may hold values from -0.625 to 0.625
- w_gate: bfloat16 [1536, 4096], P('shard', 'tensor'), may hold values from -0.15625 to 0.15625
- w_up: bfloat16 [1536, 4096], P('shard', 'tensor'), may hold values from -0.15625 to 0.15625
- w_down: bfloat16 [4096, 1536], P('tensor', 'shard'), may hold values from -0.09375 to 0.09375
- gain_attn: bfloat16 [1536], P('shard'), may hold values from 0.5 to 1.5
- gain_ffn: bfloat16 [1536], P('shard'), may hold values from 0.5 to 1.5
- segments: int32 [2, 4096], P('shard'), may hold values from 0 to 8, as said below
- positions: int32 [2, 4096], P('shard'), may hold values from 0 to 2303, as said below
- cotangent: bfloat16 [2, 4096, 1536], P('shard', 'context'), may hold values from -6 to 6
Outputs:
- output: bfloat16 [2, 4096, 1536], P('shard', 'context')
- tokens_grad: bfloat16 [2, 4096, 1536], P('shard', 'context')
- w_query_grad: float32 [1536, 1536], P('shard', 'tensor')
- w_key_grad: float32 [1536, 768], P('shard', 'tensor')
- w_value_grad: float32 [1536, 768], P('shard', 'tensor')
- w_out_grad: float32 [1536, 1536], P('tensor', 'shard')
- w_gate_grad: float32 [1536, 4096], P('shard', 'tensor')
- w_up_grad: float32 [1536, 4096], P('shard', 'tensor')
- w_down_grad: float32 [4096, 1536], P('tensor', 'shard')
- gain_attn_grad: float32 [1536], P('shard')
- gain_ffn_grad: float32 [1536], P('shard')
The draws below stay inside these ranges and needn't reach their ends.
Inputs may be any that keep to these rules, and one draw needn't show every extreme that they name: In each group, segment 0 is a prompt of 2048 tokens and segments 1 to 8 are continuations of 256 tokens each; continuation number c branches off the prompt after its first c * 256 positions. Even slots 2 i hold the prompt half and odd slots 2 i + 1 the continuation half, each half being 2048 rows indexed by i. The prompt half is made of runs of 256 rows, each run holding 256 consecutive prompt tokens in order, the order of the runs drawn; the continuation half is made of runs of 256 rows, each run one whole continuation in order, the order of the continuations drawn. A prompt token's position is its index in the prompt; a continuation's token is at 2048 plus its index in the continuation; positions rise by one along each aligned block of 256 rows of a half.
All inputs are finite; a program needn't handle non-finite values.
Results may differ from the reference program's by a relative error of at most 0.015.
Values may be sent and summed in bfloat16 or wider, within the bound.
A program may use at most 384 MiB of HBM per device.

```python
import math
import jax
import jax.numpy as jnp
from jax import lax

MODEL_DIMENSION = 1536
QUERY_HEADS = 16
KEY_VALUE_HEADS = 8
HEAD_SIZE = 96
FF = 4096
PROMPT = 2048
CONTS = 8
CLEN = 256
GROUP_TOKENS = 4096
GROUP_COUNT = 2


def layout(key):
    prompt_units = PROMPT // CLEN
    prompt_keys = jax.random.split(jax.random.fold_in(key, 7), GROUP_COUNT)
    cont_keys = jax.random.split(jax.random.fold_in(key, 11), GROUP_COUNT)
    prompt_order = jax.vmap(lambda group_key: jax.random.permutation(group_key, prompt_units))(prompt_keys).astype(jnp.int32)
    cont_order = jax.vmap(lambda group_key: jax.random.permutation(group_key, CONTS))(cont_keys).astype(jnp.int32)
    within = jnp.arange(CLEN, dtype=jnp.int32)
    prompt_pos = (prompt_order[:, :, None] * CLEN + within[None, None, :]).reshape(GROUP_COUNT, PROMPT)
    prompt_seg = jnp.zeros((GROUP_COUNT, PROMPT), jnp.int32)
    cont_seg = jnp.repeat(cont_order + 1, CLEN, axis=1).astype(jnp.int32)
    cont_pos = jnp.tile(PROMPT + within, (GROUP_COUNT, CONTS)).astype(jnp.int32)
    seg_full = jnp.stack([prompt_seg, cont_seg], axis=-1).reshape(GROUP_COUNT, GROUP_TOKENS)
    pos_full = jnp.stack([prompt_pos, cont_pos], axis=-1).reshape(GROUP_COUNT, GROUP_TOKENS)
    return (seg_full.astype(jnp.int32), pos_full.astype(jnp.int32))


def draw_segments(key, part):
    return layout(key)[0]


def draw_positions(key, part):
    return layout(key)[1]


def block_levels(own_key, dims, cuts, least, top_value):
    level, own = 1.0, jax.random.fold_in(own_key, 6)
    for position, shards_of in cuts:
        draws = jnp.exp(jax.random.uniform(jax.random.fold_in(own, position), (shards_of,), jnp.float32, least / len(cuts), top_value / len(cuts)))
        level = level * jnp.repeat(draws, dims[position] // shards_of).reshape([-1 if axis == position else 1 for axis in range(len(dims))])
    return level


def scatter_about(key, dims, deviation, limit, cuts=(), held_as=jnp.bfloat16):
    values = deviation * jax.random.normal(key, dims, jnp.float32)
    if cuts:
        values = values * block_levels(key, dims, cuts, -0.22, 0.18)
    return jnp.clip(values, -limit, limit).astype(held_as)


def setup_inputs(seed: int = 0) -> dict:
    arg_keys = jax.random.split(jax.random.key(seed), 14)
    tokens = scatter_about(arg_keys[0], (GROUP_COUNT, GROUP_TOKENS, MODEL_DIMENSION), 1.0, 6.0, ((0, 2), (1, 4)))
    w_query = scatter_about(arg_keys[1], (MODEL_DIMENSION, QUERY_HEADS * HEAD_SIZE), MODEL_DIMENSION ** -0.5, 0.15625, ((0, 2), (1, 4)))
    key_weight = scatter_about(arg_keys[2], (MODEL_DIMENSION, KEY_VALUE_HEADS * HEAD_SIZE), MODEL_DIMENSION ** -0.5, 0.15625, ((0, 2), (1, 4)))
    value_weight = scatter_about(arg_keys[3], (MODEL_DIMENSION, KEY_VALUE_HEADS * HEAD_SIZE), MODEL_DIMENSION ** -0.5, 0.15625, ((0, 2), (1, 4)))
    w_out = scatter_about(arg_keys[4], (QUERY_HEADS * HEAD_SIZE, MODEL_DIMENSION), (QUERY_HEADS * HEAD_SIZE // 16) ** -0.5, 0.625, ((0, 4), (1, 2)))
    w_gate = scatter_about(arg_keys[5], (MODEL_DIMENSION, FF), MODEL_DIMENSION ** -0.5, 0.15625, ((0, 2), (1, 4)))
    w_up = scatter_about(arg_keys[6], (MODEL_DIMENSION, FF), MODEL_DIMENSION ** -0.5, 0.15625, ((0, 2), (1, 4)))
    w_down = scatter_about(arg_keys[7], (FF, MODEL_DIMENSION), FF ** -0.5, 0.09375, ((0, 4), (1, 2)))
    gain_attn = jnp.clip(1.0 + 0.1 * jax.random.normal(arg_keys[8], (MODEL_DIMENSION,), jnp.float32), 0.5, 1.5).astype(jnp.bfloat16)
    gain_ffn = jnp.clip(1.0 + 0.1 * jax.random.normal(arg_keys[9], (MODEL_DIMENSION,), jnp.float32), 0.5, 1.5).astype(jnp.bfloat16)
    segments = draw_segments(jax.random.fold_in(arg_keys[13], 71), 0)
    positions = draw_positions(jax.random.fold_in(arg_keys[13], 71), 0)
    cotangent = scatter_about(arg_keys[12], (GROUP_COUNT, GROUP_TOKENS, MODEL_DIMENSION), 1.0, 6.0, ((0, 2), (1, 4)))
    return {"tokens": tokens, "w_query": w_query, "key_weight": key_weight, "value_weight": value_weight, "w_out": w_out, "w_gate": w_gate, "w_up": w_up, "w_down": w_down, "gain_attn": gain_attn, "gain_ffn": gain_ffn, "segments": segments, "positions": positions, "cotangent": cotangent}


@jax.custom_vjp
def lower_layer(v):
    return lax.optimization_barrier(v.astype(jnp.bfloat16)).astype(jnp.float32)

@jax.custom_vjp
def lower_layer_backward(v):
    return v

def low_keep(v):
    return (lower_layer(v), None)

def low_pass(kept, grad):
    return (grad,)

def back_keep(v):
    return (v, None)

def back_low(kept, grad):
    return (lower_layer(grad),)
lower_layer.defvjp(low_keep, low_pass)
lower_layer_backward.defvjp(back_keep, back_low)
rope_base = 100000.0
norm_eps = 1e-05
precise = lax.Precision.HIGHEST

def matrix_product(left, right):
    return jnp.dot(left, right, precision=precise, preferred_element_type=jnp.float32)

def tables(positions):
    half_width = HEAD_SIZE // 2
    frequency = jnp.exp(jnp.arange(half_width, dtype=jnp.float32) * (-2.0 * math.log(rope_base) / HEAD_SIZE))
    angles = positions.astype(jnp.float32)[:, None] * frequency[None, :]
    return (jnp.cos(angles)[:, None, :], jnp.sin(angles)[:, None, :])

def rotary_apply(heads, cosine_table, sine_values):
    half_width = HEAD_SIZE // 2
    front_half = heads[..., :half_width]
    back_half = heads[..., half_width:]
    return jnp.concatenate([front_half * cosine_table - back_half * sine_values, back_half * cosine_table + front_half * sine_values], axis=-1)

def normalize(tok_rows, gain):
    norm_scale = lax.rsqrt(lax.optimization_barrier(jnp.mean(tok_rows * tok_rows, axis=-1, keepdims=True)) + norm_eps)
    return tok_rows * norm_scale * gain

def visible(seg_query, pos_query, seg_keys, pos_keys):
    own = (seg_keys[None, :] == seg_query[:, None]) & (pos_keys[None, :] <= pos_query[:, None])
    branch = (seg_keys[None, :] == 0) & (seg_query[:, None] > 0) & (pos_keys[None, :] < seg_query[:, None] * CLEN)
    return own | branch

def attend(query_heads_rows, key_head_rows, value_head_rows, seg_query, pos_query, seg_keys, pos_keys):
    rows_per_block = query_heads_rows.shape[0]
    grouped_heads = query_heads_rows.reshape(rows_per_block, KEY_VALUE_HEADS, QUERY_HEADS // KEY_VALUE_HEADS, HEAD_SIZE)
    scores = jnp.einsum('bhgd,khd->hgbk', grouped_heads, key_head_rows, precision=precise) * (1.0 / math.sqrt(HEAD_SIZE))
    scores = lower_layer_backward(scores)
    allowed = visible(seg_query, pos_query, seg_keys, pos_keys)
    soft_weights = jax.nn.softmax(jnp.where(allowed[None, None], scores, -1e+30), axis=-1)
    attended_output = jnp.einsum('hgbk,khd->bhgd', lower_layer(soft_weights), value_head_rows, precision=precise)
    return attended_output.reshape(rows_per_block, QUERY_HEADS * HEAD_SIZE)

def attention_forward(query_heads_rows, key_head_rows, value_head_rows, segments, positions):
    rows_per_block = min(512, GROUP_TOKENS)
    per_group = GROUP_TOKENS // rows_per_block
    blocks = GROUP_COUNT * per_group
    query_blocks = query_heads_rows.reshape(blocks, rows_per_block, QUERY_HEADS, HEAD_SIZE)
    seg_blocks = segments.reshape(blocks, rows_per_block)
    pos_blocks = positions.reshape(blocks, rows_per_block)

    def one_block(inputs):
        block_query, block_seg, block_pos, block_index = inputs
        group_index = block_index // per_group
        group_keys = lax.dynamic_index_in_dim(key_head_rows, group_index, 0, keepdims=False)
        group_values = lax.dynamic_index_in_dim(value_head_rows, group_index, 0, keepdims=False)
        group_seg = lax.dynamic_index_in_dim(segments, group_index, 0, keepdims=False)
        group_pos = lax.dynamic_index_in_dim(positions, group_index, 0, keepdims=False)
        return attend(block_query.reshape(rows_per_block, QUERY_HEADS * HEAD_SIZE), group_keys, group_values, block_seg, block_pos, group_seg, group_pos)
    attended_output = lax.map(jax.checkpoint(one_block), (query_blocks, seg_blocks, pos_blocks, jnp.arange(blocks, dtype=jnp.int32)))
    return attended_output.reshape(GROUP_COUNT * GROUP_TOKENS, QUERY_HEADS * HEAD_SIZE)

def forward(tokens, w_query, key_weight, value_weight, w_out, w_gate, w_up, w_down, gain_attn, gain_ffn, segments, positions):
    token_count = GROUP_COUNT * GROUP_TOKENS
    tok_rows = tokens.reshape(token_count, MODEL_DIMENSION)
    cosine_table, sine_values = tables(positions.reshape(token_count))
    normed_input = lower_layer(normalize(tok_rows, gain_attn))
    query_heads_rows = lower_layer(rotary_apply(lower_layer_backward(matrix_product(normed_input, w_query)).reshape(token_count, QUERY_HEADS, HEAD_SIZE), cosine_table, sine_values))
    key_head_rows = lower_layer(rotary_apply(lower_layer_backward(matrix_product(normed_input, key_weight)).reshape(token_count, KEY_VALUE_HEADS, HEAD_SIZE), cosine_table, sine_values))
    value_head_rows = lower_layer(lower_layer_backward(matrix_product(normed_input, value_weight)))
    attended_output = attention_forward(query_heads_rows, key_head_rows.reshape(GROUP_COUNT, GROUP_TOKENS, KEY_VALUE_HEADS, HEAD_SIZE), value_head_rows.reshape(GROUP_COUNT, GROUP_TOKENS, KEY_VALUE_HEADS, HEAD_SIZE), segments, positions)
    middle = tok_rows + lower_layer_backward(matrix_product(lower_layer(lower_layer_backward(attended_output)), w_out))
    normed_two = lower_layer(normalize(middle, gain_ffn))
    gate_proj = lower_layer_backward(matrix_product(normed_two, w_gate))
    up_proj = lower_layer_backward(matrix_product(normed_two, w_up))
    hidden = lower_layer(jax.nn.silu(gate_proj) * up_proj)
    return middle + lower_layer_backward(matrix_product(hidden, w_down))

def reference(tokens, w_query, key_weight, value_weight, w_out, w_gate, w_up, w_down, gain_attn, gain_ffn, segments, positions, cotangent):
    floats = tuple((item.astype(jnp.float32) for item in (tokens, w_query, key_weight, value_weight, w_out, w_gate, w_up, w_down, gain_attn, gain_ffn)))

    def layer(*params):
        return forward(*params, segments, positions)
    output, pullback = jax.vjp(layer, *floats)
    gradients = pullback(cotangent.reshape(GROUP_COUNT * GROUP_TOKENS, MODEL_DIMENSION).astype(jnp.float32))
    return (output.reshape(GROUP_COUNT, GROUP_TOKENS, MODEL_DIMENSION).astype(jnp.bfloat16), gradients[0].reshape(GROUP_COUNT, GROUP_TOKENS, MODEL_DIMENSION).astype(jnp.bfloat16), gradients[1], gradients[2], gradients[3], gradients[4], gradients[5], gradients[6], gradients[7], gradients[8], gradients[9])
```

```python
import functools
import math

import jax
import jax.numpy as jnp
import numpy as np
from jax import lax
from jax.experimental import pallas as pl
from jax.experimental.pallas import tpu as pltpu
from jax.sharding import PartitionSpec as P

HEAD_SIZE = 96
CLEN = 256


rope_base = 100000.0
norm_eps = 1e-05


def tables(positions):
    half_width = HEAD_SIZE // 2
    frequency = jnp.exp(
        jnp.arange(half_width, dtype=jnp.float32) * (-2.0 * math.log(rope_base) / HEAD_SIZE)
    )
    angles = positions.astype(jnp.float32)[:, None] * frequency[None, :]
    return (jnp.cos(angles)[:, None, :], jnp.sin(angles)[:, None, :])


def rotary_apply(heads, cosine_table, sine_values):
    half_width = HEAD_SIZE // 2
    front_half = heads[..., :half_width]
    back_half = heads[..., half_width:]
    return jnp.concatenate(
        [
            front_half * cosine_table - back_half * sine_values,
            back_half * cosine_table + front_half * sine_values,
        ],
        axis=-1,
    )


def rotate_back(heads, cosine_table, sine_values):
    half_width = HEAD_SIZE // 2
    front_half = heads[..., :half_width]
    back_half = heads[..., half_width:]
    return jnp.concatenate(
        [
            front_half * cosine_table + back_half * sine_values,
            back_half * cosine_table - front_half * sine_values,
        ],
        axis=-1,
    )


def contract_rows(left, right):
    return lax.dot_general(
        left, right, (((0,), (0,)), ((), ())), preferred_element_type=jnp.float32
    )


def contract_cols(left, right):
    return lax.dot_general(
        left, right, (((1,), (1,)), ((), ())), preferred_element_type=jnp.float32
    )


def norm_back(tok_rows, norm_scale, gain, grad_normed):
    weighted = gain * grad_normed
    inner = jnp.mean(weighted * tok_rows, axis=-1, keepdims=True)
    grad_rows = norm_scale * weighted - tok_rows * (norm_scale * norm_scale * norm_scale) * inner
    grad_gain = jnp.sum(grad_normed * tok_rows * norm_scale, axis=0)
    return (grad_rows, grad_gain)


def visible(seg_query, pos_query, seg_keys, pos_keys):
    own = (seg_keys[None, :] == seg_query[:, None]) & (pos_keys[None, :] <= pos_query[:, None])
    branch = (
        (seg_keys[None, :] == 0)
        & (seg_query[:, None] > 0)
        & (pos_keys[None, :] < seg_query[:, None] * CLEN)
    )
    return own | branch


def general(
    tokens,
    w_query,
    key_weight,
    value_weight,
    w_out,
    w_gate,
    w_up,
    w_down,
    gain_attn,
    gain_ffn,
    segments,
    positions,
    cotangent,
):
    groups, tok_local, model_width = tokens.shape
    token_count = groups * tok_local
    heads_here = w_query.shape[1] // HEAD_SIZE
    kv_here = key_weight.shape[1] // HEAD_SIZE
    per_kv = heads_here // kv_here
    kv_width = kv_here * HEAD_SIZE
    score_scale = 1.0 / math.sqrt(HEAD_SIZE)
    context_index = lax.axis_index("context")
    first_row = context_index * tok_local
    seg_here = lax.dynamic_slice_in_dim(segments, first_row, tok_local, 1)
    pos_here = lax.dynamic_slice_in_dim(positions, first_row, tok_local, 1)
    w_query, key_weight, value_weight, w_gate, w_up, gain_attn, gain_ffn = (
        lax.all_gather(w_query, "shard", axis=0, tiled=True),
        lax.all_gather(key_weight, "shard", axis=0, tiled=True),
        lax.all_gather(value_weight, "shard", axis=0, tiled=True),
        lax.all_gather(w_gate, "shard", axis=0, tiled=True),
        lax.all_gather(w_up, "shard", axis=0, tiled=True),
        lax.all_gather(gain_attn, "shard", axis=0, tiled=True),
        lax.all_gather(gain_ffn, "shard", axis=0, tiled=True),
    )
    w_out, w_down = (
        lax.all_gather(w_out, "shard", axis=1, tiled=True),
        lax.all_gather(w_down, "shard", axis=1, tiled=True),
    )
    gain_one = gain_attn.astype(jnp.float32)
    gain_two = gain_ffn.astype(jnp.float32)
    tok_rows = tokens.reshape(token_count, model_width).astype(jnp.float32)
    scale_one = lax.rsqrt(jnp.mean(tok_rows * tok_rows, axis=-1, keepdims=True) + norm_eps)
    normed_input = (tok_rows * scale_one * gain_one).astype(jnp.bfloat16)
    cosine_table, sine_values = tables(pos_here.reshape(token_count))
    query_heads_rows = rotary_apply(
        jnp.dot(normed_input, w_query, preferred_element_type=jnp.float32).reshape(
            token_count, heads_here, HEAD_SIZE
        ),
        cosine_table,
        sine_values,
    )
    query_heads_rows = query_heads_rows.astype(jnp.bfloat16).reshape(
        groups, tok_local, heads_here * HEAD_SIZE
    )
    key_rows = rotary_apply(
        jnp.dot(normed_input, key_weight, preferred_element_type=jnp.float32).reshape(
            token_count, kv_here, HEAD_SIZE
        ),
        cosine_table,
        sine_values,
    )
    key_rows = key_rows.astype(jnp.bfloat16).reshape(token_count, kv_width)
    value_rows = jnp.dot(normed_input, value_weight, preferred_element_type=jnp.float32).astype(
        jnp.bfloat16
    )
    keyval = jnp.concatenate([key_rows, value_rows], axis=-1).reshape(
        groups, tok_local, 2 * kv_width
    )
    gathered = lax.all_gather(keyval, "context", axis=1, tiled=True)

    def scores_of(group_queries, group_keyval, seg_query, pos_query, seg_keys, pos_keys):
        grouped_heads = group_queries.reshape(tok_local, kv_here, per_kv, HEAD_SIZE)
        key_head_rows = group_keyval[:, :kv_width].reshape(-1, kv_here, HEAD_SIZE)
        scores = (
            jnp.einsum(
                "bhgd,khd->hgbk", grouped_heads, key_head_rows, preferred_element_type=jnp.float32
            )
            * score_scale
        )
        allowed = visible(seg_query, pos_query, seg_keys, pos_keys)
        return (jnp.where(allowed[None, None], scores, -1e30), grouped_heads, key_head_rows)

    def attend_group(inputs):
        group_queries, group_keyval, seg_query, pos_query, seg_keys, pos_keys = inputs
        scores, grouped_heads, key_head_rows = scores_of(
            group_queries, group_keyval, seg_query, pos_query, seg_keys, pos_keys
        )
        top_score = jnp.max(scores, axis=-1, keepdims=True)
        exponent = jnp.exp(scores - top_score)
        totals = jnp.sum(exponent, axis=-1, keepdims=True)
        soft_weights = (exponent / totals).astype(jnp.bfloat16)
        value_head_rows = group_keyval[:, kv_width:].reshape(-1, kv_here, HEAD_SIZE)
        attended_output = jnp.einsum(
            "hgbk,khd->bhgd", soft_weights, value_head_rows, preferred_element_type=jnp.float32
        )
        return (
            attended_output.reshape(tok_local, heads_here * HEAD_SIZE),
            (top_score + jnp.log(totals))[..., 0],
        )

    attended_output, log_total = lax.map(
        attend_group, (query_heads_rows, gathered, seg_here, pos_here, segments, positions)
    )
    attended_low = attended_output.reshape(token_count, heads_here * HEAD_SIZE).astype(jnp.bfloat16)
    attn_sum = lax.psum(jnp.dot(attended_low, w_out, preferred_element_type=jnp.float32), "tensor")
    middle = tok_rows + attn_sum
    scale_two = lax.rsqrt(jnp.mean(middle * middle, axis=-1, keepdims=True) + norm_eps)
    normed_two = (middle * scale_two * gain_two).astype(jnp.bfloat16)
    gate_proj = jnp.dot(normed_two, w_gate, preferred_element_type=jnp.float32)
    up_proj = jnp.dot(normed_two, w_up, preferred_element_type=jnp.float32)
    sigmoid_gate = jax.nn.sigmoid(gate_proj)
    silu_gate = gate_proj * sigmoid_gate
    hidden = (silu_gate * up_proj).astype(jnp.bfloat16)
    ffn_sum = lax.psum(
        jnp.dot(hidden, w_down, preferred_element_type=jnp.float32).astype(jnp.bfloat16), "tensor"
    ).astype(jnp.float32)
    output = (middle + ffn_sum).astype(jnp.bfloat16).reshape(groups, tok_local, model_width)
    grad_low = cotangent.reshape(token_count, model_width)
    grad_out = grad_low.astype(jnp.float32)
    grad_hidden = contract_cols(grad_low, w_down)
    grad_w_down_t = contract_rows(grad_low, hidden)
    grad_gate = (
        grad_hidden * up_proj * sigmoid_gate * (1.0 + gate_proj * (1.0 - sigmoid_gate))
    ).astype(jnp.bfloat16)
    grad_up = (grad_hidden * silu_gate).astype(jnp.bfloat16)
    grad_w_gate = contract_rows(normed_two, grad_gate)
    grad_w_up = contract_rows(normed_two, grad_up)
    grad_normed_two = lax.psum(
        contract_cols(grad_gate, w_gate) + contract_cols(grad_up, w_up), "tensor"
    )
    back_two, grad_gain_two = norm_back(middle, scale_two, gain_two, grad_normed_two)
    grad_middle = grad_out + back_two
    grad_mid_low = grad_middle.astype(jnp.bfloat16)
    grad_w_out_t = contract_rows(grad_mid_low, attended_low)
    grad_attended = (
        contract_cols(grad_mid_low, w_out)
        .astype(jnp.bfloat16)
        .reshape(groups, tok_local, heads_here * HEAD_SIZE)
    )

    def attend_back(inputs):
        (
            group_queries,
            group_keyval,
            group_grad,
            group_total,
            seg_query,
            pos_query,
            seg_keys,
            pos_keys,
        ) = inputs
        scores, grouped_heads, key_head_rows = scores_of(
            group_queries, group_keyval, seg_query, pos_query, seg_keys, pos_keys
        )
        soft_weights = jnp.exp(scores - group_total[..., None])
        value_head_rows = group_keyval[:, kv_width:].reshape(-1, kv_here, HEAD_SIZE)
        grad_grouped = group_grad.reshape(tok_local, kv_here, per_kv, HEAD_SIZE)
        grad_weights = jnp.einsum(
            "bhgd,khd->hgbk", grad_grouped, value_head_rows, preferred_element_type=jnp.float32
        )
        inner = jnp.sum(soft_weights * grad_weights, axis=-1, keepdims=True)
        grad_scores = (soft_weights * (grad_weights - inner)).astype(jnp.bfloat16)
        grad_queries = (
            jnp.einsum(
                "hgbk,khd->bhgd", grad_scores, key_head_rows, preferred_element_type=jnp.float32
            )
            * score_scale
        )
        grad_keys = (
            jnp.einsum(
                "hgbk,bhgd->khd", grad_scores, grouped_heads, preferred_element_type=jnp.float32
            )
            * score_scale
        )
        grad_values = jnp.einsum(
            "hgbk,bhgd->khd",
            soft_weights.astype(jnp.bfloat16),
            grad_grouped,
            preferred_element_type=jnp.float32,
        )
        grad_keyval = jnp.concatenate(
            [grad_keys.reshape(-1, kv_width), grad_values.reshape(-1, kv_width)], axis=-1
        )
        return (grad_queries.reshape(tok_local, heads_here * HEAD_SIZE), grad_keyval)

    grad_queries, grad_keyval = lax.map(
        attend_back,
        (
            query_heads_rows,
            gathered,
            grad_attended,
            log_total,
            seg_here,
            pos_here,
            segments,
            positions,
        ),
    )
    grad_keyval = lax.psum_scatter(grad_keyval, "context", scatter_dimension=1, tiled=True)
    grad_query_rows = rotate_back(
        grad_queries.reshape(token_count, heads_here, HEAD_SIZE), cosine_table, sine_values
    )
    grad_query_rows = grad_query_rows.astype(jnp.bfloat16).reshape(
        token_count, heads_here * HEAD_SIZE
    )
    grad_key_rows = rotate_back(
        grad_keyval[..., :kv_width].reshape(token_count, kv_here, HEAD_SIZE),
        cosine_table,
        sine_values,
    )
    grad_key_rows = grad_key_rows.astype(jnp.bfloat16).reshape(token_count, kv_width)
    grad_value_rows = (
        grad_keyval[..., kv_width:].reshape(token_count, kv_width).astype(jnp.bfloat16)
    )
    grad_w_query = contract_rows(normed_input, grad_query_rows)
    grad_w_key = contract_rows(normed_input, grad_key_rows)
    grad_w_value = contract_rows(normed_input, grad_value_rows)
    partial_one = (
        contract_cols(grad_query_rows, w_query)
        + contract_cols(grad_key_rows, key_weight)
        + contract_cols(grad_value_rows, value_weight)
    )
    grad_normed = lax.psum(partial_one, "tensor")
    back_one, grad_gain_one = norm_back(tok_rows, scale_one, gain_one, grad_normed)
    tokens_grad = (
        (grad_middle + back_one).astype(jnp.bfloat16).reshape(groups, tok_local, model_width)
    )
    summed = (
        lax.psum_scatter(grad_w_query, ("shard", "context"), scatter_dimension=0, tiled=True),
        lax.psum_scatter(grad_w_key, ("shard", "context"), scatter_dimension=0, tiled=True),
        lax.psum_scatter(grad_w_value, ("shard", "context"), scatter_dimension=0, tiled=True),
        lax.psum_scatter(grad_w_out_t, ("shard", "context"), scatter_dimension=0, tiled=True),
        lax.psum_scatter(grad_w_gate, ("shard", "context"), scatter_dimension=0, tiled=True),
        lax.psum_scatter(grad_w_up, ("shard", "context"), scatter_dimension=0, tiled=True),
        lax.psum_scatter(grad_w_down_t, ("shard", "context"), scatter_dimension=0, tiled=True),
        lax.psum_scatter(grad_gain_one, ("shard", "context"), scatter_dimension=0, tiled=True),
        lax.psum_scatter(grad_gain_two, ("shard", "context"), scatter_dimension=0, tiled=True),
    )
    summed = (
        lax.all_gather(summed[0].astype(jnp.bfloat16), "context", axis=0, tiled=True).astype(
            jnp.float32
        ),
        lax.all_gather(summed[1].astype(jnp.bfloat16), "context", axis=0, tiled=True).astype(
            jnp.float32
        ),
        lax.all_gather(summed[2].astype(jnp.bfloat16), "context", axis=0, tiled=True).astype(
            jnp.float32
        ),
        lax.all_gather(summed[3].astype(jnp.bfloat16), "context", axis=0, tiled=True).astype(
            jnp.float32
        ),
        lax.all_gather(summed[4].astype(jnp.bfloat16), "context", axis=0, tiled=True).astype(
            jnp.float32
        ),
        lax.all_gather(summed[5].astype(jnp.bfloat16), "context", axis=0, tiled=True).astype(
            jnp.float32
        ),
        lax.all_gather(summed[6].astype(jnp.bfloat16), "context", axis=0, tiled=True).astype(
            jnp.float32
        ),
        lax.all_gather(summed[7].astype(jnp.bfloat16), "context", axis=0, tiled=True).astype(
            jnp.float32
        ),
        lax.all_gather(summed[8].astype(jnp.bfloat16), "context", axis=0, tiled=True).astype(
            jnp.float32
        ),
    )
    return (
        output,
        tokens_grad,
        summed[0],
        summed[1],
        summed[2],
        summed[3].T,
        summed[4],
        summed[5],
        summed[6].T,
        summed[7],
        summed[8],
    )


MESH = pl.DeviceIdType.MESH
RUN = 256
PAD = 128
NEG = -1e30
LOG2E = 1.4426950408889634
BF = jnp.bfloat16
F32 = jnp.float32
VLIM = 64 * 1024 * 1024


def mm(a, b):
    return lax.dot_general(a, b, (((1,), (0,)), ((), ())), preferred_element_type=F32)


def mm_nt(a, b):
    return lax.dot_general(a, b, (((1,), (1,)), ((), ())), preferred_element_type=F32)


def mm_tn(a, b):
    return lax.dot_general(a, b, (((0,), (0,)), ((), ())), preferred_element_type=F32)


def iota(shape, axis):
    return lax.broadcasted_iota(jnp.int32, shape, axis)


def one_hot(hit):
    return jnp.where(hit, 1.0, 0.0).astype(BF)


def pad_matrix(heads):
    shape = (heads * HEAD_SIZE, heads * PAD)
    row, col = iota(shape, 0), iota(shape, 1)
    lane = col & 127
    part = jnp.where(lane < 64, lane, lane - 16)
    return one_hot((row == (col >> 7) * HEAD_SIZE + part) & ((lane & 63) < 48))


def split_matrix():
    row, col = iota((RUN, RUN), 0), iota((RUN, RUN), 1)
    return one_hot(col == jnp.where(row < 128, 2 * row, 2 * row - 255))


def merge_matrix():
    row, col = iota((RUN, RUN), 0), iota((RUN, RUN), 1)
    return one_hot(col == (row >> 1) + (row & 1) * 128)


def rope_tables(run, cb_ref, sb_ref, cj_ref, sj_ref):
    cb, sb = cb_ref[pl.ds(run, 1), :], sb_ref[pl.ds(run, 1), :]
    cj, sj = cj_ref[...], sj_ref[...]
    return cb * cj - sb * sj, sb * cj + cb * sj


def rope(u, c, s):
    return u * c + pltpu.roll(u, 64, 1) * s


def rope_back(u, c, s):
    return u * c - pltpu.roll(u, 64, 1) * s


def vmem(*shape_dtype):
    return pl.BlockSpec(memory_space=pltpu.VMEM)


def entry_barrier(targets):
    bar = pltpu.get_barrier_semaphore()
    for t in targets:
        pl.semaphore_signal(bar, inc=1, device_id=t, device_id_type=MESH)
    pl.semaphore_wait(bar, len(targets))


def remote(src, dst, send, recv, target):
    return pltpu.make_async_remote_copy(
        src_ref=src, dst_ref=dst, send_sem=send, recv_sem=recv, device_id=target, device_id_type=MESH
    )


def first_kernel(nc, x_ref, g_ref, cb_ref, sb_ref, cj_ref, sj_ref, wq_h, wk_h, wv_h, wo_h, wg_h, wu_h, wd_h,
                 xp_ref, n1_ref, q_ref, kvp_ref, kvc_ref, wp_ref, gf_ref, wo_f, wg_f, wu_f, wd_f,
                 wq_s, wk_s, wv_s, g_s, wo_v, wg_v, wu_v, wd_v, kv_send,
                 lsem, ssem, rsem, osem, csem, crem):
    s = lax.axis_index("shard")
    c = lax.axis_index("context")
    dh = g_s.shape[1] // 2
    own = pl.ds(pl.multiple_of(s * dh, dh), dh)
    other = {"shard": 1 - s}
    loads = [
        pltpu.make_async_copy(wq_h, wq_s.at[own], lsem.at[0]),
        pltpu.make_async_copy(wk_h, wk_s.at[own], lsem.at[1]),
        pltpu.make_async_copy(wv_h, wv_s.at[own], lsem.at[2]),
        pltpu.make_async_copy(g_ref, g_s.at[:, own], lsem.at[3]),
        pltpu.make_async_copy(wo_h, wo_v, lsem.at[4]),
        pltpu.make_async_copy(wg_h, wg_v, lsem.at[5]),
        pltpu.make_async_copy(wu_h, wu_v, lsem.at[6]),
        pltpu.make_async_copy(wd_h, wd_v, lsem.at[7]),
    ]
    for cp in loads:
        cp.start()
    entry_barrier([other] + [{"context": lax.rem(c + i, nc)} for i in range(1, nc)])
    sends = [
        remote(wq_s.at[own], wq_s.at[own], ssem.at[0], rsem.at[0], other),
        remote(wk_s.at[own], wk_s.at[own], ssem.at[1], rsem.at[1], other),
        remote(wv_s.at[own], wv_s.at[own], ssem.at[2], rsem.at[2], other),
        remote(g_s.at[:, own], g_s.at[:, own], ssem.at[3], rsem.at[3], other),
        remote(wo_v, wo_f.at[:, own], ssem.at[4], rsem.at[4], other),
        remote(wg_v, wg_f.at[own], ssem.at[5], rsem.at[5], other),
        remote(wu_v, wu_f.at[own], ssem.at[6], rsem.at[6], other),
        remote(wd_v, wd_f.at[:, own], ssem.at[7], rsem.at[7], other),
    ]
    keeps = [
        pltpu.make_async_copy(wo_v, wo_f.at[:, own], osem.at[0]),
        pltpu.make_async_copy(wg_v, wg_f.at[own], osem.at[1]),
        pltpu.make_async_copy(wu_v, wu_f.at[own], osem.at[2]),
        pltpu.make_async_copy(wd_v, wd_f.at[:, own], osem.at[3]),
    ]
    for i in (3, 0, 1, 2, 4, 5, 6, 7):
        loads[i].wait()
        sends[i].start()
        if i >= 4:
            keeps[i - 4].start()
    half = x_ref.shape[0] // 2
    split = split_matrix()
    for i in range(x_ref.shape[0] // RUN):
        xb = mm(split, x_ref[pl.ds(i * RUN, RUN), :])
        xp_ref[pl.ds(i * 128, 128), :] = xb[:128].astype(BF)
        xp_ref[pl.ds(half + i * 128, 128), :] = xb[128:].astype(BF)
        if i == 0:
            sends[3].wait_recv()
        r = lax.rsqrt(jnp.mean(xb * xb, axis=-1, keepdims=True) + norm_eps)
        nb = (xb * r * g_s[0:1, :]).astype(BF)
        n1_ref[pl.ds(i * 128, 128), :] = nb[:128]
        n1_ref[pl.ds(half + i * 128, 128), :] = nb[128:]
    gf_ref[...] = g_s[...]
    hq, hk = wq_s.shape[1] // HEAD_SIZE, wk_s.shape[1] // HEAD_SIZE
    selq, selk = pad_matrix(hq), pad_matrix(hk)
    nq, nk = hq * PAD, hk * PAD
    for i in range(3):
        sends[i].wait_recv()
    for i in range(wq_s.shape[0] // RUN):
        rows = pl.ds(i * RUN, RUN)
        wp_ref[rows, 0:nq] = mm(wq_s[rows, :], selq).astype(BF)
        wp_ref[rows, nq : nq + nk] = mm(wk_s[rows, :], selk).astype(BF)
        wp_ref[rows, nq + nk :] = mm(wv_s[rows, :], selk).astype(BF)
    selkv = pad_matrix(2 * hk)
    runs = x_ref.shape[0] // RUN
    per = runs // 2
    kv_copies = []
    for run in range(runs):
        rows = pl.ds(run * RUN, RUN)
        y = mm(n1_ref[rows, :], wp_ref[...])
        ct, st = rope_tables(run, cb_ref, sb_ref, cj_ref, sj_ref)
        for h in range(hq):
            q_ref[rows, h * PAD : (h + 1) * PAD] = rope(y[:, h * PAD : (h + 1) * PAD], ct, st).astype(BF)
        kv = [rope(y[:, nq + h * PAD : nq + (h + 1) * PAD], ct, st).astype(BF) for h in range(hk)]
        kv = jnp.concatenate(kv + [y[:, nq + nk :].astype(BF)], axis=1)
        if run < per:
            kv_send[pl.ds(run * RUN, RUN), :] = mm_nt(kv, selkv).astype(BF)
            mine = pl.ds(pl.multiple_of((c * per + run) * RUN, RUN), RUN)
            for i in range(1, nc):
                cp = remote(kv_send.at[pl.ds(run * RUN, RUN)], kvp_ref.at[mine], csem.at[run, i], crem.at[run, i],
                            {"context": lax.rem(c + i, nc)})
                cp.start()
                kv_copies.append(cp)
            cp = pltpu.make_async_copy(kv_send.at[pl.ds(run * RUN, RUN)], kvp_ref.at[mine], csem.at[run, 0])
            cp.start()
            kv_copies.append(cp)
        else:
            kvc_ref[pl.ds((run - per) * RUN, RUN), :] = kv
    for cp in kv_copies:
        cp.wait()
    for i in range(4):
        keeps[i].wait()
        sends[4 + i].wait_recv()
    for cp in sends:
        cp.wait_send()


def load_keys(kvp_ref, k_s, v_s, ones):
    hk = k_s.shape[0]
    sel = pad_matrix(2 * hk)
    lane = iota((RUN, PAD), 1)

    def step(i, _):
        rows = pl.ds(pl.multiple_of(i * RUN, RUN), RUN)
        kv = mm(kvp_ref[rows, :], sel)
        for g in range(hk):
            k_s[g, rows, :] = kv[:, g * PAD : (g + 1) * PAD].astype(BF)
            v = kv[:, (hk + g) * PAD : (hk + g + 1) * PAD]
            if ones:
                v = jnp.where(lane == 48, 1.0, v)
            v_s[g, rows, :] = v.astype(BF)
        return 0

    lax.fori_loop(0, kvp_ref.shape[0] // RUN, step, 0)


def attend_kernel(kbase, qlim, q_ref, kvp_ref, kvc_ref, wo_ref, o_ref, op_ref, lse_ref, p_ref, k_s, v_s, s_s):
    hk = k_s.shape[0]
    hq = q_ref.shape[1] // PAD
    rep = hq // hk
    runs = q_ref.shape[0] // RUN
    per = runs // 2
    blocks = kvp_ref.shape[0] // RUN
    scale = LOG2E / math.sqrt(HEAD_SIZE)
    load_keys(kvp_ref, k_s, v_s, True)
    lane = iota((RUN, PAD), 1)
    diff = iota((RUN, RUN), 1) - iota((RUN, RUN), 0)

    def head(run, h, own):
        rows = pl.ds(pl.multiple_of(run * RUN, RUN), RUN)
        cols = pl.ds(pl.multiple_of(h * PAD, PAD), PAD)
        g = h // rep
        q = q_ref[rows, cols]
        lim = qlim[run]
        top = None
        for b in range(blocks):
            s = mm_nt(q, k_s[g, pl.ds(b * RUN, RUN), :]) * scale
            room = lim - kbase[b]
            if own:
                s = s + jnp.where(room >= 0, 0.0, NEG)
            else:
                s = jnp.where(diff <= room, s, NEG)
            s_s[:, b * RUN : (b + 1) * RUN] = s
            top = s if top is None else jnp.maximum(top, s)
        if own:
            crow = pl.ds(pl.multiple_of((run - per) * RUN, RUN), RUN)
            kc = kvc_ref[crow, pl.ds(pl.multiple_of(g * PAD, PAD), PAD)]
            vc = kvc_ref[crow, pl.ds(pl.multiple_of((hk + g) * PAD, PAD), PAD)]
            vc = jnp.where(lane == 48, 1.0, vc.astype(F32)).astype(BF)
            s = jnp.where(diff <= 0, mm_nt(q, kc) * scale, NEG)
            s_s[:, blocks * RUN :] = s
            top = jnp.maximum(top, s)
        m = jnp.max(top, axis=1, keepdims=True)
        acc = None
        for b in range(blocks):
            p = jnp.exp2(s_s[:, b * RUN : (b + 1) * RUN] - m).astype(BF)
            o = mm(p, v_s[g, pl.ds(b * RUN, RUN), :])
            acc = o if acc is None else acc + o
        if own:
            p = jnp.exp2(s_s[:, blocks * RUN :] - m).astype(BF)
            acc = acc + mm(p, vc)
        total = acc[:, 48:49]
        op_ref[rows, cols] = (acc / total).astype(BF)
        lse = jnp.broadcast_to(m + jnp.log2(total), (RUN, PAD)).T
        lse_ref[pl.ds(pl.multiple_of((run * hq + h) * 8, 8), 8), :] = lse[0:8, :]

    def prompt(i, _):
        head(i // hq, lax.rem(i, hq), False)
        return 0

    def cont(i, _):
        head(per + i // hq, lax.rem(i, hq), True)
        return 0

    lax.fori_loop(0, per * hq, prompt, 0)
    lax.fori_loop(0, per * hq, cont, 0)
    sel = pad_matrix(hq)

    def project(i, _):
        rows = pl.ds(pl.multiple_of(i * RUN, RUN), RUN)
        o = mm_nt(op_ref[rows, :], sel).astype(BF)
        o_ref[rows, :] = o
        p_ref[rows, :] = mm(o, wo_ref[...]).astype(BF)
        return 0

    lax.fori_loop(0, runs, project, 0)


def line_sum(n, chunk, pbuf, rbuf, obuf, rs, rr, bs, br):
    z = lax.axis_index("tensor")
    rows_half = pbuf.shape[0] // 2
    count = rows_half // chunk
    lag = 4

    def pieces(h, i):
        rows = pl.ds(pl.multiple_of(h * rows_half + i * chunk, chunk), chunk)
        place = z if h == 0 else n - 1 - z
        ahead = {"tensor": jnp.minimum(z + 1, n - 1) if h == 0 else jnp.maximum(z - 1, 0)}
        back = {"tensor": jnp.maximum(z - 1, 0) if h == 0 else jnp.minimum(z + 1, n - 1)}
        up = remote(pbuf.at[rows], rbuf.at[rows], rs.at[h, i], rr.at[h, i], ahead)
        down = remote(obuf.at[rows], obuf.at[rows], bs.at[h, i], br.at[h, i], back)
        return rows, place, up, down

    def reduce_step(h, i):
        rows, place, up, down = pieces(h, i)

        @pl.when(place == 0)
        def _():
            up.start()

        @pl.when(place > 0)
        def _():
            up.wait_recv()
            total = (rbuf[rows, :].astype(F32) + pbuf[rows, :].astype(F32)).astype(BF)

            @pl.when(place < n - 1)
            def _():
                pbuf[rows, :] = total
                up.start()

            @pl.when(place == n - 1)
            def _():
                obuf[rows, :] = total
                down.start()

    def spread_step(h, i):
        rows, place, up, down = pieces(h, i)

        @pl.when(place < n - 1)
        def _():
            down.wait_recv()

        @pl.when((place < n - 1) & (place > 0))
        def _():
            down.start()

    steps = count + (2 * (n - 1) * 4 + 2) // 3 + 1

    def step(t, _):
        for h in range(2):
            place = z if h == 0 else n - 1 - z
            i = t - (place * 4) // 3

            @pl.when((i >= 0) & (i < count))
            def _():
                reduce_step(h, i)

            j = t - ((2 * (n - 1) - place) * 4) // 3

            @pl.when((j >= 0) & (j < count))
            def _():
                spread_step(h, j)

        return 0

    lax.fori_loop(0, steps, step, 0)

    def finish(i, _):
        for h in range(2):
            rows, place, up, down = pieces(h, i)

            @pl.when(place < n - 1)
            def _():
                up.wait_send()

            @pl.when(place > 0)
            def _():
                down.wait_send()

        return 0

    lax.fori_loop(0, count, finish, 0)


def line_barrier(n, peers=()):
    z = lax.axis_index("tensor")
    bar = pltpu.get_barrier_semaphore()
    for t in peers:
        pl.semaphore_signal(bar, inc=1, device_id=t, device_id_type=MESH)

    @pl.when(z > 0)
    def _():
        pl.semaphore_signal(bar, inc=1, device_id={"tensor": jnp.maximum(z - 1, 0)}, device_id_type=MESH)

    @pl.when(z < n - 1)
    def _():
        pl.semaphore_signal(bar, inc=1, device_id={"tensor": jnp.minimum(z + 1, n - 1)}, device_id_type=MESH)

    pl.semaphore_wait(bar, len(peers) + jnp.minimum(z, 1) + jnp.minimum(n - 1 - z, 1))


def sum_kernel(n, chunk, p_hbm, o_ref, pbuf, rbuf, lsem, rs, rr, bs, br):
    cp = pltpu.make_async_copy(p_hbm, pbuf, lsem)
    cp.start()
    line_barrier(n)
    cp.wait()
    line_sum(n, chunk, pbuf, rbuf, o_ref, rs, rr, bs, br)


def ffn_kernel(dy_ref, xp_ref, s1_ref, gf_ref, wg_ref, wu_ref, wd_ref,
               dyp_ref, fp_ref, dn_ref, gg_ref, gu_ref, gd_ref,
               n2_s, hid_s, dg_s, du_s):
    rows_here = xp_ref.shape[0]
    half = rows_here // 2
    split = split_matrix()

    def order(i, _):
        b = mm(split, dy_ref[pl.ds(pl.multiple_of(i * RUN, RUN), RUN), :]).astype(BF)
        dyp_ref[pl.ds(pl.multiple_of(i * 128, 128), 128), :] = b[:128]
        dyp_ref[pl.ds(pl.multiple_of(half + i * 128, 128), 128), :] = b[128:]
        return 0

    lax.fori_loop(0, rows_here // RUN, order, 0)

    def block(i, _):
        rows = pl.ds(pl.multiple_of(i * RUN, RUN), RUN)
        mid = xp_ref[rows, :].astype(F32) + s1_ref[rows, :].astype(F32)
        r = lax.rsqrt(jnp.mean(mid * mid, axis=-1, keepdims=True) + norm_eps)
        n2 = (mid * r * gf_ref[8:9, :]).astype(BF)
        n2_s[rows, :] = n2
        gate = mm(n2, wg_ref[...])
        up = mm(n2, wu_ref[...])
        sig = jax.nn.sigmoid(gate)
        silu = gate * sig
        hid = (silu * up).astype(BF)
        hid_s[rows, :] = hid
        fp_ref[rows, :] = mm(hid, wd_ref[...]).astype(BF)
        dh = mm_nt(dyp_ref[rows, :], wd_ref[...])
        dg = (dh * up * sig * (1.0 + gate * (1.0 - sig))).astype(BF)
        du = (dh * silu).astype(BF)
        dg_s[rows, :] = dg
        du_s[rows, :] = du
        dn_ref[rows, :] = (mm_nt(dg, wg_ref[...]) + mm_nt(du, wu_ref[...])).astype(BF)
        return 0

    lax.fori_loop(0, rows_here // RUN, block, 0)

    def grads(i, _):
        cols = pl.ds(pl.multiple_of(i * RUN, RUN), RUN)
        nt = n2_s[:, cols].T
        gg_ref[cols, :] = mm(nt, dg_s[...]).astype(BF)
        gu_ref[cols, :] = mm(nt, du_s[...]).astype(BF)
        return 0

    lax.fori_loop(0, n2_s.shape[1] // RUN, grads, 0)
    wide = dyp_ref.shape[1] // 2

    def grads_down(i, _):
        cols = pl.ds(pl.multiple_of(i * RUN, RUN), RUN)
        ht = hid_s[:, cols].T
        for s in range(2):
            gd_ref[s, cols, :] = mm(ht, dyp_ref[:, s * wide : (s + 1) * wide]).astype(BF)
        return 0

    lax.fori_loop(0, hid_s.shape[1] // RUN, grads_down, 0)


def back_kernel(kbase, qlim, cb_ref, sb_ref, cj_ref, sj_ref, dyp_ref, xp_ref, s1_ref, s2_ref, gf_ref, wo_ref, o_ref, op_ref,
                lse_ref, q_ref, kvp_ref, kvc_ref,
                dm_ref, g2_ref, go_ref, dqp_ref, dkvp_ref, dkvc_ref,
                dmb_s, do_s, k_s, v_s, dk_s, dv_s):
    hk = k_s.shape[0]
    hq = q_ref.shape[1] // PAD
    rep = hq // hk
    rows_here = q_ref.shape[0]
    runs = rows_here // RUN
    per = runs // 2
    blocks = kvp_ref.shape[0] // RUN
    score = 1.0 / math.sqrt(HEAD_SIZE)
    scale = LOG2E * score
    load_keys(kvp_ref, k_s, v_s, False)
    selq = pad_matrix(hq)
    g2_ref[...] = jnp.zeros_like(g2_ref)

    def middle(i, _):
        rows = pl.ds(pl.multiple_of(i * RUN, RUN), RUN)
        mid = xp_ref[rows, :].astype(F32) + s1_ref[rows, :].astype(F32)
        r = lax.rsqrt(jnp.mean(mid * mid, axis=-1, keepdims=True) + norm_eps)
        dn = s2_ref[rows, :].astype(F32)
        w = gf_ref[8:9, :] * dn
        inner = jnp.mean(w * mid, axis=-1, keepdims=True)
        dm = dyp_ref[rows, :].astype(F32) + r * w - mid * (r * r * r) * inner
        dm_ref[rows, :] = dm
        g2_ref[...] += jnp.sum((dn * mid * r).reshape(RUN // 8, 8, mid.shape[1]), axis=0)
        dmb = dm.astype(BF)
        dmb_s[rows, :] = dmb
        do = mm_nt(dmb, wo_ref[...]).astype(BF)
        do_s[rows, :] = mm(do, selq).astype(BF)
        return 0

    lax.fori_loop(0, runs, middle, 0)
    wide = dmb_s.shape[1] // 2
    ot = o_ref[...].T
    for s in range(2):
        go_ref[s] = mm(ot, dmb_s[:, s * wide : (s + 1) * wide]).astype(BF)
    dk_s[...] = jnp.zeros_like(dk_s)
    dv_s[...] = jnp.zeros_like(dv_s)
    width = rep * RUN
    diff = iota((RUN, width), 0) - (iota((RUN, width), 1) & (RUN - 1))

    def pair(run, g, own):
        rows = pl.ds(pl.multiple_of(run * RUN, RUN), RUN)

        def stack(ref):
            parts = [ref[rows, pl.ds(pl.multiple_of((g * rep + j) * PAD, PAD), PAD)] for j in range(rep)]
            return jnp.concatenate(parts, axis=0)

        q, do, op = stack(q_ref), stack(do_s), stack(op_ref)
        delta = jnp.sum((do.astype(F32) * op.astype(F32)).T, axis=0, keepdims=True)
        lse = jnp.concatenate(
            [lse_ref[pl.ds(pl.multiple_of((run * hq + g * rep + j) * 8, 8), 1), :] for j in range(rep)], axis=1
        )
        lim = qlim[run]

        def tile(k, v, hide):
            s = hide(mm_nt(k, q) * scale - lse)
            p = jnp.exp2(s)
            ds = (p * (mm_nt(v, do) - delta)).astype(BF)
            return mm(ds, q), mm(p.astype(BF), do), mm_tn(ds, k)

        dq = None
        for b in range(blocks):
            at = pl.ds(b * RUN, RUN)
            room = lim - kbase[b]
            if own:
                hide = lambda s: s + jnp.where(room >= 0, 0.0, NEG)
            else:
                hide = lambda s: jnp.where(diff <= room, s, NEG)
            dk, dv, d = tile(k_s[g, at, :], v_s[g, at, :], hide)
            dk_s[g, at, :] += dk
            dv_s[g, at, :] += dv
            dq = d if dq is None else dq + d
        ct, st = rope_tables(run, cb_ref, sb_ref, cj_ref, sj_ref)
        if own:
            crow = pl.ds(pl.multiple_of((run - per) * RUN, RUN), RUN)
            kcol = pl.ds(pl.multiple_of(g * PAD, PAD), PAD)
            vcol = pl.ds(pl.multiple_of((hk + g) * PAD, PAD), PAD)
            hide = lambda s: jnp.where(diff <= 0, s, NEG)
            dk, dv, d = tile(kvc_ref[crow, kcol], kvc_ref[crow, vcol], hide)
            dq = dq + d
            dkvc_ref[crow, kcol] = rope_back(dk * score, ct, st).astype(BF)
            dkvc_ref[crow, vcol] = dv.astype(BF)
        for j in range(rep):
            part = rope_back(dq[j * RUN : (j + 1) * RUN] * score, ct, st)
            dqp_ref[rows, pl.ds(pl.multiple_of((g * rep + j) * PAD, PAD), PAD)] = part.astype(BF)

    def prompt(i, _):
        pair(i // hk, lax.rem(i, hk), False)
        return 0

    def cont(i, _):
        pair(per + i // hk, lax.rem(i, hk), True)
        return 0

    lax.fori_loop(0, per * hk, prompt, 0)
    lax.fori_loop(0, per * hk, cont, 0)
    selkv = pad_matrix(2 * hk)

    def pack(i, _):
        rows = pl.ds(pl.multiple_of(i * RUN, RUN), RUN)
        parts = [(dk_s[g, rows, :] * score).astype(BF) for g in range(hk)]
        parts += [dv_s[g, rows, :].astype(BF) for g in range(hk)]
        dkvp_ref[rows, :] = mm_nt(jnp.concatenate(parts, axis=1), selkv).astype(BF)
        return 0

    lax.fori_loop(0, blocks, pack, 0)


def keys_kernel(nc, cb_ref, sb_ref, cj_ref, sj_ref, dkvp_ref, dkvc_ref, dqp_ref, n1_ref, wp_ref, dn_ref, gw_ref,
                recv, dkv_s, ssem, rsem):
    c = lax.axis_index("context")
    rows_here = dqp_ref.shape[0]
    half = rows_here // 2
    entry_barrier([{"context": lax.rem(c + i, nc)} for i in range(1, nc)])
    copies = []
    for i in range(1, nc):
        to = lax.rem(c + i, nc)
        cp = remote(dkvp_ref.at[pl.ds(pl.multiple_of(to * half, half), half)], recv.at[i - 1], ssem.at[i - 1], rsem.at[i - 1],
                    {"context": to})
        cp.start()
        copies.append(cp)
    nq = dqp_ref.shape[1]
    nkv = dkvc_ref.shape[1]
    hk = nkv // PAD // 2
    hq = nq // PAD
    selq, selkv = pad_matrix(hq), pad_matrix(2 * hk)
    nt_rows = n1_ref.shape[1]
    dq_u = mm_nt(dqp_ref[...], selq).astype(BF)
    wide_q = hq * HEAD_SIZE

    def grads_q(i, _):
        cols = pl.ds(pl.multiple_of(i * RUN, RUN), RUN)
        gw_ref[cols, 0:wide_q] = mm(n1_ref[:, cols].T, dq_u).astype(BF)
        return 0

    lax.fori_loop(0, nt_rows // RUN, grads_q, 0)
    for cp in copies:
        cp.wait_recv()
    for run in range(half // RUN):
        rows = pl.ds(run * RUN, RUN)
        mine = pl.ds(pl.multiple_of(c * half + run * RUN, RUN), RUN)
        total = mm(dkvp_ref[mine, :], selkv)
        for i in range(nc - 1):
            total = total + mm(recv[i, rows, :], selkv)
        ct, st = rope_tables(run, cb_ref, sb_ref, cj_ref, sj_ref)
        for g in range(hk):
            dkv_s[rows, g * PAD : (g + 1) * PAD] = rope_back(total[:, g * PAD : (g + 1) * PAD], ct, st).astype(BF)
        dkv_s[rows, hk * PAD :] = total[:, hk * PAD :].astype(BF)
    dkv_s[pl.ds(half, half), :] = dkvc_ref[...]
    dkv_u = mm_nt(dkv_s[...], selkv).astype(BF)

    def grads_kv(i, _):
        cols = pl.ds(pl.multiple_of(i * RUN, RUN), RUN)
        gw_ref[cols, wide_q:] = mm(n1_ref[:, cols].T, dkv_u).astype(BF)
        return 0

    lax.fori_loop(0, nt_rows // RUN, grads_kv, 0)

    def normed(i, _):
        rows = pl.ds(pl.multiple_of(i * RUN, RUN), RUN)
        dn = mm_nt(dqp_ref[rows, :], wp_ref[:, 0:nq]) + mm_nt(dkv_s[rows, :], wp_ref[:, nq:])
        dn_ref[rows, :] = dn.astype(BF)
        return 0

    lax.fori_loop(0, rows_here // RUN, normed, 0)
    for cp in copies:
        cp.wait_send()


def last_kernel(n, nc, chunk, fp_h, dn_h, xp_ref, s1_ref, dm_ref, gf_ref, g2_ref, out_ref, tg_ref, gg_ref,
                pbuf, rbuf, obuf, gpart, grecv, lsem, rs, rr, bs, br, gs, gr):
    rows_here = xp_ref.shape[0]
    half = rows_here // 2
    s = lax.axis_index("shard")
    c = lax.axis_index("context")
    loads = [pltpu.make_async_copy(fp_h, pbuf.at[pl.ds(0, rows_here)], lsem.at[0]),
             pltpu.make_async_copy(dn_h, pbuf.at[pl.ds(rows_here, rows_here)], lsem.at[1])]
    for cp in loads:
        cp.start()
    peers = []
    for i in range(1, 2 * nc):
        peers.append({"shard": lax.rem(s + i // nc, 2), "context": lax.rem(c + lax.rem(i, nc), nc)})
    line_barrier(n, peers)
    for cp in loads:
        cp.wait()
    line_sum(n, chunk, pbuf, rbuf, obuf, rs, rr, bs, br)
    merge = merge_matrix()
    gpart[0:8, :] = jnp.zeros((8, gpart.shape[1]), F32)
    gpart[8:16, :] = g2_ref[...]

    def block(i, _):
        a = pl.ds(pl.multiple_of(i * 128, 128), 128)
        b = pl.ds(pl.multiple_of(half + i * 128, 128), 128)

        def take(ref, base=0):
            lo = ref[pl.ds(pl.multiple_of(base + i * 128, 128), 128), :]
            hi = ref[pl.ds(pl.multiple_of(base + half + i * 128, 128), 128), :]
            return jnp.concatenate([lo, hi], axis=0).astype(F32)

        x = take(xp_ref)
        mid = x + take(s1_ref)
        rows = pl.ds(pl.multiple_of(i * RUN, RUN), RUN)
        out_ref[rows, :] = mm(merge, (mid + take(obuf)).astype(BF)).astype(BF)
        dn = take(obuf, rows_here)
        r = lax.rsqrt(jnp.mean(x * x, axis=-1, keepdims=True) + norm_eps)
        w = gf_ref[0:1, :] * dn
        inner = jnp.mean(w * x, axis=-1, keepdims=True)
        tg = take(dm_ref) + (r * w - x * (r * r * r) * inner)
        tg_ref[rows, :] = mm(merge, tg.astype(BF)).astype(BF)
        gpart[0:8, :] += jnp.sum((dn * x * r).reshape(RUN // 8, 8, x.shape[1]), axis=0)
        return 0

    lax.fori_loop(0, rows_here // RUN, block, 0)
    me = s * nc + c
    sums = jnp.concatenate(
        [jnp.broadcast_to(jnp.sum(gpart[k * 8 : (k + 1) * 8, :], axis=0, keepdims=True), (8, gpart.shape[1])) for k in range(2)], axis=0
    )
    grecv[me] = sums
    copies = []
    for i, t in enumerate(peers):
        cp = remote(grecv.at[me], grecv.at[me], gs.at[i], gr.at[i], t)
        cp.start()
        copies.append(cp)
    for cp in copies:
        cp.wait()
    total = grecv[0]
    for i in range(1, 2 * nc):
        total = total + grecv[i]
    gg_ref[...] = total


def fast(
    tokens, w_query, key_weight, value_weight, w_out, w_gate, w_up, w_down, gain_attn, gain_ffn, segments, positions, cotangent, n, nc
):
    _, rows, d = tokens.shape
    half = rows // 2
    runs = rows // RUN
    per = runs // 2
    prompt = segments.shape[1] // 2
    blocks = prompt // RUN
    dq, dk = w_query.shape[1], key_weight.shape[1]
    hq, hk = dq // HEAD_SIZE, dk // HEAD_SIZE
    nq, nk = hq * PAD, hk * PAD
    ff = w_gate.shape[1]
    dh = d // 2
    c = lax.axis_index("context")
    x = tokens.reshape(rows, d)
    dy = cotangent.reshape(rows, d)
    kbase = positions[0, 0 :: 2 * RUN]
    seg_here = lax.dynamic_slice_in_dim(segments[0], c * rows, rows, 0)
    pos_here = lax.dynamic_slice_in_dim(positions[0], c * rows, rows, 0)
    qbase = jnp.concatenate([pos_here[0 :: 2 * RUN], pos_here[1 :: 2 * RUN]])
    qlim = jnp.concatenate([pos_here[0 :: 2 * RUN], seg_here[1 :: 2 * RUN] * CLEN - 1])
    freq = np.exp(np.arange(HEAD_SIZE // 2, dtype=np.float32) * np.float32(-2.0 * math.log(rope_base) / HEAD_SIZE)).astype(np.float32)
    lanes = np.zeros((PAD,), np.float32)
    lanes[0:48] = freq
    lanes[64:112] = freq
    sign = np.where(np.arange(PAD) < 64, -1.0, 1.0).astype(np.float32)
    inner = np.arange(RUN, dtype=np.float64)[:, None] * lanes[None, :].astype(np.float64)
    cj = jnp.asarray(np.cos(inner).astype(np.float32))
    sj = jnp.asarray((np.sin(inner) * sign).astype(np.float32))
    angle = qbase.astype(F32)[:, None] * jnp.asarray(lanes)[None, :]
    cb = jnp.cos(angle)
    sb = jnp.sin(angle) * jnp.asarray(sign)[None, :]
    gains = jnp.concatenate([jnp.broadcast_to(g.astype(F32)[None, :], (8, dh)) for g in (gain_attn, gain_ffn)], axis=0)

    V = pl.BlockSpec(memory_space=pltpu.VMEM)
    S = pl.BlockSpec(memory_space=pltpu.SMEM)
    A = pl.BlockSpec(memory_space=pl.ANY)
    sds = jax.ShapeDtypeStruct
    DMA = pltpu.SemaphoreType.DMA

    def call(kernel, ins, outs, scratch, collective=None, flops=0):
        params = dict(vmem_limit_bytes=VLIM - 64 * 1024)
        if collective is not None:
            params.update(collective_id=collective, has_side_effects=True)
        args = [a for a, _ in ins]
        return pl.pallas_call(
            kernel,
            out_shape=[o for o, _ in outs],
            in_specs=[sp for _, sp in ins],
            out_specs=[sp for _, sp in outs],
            scratch_shapes=scratch,
            compiler_params=pltpu.CompilerParams(**params),
            cost_estimate=pl.CostEstimate(flops=flops, bytes_accessed=0, transcendentals=0),
        )(*args)

    rope_in = [(cb, V), (sb, V), (cj, V), (sj, V)]
    xp, n1, q, kvp, kvc, wp, gf, wo, wg, wu, wd = call(
        functools.partial(first_kernel, nc),
        [(x, V), (gains, A)] + rope_in + [(w_query, A), (key_weight, A), (value_weight, A), (w_out, A), (w_gate, A), (w_up, A), (w_down, A)],
        [
            (sds((rows, d), BF), V), (sds((rows, d), BF), V), (sds((rows, nq), BF), V),
            (sds((prompt, 2 * dk), BF), A), (sds((half, 2 * nk), BF), V), (sds((d, nq + 2 * nk), BF), V), (sds((16, d), F32), V),
            (sds((dq, d), BF), A), (sds((d, ff), BF), A), (sds((d, ff), BF), A), (sds((ff, d), BF), A),
        ],
        [
            pltpu.VMEM((d, dq), BF), pltpu.VMEM((d, dk), BF), pltpu.VMEM((d, dk), BF), pltpu.VMEM((16, d), F32),
            pltpu.VMEM((dq, dh), BF), pltpu.VMEM((dh, ff), BF), pltpu.VMEM((dh, ff), BF), pltpu.VMEM((ff, dh), BF),
            pltpu.VMEM((half, 2 * dk), BF),
            DMA((8,)), DMA((8,)), DMA((8,)), DMA((4,)), DMA((per, nc)), DMA((per, nc)),
        ],
        collective=0, flops=60 * 10**9,
    )
    o, op, lse, part = call(
        attend_kernel,
        [(kbase, S), (qlim, S), (q, V), (kvp, V), (kvc, V), (wo, V)],
        [(sds((rows, dq), BF), V), (sds((rows, nq), BF), V), (sds((runs * hq * 8, RUN), F32), V), (sds((rows, d), BF), V)],
        [pltpu.VMEM((hk, prompt, PAD), BF), pltpu.VMEM((hk, prompt, PAD), BF), pltpu.VMEM((RUN, prompt + RUN), F32)],
        flops=60 * 10**9,
    )

    def line(part, collective):
        r = part.shape[0]
        chunk = 32
        count = r // 2 // chunk
        return call(
            functools.partial(sum_kernel, n, chunk), [(part, A)], [(sds((r, d), BF), V)],
            [pltpu.VMEM((r, d), BF), pltpu.VMEM((r, d), BF), DMA] + [DMA((2, count))] * 4,
            collective=collective, flops=80 * 10**9,
        )[0]

    s1 = line(part, 1)
    dyp, fp, dn2, gg, gu, gd = call(
        ffn_kernel,
        [(dy, V), (xp, V), (s1, V), (gf, V), (wg, V), (wu, V), (wd, V)],
        [(sds((rows, d), BF), V)] * 3 + [(sds((d, ff), BF), V), (sds((d, ff), BF), V), (sds((2, ff, dh), BF), V)],
        [pltpu.VMEM((rows, d), BF), pltpu.VMEM((rows, ff), BF), pltpu.VMEM((rows, ff), BF), pltpu.VMEM((rows, ff), BF)],
        flops=60 * 10**9,
    )
    both = ("shard", "context")

    def reduce_rows(g):
        g = lax.psum_scatter(g, both, scatter_dimension=0, tiled=True)
        return lax.all_gather(g, "context", axis=0, tiled=True)

    gg, gu, gd = reduce_rows(gg), reduce_rows(gu), reduce_rows(gd.reshape(2 * ff, dh))
    s2 = line(dn2, 2)
    dm, g2, go, dqp, dkvp, dkvc = call(
        back_kernel,
        [(kbase, S), (qlim, S)] + rope_in + [(dyp, V), (xp, V), (s1, V), (s2, V), (gf, V), (wo, V), (o, V), (op, V), (lse, V), (q, V), (kvp, V), (kvc, V)],
        [
            (sds((rows, d), F32), V), (sds((8, d), F32), V), (sds((2, dq, dh), BF), V), (sds((rows, nq), BF), V),
            (sds((prompt, 2 * dk), BF), V), (sds((half, 2 * nk), BF), V),
        ],
        [
            pltpu.VMEM((rows, d), BF), pltpu.VMEM((rows, nq), BF), pltpu.VMEM((hk, prompt, PAD), BF), pltpu.VMEM((hk, prompt, PAD), BF),
            pltpu.VMEM((hk, prompt, PAD), F32), pltpu.VMEM((hk, prompt, PAD), F32),
        ],
        flops=100 * 10**9,
    )
    go = reduce_rows(go.reshape(2 * dq, dh))
    dn1, gw = call(
        functools.partial(keys_kernel, nc),
        rope_in + [(dkvp, V), (dkvc, V), (dqp, V), (n1, V), (wp, V)],
        [(sds((rows, d), BF), V), (sds((d, dq + 2 * dk), BF), V)],
        [pltpu.VMEM((nc - 1, half, 2 * dk), BF), pltpu.VMEM((rows, 2 * nk), BF), DMA((nc - 1,)), DMA((nc - 1,))],
        collective=3, flops=40 * 10**9,
    )
    gw = reduce_rows(gw)
    chunk = 32
    count = rows // chunk
    out, tg, gains_grad = call(
        functools.partial(last_kernel, n, nc, chunk),
        [(fp, A), (dn1, A), (xp, V), (s1, V), (dm, V), (gf, V), (g2, V)],
        [(sds((rows, d), BF), V), (sds((rows, d), BF), V), (sds((16, d), F32), V)],
        [
            pltpu.VMEM((2 * rows, d), BF), pltpu.VMEM((2 * rows, d), BF), pltpu.VMEM((2 * rows, d), BF),
            pltpu.VMEM((16, d), F32), pltpu.VMEM((2 * nc, 16, d), F32), DMA((2,)),
        ]
        + [DMA((2, count))] * 4
        + [DMA((2 * nc - 1,)), DMA((2 * nc - 1,))],
        collective=4, flops=160 * 10**9,
    )
    s = lax.axis_index("shard")
    g1o = lax.dynamic_slice_in_dim(gains_grad[0], s * dh, dh, 0)
    g2o = lax.dynamic_slice_in_dim(gains_grad[8], s * dh, dh, 0)
    return (
        out[None], tg[None],
        gw[:, :dq].astype(F32), gw[:, dq : dq + dk].astype(F32), gw[:, dq + dk :].astype(F32),
        go.astype(F32), gg.astype(F32), gu.astype(F32), gd.astype(F32), g1o, g2o,
    )


def body(mesh, *args):
    tokens, w_query, segments = args[0], args[1], args[10]
    n, nc = mesh.shape["tensor"], mesh.shape["context"]
    rows = tokens.shape[1]
    if (tokens.shape[0] == 1 and rows % (4 * CLEN) == 0 and n > 1 and nc > 1 and mesh.shape["shard"] == 2
            and segments.shape[1] == rows * nc):
        return fast(*args, n, nc)
    return general(*args)


def solution(mesh):
    in_specs = (
        P("shard", "context", None),
        P("shard", "tensor"),
        P("shard", "tensor"),
        P("shard", "tensor"),
        P("tensor", "shard"),
        P("shard", "tensor"),
        P("shard", "tensor"),
        P("tensor", "shard"),
        P("shard"),
        P("shard"),
        P("shard", None),
        P("shard", None),
        P("shard", "context", None),
    )
    out_specs = (
        P("shard", "context", None),
        P("shard", "context", None),
        P("shard", "tensor"),
        P("shard", "tensor"),
        P("shard", "tensor"),
        P("tensor", "shard"),
        P("shard", "tensor"),
        P("shard", "tensor"),
        P("tensor", "shard"),
        P("shard"),
        P("shard"),
    )
    return jax.shard_map(functools.partial(body, mesh), mesh=mesh, in_specs=in_specs, out_specs=out_specs, check_vma=False)
```

```python
import functools
import math

import jax
import jax.numpy as jnp
import numpy as np
from jax import lax
from jax.experimental import pallas as pl
from jax.experimental.pallas import tpu as pltpu
from jax.sharding import PartitionSpec as P

HEAD_SIZE = 96
CLEN = 256


rope_base = 100000.0
norm_eps = 1e-05


def tables(positions):
    half_width = HEAD_SIZE // 2
    frequency = jnp.exp(
        jnp.arange(half_width, dtype=jnp.float32) * (-2.0 * math.log(rope_base) / HEAD_SIZE)
    )
    angles = positions.astype(jnp.float32)[:, None] * frequency[None, :]
    return (jnp.cos(angles)[:, None, :], jnp.sin(angles)[:, None, :])


def rotary_apply(heads, cosine_table, sine_values):
    half_width = HEAD_SIZE // 2
    front_half = heads[..., :half_width]
    back_half = heads[..., half_width:]
    return jnp.concatenate(
        [
            front_half * cosine_table - back_half * sine_values,
            back_half * cosine_table + front_half * sine_values,
        ],
        axis=-1,
    )


def rotate_back(heads, cosine_table, sine_values):
    half_width = HEAD_SIZE // 2
    front_half = heads[..., :half_width]
    back_half = heads[..., half_width:]
    return jnp.concatenate(
        [
            front_half * cosine_table + back_half * sine_values,
            back_half * cosine_table - front_half * sine_values,
        ],
        axis=-1,
    )


def contract_rows(left, right):
    return lax.dot_general(
        left, right, (((0,), (0,)), ((), ())), preferred_element_type=jnp.float32
    )


def contract_cols(left, right):
    return lax.dot_general(
        left, right, (((1,), (1,)), ((), ())), preferred_element_type=jnp.float32
    )


def norm_back(tok_rows, norm_scale, gain, grad_normed):
    weighted = gain * grad_normed
    inner = jnp.mean(weighted * tok_rows, axis=-1, keepdims=True)
    grad_rows = norm_scale * weighted - tok_rows * (norm_scale * norm_scale * norm_scale) * inner
    grad_gain = jnp.sum(grad_normed * tok_rows * norm_scale, axis=0)
    return (grad_rows, grad_gain)


def visible(seg_query, pos_query, seg_keys, pos_keys):
    own = (seg_keys[None, :] == seg_query[:, None]) & (pos_keys[None, :] <= pos_query[:, None])
    branch = (
        (seg_keys[None, :] == 0)
        & (seg_query[:, None] > 0)
        & (pos_keys[None, :] < seg_query[:, None] * CLEN)
    )
    return own | branch


def general(
    tokens,
    w_query,
    key_weight,
    value_weight,
    w_out,
    w_gate,
    w_up,
    w_down,
    gain_attn,
    gain_ffn,
    segments,
    positions,
    cotangent,
):
    groups, tok_local, model_width = tokens.shape
    token_count = groups * tok_local
    heads_here = w_query.shape[1] // HEAD_SIZE
    kv_here = key_weight.shape[1] // HEAD_SIZE
    per_kv = heads_here // kv_here
    kv_width = kv_here * HEAD_SIZE
    score_scale = 1.0 / math.sqrt(HEAD_SIZE)
    context_index = lax.axis_index("context")
    first_row = context_index * tok_local
    seg_here = lax.dynamic_slice_in_dim(segments, first_row, tok_local, 1)
    pos_here = lax.dynamic_slice_in_dim(positions, first_row, tok_local, 1)
    w_query, key_weight, value_weight, w_gate, w_up, gain_attn, gain_ffn = (
        lax.all_gather(w_query, "shard", axis=0, tiled=True),
        lax.all_gather(key_weight, "shard", axis=0, tiled=True),
        lax.all_gather(value_weight, "shard", axis=0, tiled=True),
        lax.all_gather(w_gate, "shard", axis=0, tiled=True),
        lax.all_gather(w_up, "shard", axis=0, tiled=True),
        lax.all_gather(gain_attn, "shard", axis=0, tiled=True),
        lax.all_gather(gain_ffn, "shard", axis=0, tiled=True),
    )
    w_out, w_down = (
        lax.all_gather(w_out, "shard", axis=1, tiled=True),
        lax.all_gather(w_down, "shard", axis=1, tiled=True),
    )
    gain_one = gain_attn.astype(jnp.float32)
    gain_two = gain_ffn.astype(jnp.float32)
    tok_rows = tokens.reshape(token_count, model_width).astype(jnp.float32)
    scale_one = lax.rsqrt(jnp.mean(tok_rows * tok_rows, axis=-1, keepdims=True) + norm_eps)
    normed_input = (tok_rows * scale_one * gain_one).astype(jnp.bfloat16)
    cosine_table, sine_values = tables(pos_here.reshape(token_count))
    query_heads_rows = rotary_apply(
        jnp.dot(normed_input, w_query, preferred_element_type=jnp.float32).reshape(
            token_count, heads_here, HEAD_SIZE
        ),
        cosine_table,
        sine_values,
    )
    query_heads_rows = query_heads_rows.astype(jnp.bfloat16).reshape(
        groups, tok_local, heads_here * HEAD_SIZE
    )
    key_rows = rotary_apply(
        jnp.dot(normed_input, key_weight, preferred_element_type=jnp.float32).reshape(
            token_count, kv_here, HEAD_SIZE
        ),
        cosine_table,
        sine_values,
    )
    key_rows = key_rows.astype(jnp.bfloat16).reshape(token_count, kv_width)
    value_rows = jnp.dot(normed_input, value_weight, preferred_element_type=jnp.float32).astype(
        jnp.bfloat16
    )
    keyval = jnp.concatenate([key_rows, value_rows], axis=-1).reshape(
        groups, tok_local, 2 * kv_width
    )
    gathered = lax.all_gather(keyval, "context", axis=1, tiled=True)

    def scores_of(group_queries, group_keyval, seg_query, pos_query, seg_keys, pos_keys):
        grouped_heads = group_queries.reshape(tok_local, kv_here, per_kv, HEAD_SIZE)
        key_head_rows = group_keyval[:, :kv_width].reshape(-1, kv_here, HEAD_SIZE)
        scores = (
            jnp.einsum(
                "bhgd,khd->hgbk", grouped_heads, key_head_rows, preferred_element_type=jnp.float32
            )
            * score_scale
        )
        allowed = visible(seg_query, pos_query, seg_keys, pos_keys)
        return (jnp.where(allowed[None, None], scores, -1e30), grouped_heads, key_head_rows)

    def attend_group(inputs):
        group_queries, group_keyval, seg_query, pos_query, seg_keys, pos_keys = inputs
        scores, grouped_heads, key_head_rows = scores_of(
            group_queries, group_keyval, seg_query, pos_query, seg_keys, pos_keys
        )
        top_score = jnp.max(scores, axis=-1, keepdims=True)
        exponent = jnp.exp(scores - top_score)
        totals = jnp.sum(exponent, axis=-1, keepdims=True)
        soft_weights = (exponent / totals).astype(jnp.bfloat16)
        value_head_rows = group_keyval[:, kv_width:].reshape(-1, kv_here, HEAD_SIZE)
        attended_output = jnp.einsum(
            "hgbk,khd->bhgd", soft_weights, value_head_rows, preferred_element_type=jnp.float32
        )
        return (
            attended_output.reshape(tok_local, heads_here * HEAD_SIZE),
            (top_score + jnp.log(totals))[..., 0],
        )

    attended_output, log_total = lax.map(
        attend_group, (query_heads_rows, gathered, seg_here, pos_here, segments, positions)
    )
    attended_low = attended_output.reshape(token_count, heads_here * HEAD_SIZE).astype(jnp.bfloat16)
    attn_sum = lax.psum(jnp.dot(attended_low, w_out, preferred_element_type=jnp.float32), "tensor")
    middle = tok_rows + attn_sum
    scale_two = lax.rsqrt(jnp.mean(middle * middle, axis=-1, keepdims=True) + norm_eps)
    normed_two = (middle * scale_two * gain_two).astype(jnp.bfloat16)
    gate_proj = jnp.dot(normed_two, w_gate, preferred_element_type=jnp.float32)
    up_proj = jnp.dot(normed_two, w_up, preferred_element_type=jnp.float32)
    sigmoid_gate = jax.nn.sigmoid(gate_proj)
    silu_gate = gate_proj * sigmoid_gate
    hidden = (silu_gate * up_proj).astype(jnp.bfloat16)
    ffn_sum = lax.psum(
        jnp.dot(hidden, w_down, preferred_element_type=jnp.float32).astype(jnp.bfloat16), "tensor"
    ).astype(jnp.float32)
    output = (middle + ffn_sum).astype(jnp.bfloat16).reshape(groups, tok_local, model_width)
    grad_low = cotangent.reshape(token_count, model_width)
    grad_out = grad_low.astype(jnp.float32)
    grad_hidden = contract_cols(grad_low, w_down)
    grad_w_down_t = contract_rows(grad_low, hidden)
    grad_gate = (
        grad_hidden * up_proj * sigmoid_gate * (1.0 + gate_proj * (1.0 - sigmoid_gate))
    ).astype(jnp.bfloat16)
    grad_up = (grad_hidden * silu_gate).astype(jnp.bfloat16)
    grad_w_gate = contract_rows(normed_two, grad_gate)
    grad_w_up = contract_rows(normed_two, grad_up)
    grad_normed_two = lax.psum(
        contract_cols(grad_gate, w_gate) + contract_cols(grad_up, w_up), "tensor"
    )
    back_two, grad_gain_two = norm_back(middle, scale_two, gain_two, grad_normed_two)
    grad_middle = grad_out + back_two
    grad_mid_low = grad_middle.astype(jnp.bfloat16)
    grad_w_out_t = contract_rows(grad_mid_low, attended_low)
    grad_attended = (
        contract_cols(grad_mid_low, w_out)
        .astype(jnp.bfloat16)
        .reshape(groups, tok_local, heads_here * HEAD_SIZE)
    )

    def attend_back(inputs):
        (
            group_queries,
            group_keyval,
            group_grad,
            group_total,
            seg_query,
            pos_query,
            seg_keys,
            pos_keys,
        ) = inputs
        scores, grouped_heads, key_head_rows = scores_of(
            group_queries, group_keyval, seg_query, pos_query, seg_keys, pos_keys
        )
        soft_weights = jnp.exp(scores - group_total[..., None])
        value_head_rows = group_keyval[:, kv_width:].reshape(-1, kv_here, HEAD_SIZE)
        grad_grouped = group_grad.reshape(tok_local, kv_here, per_kv, HEAD_SIZE)
        grad_weights = jnp.einsum(
            "bhgd,khd->hgbk", grad_grouped, value_head_rows, preferred_element_type=jnp.float32
        )
        inner = jnp.sum(soft_weights * grad_weights, axis=-1, keepdims=True)
        grad_scores = (soft_weights * (grad_weights - inner)).astype(jnp.bfloat16)
        grad_queries = (
            jnp.einsum(
                "hgbk,khd->bhgd", grad_scores, key_head_rows, preferred_element_type=jnp.float32
            )
            * score_scale
        )
        grad_keys = (
            jnp.einsum(
                "hgbk,bhgd->khd", grad_scores, grouped_heads, preferred_element_type=jnp.float32
            )
            * score_scale
        )
        grad_values = jnp.einsum(
            "hgbk,bhgd->khd",
            soft_weights.astype(jnp.bfloat16),
            grad_grouped,
            preferred_element_type=jnp.float32,
        )
        grad_keyval = jnp.concatenate(
            [grad_keys.reshape(-1, kv_width), grad_values.reshape(-1, kv_width)], axis=-1
        )
        return (grad_queries.reshape(tok_local, heads_here * HEAD_SIZE), grad_keyval)

    grad_queries, grad_keyval = lax.map(
        attend_back,
        (
            query_heads_rows,
            gathered,
            grad_attended,
            log_total,
            seg_here,
            pos_here,
            segments,
            positions,
        ),
    )
    grad_keyval = lax.psum_scatter(grad_keyval, "context", scatter_dimension=1, tiled=True)
    grad_query_rows = rotate_back(
        grad_queries.reshape(token_count, heads_here, HEAD_SIZE), cosine_table, sine_values
    )
    grad_query_rows = grad_query_rows.astype(jnp.bfloat16).reshape(
        token_count, heads_here * HEAD_SIZE
    )
    grad_key_rows = rotate_back(
        grad_keyval[..., :kv_width].reshape(token_count, kv_here, HEAD_SIZE),
        cosine_table,
        sine_values,
    )
    grad_key_rows = grad_key_rows.astype(jnp.bfloat16).reshape(token_count, kv_width)
    grad_value_rows = (
        grad_keyval[..., kv_width:].reshape(token_count, kv_width).astype(jnp.bfloat16)
    )
    grad_w_query = contract_rows(normed_input, grad_query_rows)
    grad_w_key = contract_rows(normed_input, grad_key_rows)
    grad_w_value = contract_rows(normed_input, grad_value_rows)
    partial_one = (
        contract_cols(grad_query_rows, w_query)
        + contract_cols(grad_key_rows, key_weight)
        + contract_cols(grad_value_rows, value_weight)
    )
    grad_normed = lax.psum(partial_one, "tensor")
    back_one, grad_gain_one = norm_back(tok_rows, scale_one, gain_one, grad_normed)
    tokens_grad = (
        (grad_middle + back_one).astype(jnp.bfloat16).reshape(groups, tok_local, model_width)
    )
    summed = (
        lax.psum_scatter(grad_w_query, ("shard", "context"), scatter_dimension=0, tiled=True),
        lax.psum_scatter(grad_w_key, ("shard", "context"), scatter_dimension=0, tiled=True),
        lax.psum_scatter(grad_w_value, ("shard", "context"), scatter_dimension=0, tiled=True),
        lax.psum_scatter(grad_w_out_t, ("shard", "context"), scatter_dimension=0, tiled=True),
        lax.psum_scatter(grad_w_gate, ("shard", "context"), scatter_dimension=0, tiled=True),
        lax.psum_scatter(grad_w_up, ("shard", "context"), scatter_dimension=0, tiled=True),
        lax.psum_scatter(grad_w_down_t, ("shard", "context"), scatter_dimension=0, tiled=True),
        lax.psum_scatter(grad_gain_one, ("shard", "context"), scatter_dimension=0, tiled=True),
        lax.psum_scatter(grad_gain_two, ("shard", "context"), scatter_dimension=0, tiled=True),
    )
    summed = (
        lax.all_gather(summed[0].astype(jnp.bfloat16), "context", axis=0, tiled=True).astype(
            jnp.float32
        ),
        lax.all_gather(summed[1].astype(jnp.bfloat16), "context", axis=0, tiled=True).astype(
            jnp.float32
        ),
        lax.all_gather(summed[2].astype(jnp.bfloat16), "context", axis=0, tiled=True).astype(
            jnp.float32
        ),
        lax.all_gather(summed[3].astype(jnp.bfloat16), "context", axis=0, tiled=True).astype(
            jnp.float32
        ),
        lax.all_gather(summed[4].astype(jnp.bfloat16), "context", axis=0, tiled=True).astype(
            jnp.float32
        ),
        lax.all_gather(summed[5].astype(jnp.bfloat16), "context", axis=0, tiled=True).astype(
            jnp.float32
        ),
        lax.all_gather(summed[6].astype(jnp.bfloat16), "context", axis=0, tiled=True).astype(
            jnp.float32
        ),
        lax.all_gather(summed[7].astype(jnp.bfloat16), "context", axis=0, tiled=True).astype(
            jnp.float32
        ),
        lax.all_gather(summed[8].astype(jnp.bfloat16), "context", axis=0, tiled=True).astype(
            jnp.float32
        ),
    )
    return (
        output,
        tokens_grad,
        summed[0],
        summed[1],
        summed[2],
        summed[3].T,
        summed[4],
        summed[5],
        summed[6].T,
        summed[7],
        summed[8],
    )


MESH = pl.DeviceIdType.MESH
RUN = 256
PAD = 128
NEG = -1e30
LOG2E = 1.4426950408889634
BF = jnp.bfloat16
F32 = jnp.float32
VLIM = 64 * 1024 * 1024


def mm(a, b):
    return lax.dot_general(a, b, (((1,), (0,)), ((), ())), preferred_element_type=F32)


def mm_nt(a, b):
    return lax.dot_general(a, b, (((1,), (1,)), ((), ())), preferred_element_type=F32)


def mm_tn(a, b):
    return lax.dot_general(a, b, (((0,), (0,)), ((), ())), preferred_element_type=F32)


def iota(shape, axis):
    return lax.broadcasted_iota(jnp.int32, shape, axis)


def one_hot(hit):
    return jnp.where(hit, 1.0, 0.0).astype(BF)


def pad_matrix(heads):
    shape = (heads * HEAD_SIZE, heads * PAD)
    row, col = iota(shape, 0), iota(shape, 1)
    lane = col & 127
    part = jnp.where(lane < 64, lane, lane - 16)
    return one_hot((row == (col >> 7) * HEAD_SIZE + part) & ((lane & 63) < 48))


def split_matrix():
    row, col = iota((RUN, RUN), 0), iota((RUN, RUN), 1)
    return one_hot(col == jnp.where(row < 128, 2 * row, 2 * row - 255))


def merge_matrix():
    row, col = iota((RUN, RUN), 0), iota((RUN, RUN), 1)
    return one_hot(col == (row >> 1) + (row & 1) * 128)


def rope_tables(run, cb_ref, sb_ref, cj_ref, sj_ref):
    cb, sb = cb_ref[pl.ds(run, 1), :], sb_ref[pl.ds(run, 1), :]
    cj, sj = cj_ref[...], sj_ref[...]
    return cb * cj - sb * sj, sb * cj + cb * sj


def rope(u, c, s):
    return u * c + pltpu.roll(u, 64, 1) * s


def rope_back(u, c, s):
    return u * c - pltpu.roll(u, 64, 1) * s


def vmem(*shape_dtype):
    return pl.BlockSpec(memory_space=pltpu.VMEM)


def entry_barrier(targets):
    bar = pltpu.get_barrier_semaphore()
    for t in targets:
        pl.semaphore_signal(bar, inc=1, device_id=t, device_id_type=MESH)
    pl.semaphore_wait(bar, len(targets))


def remote(src, dst, send, recv, target):
    return pltpu.make_async_remote_copy(
        src_ref=src, dst_ref=dst, send_sem=send, recv_sem=recv, device_id=target, device_id_type=MESH
    )


def first_kernel(nc, x_ref, dy_h, g_ref, cb_ref, sb_ref, cj_ref, sj_ref, wq_h, wk_h, wv_h, wo_h, wg_h, wu_h, wd_h,
                 xp_ref, dyp_ref, n1_ref, q_ref, kvp_ref, kvc_ref, wp_ref, gf_ref, wo_f, wg_f, wu_f, wd_f,
                 dy_v, wq_s, wk_s, wv_s, g_s, wo_v, wg_v, wu_v, wd_v, kv_send,
                 lsem, ssem, rsem, osem, csem, crem):
    s = lax.axis_index("shard")
    c = lax.axis_index("context")
    dh = g_s.shape[1] // 2
    own = pl.ds(pl.multiple_of(s * dh, dh), dh)
    other = {"shard": 1 - s}
    loads = [
        pltpu.make_async_copy(wq_h, wq_s.at[own], lsem.at[0]),
        pltpu.make_async_copy(wk_h, wk_s.at[own], lsem.at[1]),
        pltpu.make_async_copy(wv_h, wv_s.at[own], lsem.at[2]),
        pltpu.make_async_copy(g_ref, g_s.at[:, own], lsem.at[3]),
        pltpu.make_async_copy(wo_h, wo_v, lsem.at[4]),
        pltpu.make_async_copy(wg_h, wg_v, lsem.at[5]),
        pltpu.make_async_copy(wu_h, wu_v, lsem.at[6]),
        pltpu.make_async_copy(wd_h, wd_v, lsem.at[7]),
        pltpu.make_async_copy(dy_h, dy_v, lsem.at[8]),
    ]
    for cp in loads:
        cp.start()
    entry_barrier([other] + [{"context": lax.rem(c + i, nc)} for i in range(1, nc)])
    sends = [
        remote(wq_s.at[own], wq_s.at[own], ssem.at[0], rsem.at[0], other),
        remote(wk_s.at[own], wk_s.at[own], ssem.at[1], rsem.at[1], other),
        remote(wv_s.at[own], wv_s.at[own], ssem.at[2], rsem.at[2], other),
        remote(g_s.at[:, own], g_s.at[:, own], ssem.at[3], rsem.at[3], other),
        remote(wo_v, wo_f.at[:, own], ssem.at[4], rsem.at[4], other),
        remote(wg_v, wg_f.at[own], ssem.at[5], rsem.at[5], other),
        remote(wu_v, wu_f.at[own], ssem.at[6], rsem.at[6], other),
        remote(wd_v, wd_f.at[:, own], ssem.at[7], rsem.at[7], other),
    ]
    keeps = [
        pltpu.make_async_copy(wo_v, wo_f.at[:, own], osem.at[0]),
        pltpu.make_async_copy(wg_v, wg_f.at[own], osem.at[1]),
        pltpu.make_async_copy(wu_v, wu_f.at[own], osem.at[2]),
        pltpu.make_async_copy(wd_v, wd_f.at[:, own], osem.at[3]),
    ]
    for i in (3, 0, 1, 2, 4, 5, 6, 7):
        loads[i].wait()
        sends[i].start()
        if i >= 4:
            keeps[i - 4].start()
    half = x_ref.shape[0] // 2
    split = split_matrix()
    for i in range(x_ref.shape[0] // RUN):
        xb = mm(split, x_ref[pl.ds(i * RUN, RUN), :])
        xp_ref[pl.ds(i * 128, 128), :] = xb[:128].astype(BF)
        xp_ref[pl.ds(half + i * 128, 128), :] = xb[128:].astype(BF)
        if i == 0:
            sends[3].wait_recv()
        r = lax.rsqrt(jnp.mean(xb * xb, axis=-1, keepdims=True) + norm_eps)
        nb = (xb * r * g_s[0:1, :]).astype(BF)
        n1_ref[pl.ds(i * 128, 128), :] = nb[:128]
        n1_ref[pl.ds(half + i * 128, 128), :] = nb[128:]
    gf_ref[...] = g_s[...]
    hq, hk = wq_s.shape[1] // HEAD_SIZE, wk_s.shape[1] // HEAD_SIZE
    selq, selk = pad_matrix(hq), pad_matrix(hk)
    nq, nk = hq * PAD, hk * PAD
    for i in range(3):
        sends[i].wait_recv()
    for i in range(wq_s.shape[0] // RUN):
        rows = pl.ds(i * RUN, RUN)
        wp_ref[rows, 0:nq] = mm(wq_s[rows, :], selq).astype(BF)
        wp_ref[rows, nq : nq + nk] = mm(wk_s[rows, :], selk).astype(BF)
        wp_ref[rows, nq + nk :] = mm(wv_s[rows, :], selk).astype(BF)
    selkv = pad_matrix(2 * hk)
    runs = x_ref.shape[0] // RUN
    per = runs // 2
    kv_copies = []
    for run in range(runs):
        rows = pl.ds(run * RUN, RUN)
        y = mm(n1_ref[rows, :], wp_ref[...])
        ct, st = rope_tables(run, cb_ref, sb_ref, cj_ref, sj_ref)
        for h in range(hq):
            q_ref[rows, h * PAD : (h + 1) * PAD] = rope(y[:, h * PAD : (h + 1) * PAD], ct, st).astype(BF)
        kv = [rope(y[:, nq + h * PAD : nq + (h + 1) * PAD], ct, st).astype(BF) for h in range(hk)]
        kv = jnp.concatenate(kv + [y[:, nq + nk :].astype(BF)], axis=1)
        if run < per:
            kv_send[pl.ds(run * RUN, RUN), :] = mm_nt(kv, selkv).astype(BF)
            mine = pl.ds(pl.multiple_of((c * per + run) * RUN, RUN), RUN)
            for i in range(1, nc):
                cp = remote(kv_send.at[pl.ds(run * RUN, RUN)], kvp_ref.at[mine], csem.at[run, i], crem.at[run, i],
                            {"context": lax.rem(c + i, nc)})
                cp.start()
                kv_copies.append(cp)
            cp = pltpu.make_async_copy(kv_send.at[pl.ds(run * RUN, RUN)], kvp_ref.at[mine], csem.at[run, 0])
            cp.start()
            kv_copies.append(cp)
        else:
            kvc_ref[pl.ds((run - per) * RUN, RUN), :] = kv
    loads[8].wait()
    for i in range(x_ref.shape[0] // RUN):
        b = mm(split, dy_v[pl.ds(i * RUN, RUN), :]).astype(BF)
        dyp_ref[pl.ds(i * 128, 128), :] = b[:128]
        dyp_ref[pl.ds(half + i * 128, 128), :] = b[128:]
    for cp in kv_copies:
        cp.wait()
    for i in range(4):
        keeps[i].wait()
        sends[4 + i].wait_recv()
    for cp in sends:
        cp.wait_send()


def load_keys(kvp_ref, k_s, v_s, ones):
    hk = k_s.shape[0]
    sel = pad_matrix(2 * hk)
    lane = iota((RUN, PAD), 1)

    def step(i, _):
        rows = pl.ds(pl.multiple_of(i * RUN, RUN), RUN)
        kv = mm(kvp_ref[rows, :], sel)
        for g in range(hk):
            k_s[g, rows, :] = kv[:, g * PAD : (g + 1) * PAD].astype(BF)
            v = kv[:, (hk + g) * PAD : (hk + g + 1) * PAD]
            if ones:
                v = jnp.where(lane == 48, 1.0, v)
            v_s[g, rows, :] = v.astype(BF)
        return 0

    lax.fori_loop(0, kvp_ref.shape[0] // RUN, step, 0)


class Line:
    def __init__(self, n, chunk, jobs, pbuf, rbuf, obuf, sems):
        self.n, self.chunk, self.per = n, chunk, RUN // 2 // chunk
        self.count = jobs * self.per
        self.pbuf, self.rbuf, self.obuf = pbuf, rbuf, obuf
        self.rs, self.rr, self.bs, self.br = sems
        self.slots = self.count + 8 * (n - 1) // 3

    def pieces(self, h, i):
        n, chunk = self.n, self.chunk
        z = lax.axis_index("tensor")
        job, off = i // self.per, h * (RUN // 2) + lax.rem(i, self.per) * chunk
        rows = pl.ds(pl.multiple_of(job * RUN + off, chunk), chunk)
        there = pl.ds(pl.multiple_of(lax.rem(job, self.rbuf.shape[0] // RUN) * RUN + off, chunk), chunk)
        place = z if h == 0 else n - 1 - z
        up, down = jnp.minimum(z + 1, n - 1), jnp.maximum(z - 1, 0)
        ahead = {"tensor": up if h == 0 else down}
        back = {"tensor": down if h == 0 else up}
        fwd = remote(self.pbuf.at[rows], self.rbuf.at[there], self.rs.at[h, i], self.rr.at[h, i], ahead)
        ret = remote(self.obuf.at[rows], self.obuf.at[rows], self.bs.at[h, i], self.br.at[h, i], back)
        return rows, there, place, fwd, ret

    def reduce_step(self, h, i):
        rows, there, place, fwd, ret = self.pieces(h, i)
        n = self.n

        @pl.when(place == 0)
        def _():
            fwd.start()

        @pl.when(place > 0)
        def _():
            fwd.wait_recv()
            total = (self.rbuf[there, :].astype(F32) + self.pbuf[rows, :].astype(F32)).astype(BF)

            @pl.when(place < n - 1)
            def _():
                self.pbuf[rows, :] = total
                fwd.start()

            @pl.when(place == n - 1)
            def _():
                self.obuf[rows, :] = total
                ret.start()

    def spread_step(self, h, i):
        rows, there, place, fwd, ret = self.pieces(h, i)

        @pl.when(place < self.n - 1)
        def _():
            ret.wait_recv()

        @pl.when((place < self.n - 1) & (place > 0))
        def _():
            ret.start()

    def serve(self, t):
        n = self.n
        z = lax.axis_index("tensor")
        for h in range(2):
            place = z if h == 0 else n - 1 - z
            i = t - (place * 4) // 3

            @pl.when((i >= 0) & (i < self.count))
            def _():
                self.reduce_step(h, i)

            j = t - ((2 * (n - 1) - place) * 4) // 3

            @pl.when((j >= 0) & (j < self.count))
            def _():
                self.spread_step(h, j)

    def finish(self):
        def step(i, _):
            for h in range(2):
                rows, there, place, fwd, ret = self.pieces(h, i)

                @pl.when(place < self.n - 1)
                def _():
                    fwd.wait_send()

                @pl.when(place > 0)
                def _():
                    ret.wait_send()

            return 0

        lax.fori_loop(0, self.count, step, 0)


def run_items(items, serve):
    total = max(e for _, e, _ in items)

    def step(k, _):
        for lo, hi, body in items:
            pl.when((k >= lo) & (k < hi))(functools.partial(body, k))
        serve(k)
        return 0

    lax.fori_loop(0, total, step, 0)


class Square:
    def __init__(self, theirs_src, mine, theirs, r1, r2, res, shard_sems, sems):
        self.src, self.mine, self.theirs, self.r1, self.r2, self.res = theirs_src, mine, theirs, r1, r2, res
        self.shard_sems, self.send, self.recv = shard_sems[0], sems[0], sems[1]
        self.shard_recv = shard_sems[1]
        self.qr, self.cols = mine.shape[0] // 4, mine.shape[1]
        c = lax.axis_index("context")
        self.cy, self.cx = c // 2, lax.rem(c, 2)

    def at(self, y, x, half):
        w = self.cols // 2
        return (pl.ds(pl.multiple_of((2 * y + x) * self.qr, self.qr), self.qr), pl.ds(half * w, w))

    def peer(self, half, first):
        if (half == 0) == first:
            return {"context": 2 * self.cy + 1 - self.cx}
        return {"context": 2 * (1 - self.cy) + self.cx}

    def shard_copy(self):
        return remote(self.src, self.theirs, self.shard_sems, self.shard_recv, {"shard": 1 - lax.axis_index("shard")})

    def outer(self, half):
        if half == 0:
            return [(y, 1 - self.cx) for y in range(2)], [(y, self.cx) for y in range(2)]
        return [(1 - self.cy, x) for x in range(2)], [(self.cy, x) for x in range(2)]

    def p1(self, half, j):
        return remote(self.mine.at[self.at(*self.outer(half)[0][j], half)], self.r1.at[half, j],
                      self.send.at[0, half, j], self.recv.at[0, half, j], self.peer(half, True))

    def p2(self, half):
        q = (1 - self.cy, self.cx) if half == 0 else (self.cy, 1 - self.cx)
        return remote(self.mine.at[self.at(*q, half)], self.r2.at[half],
                      self.send.at[1, half, 0], self.recv.at[1, half, 0], self.peer(half, False))

    def p3(self, half):
        at = self.at(self.cy, self.cx, half)
        return remote(self.res.at[at], self.res.at[at], self.send.at[1, half, 1], self.recv.at[1, half, 1], self.peer(half, False))

    def p4(self, half, j):
        at = self.at(*self.outer(half)[1][j], half)
        return remote(self.res.at[at], self.res.at[at], self.send.at[2, half, j], self.recv.at[2, half, j], self.peer(half, True))

    def e0(self):
        self.shard_copy().start()

    def e1(self):
        self.shard_copy().wait_recv()
        step = self.qr

        def add(i, _):
            rows = pl.ds(pl.multiple_of(i * step, step), step)
            self.mine[rows, :] = (self.mine[rows, :].astype(F32) + self.theirs[rows, :].astype(F32)).astype(BF)
            return 0

        lax.fori_loop(0, self.mine.shape[0] // step, add, 0)
        for j in range(2):
            for half in range(2):
                self.p1(half, j).start()

    def e2(self):
        for half in range(2):
            for j in range(2):
                self.p1(half, j).wait_recv()
                at = self.at(*self.outer(half)[1][j], half)
                self.mine[at] = (self.mine[at].astype(F32) + self.r1[half, j].astype(F32)).astype(BF)
            self.p2(half).start()

    def e3(self):
        for half in range(2):
            self.p2(half).wait_recv()
            at = self.at(self.cy, self.cx, half)
            self.res[at] = (self.mine[at].astype(F32) + self.r2[half].astype(F32)).astype(BF)
            self.p3(half).start()

    def e4(self):
        for half in range(2):
            self.p3(half).wait_recv()
            for j in range(2):
                self.p4(half, j).start()

    def e5(self):
        for half in range(2):
            for j in range(2):
                self.p4(half, j).wait_recv()

    def done(self):
        self.shard_copy().wait_send()
        for half in range(2):
            for j in range(2):
                self.p1(half, j).wait_send()
                self.p4(half, j).wait_send()
            self.p2(half).wait_send()
            self.p3(half).wait_send()


def square_scratch(rows, cols, res=True):
    q, w = rows // 4, cols // 2
    out = [pltpu.VMEM((rows, cols), BF), pltpu.VMEM((rows, cols), BF), pltpu.VMEM((2, 2, q, w), BF), pltpu.VMEM((2, q, w), BF)]
    if res:
        out.append(pltpu.VMEM((rows, cols), BF))
    DMA = pltpu.SemaphoreType.DMA
    return out + [DMA, DMA, DMA((3, 2, 2)), DMA((3, 2, 2))]


def line_barrier(n, peers=()):
    z = lax.axis_index("tensor")
    bar = pltpu.get_barrier_semaphore()
    for t in peers:
        pl.semaphore_signal(bar, inc=1, device_id=t, device_id_type=MESH)

    @pl.when(z > 0)
    def _():
        pl.semaphore_signal(bar, inc=1, device_id={"tensor": jnp.maximum(z - 1, 0)}, device_id_type=MESH)

    @pl.when(z < n - 1)
    def _():
        pl.semaphore_signal(bar, inc=1, device_id={"tensor": jnp.minimum(z + 1, n - 1)}, device_id_type=MESH)

    pl.semaphore_wait(bar, len(peers) + jnp.minimum(z, 1) + jnp.minimum(n - 1 - z, 1))


def mid_kernel(n, chunk, kbase, qlim, q_ref, kvp_ref, kvc_ref, wo_ref, gf_ref, xp_h, dyp_h, wg_h, wu_h, wd_h,
               o_ref, op_ref, lse_ref, sum_ref, fp_h, gg_h, gu_h, gd_h,
               k_s, v_s, s_s, pbuf, rbuf, xp_ref, dyp_ref, wg_ref, wu_ref, wd_ref, n2_s, hid_s, dg_s, du_s,
               st_f, st_g, st_u, st_d, lsem, osem, rs, rr, bs, br):
    hk = k_s.shape[0]
    hq = q_ref.shape[1] // PAD
    rep = hq // hk
    runs = q_ref.shape[0] // RUN
    per = runs // 2
    blocks = kvp_ref.shape[0] // RUN
    scale = LOG2E / math.sqrt(HEAD_SIZE)
    pairs = [(xp_h, xp_ref), (wg_h, wg_ref), (wu_h, wu_ref), (dyp_h, dyp_ref), (wd_h, wd_ref)]
    loads = [pltpu.make_async_copy(a, b, lsem.at[i]) for i, (a, b) in enumerate(pairs)]
    for cp in loads:
        cp.start()
    line_barrier(n)
    line = Line(n, chunk, 2 * runs, pbuf, rbuf, sum_ref, (rs, rr, bs, br))
    load_keys(kvp_ref, k_s, v_s, True)

    def head(run, h, own):
        lane = iota((RUN, PAD), 1)
        diff = iota((RUN, RUN), 1) - iota((RUN, RUN), 0)
        rows = pl.ds(pl.multiple_of(run * RUN, RUN), RUN)
        cols = pl.ds(pl.multiple_of(h * PAD, PAD), PAD)
        g = h // rep
        q = q_ref[rows, cols]
        lim = qlim[run]
        top = None
        for b in range(blocks):
            s = mm_nt(q, k_s[g, pl.ds(b * RUN, RUN), :]) * scale
            room = lim - kbase[b]
            if own:
                s = s + jnp.where(room >= 0, 0.0, NEG)
            else:
                s = jnp.where(diff <= room, s, NEG)
            s_s[:, b * RUN : (b + 1) * RUN] = s
            top = s if top is None else jnp.maximum(top, s)
        if own:
            crow = pl.ds(pl.multiple_of((run - per) * RUN, RUN), RUN)
            kc = kvc_ref[crow, pl.ds(pl.multiple_of(g * PAD, PAD), PAD)]
            vc = kvc_ref[crow, pl.ds(pl.multiple_of((hk + g) * PAD, PAD), PAD)]
            vc = jnp.where(lane == 48, 1.0, vc.astype(F32)).astype(BF)
            s = jnp.where(diff <= 0, mm_nt(q, kc) * scale, NEG)
            s_s[:, blocks * RUN :] = s
            top = jnp.maximum(top, s)
        m = jnp.max(top, axis=1, keepdims=True)
        acc = None
        for b in range(blocks):
            p = jnp.exp2(s_s[:, b * RUN : (b + 1) * RUN] - m).astype(BF)
            o = mm(p, v_s[g, pl.ds(b * RUN, RUN), :])
            acc = o if acc is None else acc + o
        if own:
            p = jnp.exp2(s_s[:, blocks * RUN :] - m).astype(BF)
            acc = acc + mm(p, vc)
        total = acc[:, 48:49]
        op_ref[rows, cols] = (acc / total).astype(BF)
        lse = jnp.broadcast_to(m + jnp.log2(total), (RUN, PAD)).T
        lse_ref[pl.ds(pl.multiple_of((run * hq + h) * 8, 8), 8), :] = lse[0:8, :]

    def prompt(k):
        head(k // hq, lax.rem(k, hq), False)

    def cont(k):
        head(k // hq, lax.rem(k, hq), True)

    def project(k):
        @pl.when(lax.rem(k, hq) == hq - 1)
        def _():
            rows = pl.ds(pl.multiple_of(k // hq * RUN, RUN), RUN)
            o = mm_nt(op_ref[rows, :], pad_matrix(hq)).astype(BF)
            o_ref[rows, :] = o
            pbuf[rows, :] = mm(o, wo_ref[...]).astype(BF)

    ff = wg_ref.shape[1]
    first = runs * hq

    def ffn(k):
        i = (k - first) // 4
        part = lax.rem(k - first, 4)
        rows = pl.ds(pl.multiple_of(i * RUN, RUN), RUN)

        @pl.when(k == first)
        def _():
            for cp in loads:
                cp.wait()

        @pl.when(part == 0)
        def _():
            mid = xp_ref[rows, :].astype(F32) + sum_ref[rows, :].astype(F32)
            r = lax.rsqrt(jnp.mean(mid * mid, axis=-1, keepdims=True) + norm_eps)
            n2 = (mid * r * gf_ref[8:9, :]).astype(BF)
            n2_s[rows, :] = n2
            s_s[:, 0:ff] = mm(n2, wg_ref[...])

        @pl.when(part == 1)
        def _():
            s_s[:, ff : 2 * ff] = mm(n2_s[rows, :], wu_ref[...])

        @pl.when(part == 2)
        def _():
            dh = mm_nt(dyp_ref[rows, :], wd_ref[...])
            gate, up = s_s[:, 0:ff], s_s[:, ff : 2 * ff]
            sig = jax.nn.sigmoid(gate)
            silu = gate * sig
            hid_s[rows, :] = (silu * up).astype(BF)
            dg_s[rows, :] = (dh * up * sig * (1.0 + gate * (1.0 - sig))).astype(BF)
            du_s[rows, :] = (dh * silu).astype(BF)

        @pl.when(part == 3)
        def _():
            dn = mm_nt(dg_s[rows, :], wg_ref[...]) + mm_nt(du_s[rows, :], wu_ref[...])
            pbuf[pl.ds(pl.multiple_of((runs + i) * RUN, RUN), RUN), :] = dn.astype(BF)

    second = first + 4 * runs

    def down(k):
        i = k - second
        rows = pl.ds(pl.multiple_of(i * RUN, RUN), RUN)
        cp = pltpu.make_async_copy(st_f, fp_h.at[rows], osem.at[0])

        @pl.when(i > 0)
        def _():
            cp.wait()

        st_f[...] = mm(hid_s[rows, :], wd_ref[...]).astype(BF)
        cp.start()

    third = second + runs
    d = n2_s.shape[1]

    def grads(k):
        i = k - third
        cols = pl.ds(pl.multiple_of(i * RUN, RUN), RUN)
        cg = pltpu.make_async_copy(st_g, gg_h.at[cols], osem.at[1])
        cu = pltpu.make_async_copy(st_u, gu_h.at[cols], osem.at[2])

        @pl.when(i > 0)
        def _():
            cg.wait()
            cu.wait()

        nt = n2_s[:, cols].T
        st_g[...] = mm(nt, dg_s[...]).astype(BF)
        cg.start()
        st_u[...] = mm(nt, du_s[...]).astype(BF)
        cu.start()

    fourth = third + d // RUN
    wide = d // 2

    def grads_down(k):
        i = k - fourth
        cols = pl.ds(pl.multiple_of(i * RUN, RUN), RUN)
        cp = pltpu.make_async_copy(st_d, gd_h.at[:, cols], osem.at[3])

        @pl.when(i > 0)
        def _():
            cp.wait()

        ht = hid_s[:, cols].T
        for s in range(2):
            st_d[s] = mm(ht, dyp_ref[:, s * wide : (s + 1) * wide]).astype(BF)
        cp.start()

    end = fourth + ff // RUN
    lag = hq - 1
    items = [(0, per * hq, prompt), (per * hq, first, cont), (0, first, project), (first, second, ffn),
             (second, third, down), (third, fourth, grads), (fourth, end, grads_down)]
    if line.slots + lag > end:
        items.append((end, line.slots + lag, lambda k: None))
    run_items(items, lambda k: line.serve(k - lag))
    pltpu.make_async_copy(st_f, fp_h.at[pl.ds(0, RUN)], osem.at[0]).wait()
    pltpu.make_async_copy(st_g, gg_h.at[pl.ds(0, RUN)], osem.at[1]).wait()
    pltpu.make_async_copy(st_u, gu_h.at[pl.ds(0, RUN)], osem.at[2]).wait()
    pltpu.make_async_copy(st_d, gd_h.at[:, pl.ds(0, RUN)], osem.at[3]).wait()
    line.finish()


def back_kernel(n, nc, chunk, kbase, qlim, cb_ref, sb_ref, cj_ref, sj_ref, gf_ref, wo_ref, o_ref, op_ref,
                lse_ref, q_ref, kvp_ref, kvc_ref, dyp_h, xp_h, sum_h, fp_h, gg_h, gu_h,
                dm_h, g2_ref, go_ref, dqp_ref, dkvp_ref, dkvc_ref, sf_ref, gg_ref, gu_ref,
                pbuf, rbuf, ins, st_m, dmb_s, do_s, k_s, v_s, dk_s, dv_s, dq_s, delta_s, lsem, isem, osem, rs, rr, bs, br, *sq):
    s = lax.axis_index("shard")
    c = lax.axis_index("context")
    hk = k_s.shape[0]
    hq = q_ref.shape[1] // PAD
    rep = hq // hk
    rows_here = q_ref.shape[0]
    runs = rows_here // RUN
    per = runs // 2
    blocks = kvp_ref.shape[0] // RUN
    score = 1.0 / math.sqrt(HEAD_SIZE)
    scale = LOG2E * score
    dh = dmb_s.shape[1] // 2
    mine = pl.ds(pl.multiple_of(s * dh, dh), dh)
    yours = pl.ds(pl.multiple_of((1 - s) * dh, dh), dh)
    q1 = Square(gg_h.at[yours], sq[0], sq[1], sq[2], sq[3], gg_ref, (sq[4], sq[5]), (sq[6], sq[7]))
    q2 = Square(gu_h.at[yours], sq[8], sq[9], sq[10], sq[11], gu_ref, (sq[12], sq[13]), (sq[14], sq[15]))
    loads = [pltpu.make_async_copy(fp_h, pbuf, lsem.at[0]), pltpu.make_async_copy(gg_h.at[mine], q1.mine, lsem.at[1]),
             pltpu.make_async_copy(gu_h.at[mine], q2.mine, lsem.at[2])]

    def fetch(i, start):
        rows = pl.ds(pl.multiple_of(i * RUN, RUN), RUN)
        late = pl.ds(pl.multiple_of(rows_here + i * RUN, RUN), RUN)
        slot = lax.rem(i, 2)
        for j, src in enumerate((xp_h.at[rows], sum_h.at[rows], dyp_h.at[rows], sum_h.at[late])):
            cp = pltpu.make_async_copy(src, ins.at[slot, j], isem.at[slot, j])
            if start:
                cp.start()
            else:
                cp.wait()

    fetch(0, True)
    for cp in loads:
        cp.start()
    peers = [{"shard": 1 - s}, {"context": lax.rem(c + 2, 4)}, {"context": c + 1 - 2 * lax.rem(c, 2)}]
    line_barrier(n, peers)
    q1.e0()
    q2.e0()
    line = Line(n, chunk, runs, pbuf, rbuf, sf_ref, (rs, rr, bs, br))
    g2_ref[...] = jnp.zeros_like(g2_ref)
    dk_s[...] = jnp.zeros_like(dk_s)
    dv_s[...] = jnp.zeros_like(dv_s)
    loads[0].wait()

    def middle(i):
        rows = pl.ds(pl.multiple_of(i * RUN, RUN), RUN)
        slot = lax.rem(i, 2)

        @pl.when(i + 1 < runs)
        def _():
            fetch(i + 1, True)

        fetch(i, False)
        mid = ins[slot, 0].astype(F32) + ins[slot, 1].astype(F32)
        r = lax.rsqrt(jnp.mean(mid * mid, axis=-1, keepdims=True) + norm_eps)
        dn = ins[slot, 3].astype(F32)
        w = gf_ref[8:9, :] * dn
        inner = jnp.mean(w * mid, axis=-1, keepdims=True)
        dm = ins[slot, 2].astype(F32) + r * w - mid * (r * r * r) * inner
        cp = pltpu.make_async_copy(st_m, dm_h.at[rows], osem)

        @pl.when(i > 0)
        def _():
            cp.wait()

        st_m[...] = dm
        cp.start()
        g2_ref[...] += jnp.sum((dn * mid * r).reshape(RUN // 8, 8, mid.shape[1]), axis=0)
        dmb = dm.astype(BF)
        dmb_s[rows, :] = dmb
        do = mm_nt(dmb, wo_ref[...]).astype(BF)
        do_s[rows, :] = mm(do, pad_matrix(hq)).astype(BF)

    def out_grad(k):
        load_keys(kvp_ref, k_s, v_s, False)
        ot = o_ref[...].T
        for j in range(2):
            go_ref[j] = mm(ot, dmb_s[:, j * dh : (j + 1) * dh]).astype(BF)

    width = rep * RUN
    begin = runs + 1

    def pair(k, own):
        i, part = (k - begin) // 2, lax.rem(k - begin, 2)
        run, g = i // hk, lax.rem(i, hk)
        rows = pl.ds(pl.multiple_of(run * RUN, RUN), RUN)
        diff = iota((RUN, width), 0) - (iota((RUN, width), 1) & (RUN - 1))

        def stack(ref):
            parts = [ref[rows, pl.ds(pl.multiple_of((g * rep + j) * PAD, PAD), PAD)] for j in range(rep)]
            return jnp.concatenate(parts, axis=0)

        q, do = stack(q_ref), stack(do_s)

        @pl.when(part == 0)
        def _():
            op = stack(op_ref)
            delta_s[0:1, :] = jnp.sum((do.astype(F32) * op.astype(F32)).T, axis=0, keepdims=True)
            dq_s[...] = jnp.zeros_like(dq_s)

        delta = delta_s[0:1, :]
        lse = jnp.concatenate(
            [lse_ref[pl.ds(pl.multiple_of((run * hq + g * rep + j) * 8, 8), 1), :] for j in range(rep)], axis=1
        )
        lim = qlim[run]

        def tile(k, v, hide):
            p = jnp.exp2(hide(mm_nt(k, q) * scale - lse))
            ds = (p * (mm_nt(v, do) - delta)).astype(BF)
            return mm(ds, q), mm(p.astype(BF), do), mm_tn(ds, k)

        dq = dq_s[...]
        for bb in range(blocks // 2):
            b = part * (blocks // 2) + bb
            at = pl.ds(pl.multiple_of(b * RUN, RUN), RUN)
            room = lim - kbase[b]
            if own:
                hide = lambda t: t + jnp.where(room >= 0, 0.0, NEG)
            else:
                hide = lambda t: jnp.where(diff <= room, t, NEG)
            dk, dv, dd = tile(k_s[g, at, :], v_s[g, at, :], hide)
            dk_s[g, at, :] += dk
            dv_s[g, at, :] += dv
            dq = dq + dd
        dq_s[...] = dq

        @pl.when(part == 1)
        def _():
            total = dq_s[...]
            ct, st = rope_tables(run, cb_ref, sb_ref, cj_ref, sj_ref)
            if own:
                crow = pl.ds(pl.multiple_of((run - per) * RUN, RUN), RUN)
                kcol = pl.ds(pl.multiple_of(g * PAD, PAD), PAD)
                vcol = pl.ds(pl.multiple_of((hk + g) * PAD, PAD), PAD)
                dk, dv, dd = tile(kvc_ref[crow, kcol], kvc_ref[crow, vcol], lambda t: jnp.where(diff <= 0, t, NEG))
                total = total + dd
                dkvc_ref[crow, kcol] = rope_back(dk * score, ct, st).astype(BF)
                dkvc_ref[crow, vcol] = dv.astype(BF)
            for j in range(rep):
                dqp_ref[rows, pl.ds(pl.multiple_of((g * rep + j) * PAD, PAD), PAD)] = rope_back(
                    total[j * RUN : (j + 1) * RUN] * score, ct, st
                ).astype(BF)

    middle_end = begin + 2 * per * hk
    end = begin + 2 * runs * hk

    def pack(k):
        def one(i, _):
            rows = pl.ds(pl.multiple_of(i * RUN, RUN), RUN)
            parts = [(dk_s[g, rows, :] * score).astype(BF) for g in range(hk)]
            parts += [dv_s[g, rows, :].astype(BF) for g in range(hk)]
            dkvp_ref[rows, :] = mm_nt(jnp.concatenate(parts, axis=1), pad_matrix(2 * hk)).astype(BF)
            return 0

        lax.fori_loop(0, blocks, one, 0)

    def when(*events):
        def body(k):
            for e in events:
                e()

        return body

    def first_wait():
        loads[1].wait()
        loads[2].wait()

    items = [(0, runs, middle), (runs, begin, out_grad), (begin, middle_end, lambda k: pair(k, False)),
             (middle_end, end, lambda k: pair(k, True)), (end, end + 1, pack)]
    order = [(2, first_wait), (3, q1.e1), (5, q2.e1), (7, q1.e2), (10, q2.e2), (11, q1.e3), (13, q1.e4), (14, q2.e3), (16, q2.e4), (18, q1.e5), (20, q2.e5)]
    items += [(k, k + 1, when(e)) for k, e in order]
    if line.slots > end + 1:
        items.append((end + 1, line.slots, lambda k: None))
    run_items(items, line.serve)
    pltpu.make_async_copy(st_m, dm_h.at[pl.ds(0, RUN)], osem).wait()
    line.finish()
    q1.done()
    q2.done()


def last_kernel(n, nc, chunk, cb_ref, sb_ref, cj_ref, sj_ref, dkvp_ref, dkvc_ref, dqp_ref, n1_h, wp_ref, gf_ref, g2_ref,
                xp_h, sum_h, sf_h, dm_h, gd_h, go_h,
                out_ref, tg_ref, gg_ref, gd_ref, go_ref, gw_ref,
                n1_ref, xp_ref, ins, st_o, st_t, dm_ref, recv, dkv_s, gw_s, pbuf, rbuf, obuf, gpart, grecv,
                lsem, isem, osem, ssem, rsem, gs, gr, rs, rr, bs, br, *sq):
    s = lax.axis_index("shard")
    c = lax.axis_index("context")
    rows_here = dqp_ref.shape[0]
    half = rows_here // 2
    runs = rows_here // RUN
    per = runs // 2
    nq, nkv = dqp_ref.shape[1], dkvc_ref.shape[1]
    hk, hq = nkv // PAD // 2, nq // PAD
    d = n1_ref.shape[1]
    dh = d // 2
    mine = pl.ds(pl.multiple_of(s * dh, dh), dh)
    yours = pl.ds(pl.multiple_of((1 - s) * dh, dh), dh)
    q1 = Square(gd_h.at[1 - s], sq[0], sq[1], sq[2], sq[3], gd_ref, (sq[4], sq[5]), (sq[6], sq[7]))
    q2 = Square(go_h.at[1 - s], sq[8], sq[9], sq[10], sq[11], go_ref, (sq[12], sq[13]), (sq[14], sq[15]))
    q3 = Square(gw_s.at[yours], gw_s.at[mine], sq[16], sq[17], sq[18], gw_ref, (sq[19], sq[20]), (sq[21], sq[22]))
    pairs = [(n1_h, n1_ref), (gd_h.at[s], q1.mine), (go_h.at[s], q2.mine), (xp_h, xp_ref), (dm_h, dm_ref)]
    loads = [pltpu.make_async_copy(a, b, lsem.at[i]) for i, (a, b) in enumerate(pairs)]
    for cp in loads:
        cp.start()
    peers = [{"shard": lax.rem(s + i // nc, 2), "context": lax.rem(c + lax.rem(i, nc), nc)} for i in range(1, 2 * nc)]
    line_barrier(n, peers)
    copies = []
    for i in range(1, nc):
        to = lax.rem(c + i, nc)
        cp = remote(dkvp_ref.at[pl.ds(pl.multiple_of(to * half, half), half)], recv.at[i - 1], ssem.at[i - 1], rsem.at[i - 1],
                    {"context": to})
        cp.start()
        copies.append(cp)
    q1.e0()
    q2.e0()
    line = Line(n, chunk, runs, pbuf, rbuf, obuf, (rs, rr, bs, br))

    def normed(run, job):
        rows = pl.ds(run * RUN, RUN)
        dn = mm_nt(dqp_ref[rows, :], wp_ref[:, 0:nq]) + mm_nt(dkv_s[rows, :], wp_ref[:, nq:])
        pbuf[pl.ds(job * RUN, RUN), :] = dn.astype(BF)

    wide_q = hq * HEAD_SIZE

    def start(k):
        dkv_s[pl.ds(half, half), :] = dkvc_ref[...]
        normed(per, 0)

    def more(k):
        for i in range(1, per):
            normed(per + i, i)

    def grads_q(k):
        i = k - 2

        @pl.when(i == 0)
        def _():
            loads[0].wait()

        dq_u = mm_nt(dqp_ref[...], pad_matrix(hq)).astype(BF)
        for j in range(2):
            cols = pl.ds(pl.multiple_of((2 * i + j) * RUN, RUN), RUN)
            gw_s[cols, 0:wide_q] = mm(n1_ref[:, cols].T, dq_u).astype(BF)

    nq_items = d // RUN // 2

    def keys(k):
        for cp in copies:
            cp.wait_recv()
        selkv = pad_matrix(2 * hk)
        for run in range(per):
            rows = pl.ds(run * RUN, RUN)
            at = pl.ds(pl.multiple_of(c * half + run * RUN, RUN), RUN)
            total = mm(dkvp_ref[at, :], selkv)
            for i in range(nc - 1):
                total = total + mm(recv[i, rows, :], selkv)
            ct, st = rope_tables(run, cb_ref, sb_ref, cj_ref, sj_ref)
            for g in range(hk):
                dkv_s[rows, g * PAD : (g + 1) * PAD] = rope_back(total[:, g * PAD : (g + 1) * PAD], ct, st).astype(BF)
            dkv_s[rows, hk * PAD :] = total[:, hk * PAD :].astype(BF)
            normed(run, per + run)

    def grads_kv(k):
        dkv_u = mm_nt(dkv_s[...], pad_matrix(2 * hk)).astype(BF)

        def one(i, _):
            cols = pl.ds(pl.multiple_of(i * RUN, RUN), RUN)
            gw_s[cols, wide_q:] = mm(n1_ref[:, cols].T, dkv_u).astype(BF)
            return 0

        lax.fori_loop(0, d // RUN, one, 0)
        q3.e0()

    def take(ref, lo, hi):
        return jnp.concatenate([ref[pl.ds(pl.multiple_of(lo, 128), 128), :], ref[pl.ds(pl.multiple_of(hi, 128), 128), :]], axis=0).astype(F32)

    def fetch(i, start):
        slot = lax.rem(i, 2)
        for j, src in enumerate((sum_h, sf_h)):
            for m in range(2):
                at = pl.ds(pl.multiple_of(m * half + i * 128, 128), 128)
                cp = pltpu.make_async_copy(src.at[at], ins.at[slot, j, pl.ds(m * 128, 128)], isem.at[slot, j, m])
                if start:
                    cp.start()
                else:
                    cp.wait()

    fetch(0, True)
    ak = 2 + nq_items
    out_at = ak + 2

    def output(k):
        i = k - out_at

        @pl.when(i == 0)
        def _():
            for cp in loads[3:]:
                cp.wait()
            gpart[0:8, :] = jnp.zeros((8, d), F32)
            gpart[8:16, :] = g2_ref[...]

        @pl.when(i + 1 < runs)
        def _():
            fetch(i + 1, True)

        fetch(i, False)
        slot = lax.rem(i, 2)
        lo, hi = i * 128, half + i * 128
        mid = take(xp_ref, lo, hi) + ins[slot, 0].astype(F32)
        rows = pl.ds(pl.multiple_of(i * RUN, RUN), RUN)
        cp = pltpu.make_async_copy(st_o, out_ref.at[rows], osem.at[0])

        @pl.when(i > 0)
        def _():
            cp.wait()

        st_o[...] = mm(merge_matrix(), (mid + ins[slot, 1].astype(F32)).astype(BF)).astype(BF)
        cp.start()

    def finals(i):
        lo, hi = i * 128, half + i * 128
        x = take(xp_ref, lo, hi)
        dn = take(obuf, half + lo, lo)
        r = lax.rsqrt(jnp.mean(x * x, axis=-1, keepdims=True) + norm_eps)
        w = gf_ref[0:1, :] * dn
        inner = jnp.mean(w * x, axis=-1, keepdims=True)
        tg = take(dm_ref, lo, hi) + (r * w - x * (r * r * r) * inner)
        rows = pl.ds(pl.multiple_of(i * RUN, RUN), RUN)
        cp = pltpu.make_async_copy(st_t, tg_ref.at[rows], osem.at[1])

        @pl.when(i > 0)
        def _():
            cp.wait()

        st_t[...] = mm(merge_matrix(), tg.astype(BF)).astype(BF)
        cp.start()
        gpart[0:8, :] += jnp.sum((dn * x * r).reshape(RUN // 8, 8, d), axis=0)

    ready = (per + 1) * line.per + 8 * (n - 1) // 3

    def tail(k):
        j = (k - ready) // line.per
        part = lax.rem(k - ready, line.per)

        @pl.when(part < 2)
        def _():
            finals(2 * j + part)

    def event(e):
        return lambda k: e()

    def begin_squares():
        loads[1].wait()
        loads[2].wait()
        q1.e1()

    last = ready + (per - 1) * line.per
    items = [(0, 1, start), (1, 2, more), (2, ak, grads_q), (ak, ak + 1, keys), (ak + 1, ak + 2, grads_kv),
             (out_at, out_at + runs, output), (ready, last, tail), (last, line.slots, lambda k: None)]
    order = [(3, begin_squares), (4, q2.e1), (6, q1.e2), (7, q2.e2), (9, q1.e3), (10, q2.e3), (10, q3.e1), (11, q1.e4), (12, q2.e4), (13, q3.e2),
             (15, q3.e3), (17, q3.e4), (18, q1.e5), (18, q2.e5), (20, q3.e5)]
    items += [(k, k + 1, event(e)) for k, e in order]
    run_items(items, line.serve)
    for i in range(2):
        finals(jnp.int32(2 * (per - 1) + i))
    me = s * nc + c
    sums = jnp.concatenate(
        [jnp.broadcast_to(jnp.sum(gpart[k * 8 : (k + 1) * 8, :], axis=0, keepdims=True), (8, d)) for k in range(2)], axis=0
    )
    grecv[me] = sums
    gcopies = []
    for i, t in enumerate(peers):
        cp = remote(grecv.at[me], grecv.at[me], gs.at[i], gr.at[i], t)
        cp.start()
        gcopies.append(cp)
    line.finish()
    for q in (q1, q2, q3):
        q.done()
    for cp in copies:
        cp.wait_send()
    for cp in gcopies:
        cp.wait()
    pltpu.make_async_copy(st_o, out_ref.at[pl.ds(0, RUN)], osem.at[0]).wait()
    pltpu.make_async_copy(st_t, tg_ref.at[pl.ds(0, RUN)], osem.at[1]).wait()
    total = grecv[0]
    for i in range(1, 2 * nc):
        total = total + grecv[i]
    gg_ref[...] = total


def fast(
    tokens, w_query, key_weight, value_weight, w_out, w_gate, w_up, w_down, gain_attn, gain_ffn, segments, positions, cotangent, n, nc
):
    _, rows, d = tokens.shape
    half = rows // 2
    runs = rows // RUN
    per = runs // 2
    prompt = segments.shape[1] // 2
    blocks = prompt // RUN
    dq, dk = w_query.shape[1], key_weight.shape[1]
    hq, hk = dq // HEAD_SIZE, dk // HEAD_SIZE
    nq, nk = hq * PAD, hk * PAD
    ff = w_gate.shape[1]
    dh = d // 2
    c = lax.axis_index("context")
    x = tokens.reshape(rows, d)
    dy = cotangent.reshape(rows, d)
    kbase = positions[0, 0 :: 2 * RUN]
    seg_here = lax.dynamic_slice_in_dim(segments[0], c * rows, rows, 0)
    pos_here = lax.dynamic_slice_in_dim(positions[0], c * rows, rows, 0)
    qbase = jnp.concatenate([pos_here[0 :: 2 * RUN], pos_here[1 :: 2 * RUN]])
    qlim = jnp.concatenate([pos_here[0 :: 2 * RUN], seg_here[1 :: 2 * RUN] * CLEN - 1])
    freq = np.exp(np.arange(HEAD_SIZE // 2, dtype=np.float32) * np.float32(-2.0 * math.log(rope_base) / HEAD_SIZE)).astype(np.float32)
    lanes = np.zeros((PAD,), np.float32)
    lanes[0:48] = freq
    lanes[64:112] = freq
    sign = np.where(np.arange(PAD) < 64, -1.0, 1.0).astype(np.float32)
    inner = np.arange(RUN, dtype=np.float64)[:, None] * lanes[None, :].astype(np.float64)
    cj = jnp.asarray(np.cos(inner).astype(np.float32))
    sj = jnp.asarray((np.sin(inner) * sign).astype(np.float32))
    angle = qbase.astype(F32)[:, None] * jnp.asarray(lanes)[None, :]
    cb = jnp.cos(angle)
    sb = jnp.sin(angle) * jnp.asarray(sign)[None, :]
    gains = jnp.concatenate([jnp.broadcast_to(g.astype(F32)[None, :], (8, dh)) for g in (gain_attn, gain_ffn)], axis=0)

    V = pl.BlockSpec(memory_space=pltpu.VMEM)
    S = pl.BlockSpec(memory_space=pltpu.SMEM)
    A = pl.BlockSpec(memory_space=pl.ANY)
    sds = jax.ShapeDtypeStruct
    DMA = pltpu.SemaphoreType.DMA

    def call(kernel, ins, outs, scratch, collective=None, flops=0):
        params = dict(vmem_limit_bytes=VLIM - 64 * 1024)
        if collective is not None:
            params.update(collective_id=collective, has_side_effects=True)
        args = [a for a, _ in ins]
        return pl.pallas_call(
            kernel,
            out_shape=[o for o, _ in outs],
            in_specs=[sp for _, sp in ins],
            out_specs=[sp for _, sp in outs],
            scratch_shapes=scratch,
            compiler_params=pltpu.CompilerParams(**params),
            cost_estimate=pl.CostEstimate(flops=flops, bytes_accessed=0, transcendentals=0),
        )(*args)

    rope_in = [(cb, V), (sb, V), (cj, V), (sj, V)]
    xp, dyp, n1, q, kvp, kvc, wp, gf, wo, wg, wu, wd = call(
        functools.partial(first_kernel, nc),
        [(x, V), (dy, A), (gains, A)] + rope_in + [(w_query, A), (key_weight, A), (value_weight, A), (w_out, A), (w_gate, A), (w_up, A), (w_down, A)],
        [
            (sds((rows, d), BF), V), (sds((rows, d), BF), V), (sds((rows, d), BF), V), (sds((rows, nq), BF), V),
            (sds((prompt, 2 * dk), BF), A), (sds((half, 2 * nk), BF), V), (sds((d, nq + 2 * nk), BF), V), (sds((16, d), F32), V),
            (sds((dq, d), BF), A), (sds((d, ff), BF), A), (sds((d, ff), BF), A), (sds((ff, d), BF), A),
        ],
        [
            pltpu.VMEM((rows, d), BF), pltpu.VMEM((d, dq), BF), pltpu.VMEM((d, dk), BF), pltpu.VMEM((d, dk), BF), pltpu.VMEM((16, d), F32),
            pltpu.VMEM((dq, dh), BF), pltpu.VMEM((dh, ff), BF), pltpu.VMEM((dh, ff), BF), pltpu.VMEM((ff, dh), BF),
            pltpu.VMEM((half, 2 * dk), BF),
            DMA((9,)), DMA((8,)), DMA((8,)), DMA((4,)), DMA((per, nc)), DMA((per, nc)),
        ],
        collective=0, flops=60 * 10**9,
    )

    chunk = 32
    per_half = RUN // 2 // chunk

    def sums(jobs):
        return [DMA((2, jobs * per_half))] * 4

    o, op, lse, sum12, fp, gg, gu, gd = call(
        functools.partial(mid_kernel, n, chunk),
        [(kbase, S), (qlim, S), (q, V), (kvp, V), (kvc, V), (wo, V), (gf, V), (xp, A), (dyp, A), (wg, A), (wu, A), (wd, A)],
        [(sds((rows, dq), BF), V), (sds((rows, nq), BF), V), (sds((runs * hq * 8, RUN), F32), V), (sds((2 * rows, d), BF), V),
         (sds((rows, d), BF), A), (sds((d, ff), BF), A), (sds((d, ff), BF), A), (sds((2, ff, dh), BF), A)],
        [pltpu.VMEM((hk, prompt, PAD), BF), pltpu.VMEM((hk, prompt, PAD), BF), pltpu.VMEM((RUN, prompt + RUN), F32),
         pltpu.VMEM((2 * rows, d), BF), pltpu.VMEM((rows, d), BF), pltpu.VMEM((rows, d), BF), pltpu.VMEM((rows, d), BF),
         pltpu.VMEM((d, ff), BF), pltpu.VMEM((d, ff), BF), pltpu.VMEM((ff, d), BF),
         pltpu.VMEM((rows, d), BF), pltpu.VMEM((rows, ff), BF), pltpu.VMEM((rows, ff), BF), pltpu.VMEM((rows, ff), BF),
         pltpu.VMEM((RUN, d), BF), pltpu.VMEM((RUN, ff), BF), pltpu.VMEM((RUN, ff), BF), pltpu.VMEM((2, RUN, dh), BF),
         DMA((5,)), DMA((4,))] + sums(2 * runs),
        collective=1, flops=160 * 10**9,
    )
    dm, g2, go, dqp, dkvp, dkvc, sf, gg, gu = call(
        functools.partial(back_kernel, n, nc, chunk),
        [(kbase, S), (qlim, S)] + rope_in
        + [(gf, V), (wo, V), (o, V), (op, V), (lse, V), (q, V), (kvp, V), (kvc, V), (dyp, A), (xp, A), (sum12, A), (fp, A), (gg, A), (gu, A)],
        [(sds((rows, d), F32), A), (sds((8, d), F32), V), (sds((2, dq, dh), BF), V), (sds((rows, nq), BF), V),
         (sds((prompt, 2 * dk), BF), V), (sds((half, 2 * nk), BF), V), (sds((rows, d), BF), V), (sds((dh, ff), BF), V), (sds((dh, ff), BF), V)],
        [pltpu.VMEM((rows, d), BF), pltpu.VMEM((rows, d), BF), pltpu.VMEM((2, 4, RUN, d), BF), pltpu.VMEM((RUN, d), F32),
         pltpu.VMEM((rows, d), BF), pltpu.VMEM((rows, nq), BF), pltpu.VMEM((hk, prompt, PAD), BF), pltpu.VMEM((hk, prompt, PAD), BF),
         pltpu.VMEM((hk, prompt, PAD), F32), pltpu.VMEM((hk, prompt, PAD), F32), pltpu.VMEM((hq // hk * RUN, PAD), F32),
         pltpu.VMEM((8, hq // hk * RUN), F32), DMA((3,)), DMA((2, 4)), DMA] + sums(runs)
        + square_scratch(dh, ff, False) + square_scratch(dh, ff, False),
        collective=2, flops=100 * 10**9,
    )
    out, tg, gains_grad, gd, go, gw = call(
        functools.partial(last_kernel, n, nc, chunk),
        rope_in + [(dkvp, V), (dkvc, V), (dqp, V), (n1, A), (wp, V), (gf, V), (g2, V), (xp, A), (sum12, A), (sf, A), (dm, A), (gd, A), (go, A)],
        [(sds((rows, d), BF), A), (sds((rows, d), BF), A), (sds((16, d), F32), V), (sds((ff, dh), BF), V), (sds((dq, dh), BF), V),
         (sds((dh, dq + 2 * dk), BF), V)],
        [pltpu.VMEM((rows, d), BF), pltpu.VMEM((rows, d), BF), pltpu.VMEM((2, 2, RUN, d), BF), pltpu.VMEM((RUN, d), BF), pltpu.VMEM((RUN, d), BF),
         pltpu.VMEM((rows, d), F32),
         pltpu.VMEM((nc - 1, half, 2 * dk), BF), pltpu.VMEM((rows, 2 * nk), BF), pltpu.VMEM((d, dq + 2 * dk), BF),
         pltpu.VMEM((rows, d), BF), pltpu.VMEM((rows, d), BF), pltpu.VMEM((rows, d), BF),
         pltpu.VMEM((16, d), F32), pltpu.VMEM((2 * nc, 16, d), F32), DMA((5,)), DMA((2, 2, 2)), DMA((2,)), DMA((nc - 1,)), DMA((nc - 1,)),
         DMA((2 * nc - 1,)), DMA((2 * nc - 1,))] + sums(runs)
        + square_scratch(ff, dh, False) + square_scratch(dq, dh, False) + square_scratch(dh, dq + 2 * dk, False)[1:],
        collective=3, flops=160 * 10**9,
    )
    s = lax.axis_index("shard")
    g1o = lax.dynamic_slice_in_dim(gains_grad[0], s * dh, dh, 0)
    g2o = lax.dynamic_slice_in_dim(gains_grad[8], s * dh, dh, 0)
    return (
        out[None], tg[None],
        gw[:, :dq].astype(F32), gw[:, dq : dq + dk].astype(F32), gw[:, dq + dk :].astype(F32),
        go.astype(F32), gg.astype(F32), gu.astype(F32), gd.astype(F32), g1o, g2o,
    )


def body(mesh, *args):
    tokens, w_query, segments = args[0], args[1], args[10]
    n, nc = mesh.shape["tensor"], mesh.shape["context"]
    rows = tokens.shape[1]
    if (tokens.shape[0] == 1 and rows % (4 * CLEN) == 0 and n > 1 and nc == 4 and mesh.shape["shard"] == 2
            and segments.shape[1] == rows * nc):
        return fast(*args, n, nc)
    return general(*args)


def solution(mesh):
    in_specs = (
        P("shard", "context", None),
        P("shard", "tensor"),
        P("shard", "tensor"),
        P("shard", "tensor"),
        P("tensor", "shard"),
        P("shard", "tensor"),
        P("shard", "tensor"),
        P("tensor", "shard"),
        P("shard"),
        P("shard"),
        P("shard", None),
        P("shard", None),
        P("shard", "context", None),
    )
    out_specs = (
        P("shard", "context", None),
        P("shard", "context", None),
        P("shard", "tensor"),
        P("shard", "tensor"),
        P("shard", "tensor"),
        P("tensor", "shard"),
        P("shard", "tensor"),
        P("shard", "tensor"),
        P("tensor", "shard"),
        P("shard"),
        P("shard"),
    )
    return jax.shard_map(functools.partial(body, mesh), mesh=mesh, in_specs=in_specs, out_specs=out_specs, check_vma=False)
```

```python
import functools
import math

import jax
import jax.numpy as jnp
import numpy as np
from jax import lax
from jax.experimental import pallas as pl
from jax.experimental.pallas import tpu as pltpu
from jax.sharding import PartitionSpec as P

HEAD_SIZE = 96
CLEN = 256


rope_base = 100000.0
norm_eps = 1e-05


def tables(positions):
    half_width = HEAD_SIZE // 2
    frequency = jnp.exp(
        jnp.arange(half_width, dtype=jnp.float32) * (-2.0 * math.log(rope_base) / HEAD_SIZE)
    )
    angles = positions.astype(jnp.float32)[:, None] * frequency[None, :]
    return (jnp.cos(angles)[:, None, :], jnp.sin(angles)[:, None, :])


def rotary_apply(heads, cosine_table, sine_values):
    half_width = HEAD_SIZE // 2
    front_half = heads[..., :half_width]
    back_half = heads[..., half_width:]
    return jnp.concatenate(
        [
            front_half * cosine_table - back_half * sine_values,
            back_half * cosine_table + front_half * sine_values,
        ],
        axis=-1,
    )


def rotate_back(heads, cosine_table, sine_values):
    half_width = HEAD_SIZE // 2
    front_half = heads[..., :half_width]
    back_half = heads[..., half_width:]
    return jnp.concatenate(
        [
            front_half * cosine_table + back_half * sine_values,
            back_half * cosine_table - front_half * sine_values,
        ],
        axis=-1,
    )


def contract_rows(left, right):
    return lax.dot_general(
        left, right, (((0,), (0,)), ((), ())), preferred_element_type=jnp.float32
    )


def contract_cols(left, right):
    return lax.dot_general(
        left, right, (((1,), (1,)), ((), ())), preferred_element_type=jnp.float32
    )


def norm_back(tok_rows, norm_scale, gain, grad_normed):
    weighted = gain * grad_normed
    inner = jnp.mean(weighted * tok_rows, axis=-1, keepdims=True)
    grad_rows = norm_scale * weighted - tok_rows * (norm_scale * norm_scale * norm_scale) * inner
    grad_gain = jnp.sum(grad_normed * tok_rows * norm_scale, axis=0)
    return (grad_rows, grad_gain)


def visible(seg_query, pos_query, seg_keys, pos_keys):
    own = (seg_keys[None, :] == seg_query[:, None]) & (pos_keys[None, :] <= pos_query[:, None])
    branch = (
        (seg_keys[None, :] == 0)
        & (seg_query[:, None] > 0)
        & (pos_keys[None, :] < seg_query[:, None] * CLEN)
    )
    return own | branch


def general(
    tokens,
    w_query,
    key_weight,
    value_weight,
    w_out,
    w_gate,
    w_up,
    w_down,
    gain_attn,
    gain_ffn,
    segments,
    positions,
    cotangent,
):
    groups, tok_local, model_width = tokens.shape
    token_count = groups * tok_local
    heads_here = w_query.shape[1] // HEAD_SIZE
    kv_here = key_weight.shape[1] // HEAD_SIZE
    per_kv = heads_here // kv_here
    kv_width = kv_here * HEAD_SIZE
    score_scale = 1.0 / math.sqrt(HEAD_SIZE)
    context_index = lax.axis_index("context")
    first_row = context_index * tok_local
    seg_here = lax.dynamic_slice_in_dim(segments, first_row, tok_local, 1)
    pos_here = lax.dynamic_slice_in_dim(positions, first_row, tok_local, 1)
    w_query, key_weight, value_weight, w_gate, w_up, gain_attn, gain_ffn = (
        lax.all_gather(w_query, "shard", axis=0, tiled=True),
        lax.all_gather(key_weight, "shard", axis=0, tiled=True),
        lax.all_gather(value_weight, "shard", axis=0, tiled=True),
        lax.all_gather(w_gate, "shard", axis=0, tiled=True),
        lax.all_gather(w_up, "shard", axis=0, tiled=True),
        lax.all_gather(gain_attn, "shard", axis=0, tiled=True),
        lax.all_gather(gain_ffn, "shard", axis=0, tiled=True),
    )
    w_out, w_down = (
        lax.all_gather(w_out, "shard", axis=1, tiled=True),
        lax.all_gather(w_down, "shard", axis=1, tiled=True),
    )
    gain_one = gain_attn.astype(jnp.float32)
    gain_two = gain_ffn.astype(jnp.float32)
    tok_rows = tokens.reshape(token_count, model_width).astype(jnp.float32)
    scale_one = lax.rsqrt(jnp.mean(tok_rows * tok_rows, axis=-1, keepdims=True) + norm_eps)
    normed_input = (tok_rows * scale_one * gain_one).astype(jnp.bfloat16)
    cosine_table, sine_values = tables(pos_here.reshape(token_count))
    query_heads_rows = rotary_apply(
        jnp.dot(normed_input, w_query, preferred_element_type=jnp.float32).reshape(
            token_count, heads_here, HEAD_SIZE
        ),
        cosine_table,
        sine_values,
    )
    query_heads_rows = query_heads_rows.astype(jnp.bfloat16).reshape(
        groups, tok_local, heads_here * HEAD_SIZE
    )
    key_rows = rotary_apply(
        jnp.dot(normed_input, key_weight, preferred_element_type=jnp.float32).reshape(
            token_count, kv_here, HEAD_SIZE
        ),
        cosine_table,
        sine_values,
    )
    key_rows = key_rows.astype(jnp.bfloat16).reshape(token_count, kv_width)
    value_rows = jnp.dot(normed_input, value_weight, preferred_element_type=jnp.float32).astype(
        jnp.bfloat16
    )
    keyval = jnp.concatenate([key_rows, value_rows], axis=-1).reshape(
        groups, tok_local, 2 * kv_width
    )
    gathered = lax.all_gather(keyval, "context", axis=1, tiled=True)

    def scores_of(group_queries, group_keyval, seg_query, pos_query, seg_keys, pos_keys):
        grouped_heads = group_queries.reshape(tok_local, kv_here, per_kv, HEAD_SIZE)
        key_head_rows = group_keyval[:, :kv_width].reshape(-1, kv_here, HEAD_SIZE)
        scores = (
            jnp.einsum(
                "bhgd,khd->hgbk", grouped_heads, key_head_rows, preferred_element_type=jnp.float32
            )
            * score_scale
        )
        allowed = visible(seg_query, pos_query, seg_keys, pos_keys)
        return (jnp.where(allowed[None, None], scores, -1e30), grouped_heads, key_head_rows)

    def attend_group(inputs):
        group_queries, group_keyval, seg_query, pos_query, seg_keys, pos_keys = inputs
        scores, grouped_heads, key_head_rows = scores_of(
            group_queries, group_keyval, seg_query, pos_query, seg_keys, pos_keys
        )
        top_score = jnp.max(scores, axis=-1, keepdims=True)
        exponent = jnp.exp(scores - top_score)
        totals = jnp.sum(exponent, axis=-1, keepdims=True)
        soft_weights = (exponent / totals).astype(jnp.bfloat16)
        value_head_rows = group_keyval[:, kv_width:].reshape(-1, kv_here, HEAD_SIZE)
        attended_output = jnp.einsum(
            "hgbk,khd->bhgd", soft_weights, value_head_rows, preferred_element_type=jnp.float32
        )
        return (
            attended_output.reshape(tok_local, heads_here * HEAD_SIZE),
            (top_score + jnp.log(totals))[..., 0],
        )

    attended_output, log_total = lax.map(
        attend_group, (query_heads_rows, gathered, seg_here, pos_here, segments, positions)
    )
    attended_low = attended_output.reshape(token_count, heads_here * HEAD_SIZE).astype(jnp.bfloat16)
    attn_sum = lax.psum(jnp.dot(attended_low, w_out, preferred_element_type=jnp.float32), "tensor")
    middle = tok_rows + attn_sum
    scale_two = lax.rsqrt(jnp.mean(middle * middle, axis=-1, keepdims=True) + norm_eps)
    normed_two = (middle * scale_two * gain_two).astype(jnp.bfloat16)
    gate_proj = jnp.dot(normed_two, w_gate, preferred_element_type=jnp.float32)
    up_proj = jnp.dot(normed_two, w_up, preferred_element_type=jnp.float32)
    sigmoid_gate = jax.nn.sigmoid(gate_proj)
    silu_gate = gate_proj * sigmoid_gate
    hidden = (silu_gate * up_proj).astype(jnp.bfloat16)
    ffn_sum = lax.psum(
        jnp.dot(hidden, w_down, preferred_element_type=jnp.float32).astype(jnp.bfloat16), "tensor"
    ).astype(jnp.float32)
    output = (middle + ffn_sum).astype(jnp.bfloat16).reshape(groups, tok_local, model_width)
    grad_low = cotangent.reshape(token_count, model_width)
    grad_out = grad_low.astype(jnp.float32)
    grad_hidden = contract_cols(grad_low, w_down)
    grad_w_down_t = contract_rows(grad_low, hidden)
    grad_gate = (
        grad_hidden * up_proj * sigmoid_gate * (1.0 + gate_proj * (1.0 - sigmoid_gate))
    ).astype(jnp.bfloat16)
    grad_up = (grad_hidden * silu_gate).astype(jnp.bfloat16)
    grad_w_gate = contract_rows(normed_two, grad_gate)
    grad_w_up = contract_rows(normed_two, grad_up)
    grad_normed_two = lax.psum(
        contract_cols(grad_gate, w_gate) + contract_cols(grad_up, w_up), "tensor"
    )
    back_two, grad_gain_two = norm_back(middle, scale_two, gain_two, grad_normed_two)
    grad_middle = grad_out + back_two
    grad_mid_low = grad_middle.astype(jnp.bfloat16)
    grad_w_out_t = contract_rows(grad_mid_low, attended_low)
    grad_attended = (
        contract_cols(grad_mid_low, w_out)
        .astype(jnp.bfloat16)
        .reshape(groups, tok_local, heads_here * HEAD_SIZE)
    )

    def attend_back(inputs):
        (
            group_queries,
            group_keyval,
            group_grad,
            group_total,
            seg_query,
            pos_query,
            seg_keys,
            pos_keys,
        ) = inputs
        scores, grouped_heads, key_head_rows = scores_of(
            group_queries, group_keyval, seg_query, pos_query, seg_keys, pos_keys
        )
        soft_weights = jnp.exp(scores - group_total[..., None])
        value_head_rows = group_keyval[:, kv_width:].reshape(-1, kv_here, HEAD_SIZE)
        grad_grouped = group_grad.reshape(tok_local, kv_here, per_kv, HEAD_SIZE)
        grad_weights = jnp.einsum(
            "bhgd,khd->hgbk", grad_grouped, value_head_rows, preferred_element_type=jnp.float32
        )
        inner = jnp.sum(soft_weights * grad_weights, axis=-1, keepdims=True)
        grad_scores = (soft_weights * (grad_weights - inner)).astype(jnp.bfloat16)
        grad_queries = (
            jnp.einsum(
                "hgbk,khd->bhgd", grad_scores, key_head_rows, preferred_element_type=jnp.float32
            )
            * score_scale
        )
        grad_keys = (
            jnp.einsum(
                "hgbk,bhgd->khd", grad_scores, grouped_heads, preferred_element_type=jnp.float32
            )
            * score_scale
        )
        grad_values = jnp.einsum(
            "hgbk,bhgd->khd",
            soft_weights.astype(jnp.bfloat16),
            grad_grouped,
            preferred_element_type=jnp.float32,
        )
        grad_keyval = jnp.concatenate(
            [grad_keys.reshape(-1, kv_width), grad_values.reshape(-1, kv_width)], axis=-1
        )
        return (grad_queries.reshape(tok_local, heads_here * HEAD_SIZE), grad_keyval)

    grad_queries, grad_keyval = lax.map(
        attend_back,
        (
            query_heads_rows,
            gathered,
            grad_attended,
            log_total,
            seg_here,
            pos_here,
            segments,
            positions,
        ),
    )
    grad_keyval = lax.psum_scatter(grad_keyval, "context", scatter_dimension=1, tiled=True)
    grad_query_rows = rotate_back(
        grad_queries.reshape(token_count, heads_here, HEAD_SIZE), cosine_table, sine_values
    )
    grad_query_rows = grad_query_rows.astype(jnp.bfloat16).reshape(
        token_count, heads_here * HEAD_SIZE
    )
    grad_key_rows = rotate_back(
        grad_keyval[..., :kv_width].reshape(token_count, kv_here, HEAD_SIZE),
        cosine_table,
        sine_values,
    )
    grad_key_rows = grad_key_rows.astype(jnp.bfloat16).reshape(token_count, kv_width)
    grad_value_rows = (
        grad_keyval[..., kv_width:].reshape(token_count, kv_width).astype(jnp.bfloat16)
    )
    grad_w_query = contract_rows(normed_input, grad_query_rows)
    grad_w_key = contract_rows(normed_input, grad_key_rows)
    grad_w_value = contract_rows(normed_input, grad_value_rows)
    partial_one = (
        contract_cols(grad_query_rows, w_query)
        + contract_cols(grad_key_rows, key_weight)
        + contract_cols(grad_value_rows, value_weight)
    )
    grad_normed = lax.psum(partial_one, "tensor")
    back_one, grad_gain_one = norm_back(tok_rows, scale_one, gain_one, grad_normed)
    tokens_grad = (
        (grad_middle + back_one).astype(jnp.bfloat16).reshape(groups, tok_local, model_width)
    )
    summed = (
        lax.psum_scatter(grad_w_query, ("shard", "context"), scatter_dimension=0, tiled=True),
        lax.psum_scatter(grad_w_key, ("shard", "context"), scatter_dimension=0, tiled=True),
        lax.psum_scatter(grad_w_value, ("shard", "context"), scatter_dimension=0, tiled=True),
        lax.psum_scatter(grad_w_out_t, ("shard", "context"), scatter_dimension=0, tiled=True),
        lax.psum_scatter(grad_w_gate, ("shard", "context"), scatter_dimension=0, tiled=True),
        lax.psum_scatter(grad_w_up, ("shard", "context"), scatter_dimension=0, tiled=True),
        lax.psum_scatter(grad_w_down_t, ("shard", "context"), scatter_dimension=0, tiled=True),
        lax.psum_scatter(grad_gain_one, ("shard", "context"), scatter_dimension=0, tiled=True),
        lax.psum_scatter(grad_gain_two, ("shard", "context"), scatter_dimension=0, tiled=True),
    )
    summed = (
        lax.all_gather(summed[0].astype(jnp.bfloat16), "context", axis=0, tiled=True).astype(
            jnp.float32
        ),
        lax.all_gather(summed[1].astype(jnp.bfloat16), "context", axis=0, tiled=True).astype(
            jnp.float32
        ),
        lax.all_gather(summed[2].astype(jnp.bfloat16), "context", axis=0, tiled=True).astype(
            jnp.float32
        ),
        lax.all_gather(summed[3].astype(jnp.bfloat16), "context", axis=0, tiled=True).astype(
            jnp.float32
        ),
        lax.all_gather(summed[4].astype(jnp.bfloat16), "context", axis=0, tiled=True).astype(
            jnp.float32
        ),
        lax.all_gather(summed[5].astype(jnp.bfloat16), "context", axis=0, tiled=True).astype(
            jnp.float32
        ),
        lax.all_gather(summed[6].astype(jnp.bfloat16), "context", axis=0, tiled=True).astype(
            jnp.float32
        ),
        lax.all_gather(summed[7].astype(jnp.bfloat16), "context", axis=0, tiled=True).astype(
            jnp.float32
        ),
        lax.all_gather(summed[8].astype(jnp.bfloat16), "context", axis=0, tiled=True).astype(
            jnp.float32
        ),
    )
    return (
        output,
        tokens_grad,
        summed[0],
        summed[1],
        summed[2],
        summed[3].T,
        summed[4],
        summed[5],
        summed[6].T,
        summed[7],
        summed[8],
    )


MESH = pl.DeviceIdType.MESH
RUN = 256
PAD = 128
NEG = -1e30
LOG2E = 1.4426950408889634
BF = jnp.bfloat16
F32 = jnp.float32
VLIM = 64 * 1024 * 1024


def mm(a, b):
    return lax.dot_general(a, b, (((1,), (0,)), ((), ())), preferred_element_type=F32)


def mm_nt(a, b):
    return lax.dot_general(a, b, (((1,), (1,)), ((), ())), preferred_element_type=F32)


def mm_tn(a, b):
    return lax.dot_general(a, b, (((0,), (0,)), ((), ())), preferred_element_type=F32)


def iota(shape, axis):
    return lax.broadcasted_iota(jnp.int32, shape, axis)


def one_hot(hit):
    return jnp.where(hit, 1.0, 0.0).astype(BF)


def pad_matrix(heads, flip=False):
    shape = (heads * HEAD_SIZE, heads * PAD)
    if flip:
        row, col = iota(shape[::-1], 1), iota(shape[::-1], 0)
    else:
        row, col = iota(shape, 0), iota(shape, 1)
    lane = col & 127
    part = jnp.where(lane < 64, lane, lane - 16)
    return one_hot((row == (col >> 7) * HEAD_SIZE + part) & ((lane & 63) < 48))


def split_matrix():
    row, col = iota((RUN, RUN), 0), iota((RUN, RUN), 1)
    return one_hot(col == jnp.where(row < 128, 2 * row, 2 * row - 255))


def merge_matrix():
    row, col = iota((RUN, RUN), 0), iota((RUN, RUN), 1)
    return one_hot(col == (row >> 1) + (row & 1) * 128)


def rope_tables(run, cb_ref, sb_ref, cj_ref, sj_ref):
    cb, sb = cb_ref[pl.ds(run, 1), :], sb_ref[pl.ds(run, 1), :]
    cj, sj = cj_ref[...], sj_ref[...]
    return cb * cj - sb * sj, sb * cj + cb * sj


def rope(u, c, s):
    return u * c + pltpu.roll(u, 64, 1) * s


def rope_back(u, c, s):
    return u * c - pltpu.roll(u, 64, 1) * s


def vmem(*shape_dtype):
    return pl.BlockSpec(memory_space=pltpu.VMEM)


def entry_barrier(targets):
    bar = pltpu.get_barrier_semaphore()
    for t in targets:
        pl.semaphore_signal(bar, inc=1, device_id=t, device_id_type=MESH)
    pl.semaphore_wait(bar, len(targets))


def remote(src, dst, send, recv, target):
    return pltpu.make_async_remote_copy(
        src_ref=src, dst_ref=dst, send_sem=send, recv_sem=recv, device_id=target, device_id_type=MESH
    )


def first_kernel(nc, x_ref, dy_h, g_ref, cb_ref, sb_ref, cj_ref, sj_ref, wq_h, wk_h, wv_h, wo_h, wg_h, wu_h, wd_h,
                 xp_ref, dyp_ref, n1_ref, q_ref, kvp_ref, kvc_ref, wp_ref, gf_ref, wo_f, wg_f, wu_f, wd_f,
                 dy_v, wq_s, wk_s, wv_s, g_s, wo_v, wg_v, wu_v, wd_v, kv_send,
                 lsem, ssem, rsem, osem, csem, crem):
    s = lax.axis_index("shard")
    c = lax.axis_index("context")
    dh = g_s.shape[1] // 2
    own = pl.ds(pl.multiple_of(s * dh, dh), dh)
    other = {"shard": 1 - s}
    loads = [
        pltpu.make_async_copy(wq_h, wq_s.at[own], lsem.at[0]),
        pltpu.make_async_copy(wk_h, wk_s.at[own], lsem.at[1]),
        pltpu.make_async_copy(wv_h, wv_s.at[own], lsem.at[2]),
        pltpu.make_async_copy(g_ref, g_s.at[:, own], lsem.at[3]),
        pltpu.make_async_copy(wo_h, wo_v, lsem.at[4]),
        pltpu.make_async_copy(wg_h, wg_v, lsem.at[5]),
        pltpu.make_async_copy(wu_h, wu_v, lsem.at[6]),
        pltpu.make_async_copy(wd_h, wd_v, lsem.at[7]),
        pltpu.make_async_copy(dy_h, dy_v, lsem.at[8]),
    ]
    for cp in loads:
        cp.start()
    entry_barrier([other] + [{"context": lax.rem(c + i, nc)} for i in range(1, nc)])
    sends = [
        remote(wq_s.at[own], wq_s.at[own], ssem.at[0], rsem.at[0], other),
        remote(wk_s.at[own], wk_s.at[own], ssem.at[1], rsem.at[1], other),
        remote(wv_s.at[own], wv_s.at[own], ssem.at[2], rsem.at[2], other),
        remote(g_s.at[:, own], g_s.at[:, own], ssem.at[3], rsem.at[3], other),
        remote(wo_v, wo_f.at[:, own], ssem.at[4], rsem.at[4], other),
        remote(wg_v, wg_f.at[own], ssem.at[5], rsem.at[5], other),
        remote(wu_v, wu_f.at[own], ssem.at[6], rsem.at[6], other),
        remote(wd_v, wd_f.at[:, own], ssem.at[7], rsem.at[7], other),
    ]
    keeps = [
        pltpu.make_async_copy(wo_v, wo_f.at[:, own], osem.at[0]),
        pltpu.make_async_copy(wg_v, wg_f.at[own], osem.at[1]),
        pltpu.make_async_copy(wu_v, wu_f.at[own], osem.at[2]),
        pltpu.make_async_copy(wd_v, wd_f.at[:, own], osem.at[3]),
    ]
    for i in (3, 0, 1, 2, 4, 5, 6, 7):
        loads[i].wait()
        sends[i].start()
        if i >= 4:
            keeps[i - 4].start()
    half = x_ref.shape[0] // 2
    split = split_matrix()
    for i in range(x_ref.shape[0] // RUN):
        xb = mm(split, x_ref[pl.ds(i * RUN, RUN), :])
        xp_ref[pl.ds(i * 128, 128), :] = xb[:128].astype(BF)
        xp_ref[pl.ds(half + i * 128, 128), :] = xb[128:].astype(BF)
        if i == 0:
            sends[3].wait_recv()
        r = lax.rsqrt(jnp.mean(xb * xb, axis=-1, keepdims=True) + norm_eps)
        nb = (xb * r * g_s[0:1, :]).astype(BF)
        n1_ref[pl.ds(i * 128, 128), :] = nb[:128]
        n1_ref[pl.ds(half + i * 128, 128), :] = nb[128:]
    gf_ref[...] = g_s[...]
    hq, hk = wq_s.shape[1] // HEAD_SIZE, wk_s.shape[1] // HEAD_SIZE
    selq, selk = pad_matrix(hq, True), pad_matrix(hk, True)
    nq, nk = hq * PAD, hk * PAD
    for i in range(3):
        sends[i].wait_recv()
    wp_ref[0:nq, :] = mm_nt(selq, wq_s[...]).astype(BF)
    wp_ref[nq : nq + nk, :] = mm_nt(selk, wk_s[...]).astype(BF)
    wp_ref[nq + nk :, :] = mm_nt(selk, wv_s[...]).astype(BF)
    selkv = pad_matrix(2 * hk)
    runs = x_ref.shape[0] // RUN
    per = runs // 2
    kv_copies = []
    for run in range(runs):
        rows = pl.ds(run * RUN, RUN)
        y = mm_nt(n1_ref[rows, :], wp_ref[...])
        ct, st = rope_tables(run, cb_ref, sb_ref, cj_ref, sj_ref)
        for h in range(hq):
            q_ref[rows, h * PAD : (h + 1) * PAD] = rope(y[:, h * PAD : (h + 1) * PAD], ct, st).astype(BF)
        kv = [rope(y[:, nq + h * PAD : nq + (h + 1) * PAD], ct, st).astype(BF) for h in range(hk)]
        kv = jnp.concatenate(kv + [y[:, nq + nk :].astype(BF)], axis=1)
        if run < per:
            kv_send[pl.ds(run * RUN, RUN), :] = mm_nt(kv, selkv).astype(BF)
            mine = pl.ds(pl.multiple_of((c * per + run) * RUN, RUN), RUN)
            for i in range(1, nc):
                cp = remote(kv_send.at[pl.ds(run * RUN, RUN)], kvp_ref.at[mine], csem.at[run, i], crem.at[run, i],
                            {"context": lax.rem(c + i, nc)})
                cp.start()
                kv_copies.append(cp)
            cp = pltpu.make_async_copy(kv_send.at[pl.ds(run * RUN, RUN)], kvp_ref.at[mine], csem.at[run, 0])
            cp.start()
            kv_copies.append(cp)
        else:
            kvc_ref[pl.ds((run - per) * RUN, RUN), :] = kv
    loads[8].wait()
    for i in range(x_ref.shape[0] // RUN):
        b = mm(split, dy_v[pl.ds(i * RUN, RUN), :]).astype(BF)
        dyp_ref[pl.ds(i * 128, 128), :] = b[:128]
        dyp_ref[pl.ds(half + i * 128, 128), :] = b[128:]
    for cp in kv_copies:
        cp.wait()
    for i in range(4):
        keeps[i].wait()
        sends[4 + i].wait_recv()
    for cp in sends:
        cp.wait_send()


class Line:
    F_AT = (8, 9, 10, 12)
    D_AT = (11, 13, 14, 15)

    def __init__(self, n, chunk, pbuf, rbuf, obuf, sems):
        self.n, self.chunk, self.per = n, chunk, RUN // 2 // chunk
        self.count = 16 * self.per
        self.pbuf, self.rbuf, self.obuf = pbuf, rbuf, obuf
        self.rs, self.rr, self.bs, self.br = sems
        self.turn = 8 * (n - 1) // 3
        self.slots = self.count + self.turn

    def pieces(self, h, i):
        n, chunk = self.n, self.chunk
        z = lax.axis_index("tensor")
        job = i // self.per
        late = jnp.where((job == 11) | (job > 12), 1, 0)
        row = jnp.where(job < 8, lax.rem(job, 4), jnp.where(late == 1, jnp.maximum(job - 12, 0), jnp.minimum(job - 8, 3)))
        part = jnp.where(job < 8, job // 4, 2 - late)
        off = row * RUN + h * (RUN // 2) + lax.rem(i, self.per) * chunk
        rows = pl.ds(pl.multiple_of(off, chunk), chunk)
        orows = pl.ds(pl.multiple_of(part * (4 * RUN) + off, chunk), chunk)
        place = z if h == 0 else n - 1 - z
        up, down = jnp.minimum(z + 1, n - 1), jnp.maximum(z - 1, 0)
        ahead = {"tensor": up if h == 0 else down}
        back = {"tensor": down if h == 0 else up}
        fwd = remote(self.pbuf.at[rows], self.rbuf.at[rows], self.rs.at[h, i], self.rr.at[h, i], ahead)
        ret = remote(self.obuf.at[orows], self.obuf.at[orows], self.bs.at[h, i], self.br.at[h, i], back)
        return rows, orows, place, fwd, ret

    def reduce_step(self, h, i):
        rows, orows, place, fwd, ret = self.pieces(h, i)
        n = self.n

        @pl.when(place == 0)
        def _():
            fwd.start()

        @pl.when(place > 0)
        def _():
            fwd.wait_recv()
            total = (self.rbuf[rows, :].astype(F32) + self.pbuf[rows, :].astype(F32)).astype(BF)

            @pl.when(place < n - 1)
            def _():
                self.pbuf[rows, :] = total
                fwd.start()

            @pl.when(place == n - 1)
            def _():
                self.obuf[orows, :] = total
                ret.start()

    def spread_step(self, h, i):
        rows, orows, place, fwd, ret = self.pieces(h, i)

        @pl.when(place < self.n - 1)
        def _():
            ret.wait_recv()

        @pl.when((place < self.n - 1) & (place > 0))
        def _():
            ret.start()

    def serve(self, t):
        n = self.n
        z = lax.axis_index("tensor")
        for h in range(2):
            place = z if h == 0 else n - 1 - z
            i = t - (place * 4) // 3

            @pl.when((i >= 0) & (i < self.count))
            def _():
                self.reduce_step(h, i)

            j = t - ((2 * (n - 1) - place) * 4) // 3

            @pl.when((j >= 0) & (j < self.count))
            def _():
                self.spread_step(h, j)

    def sent(self, job, fwd=True, ret=False):
        def step(i, _):
            for h in range(2):
                rows, orows, place, f, r = self.pieces(h, job * self.per + i)
                if fwd:

                    @pl.when(place < self.n - 1)
                    def _():
                        f.wait_send()

                if ret:

                    @pl.when(place > 0)
                    def _():
                        r.wait_send()

            return 0

        lax.fori_loop(0, self.per, step, 0)


def run_items(items, serve):
    total = max(e for _, e, _ in items)

    def step(k, _):
        for lo, hi, body in items:
            pl.when((k >= lo) & (k < hi))(functools.partial(body, k))
        serve(k)
        return 0

    lax.fori_loop(0, total, step, 0)


class Square:
    def __init__(self, rows, cols, src, mine, theirs, spare, out, credit, shard_send, shard_recv, send, recv, store):
        self.src, self.mine, self.theirs, self.res, self.out = src, mine, theirs, theirs, out
        self.r1, self.r2 = [spare[0:2], spare[2:4]], spare[4:6]
        self.credit, self.shard_sems, self.shard_recv, self.send, self.recv, self.store_sem = credit, shard_send, shard_recv, send, recv, store
        self.rows, self.qr, self.cols = rows, rows // 4, cols
        c = lax.axis_index("context")
        self.cy, self.cx = c // 2, lax.rem(c, 2)

    def at(self, y, x, half):
        w = self.cols // 2
        return (pl.ds(pl.multiple_of((2 * y + x) * self.qr, self.qr), self.qr), pl.ds(half * w, w))

    def peer(self, half, first):
        if (half == 0) == first:
            return {"context": 2 * self.cy + 1 - self.cx}
        return {"context": 2 * (1 - self.cy) + self.cx}

    def shard_copy(self):
        return remote(self.src, self.theirs, self.shard_sems, self.shard_recv, {"shard": 1 - lax.axis_index("shard")})

    def outer(self, half):
        if half == 0:
            return [(y, 1 - self.cx) for y in range(2)], [(y, self.cx) for y in range(2)]
        return [(1 - self.cy, x) for x in range(2)], [(self.cy, x) for x in range(2)]

    def p1(self, half, j):
        return remote(self.mine.at[self.at(*self.outer(half)[0][j], half)], self.r1[half][j],
                      self.send.at[0, half, j], self.recv.at[0, half, j], self.peer(half, True))

    def p2(self, half):
        q = (1 - self.cy, self.cx) if half == 0 else (self.cy, 1 - self.cx)
        return remote(self.mine.at[self.at(*q, half)], self.r2[half],
                      self.send.at[1, half, 0], self.recv.at[1, half, 0], self.peer(half, False))

    def p3(self, half):
        at = self.at(self.cy, self.cx, half)
        return remote(self.res.at[at], self.res.at[at], self.send.at[1, half, 1], self.recv.at[1, half, 1], self.peer(half, False))

    def p4(self, half, j):
        at = self.at(*self.outer(half)[1][j], half)
        return remote(self.res.at[at], self.res.at[at], self.send.at[2, half, j], self.recv.at[2, half, j], self.peer(half, True))

    def free(self):
        for t in ({"shard": 1 - lax.axis_index("shard")}, self.peer(0, True), self.peer(0, False)):
            pl.semaphore_signal(self.credit, inc=1, device_id=t, device_id_type=MESH)

    def e0(self):
        pl.semaphore_wait(self.credit, 3)
        self.shard_copy().start()

    def e1(self):
        self.shard_copy().wait_recv()
        step = self.qr

        def add(i, _):
            rows = pl.ds(pl.multiple_of(i * step, step), step)
            self.mine[rows, :] = (self.mine[rows, :].astype(F32) + self.theirs[rows, :].astype(F32)).astype(BF)
            return 0

        lax.fori_loop(0, self.rows // step, add, 0)
        for j in range(2):
            for half in range(2):
                self.p1(half, j).start()

    def e2(self):
        for half in range(2):
            for j in range(2):
                self.p1(half, j).wait_recv()
                at = self.at(*self.outer(half)[1][j], half)
                self.mine[at] = (self.mine[at].astype(F32) + self.r1[half][j][...].astype(F32)).astype(BF)
            self.p2(half).start()

    def e3(self):
        for half in range(2):
            self.p2(half).wait_recv()
            at = self.at(self.cy, self.cx, half)
            self.res[at] = (self.mine[at].astype(F32) + self.r2[half][...].astype(F32)).astype(BF)
            self.p3(half).start()

    def e4(self):
        for half in range(2):
            self.p3(half).wait_recv()
            for j in range(2):
                self.p4(half, j).start()

    def e5(self):
        for half in range(2):
            for j in range(2):
                self.p4(half, j).wait_recv()

    def store(self):
        return pltpu.make_async_copy(self.res, self.out, self.store_sem)

    def done(self):
        self.shard_copy().wait_send()
        for half in range(2):
            for j in range(2):
                self.p1(half, j).wait_send()
                self.p4(half, j).wait_send()
            self.p2(half).wait_send()
            self.p3(half).wait_send()


def line_barrier(n, peers=()):
    z = lax.axis_index("tensor")
    bar = pltpu.get_barrier_semaphore()
    for t in peers:
        pl.semaphore_signal(bar, inc=1, device_id=t, device_id_type=MESH)

    @pl.when(z > 0)
    def _():
        pl.semaphore_signal(bar, inc=1, device_id={"tensor": jnp.maximum(z - 1, 0)}, device_id_type=MESH)

    @pl.when(z < n - 1)
    def _():
        pl.semaphore_signal(bar, inc=1, device_id={"tensor": jnp.minimum(z + 1, n - 1)}, device_id_type=MESH)

    pl.semaphore_wait(bar, len(peers) + jnp.minimum(z, 1) + jnp.minimum(n - 1 - z, 1))


def main_kernel(n, nc, chunk, kbase, qlim, cb_ref, sb_ref, cj_ref, sj_ref, gf_ref, q_ref, kvc_ref, wo_ref,
                kvp_h, xp_h, dyp_h, wg_h, wu_h, wd_h, n1_h, wp_h,
                out_h, tg_h, gg_h, gu_h, gd_h, go_h, gw_h, dm_h, gds_h, fp_h, gains_ref,
                k_s, v_s, s_s, o_v, op_v, lse_v, xs, ys, pbuf, rbuf, obuf, wd, n2, wg, wu, hid, dg, du, gt,
                dk_s, dv_s, do_v, dq_s, delta_s, dqp, dkv_s, go_v, st_o, st_t, st_p, gpart, grecv,
                lsem, ksem, osem, fsem, msem, nsem, qsend, qrecv, gs, gr, rs, rr, bs, br, credits, shard_send, shard_recv, send, recv, store):
    s = lax.axis_index("shard")
    c = lax.axis_index("context")
    rows_here, d = xs.shape
    runs = rows_here // RUN
    per = runs // 2
    half = rows_here // 2
    hk = k_s.shape[0]
    hq = q_ref.shape[1] // PAD
    rep = hq // hk
    blocks = k_s.shape[1] // RUN
    ff = wg.shape[1]
    dh = d // 2
    nq, nk = hq * PAD, hk * PAD
    score = 1.0 / math.sqrt(HEAD_SIZE)
    scale = LOG2E * score
    own = pl.ds(pl.multiple_of(s * dh, dh), dh)
    yours = pl.ds(pl.multiple_of((1 - s) * dh, dh), dh)
    wide = 2 * hk * HEAD_SIZE

    def at(i, size=RUN):
        return pl.ds(pl.multiple_of(i * size, size), size)

    kv_in = [dg.at[pl.ds((b % 4) * RUN, RUN), pl.ds(b // 4 * wide, wide)] for b in range(blocks)]
    key_loads = [pltpu.make_async_copy(kvp_h.at[pl.ds(b * RUN, RUN)], kv_in[b], ksem.at[b]) for b in range(blocks)]
    for cp in key_loads:
        cp.start()
    pairs = [(xp_h, xs), (wg_h, wg), (wu_h, wu), (dyp_h, ys), (wd_h, wd)]
    loads = [pltpu.make_async_copy(a, b, lsem.at[i]) for i, (a, b) in enumerate(pairs)]
    for cp in loads:
        cp.start()
    peers = [{"shard": lax.rem(s + i // nc, 2), "context": lax.rem(c + lax.rem(i, nc), nc)} for i in range(1, 2 * nc)]
    line_barrier(n, peers)
    line = Line(n, chunk, pbuf, rbuf, obuf, (rs, rr, bs, br))
    a_of = lambda job: at(job)
    b_of = lambda job: at(runs + job)
    lane = iota((RUN, PAD), 1)
    for b in range(blocks):
        key_loads[b].wait()
        kv = mm(kv_in[b][...], pad_matrix(2 * hk))
        rows = pl.ds(b * RUN, RUN)
        for g in range(hk):
            k_s[g, rows, :] = kv[:, g * PAD : (g + 1) * PAD].astype(BF)
            v_s[g, rows, :] = jnp.where(lane == 48, 1.0, kv[:, (hk + g) * PAD : (hk + g + 1) * PAD]).astype(BF)
    dk_s[...] = jnp.zeros_like(dk_s)
    dv_s[...] = jnp.zeros_like(dv_s)
    gpart[...] = jnp.zeros_like(gpart)

    def across(total, width, body):
        def step(i, _):
            body(at(i, width))
            return 0

        lax.fori_loop(0, total // width, step, 0)

    def down_rows(start, count, size, body):
        def step(i, _):
            body(pl.ds(pl.multiple_of(start + i * size, size), size), pl.ds(pl.multiple_of(i * size, size), size))
            return 0

        lax.fori_loop(0, count // size, step, 0)

    def head(k, mixed):
        job, h = k // hq, lax.rem(k, hq)
        run = job + per if mixed else job - per
        diff = iota((RUN, RUN), 1) - iota((RUN, RUN), 0)
        rows, cols = at(run), at(h, PAD)
        g = h // rep
        q = q_ref[rows, cols]
        lim = qlim[run]
        top = None
        for b in range(blocks):
            t = mm_nt(q, k_s[g, pl.ds(b * RUN, RUN), :]) * scale
            room = lim - kbase[b]
            if mixed:
                t = t + jnp.where(room >= 0, 0.0, NEG)
            else:
                t = jnp.where(diff <= room, t, NEG)
            s_s[:, b * RUN : (b + 1) * RUN] = t
            top = t if top is None else jnp.maximum(top, t)
        if mixed:
            crow = at(run - per)
            kc = kvc_ref[crow, at(g, PAD)]
            vc = kvc_ref[crow, at(hk + g, PAD)]
            vc = jnp.where(lane == 48, 1.0, vc.astype(F32)).astype(BF)
            t = jnp.where(diff <= 0, mm_nt(q, kc) * scale, NEG)
            s_s[:, blocks * RUN :] = t
            top = jnp.maximum(top, t)
        m = jnp.max(top, axis=1, keepdims=True)
        acc = None
        for b in range(blocks):
            p = jnp.exp2(s_s[:, b * RUN : (b + 1) * RUN] - m).astype(BF)
            o = mm(p, v_s[g, pl.ds(b * RUN, RUN), :])
            acc = o if acc is None else acc + o
        if mixed:
            p = jnp.exp2(s_s[:, blocks * RUN :] - m).astype(BF)
            acc = acc + mm(p, vc)
        total = acc[:, 48:49]
        op_v[rows, cols] = (acc / total).astype(BF)
        lse = jnp.broadcast_to(m + jnp.log2(total), (RUN, PAD)).T
        lse_v[at(run * hq + h, 8), :] = lse[0:8, :]

        @pl.when(h == hq - 1)
        def _():
            o = mm_nt(op_v[rows, :], pad_matrix(hq)).astype(BF)
            o_v[rows, :] = o


            def out(cols):
                pbuf[at(job), cols] = mm(o, wo_ref[:, cols]).astype(BF)

            across(d, 512, out)

    first = runs * hq

    def ffn(k):
        job = (k - first) // 4
        part = lax.rem(k - first, 4)
        run = lax.rem(job + per, runs)
        rows = at(run)

        @pl.when(k == first)
        def _():
            for cp in loads:
                cp.wait()

        @pl.when(part == 0)
        def _():
            def norm(to, sub):
                srows = pl.ds(pl.multiple_of(job * RUN + sub.start, 32), 32)
                mid = xs[to, :].astype(F32) + obuf[srows, :].astype(F32)
                r = lax.rsqrt(jnp.mean(mid * mid, axis=-1, keepdims=True) + norm_eps)
                n2[to, :] = (mid * r * gf_ref[8:9, :]).astype(BF)

            down_rows(run * RUN, RUN, 32, norm)

            def gate(cols):
                s_s[:, cols] = mm(n2[rows, :], wg[:, cols])

            across(ff, 512, gate)

        @pl.when(part == 1)
        def _():
            def up(i, _):
                s_s[:, pl.ds(pl.multiple_of(ff + i * 512, 512), 512)] = mm(n2[rows, :], wu[:, at(i, 512)])
                return 0

            lax.fori_loop(0, ff // 512, up, 0)

        @pl.when(part == 2)
        def _():
            def gated(i, _):
                cols = at(i)
                dhid = mm_nt(ys[rows, :], wd[cols, :])
                gate, up = s_s[:, cols], s_s[:, pl.ds(pl.multiple_of(ff + i * RUN, RUN), RUN)]
                sig = jax.nn.sigmoid(gate)
                silu = gate * sig
                hid[rows, cols] = (silu * up).astype(BF)
                dg[rows, cols] = (dhid * up * sig * (1.0 + gate * (1.0 - sig))).astype(BF)
                du[rows, cols] = (dhid * silu).astype(BF)
                return 0

            lax.fori_loop(0, ff // RUN, gated, 0)

        @pl.when(part == 3)
        def _():
            line.sent(job)

            def normed_two(cols):
                pbuf[at(job), cols] = (mm_nt(dg[rows, :], wg[cols, :]) + mm_nt(du[rows, :], wu[cols, :])).astype(BF)

            across(d, 512, normed_two)
            cp = pltpu.make_async_copy(st_o, fp_h.at[at(job)], osem.at[0])

            @pl.when(job > 0)
            def _():
                cp.wait()

            def project(cols):
                st_o[:, cols] = mm(hid[rows, :], wd[:, cols]).astype(BF)

            across(d, 512, project)
            cp.start()

    second = first + 4 * runs

    def stage(st, sem, dst, value, busy=True):
        cp = pltpu.make_async_copy(st, dst, sem)
        if busy is True:
            cp.wait()
        else:
            pl.when(busy)(cp.wait)

        def fill(cols):
            st[:, cols] = value(cols)

        across(d, 512, fill)
        cp.start()

    def grads_down(k):
        i = k - second
        for j in range(2):
            cols = at(2 * i + j)
            ht = hid[:, cols].T
            stage(st_o, osem.at[0], gds_h.at[cols], lambda to: mm(ht, ys[:, to]).astype(BF))

    def grads_up(k):
        i = k - second - 2
        for j in range(2):
            cols = at(2 * i + j)
            nt = n2[:, cols].T


            def both(to):
                wg[cols, to] = mm(nt, dg[:, to]).astype(BF)
                wu[cols, to] = mm(nt, du[:, to]).astype(BF)

            across(ff, 512, both)

    back = second + 5

    def middle(k):
        job = (k - back) // 5
        run = lax.rem(job + per, runs)
        rows = at(run)
        cp = pltpu.make_async_copy(s_s.at[:, pl.ds(0, d)], dm_h.at[rows], osem.at[1])

        @pl.when(job > 0)
        def _():
            cp.wait()

        def one(to, sub):
            def there(base):
                return pl.ds(pl.multiple_of(base + sub.start, 32), 32)

            mid = xs[to, :].astype(F32) + obuf[there(job * RUN), :].astype(F32)
            r = lax.rsqrt(jnp.mean(mid * mid, axis=-1, keepdims=True) + norm_eps)
            dn = obuf[there((runs + job) * RUN), :].astype(F32)
            w = gf_ref[8:9, :] * dn
            inner = jnp.mean(w * mid, axis=-1, keepdims=True)
            dm = ys[to, :].astype(F32) + r * w - mid * (r * r * r) * inner
            s_s[sub, 0:d] = dm
            gpart[8:16, :] += jnp.sum((dn * mid * r).reshape(4, 8, d), axis=0)
            ys[to, :] = dm.astype(BF)

        down_rows(run * RUN, RUN, 32, one)
        cp.start()
        do = mm_nt(ys[rows, :], wo_ref[...]).astype(BF)
        do_v[rows, :] = mm(do, pad_matrix(hq)).astype(BF)

    width = rep * RUN

    def pair(k, mixed):
        job = (k - back) // 5
        idx = lax.rem(k - back, 5) - 1
        g, part = idx // 2, lax.rem(idx, 2)
        run = lax.rem(job + per, runs)
        rows = at(run)
        diff = iota((RUN, width), 0) - (iota((RUN, width), 1) & (RUN - 1))

        def stack(ref):
            return jnp.concatenate([ref[rows, at(g * rep + j, PAD)] for j in range(rep)], axis=0)

        q, do = stack(q_ref), stack(do_v)

        @pl.when(part == 0)
        def _():
            op = stack(op_v)
            delta_s[0:1, :] = jnp.sum((do.astype(F32) * op.astype(F32)).T, axis=0, keepdims=True)
            dq_s[...] = jnp.zeros_like(dq_s)

        delta = delta_s[0:1, :]
        lse = jnp.concatenate(
            [lse_v[pl.ds(pl.multiple_of((run * hq + g * rep + j) * 8, 8), 1), :] for j in range(rep)], axis=1
        )
        lim = qlim[run]

        def tile(kk, vv, hide):
            p = jnp.exp2(hide(mm_nt(kk, q) * scale - lse))
            ds = (p * (mm_nt(vv, do) - delta)).astype(BF)
            return mm(ds, q), mm(p.astype(BF), do), mm_tn(ds, kk)

        dq = dq_s[...]
        for bb in range(blocks // 2):
            b = part * (blocks // 2) + bb
            room = lim - kbase[b]
            if mixed:
                hide = lambda t: t + jnp.where(room >= 0, 0.0, NEG)
            else:
                hide = lambda t: jnp.where(diff <= room, t, NEG)
            dk, dv, dd = tile(k_s[g, at(b), :], v_s[g, at(b), :], hide)
            dk_s[g, at(b), :] += dk
            dv_s[g, at(b), :] += dv
            dq = dq + dd
        dq_s[...] = dq

        @pl.when(part == 1)
        def _():
            total = dq_s[...]
            ct, st = rope_tables(run, cb_ref, sb_ref, cj_ref, sj_ref)
            if mixed:
                crow = at(run - per)
                dk, dv, dd = tile(kvc_ref[crow, at(g, PAD)], kvc_ref[crow, at(hk + g, PAD)], lambda t: jnp.where(diff <= 0, t, NEG))
                total = total + dd
                dkv_s[rows, at(g, PAD)] = rope_back(dk * score, ct, st).astype(BF)
                dkv_s[rows, at(hk + g, PAD)] = dv.astype(BF)
            for j in range(rep):
                dqp[rows, at(g * rep + j, PAD)] = rope_back(total[j * RUN : (j + 1) * RUN] * score, ct, st).astype(BF)

    def spare(ref, r0, c0, rows, cols, across, count):
        return [ref.at[pl.ds(r0 + i // across * rows, rows), pl.ds(c0 + i % across * cols, cols)] for i in range(count)]

    def square(i, rows, cols, src, mine, theirs, views, out):
        return Square(rows, cols, src, mine, theirs, views, out, credits.at[i], shard_send.at[i], shard_recv.at[i], send.at[i], recv.at[i], store.at[i])

    q4, w4 = dh // 4, ff // 2
    sq_g = square(0, dh, ff, wg.at[yours], wg.at[own], dg.at[pl.ds(0, dh)], spare(n2, 0, 0, q4, w4, 2, 6), gg_h)
    left = spare(n2, 0, 2 * w4, q4, w4, 1, 3) + spare(n2, 3 * q4, 0, q4, w4, 3, 3)
    sq_u = square(1, dh, ff, wu.at[yours], wu.at[own], du.at[pl.ds(0, dh)], left, gu_h)
    f4, d4 = ff // 4, dh // 2
    sq_d = square(2, ff, dh, gds_h.at[:, yours], hid.at[:, pl.ds(0, dh)], gt,
                  spare(n2, dh, 0, f4, d4, 4, 4) + spare(dg, dh, 0, f4, d4, 2, 2), gd_h)
    dq_cols = hq * HEAD_SIZE
    sq_o = square(3, dq_cols, dh, go_v.at[1 - s], go_v.at[s], wg.at[pl.ds(0, dq_cols), pl.ds(0, dh)],
                  spare(wg, dq_cols, 0, dq_cols // 4, d4, 2, 6), go_h)
    gw_cols = dq_cols + wide
    sq_w = square(4, dh, gw_cols, wu.at[yours, pl.ds(0, gw_cols)], wu.at[own, pl.ds(0, gw_cols)], hid.at[pl.ds(0, dh), pl.ds(0, gw_cols)],
                  spare(gt, 0, 0, q4, gw_cols // 2, 2, 6), gw_h)
    down_load = pltpu.make_async_copy(gds_h.at[:, own], hid.at[:, pl.ds(0, dh)], lsem.at[5])
    wp_load = pltpu.make_async_copy(wp_h, wd, lsem.at[6])

    def f_load(job):
        return pltpu.make_async_copy(fp_h.at[pl.ds(job * RUN, RUN)], pbuf.at[pl.ds(job * RUN, RUN)], fsem.at[job])

    def f_start(job):
        def body():
            line.sent(4 + job)
            f_load(job).start()

        return body

    def key_piece(b):
        return ys.at[pl.ds(pl.multiple_of(lax.rem(b, 4) * RUN, RUN), RUN), pl.ds(pl.multiple_of(b // 4 * wide, wide), wide)]

    def key_recv(i, run):
        m = (i - 1) * per + run
        return ys.at[pl.ds(m % 4 * RUN, RUN), pl.ds(dh + m // 4 * wide, wide)]

    def key_copy(i, run):
        to = lax.rem(c + i, nc)
        return remote(key_piece(to * per + run), key_recv(i, run), qsend.at[i, run], qrecv.at[i, run], {"context": to})

    def pack():
        ot = o_v[...].T
        for j in range(2):


            def part(cols, j=j):
                go_v[j, :, cols] = mm(ot, ys[:, pl.ds(pl.multiple_of(j * dh + cols.start, RUN), RUN)]).astype(BF)

            across(dh, RUN, part)
        for i in range(1, nc):
            pl.semaphore_signal(credits.at[5], inc=1, device_id={"context": lax.rem(c + i, nc)}, device_id_type=MESH)

        def one(b, _):
            rows = at(b)
            parts = [(dk_s[g, rows, :] * score).astype(BF) for g in range(hk)]
            parts += [dv_s[g, rows, :].astype(BF) for g in range(hk)]
            value = mm_nt(jnp.concatenate(parts, axis=1), pad_matrix(2 * hk)).astype(BF)
            key_piece(b)[...] = value
            return 0

        lax.fori_loop(0, blocks, one, 0)
        pl.semaphore_wait(credits.at[5], nc - 1)
        for i in range(1, nc):
            for run in range(per):
                key_copy(i, run).start()

    def normed(job):
        rows = pl.ds((job + per) % runs * RUN, RUN)
        line.sent(Line.F_AT[job])
        line.sent(4 + job, fwd=False, ret=True)

        def part(cols):
            dn = mm(dqp[rows, :], wd[0:nq, cols]) + mm(dkv_s[rows, :], wd[nq:, cols])
            pbuf[pl.ds(job * RUN, RUN), cols] = dn.astype(BF)

        across(d, 512, part)

    def keys():
        for i in range(1, nc):
            for run in range(per):
                key_copy(i, run).wait_recv()
        selkv = pad_matrix(2 * hk)
        for run in range(per):
            rows = pl.ds(run * RUN, RUN)
            total = mm(key_piece(c * per + run)[...], selkv)
            for i in range(1, nc):
                total = total + mm(key_recv(i, run)[...], selkv)
            ct, st = rope_tables(run, cb_ref, sb_ref, cj_ref, sj_ref)
            for g in range(hk):
                dkv_s[rows, g * PAD : (g + 1) * PAD] = rope_back(total[:, g * PAD : (g + 1) * PAD], ct, st).astype(BF)
            dkv_s[rows, hk * PAD :] = total[:, hk * PAD :].astype(BF)

    tile_v = hid.at[:, pl.ds(dh, RUN)]

    def tile_load(i):
        return pltpu.make_async_copy(n1_h.at[:, at(i)], tile_v, nsem)

    def grads_in(k):
        i = k - into

        @pl.when(i == 0)
        def _():
            def pack_rows(to, sub):
                du[to, 0:dq_cols] = mm_nt(dqp[to, :], pad_matrix(hq)).astype(BF)
                du[to, dq_cols:gw_cols] = mm_nt(dkv_s[to, :], pad_matrix(2 * hk)).astype(BF)

            down_rows(0, rows_here, RUN, pack_rows)

        for j in range(2):
            tile_load(2 * i + j).wait()
            nt = tile_v[...].T


            def part(cols, j=j):
                wu[at(2 * i + j), cols] = mm(nt, du[:, cols]).astype(BF)

            across(gw_cols, gw_cols // 2, part)

            @pl.when(2 * i + j + 1 < d // RUN)
            def _():
                tile_load(2 * i + j + 1).start()

    def halves(i, body):
        for j in range(2):

            def step(m, _, j=j):
                natural = pl.ds(pl.multiple_of(j * half + i * 128 + m * 32, 32), 32)
                by_job = lambda part: pl.ds(pl.multiple_of(part * rows_here + (1 - j) * half + i * 128 + m * 32, 32), 32)
                body(natural, by_job, pl.ds(pl.multiple_of(j * 128 + m * 32, 32), 32))
                return 0

            lax.fori_loop(0, 4, step, 0)

    def output(k):
        i = k - outs

        def one(natural, by_job, to):
            total = xs[natural, :].astype(F32) + obuf[by_job(0), :].astype(F32)
            st_p[to, :] = (total + obuf[by_job(2), :].astype(F32)).astype(BF)

        halves(i, one)
        stage(st_o, osem.at[0], out_h.at[at(i)], lambda cols: mm(merge_matrix(), st_p[:, cols]).astype(BF), i > 0)

    def m_load(i, j):
        src = dm_h.at[pl.ds(pl.multiple_of(j * half + i * 128, 128), 128)]
        return pltpu.make_async_copy(src, s_s.at[pl.ds(j * 128, 128), pl.ds(0, d)], msem.at[j])

    def finals(i):
        for j in range(2):
            m_load(i, j).wait()

        def one(natural, by_job, to):
            x = xs[natural, :].astype(F32)
            dn = obuf[by_job(1), :].astype(F32)
            r = lax.rsqrt(jnp.mean(x * x, axis=-1, keepdims=True) + norm_eps)
            w = gf_ref[0:1, :] * dn
            inner = jnp.mean(w * x, axis=-1, keepdims=True)
            st_p[to, :] = (s_s[to, 0:d] + (r * w - x * (r * r * r) * inner)).astype(BF)
            gpart[0:8, :] += jnp.sum((dn * x * r).reshape(4, 8, d), axis=0)

        halves(i, one)

        @pl.when(i + 1 < runs)
        def _():
            for j in range(2):
                m_load(i + 1, j).start()

        cp = pltpu.make_async_copy(st_t, tg_h.at[at(i)], osem.at[2])

        @pl.when(i > 0)
        def _():
            cp.wait()

        def fill(cols):
            st_t[:, cols] = mm(merge_matrix(), st_p[:, cols]).astype(BF)

        across(d, 512, fill)
        cp.start()

    packed = back + 5 * runs
    into = packed + 3
    outs = into + 4
    lag = hq - 1

    def due(job):
        return 4 * job + 3 + line.turn + lag + 1

    items = [(0, per * hq, lambda k: head(k, True)), (per * hq, first, lambda k: head(k, False)), (first, second, ffn),
             (second, second + 2, grads_down), (second + 2, back, grads_up)]
    for job in range(runs):
        begin = back + 5 * job
        items.append((begin, begin + 1, middle))
        items.append((begin + 1, begin + 5, functools.partial(lambda mixed, k: pair(k, mixed), job < per)))
    items += [(into, into + 3, grads_in), (outs, outs + runs, output)]
    fin = due(Line.D_AT[per])
    for i in range(2):
        items.append((fin + i, fin + i + 1, functools.partial(lambda i, k: finals(jnp.int32(i)), i)))

    def begin_down():
        pltpu.make_async_copy(st_o, gds_h.at[pl.ds(0, RUN)], osem.at[0]).wait()
        down_load.start()
        wp_load.start()

    def free_three():
        for sq in (sq_g, sq_u, sq_d):
            sq.free()
        for sq in (sq_g, sq_u, sq_d):
            sq.e0()

    def store_start(sq):
        def body():
            sq.e5()
            sq.store().start()

        return body

    def dm_begin():
        pltpu.make_async_copy(s_s.at[:, pl.ds(0, d)], dm_h.at[pl.ds(0, RUN)], osem.at[1]).wait()
        for j in range(2):
            m_load(0, j).start()

    def first_e1():
        down_load.wait()
        sq_d.e1()

    def give_o():
        sq_g.store().wait()
        sq_g.done()
        sq_o.free()

    def give_w():
        sq_d.store().wait()
        sq_d.done()
        sq_w.free()

    def release_u():
        sq_u.store().wait()
        sq_u.done()

    events = [(second + 2, begin_down), (second + 4, free_three)]
    for job in range(runs):
        first_slot = 4 * Line.F_AT[job] + lag
        events.append((first_slot - 2, f_start(job)))
        events.append((first_slot - 1, f_load(job).wait))
    events += [
        (39, first_e1), (40, sq_g.e1), (41, sq_d.e2), (41, sq_u.e1), (42, sq_g.e2), (43, sq_d.e3), (44, sq_u.e2), (44, sq_g.e3),
        (45, wp_load.wait), (45, lambda: normed(0)), (45, sq_d.e4), (46, sq_g.e4), (47, sq_u.e3), (48, store_start(sq_d)), (49, store_start(sq_g)),
        (50, lambda: normed(1)), (50, sq_u.e4), (51, give_o), (53, store_start(sq_u)), (54, give_w), (55, release_u),
        (packed, pack), (packed, lambda: tile_load(0).start()), (packed, dm_begin), (packed + 1, sq_o.e0),
        (packed + 2, keys), (packed + 2, lambda: normed(2)), (packed + 3, lambda: normed(3)),
        (61, sq_o.e1), (62, sq_w.e0), (63, sq_o.e2), (63, sq_w.e1), (65, sq_w.e2), (65, sq_o.e3), (67, sq_w.e3), (67, sq_o.e4), (69, sq_w.e4),
        (69, store_start(sq_o)), (71, store_start(sq_w)),
    ]
    items += [(k, k + 1, functools.partial(lambda e, k: e(), e)) for k, e in events]
    items.append((0, line.slots + lag, lambda k: None))
    run_items(items, lambda k: line.serve(k - lag))
    for i in range(2):
        finals(jnp.int32(2 + i))
    me = s * nc + c
    sums = jnp.concatenate(
        [jnp.broadcast_to(jnp.sum(gpart[k * 8 : (k + 1) * 8, :], axis=0, keepdims=True), (8, d)) for k in range(2)], axis=0
    )
    grecv[me] = sums
    gcopies = []
    for i, t in enumerate(peers):
        cp = remote(grecv.at[me], grecv.at[me], gs.at[i], gr.at[i], t)
        cp.start()
        gcopies.append(cp)
    for job in range(runs):
        line.sent(job, fwd=False, ret=True)
        line.sent(Line.F_AT[job], fwd=False, ret=True)
        line.sent(Line.D_AT[job], ret=True)
    for sq in (sq_o, sq_w):
        sq.store().wait()
        sq.done()
    for i in range(1, nc):
        for run in range(per):
            key_copy(i, run).wait_send()
    pltpu.make_async_copy(st_o, out_h.at[pl.ds(0, RUN)], osem.at[0]).wait()
    pltpu.make_async_copy(st_t, tg_h.at[pl.ds(0, RUN)], osem.at[2]).wait()
    for cp in gcopies:
        cp.wait()
    total = grecv[0]
    for i in range(1, 2 * nc):
        total = total + grecv[i]
    gains_ref[...] = total


def fast(
    tokens, w_query, key_weight, value_weight, w_out, w_gate, w_up, w_down, gain_attn, gain_ffn, segments, positions, cotangent, n, nc
):
    _, rows, d = tokens.shape
    half = rows // 2
    runs = rows // RUN
    per = runs // 2
    prompt = segments.shape[1] // 2
    blocks = prompt // RUN
    dq, dk = w_query.shape[1], key_weight.shape[1]
    hq, hk = dq // HEAD_SIZE, dk // HEAD_SIZE
    nq, nk = hq * PAD, hk * PAD
    ff = w_gate.shape[1]
    dh = d // 2
    c = lax.axis_index("context")
    x = tokens.reshape(rows, d)
    dy = cotangent.reshape(rows, d)
    kbase = positions[0, 0 :: 2 * RUN]
    seg_here = lax.dynamic_slice_in_dim(segments[0], c * rows, rows, 0)
    pos_here = lax.dynamic_slice_in_dim(positions[0], c * rows, rows, 0)
    qbase = jnp.concatenate([pos_here[0 :: 2 * RUN], pos_here[1 :: 2 * RUN]])
    qlim = jnp.concatenate([pos_here[0 :: 2 * RUN], seg_here[1 :: 2 * RUN] * CLEN - 1])
    freq = np.exp(np.arange(HEAD_SIZE // 2, dtype=np.float32) * np.float32(-2.0 * math.log(rope_base) / HEAD_SIZE)).astype(np.float32)
    lanes = np.zeros((PAD,), np.float32)
    lanes[0:48] = freq
    lanes[64:112] = freq
    sign = np.where(np.arange(PAD) < 64, -1.0, 1.0).astype(np.float32)
    inner = np.arange(RUN, dtype=np.float64)[:, None] * lanes[None, :].astype(np.float64)
    cj = jnp.asarray(np.cos(inner).astype(np.float32))
    sj = jnp.asarray((np.sin(inner) * sign).astype(np.float32))
    angle = qbase.astype(F32)[:, None] * jnp.asarray(lanes)[None, :]
    cb = jnp.cos(angle)
    sb = jnp.sin(angle) * jnp.asarray(sign)[None, :]
    gains = jnp.concatenate([jnp.broadcast_to(g.astype(F32)[None, :], (8, dh)) for g in (gain_attn, gain_ffn)], axis=0)

    V = pl.BlockSpec(memory_space=pltpu.VMEM)
    S = pl.BlockSpec(memory_space=pltpu.SMEM)
    A = pl.BlockSpec(memory_space=pl.ANY)
    sds = jax.ShapeDtypeStruct
    DMA = pltpu.SemaphoreType.DMA

    def call(kernel, ins, outs, scratch, collective=None, flops=0):
        params = dict(vmem_limit_bytes=VLIM - 64 * 1024)
        if collective is not None:
            params.update(collective_id=collective, has_side_effects=True)
        args = [a for a, _ in ins]
        return pl.pallas_call(
            kernel,
            out_shape=[o for o, _ in outs],
            in_specs=[sp for _, sp in ins],
            out_specs=[sp for _, sp in outs],
            scratch_shapes=scratch,
            compiler_params=pltpu.CompilerParams(**params),
            cost_estimate=pl.CostEstimate(flops=flops, bytes_accessed=0, transcendentals=0),
        )(*args)

    rope_in = [(cb, V), (sb, V), (cj, V), (sj, V)]
    xp, dyp, n1, q, kvp, kvc, wp, gf, wo, wg, wu, wd = call(
        functools.partial(first_kernel, nc),
        [(x, V), (dy, A), (gains, A)] + rope_in + [(w_query, A), (key_weight, A), (value_weight, A), (w_out, A), (w_gate, A), (w_up, A), (w_down, A)],
        [
            (sds((rows, d), BF), V), (sds((rows, d), BF), V), (sds((rows, d), BF), V), (sds((rows, nq), BF), V),
            (sds((prompt, 2 * dk), BF), A), (sds((half, 2 * nk), BF), V), (sds((nq + 2 * nk, d), BF), V), (sds((16, d), F32), V),
            (sds((dq, d), BF), A), (sds((d, ff), BF), A), (sds((d, ff), BF), A), (sds((ff, d), BF), A),
        ],
        [
            pltpu.VMEM((rows, d), BF), pltpu.VMEM((d, dq), BF), pltpu.VMEM((d, dk), BF), pltpu.VMEM((d, dk), BF), pltpu.VMEM((16, d), F32),
            pltpu.VMEM((dq, dh), BF), pltpu.VMEM((dh, ff), BF), pltpu.VMEM((dh, ff), BF), pltpu.VMEM((ff, dh), BF),
            pltpu.VMEM((half, 2 * dk), BF),
            DMA((9,)), DMA((8,)), DMA((8,)), DMA((4,)), DMA((per, nc)), DMA((per, nc)),
        ],
        collective=0, flops=60 * 10**9,
    )

    chunk = 32
    count = 16 * (RUN // 2 // chunk)
    U = pltpu.VMEM((rows, d), BF)
    W = pltpu.VMEM((d, ff), BF)
    H = pltpu.VMEM((rows, ff), BF)
    KV = pltpu.VMEM((hk, prompt, PAD), BF)
    KVF = pltpu.VMEM((hk, prompt, PAD), F32)
    width = hq // hk * RUN
    out, tg, gg, gu, gd, go, gw, _, _, _, gains_grad = call(
        functools.partial(main_kernel, n, nc, chunk),
        [(kbase, S), (qlim, S)] + rope_in
        + [(gf, V), (q, V), (kvc, V), (wo, V), (kvp, A), (xp, A), (dyp, A), (wg, A), (wu, A), (wd, A), (n1, A), (wp, A)],
        [(sds((rows, d), BF), A), (sds((rows, d), BF), A), (sds((dh, ff), BF), A), (sds((dh, ff), BF), A), (sds((ff, dh), BF), A),
         (sds((dq, dh), BF), A), (sds((dh, dq + 2 * dk), BF), A), (sds((rows, d), F32), A), (sds((ff, d), BF), A), (sds((rows, d), BF), A),
         (sds((16, d), F32), V)],
        [KV, KV, pltpu.VMEM((RUN, prompt + RUN), F32), pltpu.VMEM((rows, dq), BF), pltpu.VMEM((rows, nq), BF), pltpu.VMEM((runs * hq * 8, RUN), F32),
         U, U, U, U, pltpu.VMEM((3 * rows, d), BF), pltpu.VMEM((ff, d), BF), U, W, W, H, H, H, pltpu.VMEM((ff, dh), BF),
         KVF, KVF, pltpu.VMEM((rows, nq), BF), pltpu.VMEM((width, PAD), F32), pltpu.VMEM((8, width), F32), pltpu.VMEM((rows, nq), BF),
         pltpu.VMEM((rows, 2 * nk), BF), pltpu.VMEM((2, dq, dh), BF), pltpu.VMEM((RUN, d), BF), pltpu.VMEM((RUN, d), BF), pltpu.VMEM((RUN, d), BF),
         pltpu.VMEM((16, d), F32), pltpu.VMEM((2 * nc, 16, d), F32),
         DMA((7,)), DMA((blocks,)), DMA((3,)), DMA((runs,)), DMA((2,)), DMA, DMA((nc, per)), DMA((nc, per)), DMA((2 * nc - 1,)), DMA((2 * nc - 1,))]
        + [DMA((2, count))] * 4
        + [pltpu.SemaphoreType.REGULAR((6,)), DMA((5,)), DMA((5,)), DMA((5, 3, 2, 2)), DMA((5, 3, 2, 2)), DMA((5,))],
        collective=1, flops=300 * 10**9,
    )
    s = lax.axis_index("shard")
    g1o = lax.dynamic_slice_in_dim(gains_grad[0], s * dh, dh, 0)
    g2o = lax.dynamic_slice_in_dim(gains_grad[8], s * dh, dh, 0)
    return (
        out[None], tg[None],
        gw[:, :dq].astype(F32), gw[:, dq : dq + dk].astype(F32), gw[:, dq + dk :].astype(F32),
        go.astype(F32), gg.astype(F32), gu.astype(F32), gd.astype(F32), g1o, g2o,
    )


def body(mesh, *args):
    tokens, w_query, segments = args[0], args[1], args[10]
    n, nc = mesh.shape["tensor"], mesh.shape["context"]
    rows = tokens.shape[1]
    if (tokens.shape[0] == 1 and rows % (4 * CLEN) == 0 and n == 4 and nc == 4 and mesh.shape["shard"] == 2
            and segments.shape[1] == rows * nc):
        return fast(*args, n, nc)
    return general(*args)


def solution(mesh):
    in_specs = (
        P("shard", "context", None),
        P("shard", "tensor"),
        P("shard", "tensor"),
        P("shard", "tensor"),
        P("tensor", "shard"),
        P("shard", "tensor"),
        P("shard", "tensor"),
        P("tensor", "shard"),
        P("shard"),
        P("shard"),
        P("shard", None),
        P("shard", None),
        P("shard", "context", None),
    )
    out_specs = (
        P("shard", "context", None),
        P("shard", "context", None),
        P("shard", "tensor"),
        P("shard", "tensor"),
        P("shard", "tensor"),
        P("tensor", "shard"),
        P("shard", "tensor"),
        P("shard", "tensor"),
        P("tensor", "shard"),
        P("shard"),
        P("shard"),
    )
    return jax.shard_map(functools.partial(body, mesh), mesh=mesh, in_specs=in_specs, out_specs=out_specs, check_vma=False)
```

```python
import functools
import math

import jax
import jax.numpy as jnp
import numpy as np
from jax import lax
from jax.experimental import pallas as pl
from jax.experimental.pallas import tpu as pltpu
from jax.sharding import PartitionSpec as P

HEAD_SIZE = 96
CLEN = 256


rope_base = 100000.0
norm_eps = 1e-05


def tables(positions):
    half_width = HEAD_SIZE // 2
    frequency = jnp.exp(
        jnp.arange(half_width, dtype=jnp.float32) * (-2.0 * math.log(rope_base) / HEAD_SIZE)
    )
    angles = positions.astype(jnp.float32)[:, None] * frequency[None, :]
    return (jnp.cos(angles)[:, None, :], jnp.sin(angles)[:, None, :])


def rotary_apply(heads, cosine_table, sine_values):
    half_width = HEAD_SIZE // 2
    front_half = heads[..., :half_width]
    back_half = heads[..., half_width:]
    return jnp.concatenate(
        [
            front_half * cosine_table - back_half * sine_values,
            back_half * cosine_table + front_half * sine_values,
        ],
        axis=-1,
    )


def rotate_back(heads, cosine_table, sine_values):
    half_width = HEAD_SIZE // 2
    front_half = heads[..., :half_width]
    back_half = heads[..., half_width:]
    return jnp.concatenate(
        [
            front_half * cosine_table + back_half * sine_values,
            back_half * cosine_table - front_half * sine_values,
        ],
        axis=-1,
    )


def contract_rows(left, right):
    return lax.dot_general(
        left, right, (((0,), (0,)), ((), ())), preferred_element_type=jnp.float32
    )


def contract_cols(left, right):
    return lax.dot_general(
        left, right, (((1,), (1,)), ((), ())), preferred_element_type=jnp.float32
    )


def norm_back(tok_rows, norm_scale, gain, grad_normed):
    weighted = gain * grad_normed
    inner = jnp.mean(weighted * tok_rows, axis=-1, keepdims=True)
    grad_rows = norm_scale * weighted - tok_rows * (norm_scale * norm_scale * norm_scale) * inner
    grad_gain = jnp.sum(grad_normed * tok_rows * norm_scale, axis=0)
    return (grad_rows, grad_gain)


def visible(seg_query, pos_query, seg_keys, pos_keys):
    own = (seg_keys[None, :] == seg_query[:, None]) & (pos_keys[None, :] <= pos_query[:, None])
    branch = (
        (seg_keys[None, :] == 0)
        & (seg_query[:, None] > 0)
        & (pos_keys[None, :] < seg_query[:, None] * CLEN)
    )
    return own | branch


def general(
    tokens,
    w_query,
    key_weight,
    value_weight,
    w_out,
    w_gate,
    w_up,
    w_down,
    gain_attn,
    gain_ffn,
    segments,
    positions,
    cotangent,
):
    groups, tok_local, model_width = tokens.shape
    token_count = groups * tok_local
    heads_here = w_query.shape[1] // HEAD_SIZE
    kv_here = key_weight.shape[1] // HEAD_SIZE
    per_kv = heads_here // kv_here
    kv_width = kv_here * HEAD_SIZE
    score_scale = 1.0 / math.sqrt(HEAD_SIZE)
    context_index = lax.axis_index("context")
    first_row = context_index * tok_local
    seg_here = lax.dynamic_slice_in_dim(segments, first_row, tok_local, 1)
    pos_here = lax.dynamic_slice_in_dim(positions, first_row, tok_local, 1)
    w_query, key_weight, value_weight, w_gate, w_up, gain_attn, gain_ffn = (
        lax.all_gather(w_query, "shard", axis=0, tiled=True),
        lax.all_gather(key_weight, "shard", axis=0, tiled=True),
        lax.all_gather(value_weight, "shard", axis=0, tiled=True),
        lax.all_gather(w_gate, "shard", axis=0, tiled=True),
        lax.all_gather(w_up, "shard", axis=0, tiled=True),
        lax.all_gather(gain_attn, "shard", axis=0, tiled=True),
        lax.all_gather(gain_ffn, "shard", axis=0, tiled=True),
    )
    w_out, w_down = (
        lax.all_gather(w_out, "shard", axis=1, tiled=True),
        lax.all_gather(w_down, "shard", axis=1, tiled=True),
    )
    gain_one = gain_attn.astype(jnp.float32)
    gain_two = gain_ffn.astype(jnp.float32)
    tok_rows = tokens.reshape(token_count, model_width).astype(jnp.float32)
    scale_one = lax.rsqrt(jnp.mean(tok_rows * tok_rows, axis=-1, keepdims=True) + norm_eps)
    normed_input = (tok_rows * scale_one * gain_one).astype(jnp.bfloat16)
    cosine_table, sine_values = tables(pos_here.reshape(token_count))
    query_heads_rows = rotary_apply(
        jnp.dot(normed_input, w_query, preferred_element_type=jnp.float32).reshape(
            token_count, heads_here, HEAD_SIZE
        ),
        cosine_table,
        sine_values,
    )
    query_heads_rows = query_heads_rows.astype(jnp.bfloat16).reshape(
        groups, tok_local, heads_here * HEAD_SIZE
    )
    key_rows = rotary_apply(
        jnp.dot(normed_input, key_weight, preferred_element_type=jnp.float32).reshape(
            token_count, kv_here, HEAD_SIZE
        ),
        cosine_table,
        sine_values,
    )
    key_rows = key_rows.astype(jnp.bfloat16).reshape(token_count, kv_width)
    value_rows = jnp.dot(normed_input, value_weight, preferred_element_type=jnp.float32).astype(
        jnp.bfloat16
    )
    keyval = jnp.concatenate([key_rows, value_rows], axis=-1).reshape(
        groups, tok_local, 2 * kv_width
    )
    gathered = lax.all_gather(keyval, "context", axis=1, tiled=True)

    def scores_of(group_queries, group_keyval, seg_query, pos_query, seg_keys, pos_keys):
        grouped_heads = group_queries.reshape(tok_local, kv_here, per_kv, HEAD_SIZE)
        key_head_rows = group_keyval[:, :kv_width].reshape(-1, kv_here, HEAD_SIZE)
        scores = (
            jnp.einsum(
                "bhgd,khd->hgbk", grouped_heads, key_head_rows, preferred_element_type=jnp.float32
            )
            * score_scale
        )
        allowed = visible(seg_query, pos_query, seg_keys, pos_keys)
        return (jnp.where(allowed[None, None], scores, -1e30), grouped_heads, key_head_rows)

    def attend_group(inputs):
        group_queries, group_keyval, seg_query, pos_query, seg_keys, pos_keys = inputs
        scores, grouped_heads, key_head_rows = scores_of(
            group_queries, group_keyval, seg_query, pos_query, seg_keys, pos_keys
        )
        top_score = jnp.max(scores, axis=-1, keepdims=True)
        exponent = jnp.exp(scores - top_score)
        totals = jnp.sum(exponent, axis=-1, keepdims=True)
        soft_weights = (exponent / totals).astype(jnp.bfloat16)
        value_head_rows = group_keyval[:, kv_width:].reshape(-1, kv_here, HEAD_SIZE)
        attended_output = jnp.einsum(
            "hgbk,khd->bhgd", soft_weights, value_head_rows, preferred_element_type=jnp.float32
        )
        return (
            attended_output.reshape(tok_local, heads_here * HEAD_SIZE),
            (top_score + jnp.log(totals))[..., 0],
        )

    attended_output, log_total = lax.map(
        attend_group, (query_heads_rows, gathered, seg_here, pos_here, segments, positions)
    )
    attended_low = attended_output.reshape(token_count, heads_here * HEAD_SIZE).astype(jnp.bfloat16)
    attn_sum = lax.psum(jnp.dot(attended_low, w_out, preferred_element_type=jnp.float32), "tensor")
    middle = tok_rows + attn_sum
    scale_two = lax.rsqrt(jnp.mean(middle * middle, axis=-1, keepdims=True) + norm_eps)
    normed_two = (middle * scale_two * gain_two).astype(jnp.bfloat16)
    gate_proj = jnp.dot(normed_two, w_gate, preferred_element_type=jnp.float32)
    up_proj = jnp.dot(normed_two, w_up, preferred_element_type=jnp.float32)
    sigmoid_gate = jax.nn.sigmoid(gate_proj)
    silu_gate = gate_proj * sigmoid_gate
    hidden = (silu_gate * up_proj).astype(jnp.bfloat16)
    ffn_sum = lax.psum(
        jnp.dot(hidden, w_down, preferred_element_type=jnp.float32).astype(jnp.bfloat16), "tensor"
    ).astype(jnp.float32)
    output = (middle + ffn_sum).astype(jnp.bfloat16).reshape(groups, tok_local, model_width)
    grad_low = cotangent.reshape(token_count, model_width)
    grad_out = grad_low.astype(jnp.float32)
    grad_hidden = contract_cols(grad_low, w_down)
    grad_w_down_t = contract_rows(grad_low, hidden)
    grad_gate = (
        grad_hidden * up_proj * sigmoid_gate * (1.0 + gate_proj * (1.0 - sigmoid_gate))
    ).astype(jnp.bfloat16)
    grad_up = (grad_hidden * silu_gate).astype(jnp.bfloat16)
    grad_w_gate = contract_rows(normed_two, grad_gate)
    grad_w_up = contract_rows(normed_two, grad_up)
    grad_normed_two = lax.psum(
        contract_cols(grad_gate, w_gate) + contract_cols(grad_up, w_up), "tensor"
    )
    back_two, grad_gain_two = norm_back(middle, scale_two, gain_two, grad_normed_two)
    grad_middle = grad_out + back_two
    grad_mid_low = grad_middle.astype(jnp.bfloat16)
    grad_w_out_t = contract_rows(grad_mid_low, attended_low)
    grad_attended = (
        contract_cols(grad_mid_low, w_out)
        .astype(jnp.bfloat16)
        .reshape(groups, tok_local, heads_here * HEAD_SIZE)
    )

    def attend_back(inputs):
        (
            group_queries,
            group_keyval,
            group_grad,
            group_total,
            seg_query,
            pos_query,
            seg_keys,
            pos_keys,
        ) = inputs
        scores, grouped_heads, key_head_rows = scores_of(
            group_queries, group_keyval, seg_query, pos_query, seg_keys, pos_keys
        )
        soft_weights = jnp.exp(scores - group_total[..., None])
        value_head_rows = group_keyval[:, kv_width:].reshape(-1, kv_here, HEAD_SIZE)
        grad_grouped = group_grad.reshape(tok_local, kv_here, per_kv, HEAD_SIZE)
        grad_weights = jnp.einsum(
            "bhgd,khd->hgbk", grad_grouped, value_head_rows, preferred_element_type=jnp.float32
        )
        inner = jnp.sum(soft_weights * grad_weights, axis=-1, keepdims=True)
        grad_scores = (soft_weights * (grad_weights - inner)).astype(jnp.bfloat16)
        grad_queries = (
            jnp.einsum(
                "hgbk,khd->bhgd", grad_scores, key_head_rows, preferred_element_type=jnp.float32
            )
            * score_scale
        )
        grad_keys = (
            jnp.einsum(
                "hgbk,bhgd->khd", grad_scores, grouped_heads, preferred_element_type=jnp.float32
            )
            * score_scale
        )
        grad_values = jnp.einsum(
            "hgbk,bhgd->khd",
            soft_weights.astype(jnp.bfloat16),
            grad_grouped,
            preferred_element_type=jnp.float32,
        )
        grad_keyval = jnp.concatenate(
            [grad_keys.reshape(-1, kv_width), grad_values.reshape(-1, kv_width)], axis=-1
        )
        return (grad_queries.reshape(tok_local, heads_here * HEAD_SIZE), grad_keyval)

    grad_queries, grad_keyval = lax.map(
        attend_back,
        (
            query_heads_rows,
            gathered,
            grad_attended,
            log_total,
            seg_here,
            pos_here,
            segments,
            positions,
        ),
    )
    grad_keyval = lax.psum_scatter(grad_keyval, "context", scatter_dimension=1, tiled=True)
    grad_query_rows = rotate_back(
        grad_queries.reshape(token_count, heads_here, HEAD_SIZE), cosine_table, sine_values
    )
    grad_query_rows = grad_query_rows.astype(jnp.bfloat16).reshape(
        token_count, heads_here * HEAD_SIZE
    )
    grad_key_rows = rotate_back(
        grad_keyval[..., :kv_width].reshape(token_count, kv_here, HEAD_SIZE),
        cosine_table,
        sine_values,
    )
    grad_key_rows = grad_key_rows.astype(jnp.bfloat16).reshape(token_count, kv_width)
    grad_value_rows = (
        grad_keyval[..., kv_width:].reshape(token_count, kv_width).astype(jnp.bfloat16)
    )
    grad_w_query = contract_rows(normed_input, grad_query_rows)
    grad_w_key = contract_rows(normed_input, grad_key_rows)
    grad_w_value = contract_rows(normed_input, grad_value_rows)
    partial_one = (
        contract_cols(grad_query_rows, w_query)
        + contract_cols(grad_key_rows, key_weight)
        + contract_cols(grad_value_rows, value_weight)
    )
    grad_normed = lax.psum(partial_one, "tensor")
    back_one, grad_gain_one = norm_back(tok_rows, scale_one, gain_one, grad_normed)
    tokens_grad = (
        (grad_middle + back_one).astype(jnp.bfloat16).reshape(groups, tok_local, model_width)
    )
    summed = (
        lax.psum_scatter(grad_w_query, ("shard", "context"), scatter_dimension=0, tiled=True),
        lax.psum_scatter(grad_w_key, ("shard", "context"), scatter_dimension=0, tiled=True),
        lax.psum_scatter(grad_w_value, ("shard", "context"), scatter_dimension=0, tiled=True),
        lax.psum_scatter(grad_w_out_t, ("shard", "context"), scatter_dimension=0, tiled=True),
        lax.psum_scatter(grad_w_gate, ("shard", "context"), scatter_dimension=0, tiled=True),
        lax.psum_scatter(grad_w_up, ("shard", "context"), scatter_dimension=0, tiled=True),
        lax.psum_scatter(grad_w_down_t, ("shard", "context"), scatter_dimension=0, tiled=True),
        lax.psum_scatter(grad_gain_one, ("shard", "context"), scatter_dimension=0, tiled=True),
        lax.psum_scatter(grad_gain_two, ("shard", "context"), scatter_dimension=0, tiled=True),
    )
    summed = (
        lax.all_gather(summed[0].astype(jnp.bfloat16), "context", axis=0, tiled=True).astype(
            jnp.float32
        ),
        lax.all_gather(summed[1].astype(jnp.bfloat16), "context", axis=0, tiled=True).astype(
            jnp.float32
        ),
        lax.all_gather(summed[2].astype(jnp.bfloat16), "context", axis=0, tiled=True).astype(
            jnp.float32
        ),
        lax.all_gather(summed[3].astype(jnp.bfloat16), "context", axis=0, tiled=True).astype(
            jnp.float32
        ),
        lax.all_gather(summed[4].astype(jnp.bfloat16), "context", axis=0, tiled=True).astype(
            jnp.float32
        ),
        lax.all_gather(summed[5].astype(jnp.bfloat16), "context", axis=0, tiled=True).astype(
            jnp.float32
        ),
        lax.all_gather(summed[6].astype(jnp.bfloat16), "context", axis=0, tiled=True).astype(
            jnp.float32
        ),
        lax.all_gather(summed[7].astype(jnp.bfloat16), "context", axis=0, tiled=True).astype(
            jnp.float32
        ),
        lax.all_gather(summed[8].astype(jnp.bfloat16), "context", axis=0, tiled=True).astype(
            jnp.float32
        ),
    )
    return (
        output,
        tokens_grad,
        summed[0],
        summed[1],
        summed[2],
        summed[3].T,
        summed[4],
        summed[5],
        summed[6].T,
        summed[7],
        summed[8],
    )


MESH = pl.DeviceIdType.MESH
RUN = 256
PAD = 128
NEG = -1e30
LOG2E = 1.4426950408889634
BF = jnp.bfloat16
F32 = jnp.float32
VLIM = 64 * 1024 * 1024


def mm(a, b):
    return lax.dot_general(a, b, (((1,), (0,)), ((), ())), preferred_element_type=F32)


def mm_nt(a, b):
    return lax.dot_general(a, b, (((1,), (1,)), ((), ())), preferred_element_type=F32)


def mm_tn(a, b):
    return lax.dot_general(a, b, (((0,), (0,)), ((), ())), preferred_element_type=F32)


def iota(shape, axis):
    return lax.broadcasted_iota(jnp.int32, shape, axis)


def one_hot(hit):
    return jnp.where(hit, 1.0, 0.0).astype(BF)


def pad_matrix(heads, flip=False):
    shape = (heads * HEAD_SIZE, heads * PAD)
    if flip:
        row, col = iota(shape[::-1], 1), iota(shape[::-1], 0)
    else:
        row, col = iota(shape, 0), iota(shape, 1)
    lane = col & 127
    part = jnp.where(lane < 64, lane, lane - 16)
    return one_hot((row == (col >> 7) * HEAD_SIZE + part) & ((lane & 63) < 48))


def split_matrix():
    row, col = iota((RUN, RUN), 0), iota((RUN, RUN), 1)
    return one_hot(col == jnp.where(row < 128, 2 * row, 2 * row - 255))


def merge_matrix():
    row, col = iota((RUN, RUN), 0), iota((RUN, RUN), 1)
    return one_hot(col == (row >> 1) + (row & 1) * 128)


def rope_tables(run, cb_ref, sb_ref, cj_ref, sj_ref):
    cb, sb = cb_ref[pl.ds(run, 1), :], sb_ref[pl.ds(run, 1), :]
    cj, sj = cj_ref[...], sj_ref[...]
    return cb * cj - sb * sj, sb * cj + cb * sj


def rope(u, c, s):
    return u * c + pltpu.roll(u, 64, 1) * s


def rope_back(u, c, s):
    return u * c - pltpu.roll(u, 64, 1) * s


def vmem(*shape_dtype):
    return pl.BlockSpec(memory_space=pltpu.VMEM)


def entry_barrier(targets):
    bar = pltpu.get_barrier_semaphore()
    for t in targets:
        pl.semaphore_signal(bar, inc=1, device_id=t, device_id_type=MESH)
    pl.semaphore_wait(bar, len(targets))


def remote(src, dst, send, recv, target):
    return pltpu.make_async_remote_copy(
        src_ref=src, dst_ref=dst, send_sem=send, recv_sem=recv, device_id=target, device_id_type=MESH
    )


def first_kernel(nc, x_ref, dy_h, g_ref, cb_ref, sb_ref, cj_ref, sj_ref, wq_h, wk_h, wv_h, wo_h, wg_h, wu_h, wd_h,
                 xp_ref, dyp_ref, n1_ref, q_ref, kvp_ref, kvc_ref, wp_ref, gf_ref, wo_f, wg_f, wu_f, wd_f,
                 dy_v, wq_s, wk_s, wv_s, g_s, wo_v, wg_v, wu_v, wd_v, kv_send,
                 lsem, ssem, rsem, osem, csem, crem):
    s = lax.axis_index("shard")
    c = lax.axis_index("context")
    dh = g_s.shape[1] // 2
    own = pl.ds(pl.multiple_of(s * dh, dh), dh)
    other = {"shard": 1 - s}
    loads = [
        pltpu.make_async_copy(wq_h, wq_s.at[own], lsem.at[0]),
        pltpu.make_async_copy(wk_h, wk_s.at[:, own], lsem.at[1]),
        pltpu.make_async_copy(wv_h, wv_s.at[:, own], lsem.at[2]),
        pltpu.make_async_copy(g_ref, g_s.at[:, own], lsem.at[3]),
        pltpu.make_async_copy(wo_h, wo_v, lsem.at[4]),
        pltpu.make_async_copy(wg_h, wg_v, lsem.at[5]),
        pltpu.make_async_copy(wu_h, wu_v, lsem.at[6]),
        pltpu.make_async_copy(wd_h, wd_v, lsem.at[7]),
        pltpu.make_async_copy(dy_h, dy_v, lsem.at[8]),
    ]
    for cp in loads:
        cp.start()
    entry_barrier([other] + [{"context": lax.rem(c + i, nc)} for i in range(1, nc)])
    sends = [
        remote(wq_s.at[own], wq_s.at[own], ssem.at[0], rsem.at[0], other),
        remote(wk_s.at[:, own], wk_s.at[:, own], ssem.at[1], rsem.at[1], other),
        remote(wv_s.at[:, own], wv_s.at[:, own], ssem.at[2], rsem.at[2], other),
        remote(g_s.at[:, own], g_s.at[:, own], ssem.at[3], rsem.at[3], other),
        remote(wo_v, wo_f.at[:, own], ssem.at[4], rsem.at[4], other),
        remote(wg_v, wg_f.at[own], ssem.at[5], rsem.at[5], other),
        remote(wu_v, wu_f.at[own], ssem.at[6], rsem.at[6], other),
        remote(wd_v, wd_f.at[:, own], ssem.at[7], rsem.at[7], other),
    ]
    keeps = [
        pltpu.make_async_copy(wo_v, wo_f.at[:, own], osem.at[0]),
        pltpu.make_async_copy(wg_v, wg_f.at[own], osem.at[1]),
        pltpu.make_async_copy(wu_v, wu_f.at[own], osem.at[2]),
        pltpu.make_async_copy(wd_v, wd_f.at[:, own], osem.at[3]),
    ]
    for i in (3, 0, 1, 2, 4, 5, 6, 7):
        loads[i].wait()
        sends[i].start()
        if i >= 4:
            keeps[i - 4].start()
    half = x_ref.shape[0] // 2
    split = split_matrix()
    for i in range(x_ref.shape[0] // RUN):
        xb = mm(split, x_ref[pl.ds(i * RUN, RUN), :])
        xp_ref[pl.ds(i * 128, 128), :] = xb[:128].astype(BF)
        xp_ref[pl.ds(half + i * 128, 128), :] = xb[128:].astype(BF)
        if i == 0:
            sends[3].wait_recv()
        r = lax.rsqrt(jnp.mean(xb * xb, axis=-1, keepdims=True) + norm_eps)
        nb = (xb * r * g_s[0:1, :]).astype(BF)
        n1_ref[pl.ds(i * 128, 128), :] = nb[:128]
        n1_ref[pl.ds(half + i * 128, 128), :] = nb[128:]
    gf_ref[...] = g_s[...]
    hq, hk = wq_s.shape[1] // HEAD_SIZE, wk_s.shape[0] // HEAD_SIZE
    selq, selk = pad_matrix(hq, True), pad_matrix(hk, True)
    nq, nk = hq * PAD, hk * PAD
    for i in range(3):
        sends[i].wait_recv()
    wp_ref[0:nq, :] = mm_nt(selq, wq_s[...]).astype(BF)
    wp_ref[nq : nq + nk, :] = mm(selk, wk_s[...]).astype(BF)
    wp_ref[nq + nk :, :] = mm(selk, wv_s[...]).astype(BF)
    selkv = pad_matrix(2 * hk)
    runs = x_ref.shape[0] // RUN
    per = runs // 2
    kv_copies = []
    for run in range(runs):
        rows = pl.ds(run * RUN, RUN)
        y = mm_nt(n1_ref[rows, :], wp_ref[...])
        ct, st = rope_tables(run, cb_ref, sb_ref, cj_ref, sj_ref)
        for h in range(hq):
            q_ref[rows, h * PAD : (h + 1) * PAD] = rope(y[:, h * PAD : (h + 1) * PAD], ct, st).astype(BF)
        kv = [rope(y[:, nq + h * PAD : nq + (h + 1) * PAD], ct, st).astype(BF) for h in range(hk)]
        kv = jnp.concatenate(kv + [y[:, nq + nk :].astype(BF)], axis=1)
        if run < per:
            kv_send[pl.ds(run * RUN, RUN), :] = mm_nt(kv, selkv).astype(BF)
            mine = pl.ds(pl.multiple_of((c * per + run) * RUN, RUN), RUN)
            for i in range(1, nc):
                cp = remote(kv_send.at[pl.ds(run * RUN, RUN)], kvp_ref.at[mine], csem.at[run, i], crem.at[run, i],
                            {"context": lax.rem(c + i, nc)})
                cp.start()
                kv_copies.append(cp)
            cp = pltpu.make_async_copy(kv_send.at[pl.ds(run * RUN, RUN)], kvp_ref.at[mine], csem.at[run, 0])
            cp.start()
            kv_copies.append(cp)
        else:
            kvc_ref[pl.ds((run - per) * RUN, RUN), :] = kv
    loads[8].wait()
    for i in range(x_ref.shape[0] // RUN):
        b = mm(split, dy_v[pl.ds(i * RUN, RUN), :]).astype(BF)
        dyp_ref[pl.ds(i * 128, 128), :] = b[:128]
        dyp_ref[pl.ds(half + i * 128, 128), :] = b[128:]
    for cp in kv_copies:
        cp.wait()
    for i in range(4):
        keeps[i].wait()
        sends[4 + i].wait_recv()
    for cp in sends:
        cp.wait_send()


class Line:
    F_AT = (8, 9, 10, 12)
    D_AT = (11, 13, 14, 15)

    def __init__(self, n, chunk, pbuf, rbuf, obuf, sems):
        self.n, self.chunk, self.per = n, chunk, RUN // 2 // chunk
        self.count = 16 * self.per
        self.pbuf, self.rbuf, self.obuf = pbuf, rbuf, obuf
        self.rs, self.rr, self.bs, self.br = sems
        self.hop = 3
        self.turn = 2 * (n - 1) * self.hop
        self.slots = self.count + self.turn

    def pieces(self, h, i):
        n, chunk = self.n, self.chunk
        z = lax.axis_index("tensor")
        job = i // self.per
        late = jnp.where((job == 11) | (job > 12), 1, 0)
        row = jnp.where(job < 8, lax.rem(job, 4), jnp.where(late == 1, jnp.maximum(job - 12, 0), jnp.minimum(job - 8, 3)))
        part = jnp.where(job < 8, job // 4, 2 - late)
        off = row * RUN + h * (RUN // 2) + lax.rem(i, self.per) * chunk
        rows = pl.ds(pl.multiple_of(off, chunk), chunk)
        orows = pl.ds(pl.multiple_of(part * (4 * RUN) + off, chunk), chunk)
        place = z if h == 0 else n - 1 - z
        up, down = jnp.minimum(z + 1, n - 1), jnp.maximum(z - 1, 0)
        ahead = {"tensor": up if h == 0 else down}
        back = {"tensor": down if h == 0 else up}
        fwd = remote(self.pbuf.at[rows], self.rbuf.at[rows], self.rs.at[h, i], self.rr.at[h, i], ahead)
        ret = remote(self.obuf.at[orows], self.obuf.at[orows], self.bs.at[h, i], self.br.at[h, i], back)
        return rows, orows, place, fwd, ret

    def reduce_step(self, h, i):
        rows, orows, place, fwd, ret = self.pieces(h, i)
        n = self.n

        @pl.when(place == 0)
        def _():
            fwd.start()

        @pl.when(place > 0)
        def _():
            fwd.wait_recv()
            total = (self.rbuf[rows, :].astype(F32) + self.pbuf[rows, :].astype(F32)).astype(BF)

            @pl.when(place < n - 1)
            def _():
                self.pbuf[rows, :] = total
                fwd.start()

            @pl.when(place == n - 1)
            def _():
                self.obuf[orows, :] = total
                ret.start()

    def spread_step(self, h, i):
        rows, orows, place, fwd, ret = self.pieces(h, i)

        @pl.when(place < self.n - 1)
        def _():
            ret.wait_recv()

        @pl.when((place < self.n - 1) & (place > 0))
        def _():
            ret.start()

    def serve(self, t):
        n = self.n
        z = lax.axis_index("tensor")
        for h in range(2):
            place = z if h == 0 else n - 1 - z
            i = t - place * self.hop

            @pl.when((i >= 0) & (i < self.count))
            def _():
                self.reduce_step(h, i)

            j = t - (2 * (n - 1) - place) * self.hop

            @pl.when((j >= 0) & (j < self.count))
            def _():
                self.spread_step(h, j)

    def sent(self, job, fwd=True, ret=False):
        def step(i, _):
            for h in range(2):
                rows, orows, place, f, r = self.pieces(h, job * self.per + i)
                if fwd:

                    @pl.when(place < self.n - 1)
                    def _():
                        f.wait_send()

                if ret:

                    @pl.when(place > 0)
                    def _():
                        r.wait_send()

            return 0

        lax.fori_loop(0, self.per, step, 0)


def run_items(items, serve):
    total = max(e for spans, _ in items for _, e in spans)

    def step(k, _):
        for spans, body in items:
            hit = functools.reduce(jnp.logical_or, [(k >= lo) & (k < hi) for lo, hi in spans])
            pl.when(hit)(functools.partial(body, k))
        serve(k)
        return 0

    lax.fori_loop(0, total, step, 0)


class Square:
    def __init__(self, rows, cols, src, mine, theirs, spare, out, credit, shard_send, shard_recv, send, recv, store):
        self.src, self.mine, self.theirs, self.res, self.out = src, mine, theirs, theirs, out
        self.r1, self.r2 = [spare[0:2], spare[2:4]], spare[4:6]
        self.credit, self.shard_sems, self.shard_recv, self.send, self.recv, self.store_sem = credit, shard_send, shard_recv, send, recv, store
        self.rows, self.qr, self.cols = rows, rows // 4, cols
        c = lax.axis_index("context")
        self.cy, self.cx = c // 2, lax.rem(c, 2)

    def at(self, y, x, half):
        w = self.cols // 2
        return (pl.ds(pl.multiple_of((2 * y + x) * self.qr, self.qr), self.qr), pl.ds(half * w, w))

    def peer(self, half, first):
        if (half == 0) == first:
            return {"context": 2 * self.cy + 1 - self.cx}
        return {"context": 2 * (1 - self.cy) + self.cx}

    def shard_copy(self):
        return remote(self.src, self.theirs, self.shard_sems, self.shard_recv, {"shard": 1 - lax.axis_index("shard")})

    def outer(self, half):
        if half == 0:
            return [(y, 1 - self.cx) for y in range(2)], [(y, self.cx) for y in range(2)]
        return [(1 - self.cy, x) for x in range(2)], [(self.cy, x) for x in range(2)]

    def p1(self, half, j):
        return remote(self.mine.at[self.at(*self.outer(half)[0][j], half)], self.r1[half][j],
                      self.send.at[0, half, j], self.recv.at[0, half, j], self.peer(half, True))

    def p2(self, half):
        q = (1 - self.cy, self.cx) if half == 0 else (self.cy, 1 - self.cx)
        return remote(self.mine.at[self.at(*q, half)], self.r2[half],
                      self.send.at[1, half, 0], self.recv.at[1, half, 0], self.peer(half, False))

    def p3(self, half):
        at = self.at(self.cy, self.cx, half)
        return remote(self.res.at[at], self.res.at[at], self.send.at[1, half, 1], self.recv.at[1, half, 1], self.peer(half, False))

    def p4(self, half, j):
        at = self.at(*self.outer(half)[1][j], half)
        return remote(self.res.at[at], self.res.at[at], self.send.at[2, half, j], self.recv.at[2, half, j], self.peer(half, True))

    def free(self):
        for t in ({"shard": 1 - lax.axis_index("shard")}, self.peer(0, True), self.peer(0, False)):
            pl.semaphore_signal(self.credit, inc=1, device_id=t, device_id_type=MESH)

    def e0(self):
        pl.semaphore_wait(self.credit, 3)
        self.shard_copy().start()

    def e1(self):
        self.shard_copy().wait_recv()
        step = self.qr

        def add(i, _):
            rows = pl.ds(pl.multiple_of(i * step, step), step)
            self.mine[rows, :] = (self.mine[rows, :].astype(F32) + self.theirs[rows, :].astype(F32)).astype(BF)
            return 0

        lax.fori_loop(0, self.rows // step, add, 0)
        for j in range(2):
            for half in range(2):
                self.p1(half, j).start()

    def e2(self):
        for half in range(2):
            for j in range(2):
                self.p1(half, j).wait_recv()
                at = self.at(*self.outer(half)[1][j], half)
                self.mine[at] = (self.mine[at].astype(F32) + self.r1[half][j][...].astype(F32)).astype(BF)
            self.p2(half).start()

    def e3(self):
        for half in range(2):
            self.p2(half).wait_recv()
            at = self.at(self.cy, self.cx, half)
            self.res[at] = (self.mine[at].astype(F32) + self.r2[half][...].astype(F32)).astype(BF)
            self.p3(half).start()

    def e4(self):
        for half in range(2):
            self.p3(half).wait_recv()
            for j in range(2):
                self.p4(half, j).start()

    def e5(self):
        for half in range(2):
            for j in range(2):
                self.p4(half, j).wait_recv()

    def store(self):
        return pltpu.make_async_copy(self.res, self.out, self.store_sem)

    def done(self):
        self.shard_copy().wait_send()
        for half in range(2):
            for j in range(2):
                self.p1(half, j).wait_send()
                self.p4(half, j).wait_send()
            self.p2(half).wait_send()
            self.p3(half).wait_send()


def line_barrier(n, peers=()):
    z = lax.axis_index("tensor")
    bar = pltpu.get_barrier_semaphore()
    for t in peers:
        pl.semaphore_signal(bar, inc=1, device_id=t, device_id_type=MESH)

    @pl.when(z > 0)
    def _():
        pl.semaphore_signal(bar, inc=1, device_id={"tensor": jnp.maximum(z - 1, 0)}, device_id_type=MESH)

    @pl.when(z < n - 1)
    def _():
        pl.semaphore_signal(bar, inc=1, device_id={"tensor": jnp.minimum(z + 1, n - 1)}, device_id_type=MESH)

    pl.semaphore_wait(bar, len(peers) + jnp.minimum(z, 1) + jnp.minimum(n - 1 - z, 1))


def main_kernel(n, nc, chunk, kbase, qlim, cb_ref, sb_ref, cj_ref, sj_ref, gf_ref, q_ref, kvc_ref, wo_ref,
                kvp_h, xp_h, dyp_h, wg_h, wu_h, wd_h, n1_h, wp_h,
                out_h, tg_h, gg_h, gu_h, gd_h, go_h, gw_h, dm_h, gds_h, fp_h, gains_ref,
                k_s, v_s, s_s, o_v, op_v, lse_v, xs, ys, pbuf, rbuf, obuf, wd, n2, wg, wu, hid, dg, du, gt,
                dk_s, dv_s, do_v, dq_s, delta_s, dqp, dkv_s, go_v, st_o, st_t, st_p, gpart, grecv,
                lsem, ksem, osem, fsem, msem, nsem, qsend, qrecv, gs, gr, rs, rr, bs, br, credits, shard_send, shard_recv, send, recv, store):
    s = lax.axis_index("shard")
    c = lax.axis_index("context")
    rows_here, d = xs.shape
    runs = rows_here // RUN
    per = runs // 2
    half = rows_here // 2
    hk = k_s.shape[0]
    hq = q_ref.shape[1] // PAD
    rep = hq // hk
    blocks = k_s.shape[1] // RUN
    ff = wg.shape[1]
    dh = d // 2
    nq, nk = hq * PAD, hk * PAD
    score = 1.0 / math.sqrt(HEAD_SIZE)
    scale = LOG2E * score
    own = pl.ds(pl.multiple_of(s * dh, dh), dh)
    yours = pl.ds(pl.multiple_of((1 - s) * dh, dh), dh)
    wide = 2 * hk * HEAD_SIZE

    def at(i, size=RUN):
        return pl.ds(pl.multiple_of(i * size, size), size)

    kv_in = [dg.at[pl.ds((b % 4) * RUN, RUN), pl.ds(b // 4 * wide, wide)] for b in range(blocks)]
    key_loads = [pltpu.make_async_copy(kvp_h.at[pl.ds(b * RUN, RUN)], kv_in[b], ksem.at[b]) for b in range(blocks)]
    for cp in key_loads:
        cp.start()
    pairs = [(xp_h, xs), (wg_h, wg), (wu_h, wu), (dyp_h, ys), (wd_h, wd)]
    loads = [pltpu.make_async_copy(a, b, lsem.at[i]) for i, (a, b) in enumerate(pairs)]
    for cp in loads:
        cp.start()
    peers = [{"shard": lax.rem(s + i // nc, 2), "context": lax.rem(c + lax.rem(i, nc), nc)} for i in range(1, 2 * nc)]
    line_barrier(n, peers)
    line = Line(n, chunk, pbuf, rbuf, obuf, (rs, rr, bs, br))
    a_of = lambda job: at(job)
    b_of = lambda job: at(runs + job)
    lane = iota((RUN, PAD), 1)
    for b in range(blocks):
        key_loads[b].wait()
        kv = mm(kv_in[b][...], pad_matrix(2 * hk))
        rows = pl.ds(b * RUN, RUN)
        for g in range(hk):
            k_s[g, rows, :] = kv[:, g * PAD : (g + 1) * PAD].astype(BF)
            v_s[g, rows, :] = jnp.where(lane == 48, 1.0, kv[:, (hk + g) * PAD : (hk + g + 1) * PAD]).astype(BF)
    dk_s[...] = jnp.zeros_like(dk_s)
    dv_s[...] = jnp.zeros_like(dv_s)
    gpart[...] = jnp.zeros_like(gpart)

    def across(total, width, body):
        def step(i, _):
            body(at(i, width))
            return 0

        lax.fori_loop(0, total // width, step, 0)

    def down_rows(start, count, size, body):
        def step(i, _):
            body(pl.ds(pl.multiple_of(start + i * size, size), size), pl.ds(pl.multiple_of(i * size, size), size))
            return 0

        lax.fori_loop(0, count // size, step, 0)

    def head(k, mixed):
        job, h = k // hq, lax.rem(k, hq)
        run = job + per if mixed else job - per
        diff = iota((RUN, RUN), 1) - iota((RUN, RUN), 0)
        rows, cols = at(run), at(h, PAD)
        g = h // rep
        q = q_ref[rows, cols]
        lim = qlim[run]
        top = None
        for b in range(blocks):
            t = mm_nt(q, k_s[g, pl.ds(b * RUN, RUN), :]) * scale
            room = lim - kbase[b]
            if mixed:
                t = t + jnp.where(room >= 0, 0.0, NEG)
            else:
                t = jnp.where(diff <= room, t, NEG)
            s_s[:, b * RUN : (b + 1) * RUN] = t
            top = t if top is None else jnp.maximum(top, t)
        if mixed:
            crow = at(run - per)
            kc = kvc_ref[crow, at(g, PAD)]
            vc = kvc_ref[crow, at(hk + g, PAD)]
            vc = jnp.where(lane == 48, 1.0, vc.astype(F32)).astype(BF)
            t = jnp.where(diff <= 0, mm_nt(q, kc) * scale, NEG)
            s_s[:, blocks * RUN :] = t
            top = jnp.maximum(top, t)
        m = jnp.max(top, axis=1, keepdims=True)
        acc = None
        for b in range(blocks):
            p = jnp.exp2(s_s[:, b * RUN : (b + 1) * RUN] - m).astype(BF)
            o = mm(p, v_s[g, pl.ds(b * RUN, RUN), :])
            acc = o if acc is None else acc + o
        if mixed:
            p = jnp.exp2(s_s[:, blocks * RUN :] - m).astype(BF)
            acc = acc + mm(p, vc)
        total = acc[:, 48:49]
        op_v[rows, cols] = (acc / total).astype(BF)
        lse = jnp.broadcast_to(m + jnp.log2(total), (RUN, PAD)).T
        lse_v[at(run * hq + h, 8), :] = lse[0:8, :]

        @pl.when(h == hq - 1)
        def _():
            o = mm_nt(op_v[rows, :], pad_matrix(hq)).astype(BF)
            o_v[rows, :] = o


            def out(cols):
                pbuf[at(job), cols] = mm(o, wo_ref[:, cols]).astype(BF)

            across(d, 512, out)

    first = runs * hq

    def ffn(k):
        job = (k - first) // 4
        part = lax.rem(k - first, 4)
        run = lax.rem(job + per, runs)
        rows = at(run)

        @pl.when(k == first)
        def _():
            for cp in loads:
                cp.wait()

        @pl.when(part == 0)
        def _():
            def norm(to, sub):
                srows = pl.ds(pl.multiple_of(job * RUN + sub.start, 32), 32)
                mid = xs[to, :].astype(F32) + obuf[srows, :].astype(F32)
                r = lax.rsqrt(jnp.mean(mid * mid, axis=-1, keepdims=True) + norm_eps)
                n2[to, :] = (mid * r * gf_ref[8:9, :]).astype(BF)

            down_rows(run * RUN, RUN, 32, norm)

            def gate(cols):
                s_s[:, cols] = mm(n2[rows, :], wg[:, cols])

            across(ff, 512, gate)

        @pl.when(part == 1)
        def _():
            def up(i, _):
                s_s[:, pl.ds(pl.multiple_of(ff + i * 512, 512), 512)] = mm(n2[rows, :], wu[:, at(i, 512)])
                return 0

            lax.fori_loop(0, ff // 512, up, 0)

        @pl.when(part == 2)
        def _():
            def gated(i, _):
                cols = at(i)
                dhid = mm_nt(ys[rows, :], wd[cols, :])
                gate, up = s_s[:, cols], s_s[:, pl.ds(pl.multiple_of(ff + i * RUN, RUN), RUN)]
                sig = jax.nn.sigmoid(gate)
                silu = gate * sig
                hid[rows, cols] = (silu * up).astype(BF)
                dg[rows, cols] = (dhid * up * sig * (1.0 + gate * (1.0 - sig))).astype(BF)
                du[rows, cols] = (dhid * silu).astype(BF)
                return 0

            lax.fori_loop(0, ff // RUN, gated, 0)

        @pl.when(part == 3)
        def _():
            line.sent(job)

            def normed_two(cols):
                pbuf[at(job), cols] = (mm_nt(dg[rows, :], wg[cols, :]) + mm_nt(du[rows, :], wu[cols, :])).astype(BF)

            across(d, 512, normed_two)
            cp = pltpu.make_async_copy(st_o, fp_h.at[at(job)], osem.at[0])

            @pl.when(job > 0)
            def _():
                cp.wait()

            def project(cols):
                st_o[:, cols] = mm(hid[rows, :], wd[:, cols]).astype(BF)

            across(d, 512, project)
            cp.start()

    second = first + 4 * runs

    def stage(st, sem, dst, value, busy=True):
        cp = pltpu.make_async_copy(st, dst, sem)
        if busy is True:
            cp.wait()
        else:
            pl.when(busy)(cp.wait)

        def fill(cols):
            st[:, cols] = value(cols)

        across(d, 512, fill)
        cp.start()

    def grads_down(k):
        i = k - second
        for j in range(2):
            cols = at(2 * i + j)
            ht = hid[:, cols].T
            stage(st_o, osem.at[0], gds_h.at[cols], lambda to: mm(ht, ys[:, to]).astype(BF))

    def grads_up(k):
        i = k - second - 2
        for j in range(2):
            cols = at(2 * i + j)
            nt = n2[:, cols].T


            def both(to):
                wg[cols, to] = mm(nt, dg[:, to]).astype(BF)
                wu[cols, to] = mm(nt, du[:, to]).astype(BF)

            across(ff, 512, both)

    back = second + 5

    def middle(k):
        job = (k - back) // 5
        run = lax.rem(job + per, runs)
        rows = at(run)
        cp = pltpu.make_async_copy(s_s.at[:, pl.ds(0, d)], dm_h.at[rows], osem.at[1])

        @pl.when(job > 0)
        def _():
            cp.wait()

        def one(to, sub):
            def there(base):
                return pl.ds(pl.multiple_of(base + sub.start, 32), 32)

            mid = xs[to, :].astype(F32) + obuf[there(job * RUN), :].astype(F32)
            r = lax.rsqrt(jnp.mean(mid * mid, axis=-1, keepdims=True) + norm_eps)
            dn = obuf[there((runs + job) * RUN), :].astype(F32)
            w = gf_ref[8:9, :] * dn
            inner = jnp.mean(w * mid, axis=-1, keepdims=True)
            dm = ys[to, :].astype(F32) + r * w - mid * (r * r * r) * inner
            s_s[sub, 0:d] = dm
            gpart[8:16, :] += jnp.sum((dn * mid * r).reshape(4, 8, d), axis=0)
            ys[to, :] = dm.astype(BF)

        down_rows(run * RUN, RUN, 32, one)
        cp.start()
        do = mm_nt(ys[rows, :], wo_ref[...]).astype(BF)
        do_v[rows, :] = mm(do, pad_matrix(hq)).astype(BF)

    width = rep * RUN

    def pair(k, mixed):
        job = (k - back) // 5
        idx = lax.rem(k - back, 5) - 1
        g, part = idx // 2, lax.rem(idx, 2)
        run = lax.rem(job + per, runs)
        rows = at(run)
        diff = iota((RUN, width), 0) - (iota((RUN, width), 1) & (RUN - 1))

        def stack(ref):
            return jnp.concatenate([ref[rows, at(g * rep + j, PAD)] for j in range(rep)], axis=0)

        q, do = stack(q_ref), stack(do_v)

        @pl.when(part == 0)
        def _():
            op = stack(op_v)
            delta_s[0:1, :] = jnp.sum((do.astype(F32) * op.astype(F32)).T, axis=0, keepdims=True)
            dq_s[...] = jnp.zeros_like(dq_s)

        delta = delta_s[0:1, :]
        lse = jnp.concatenate(
            [lse_v[pl.ds(pl.multiple_of((run * hq + g * rep + j) * 8, 8), 1), :] for j in range(rep)], axis=1
        )
        lim = qlim[run]

        def tile(kk, vv, hide):
            p = jnp.exp2(hide(mm_nt(kk, q) * scale - lse))
            ds = (p * (mm_nt(vv, do) - delta)).astype(BF)
            return mm(ds, q), mm(p.astype(BF), do), mm_tn(ds, kk)

        dq = dq_s[...]
        for bb in range(blocks // 2):
            b = part * (blocks // 2) + bb
            room = lim - kbase[b]
            if mixed:
                hide = lambda t: t + jnp.where(room >= 0, 0.0, NEG)
            else:
                hide = lambda t: jnp.where(diff <= room, t, NEG)
            dk, dv, dd = tile(k_s[g, at(b), :], v_s[g, at(b), :], hide)
            dk_s[g, at(b), :] += dk
            dv_s[g, at(b), :] += dv
            dq = dq + dd
        dq_s[...] = dq

        @pl.when(part == 1)
        def _():
            total = dq_s[...]
            ct, st = rope_tables(run, cb_ref, sb_ref, cj_ref, sj_ref)
            if mixed:
                crow = at(run - per)
                dk, dv, dd = tile(kvc_ref[crow, at(g, PAD)], kvc_ref[crow, at(hk + g, PAD)], lambda t: jnp.where(diff <= 0, t, NEG))
                total = total + dd
                dkv_s[rows, at(g, PAD)] = rope_back(dk * score, ct, st).astype(BF)
                dkv_s[rows, at(hk + g, PAD)] = dv.astype(BF)
            for j in range(rep):
                dqp[rows, at(g * rep + j, PAD)] = rope_back(total[j * RUN : (j + 1) * RUN] * score, ct, st).astype(BF)

    def spare(ref, r0, c0, rows, cols, across, count):
        return [ref.at[pl.ds(r0 + i // across * rows, rows), pl.ds(c0 + i % across * cols, cols)] for i in range(count)]

    def square(i, rows, cols, src, mine, theirs, views, out):
        return Square(rows, cols, src, mine, theirs, views, out, credits.at[i], shard_send.at[i], shard_recv.at[i], send.at[i], recv.at[i], store.at[i])

    q4, w4 = dh // 4, ff // 2
    sq_g = square(0, dh, ff, wg.at[yours], wg.at[own], dg.at[pl.ds(0, dh)], spare(n2, 0, 0, q4, w4, 2, 6), gg_h)
    left = spare(n2, 0, 2 * w4, q4, w4, 1, 3) + spare(n2, 3 * q4, 0, q4, w4, 3, 3)
    sq_u = square(1, dh, ff, wu.at[yours], wu.at[own], du.at[pl.ds(0, dh)], left, gu_h)
    f4, d4 = ff // 4, dh // 2
    sq_d = square(2, ff, dh, gds_h.at[:, yours], hid.at[:, pl.ds(0, dh)], gt,
                  spare(n2, dh, 0, f4, d4, 4, 4) + spare(dg, dh, 0, f4, d4, 2, 2), gd_h)
    dq_cols = hq * HEAD_SIZE
    sq_o = square(3, dq_cols, dh, go_v.at[1 - s], go_v.at[s], wg.at[pl.ds(0, dq_cols), pl.ds(0, dh)],
                  spare(wg, dq_cols, 0, dq_cols // 4, d4, 2, 6), go_h)
    gw_cols = dq_cols + wide
    sq_w = square(4, dh, gw_cols, wu.at[yours, pl.ds(0, gw_cols)], wu.at[own, pl.ds(0, gw_cols)], hid.at[pl.ds(0, dh), pl.ds(0, gw_cols)],
                  spare(gt, 0, 0, q4, gw_cols // 2, 2, 6), gw_h)
    down_load = pltpu.make_async_copy(gds_h.at[:, own], hid.at[:, pl.ds(0, dh)], lsem.at[5])
    wp_load = pltpu.make_async_copy(wp_h, wd, lsem.at[6])

    def f_load(job):
        return pltpu.make_async_copy(fp_h.at[at(job)], pbuf.at[at(job)], fsem.at[job])

    def f_start(job):
        line.sent(4 + job)
        f_load(job).start()

    def key_piece(b):
        return ys.at[pl.ds(pl.multiple_of(lax.rem(b, 4) * RUN, RUN), RUN), pl.ds(pl.multiple_of(b // 4 * wide, wide), wide)]

    def key_recv(i, run):
        m = (i - 1) * per + run
        return ys.at[pl.ds(m % 4 * RUN, RUN), pl.ds(dh + m // 4 * wide, wide)]

    def key_copy(i, run):
        to = lax.rem(c + i, nc)
        return remote(key_piece(to * per + run), key_recv(i, run), qsend.at[i, run], qrecv.at[i, run], {"context": to})

    def pack():
        ot = o_v[...].T
        for j in range(2):


            def part(cols, j=j):
                go_v[j, :, cols] = mm(ot, ys[:, pl.ds(pl.multiple_of(j * dh + cols.start, RUN), RUN)]).astype(BF)

            across(dh, RUN, part)
        for i in range(1, nc):
            pl.semaphore_signal(credits.at[5], inc=1, device_id={"context": lax.rem(c + i, nc)}, device_id_type=MESH)

        def one(b, _):
            rows = at(b)
            parts = [(dk_s[g, rows, :] * score).astype(BF) for g in range(hk)]
            parts += [dv_s[g, rows, :].astype(BF) for g in range(hk)]
            value = mm_nt(jnp.concatenate(parts, axis=1), pad_matrix(2 * hk)).astype(BF)
            key_piece(b)[...] = value
            return 0

        lax.fori_loop(0, blocks, one, 0)
        pl.semaphore_wait(credits.at[5], nc - 1)
        for i in range(1, nc):
            for run in range(per):
                key_copy(i, run).start()

    def normed(job):
        rows = at(lax.rem(job + per, runs))
        line.sent(8 + job + jnp.where(job == 3, 1, 0))
        line.sent(4 + job, fwd=False, ret=True)

        def part(cols):
            dn = mm(dqp[rows, :], wd[0:nq, cols]) + mm(dkv_s[rows, :], wd[nq:, cols])
            pbuf[at(job), cols] = dn.astype(BF)

        across(d, 512, part)

    def keys():
        for i in range(1, nc):
            for run in range(per):
                key_copy(i, run).wait_recv()
        selkv = pad_matrix(2 * hk)
        for run in range(per):
            rows = pl.ds(run * RUN, RUN)
            total = mm(key_piece(c * per + run)[...], selkv)
            for i in range(1, nc):
                total = total + mm(key_recv(i, run)[...], selkv)
            ct, st = rope_tables(run, cb_ref, sb_ref, cj_ref, sj_ref)
            for g in range(hk):
                dkv_s[rows, g * PAD : (g + 1) * PAD] = rope_back(total[:, g * PAD : (g + 1) * PAD], ct, st).astype(BF)
            dkv_s[rows, hk * PAD :] = total[:, hk * PAD :].astype(BF)

    tile_v = hid.at[:, pl.ds(dh, RUN)]

    def tile_load(i):
        return pltpu.make_async_copy(n1_h.at[:, at(i)], tile_v, nsem)

    def grads_in(k):
        i = k - into

        @pl.when(i == 0)
        def _():
            def pack_rows(to, sub):
                du[to, 0:dq_cols] = mm_nt(dqp[to, :], pad_matrix(hq)).astype(BF)
                du[to, dq_cols:gw_cols] = mm_nt(dkv_s[to, :], pad_matrix(2 * hk)).astype(BF)

            down_rows(0, rows_here, RUN, pack_rows)

        for j in range(2):
            tile_load(2 * i + j).wait()
            nt = tile_v[...].T


            def part(cols, j=j):
                wu[at(2 * i + j), cols] = mm(nt, du[:, cols]).astype(BF)

            across(gw_cols, gw_cols // 2, part)

            @pl.when(2 * i + j + 1 < d // RUN)
            def _():
                tile_load(2 * i + j + 1).start()

    def halves(i, body):
        for j in range(2):

            def step(m, _, j=j):
                natural = pl.ds(pl.multiple_of(j * half + i * 128 + m * 32, 32), 32)
                by_job = lambda part: pl.ds(pl.multiple_of(part * rows_here + (1 - j) * half + i * 128 + m * 32, 32), 32)
                body(natural, by_job, pl.ds(pl.multiple_of(j * 128 + m * 32, 32), 32))
                return 0

            lax.fori_loop(0, 4, step, 0)

    def output(k):
        i = k - outs

        def one(natural, by_job, to):
            total = xs[natural, :].astype(F32) + obuf[by_job(0), :].astype(F32)
            st_p[to, :] = (total + obuf[by_job(2), :].astype(F32)).astype(BF)

        halves(i, one)
        stage(st_o, osem.at[0], out_h.at[at(i)], lambda cols: mm(merge_matrix(), st_p[:, cols]).astype(BF), i > 0)

    def m_load(i, j):
        src = dm_h.at[pl.ds(pl.multiple_of(j * half + i * 128, 128), 128)]
        return pltpu.make_async_copy(src, s_s.at[pl.ds(j * 128, 128), pl.ds(0, d)], msem.at[j])

    def finals(i):
        for j in range(2):
            m_load(i, j).wait()

        def one(natural, by_job, to):
            x = xs[natural, :].astype(F32)
            dn = obuf[by_job(1), :].astype(F32)
            r = lax.rsqrt(jnp.mean(x * x, axis=-1, keepdims=True) + norm_eps)
            w = gf_ref[0:1, :] * dn
            inner = jnp.mean(w * x, axis=-1, keepdims=True)
            st_p[to, :] = (s_s[to, 0:d] + (r * w - x * (r * r * r) * inner)).astype(BF)
            gpart[0:8, :] += jnp.sum((dn * x * r).reshape(4, 8, d), axis=0)

        halves(i, one)

        @pl.when(i + 1 < runs)
        def _():
            for j in range(2):
                m_load(i + 1, j).start()

        cp = pltpu.make_async_copy(st_t, tg_h.at[at(i)], osem.at[2])

        @pl.when(i > 0)
        def _():
            cp.wait()

        def fill(cols):
            st_t[:, cols] = mm(merge_matrix(), st_p[:, cols]).astype(BF)

        across(d, 512, fill)
        cp.start()

    packed = back + 5 * runs
    into = packed + 3
    outs = into + 4
    lag = hq - 1

    def due(job):
        return (line.per * (job + 1) - 1 + line.turn) // 2 + lag + 1

    begins = [back + 5 * job for job in range(runs)]
    items = [([(0, per * hq)], lambda k: head(k, True)), ([(per * hq, first)], lambda k: head(k, False)), ([(first, second)], ffn),
             ([(second, second + 2)], grads_down), ([(second + 2, back)], grads_up), ([(b, b + 1) for b in begins], middle),
             ([(b + 1, b + 5) for b in begins[:per]], lambda k: pair(k, True)),
             ([(b + 1, b + 5) for b in begins[per:]], lambda k: pair(k, False)),
             ([(into, into + 3)], grads_in), ([(outs, outs + runs)], output)]
    fin = due(Line.D_AT[per])

    def begin_down():
        pltpu.make_async_copy(st_o, gds_h.at[pl.ds(0, RUN)], osem.at[0]).wait()
        down_load.start()
        wp_load.start()

    def free_three():
        for sq in (sq_g, sq_u, sq_d):
            sq.free()
        for sq in (sq_g, sq_u, sq_d):
            sq.e0()

    def store_start(sq):
        def body():
            sq.e5()
            sq.store().start()

        return body

    def dm_begin():
        pltpu.make_async_copy(s_s.at[:, pl.ds(0, d)], dm_h.at[pl.ds(0, RUN)], osem.at[1]).wait()
        for j in range(2):
            m_load(0, j).start()

    def first_e1():
        down_load.wait()
        sq_d.e1()

    def give_o():
        sq_g.store().wait()
        sq_g.done()
        sq_o.free()

    def give_w():
        sq_d.store().wait()
        sq_d.done()
        sq_w.free()

    def release_u():
        sq_u.store().wait()
        sq_u.done()

    def number(k, steps):
        return sum(jnp.where(k >= step, 1, 0) for step in steps[1:])

    events = [(second + 2, begin_down), (second + 4, free_three)]
    at_f = [4 * Line.F_AT[job] + lag - 2 for job in range(runs)]
    events += [
        (39, first_e1), (40, sq_g.e1), (41, sq_d.e2), (41, sq_u.e1), (42, sq_g.e2), (43, sq_d.e3), (44, sq_u.e2), (44, sq_g.e3),
        (45, wp_load.wait), (45, sq_d.e4), (46, sq_g.e4), (47, sq_u.e3), (48, store_start(sq_d)), (49, store_start(sq_g)),
        (50, sq_u.e4), (51, give_o), (53, store_start(sq_u)), (54, give_w), (55, release_u),
        (packed, pack), (packed, lambda: tile_load(0).start()), (packed, dm_begin), (packed + 1, sq_o.e0),
        (packed + 2, keys),
        (61, sq_o.e1), (62, sq_w.e0), (63, sq_o.e2), (63, sq_w.e1), (65, sq_w.e2), (65, sq_o.e3), (67, sq_w.e3), (67, sq_o.e4), (69, sq_w.e4),
        (69, store_start(sq_o)), (71, store_start(sq_w)),
    ]
    items += [([(k, k + 1)], functools.partial(lambda e, k: e(), e)) for k, e in events]
    at_normed = (45, 50, packed + 2, packed + 3)
    items.append(([(k, k + 1) for k in at_f], lambda k: f_start(number(k, at_f))))
    items.append(([(k + 1, k + 2) for k in at_f], lambda k: f_load(number(k, at_f)).wait()))
    items.append(([(k, k + 1) for k in at_normed], lambda k: normed(number(k, at_normed))))
    end = line.slots // 2 + lag
    items.append(([(fin, fin + 2), (end, end + 2)], lambda k: finals(jnp.where(k < end, k - fin, k - end + 2))))

    def serve(k):
        def tick(j, _):
            line.serve(2 * (k - lag) + j)
            return 0

        lax.fori_loop(0, 2, tick, 0)

    run_items(items, serve)
    me = s * nc + c
    sums = jnp.concatenate(
        [jnp.broadcast_to(jnp.sum(gpart[k * 8 : (k + 1) * 8, :], axis=0, keepdims=True), (8, d)) for k in range(2)], axis=0
    )
    grecv[me] = sums
    gcopies = []
    for i, t in enumerate(peers):
        cp = remote(grecv.at[me], grecv.at[me], gs.at[i], gr.at[i], t)
        cp.start()
        gcopies.append(cp)

    def rest(job, _):
        line.sent(jnp.where(job < runs, job, job + runs), fwd=False, ret=True)
        return 0

    lax.fori_loop(0, 3 * runs, rest, 0)
    for job in Line.D_AT:
        line.sent(job)
    for sq in (sq_o, sq_w):
        sq.store().wait()
        sq.done()
    for i in range(1, nc):
        for run in range(per):
            key_copy(i, run).wait_send()
    pltpu.make_async_copy(st_o, out_h.at[pl.ds(0, RUN)], osem.at[0]).wait()
    pltpu.make_async_copy(st_t, tg_h.at[pl.ds(0, RUN)], osem.at[2]).wait()
    for cp in gcopies:
        cp.wait()
    total = grecv[0]
    for i in range(1, 2 * nc):
        total = total + grecv[i]
    gpart[...] = total
    gains_ref[...] = gpart[:, own]


def finish_kernel(out_h, tg_h, gw_h, go_h, gg_h, gu_h, gd_h, out_f, tg_f, gq_f, gk_f, gv_f, go_f, gg_f, gu_f, gd_f,
                  out_v, tg_v, gw_v, go_v, gg_v, gu_v, gd_v, q_v, kv_v, o_v, g_v, u_v, d_v, lsem, ssem):
    kw = gk_f.shape[0]
    nq = gw_h.shape[1] - 2 * kw
    pairs = [(gg_h, gg_v), (gu_h, gu_v), (gd_h, gd_v), (gw_h, gw_v), (go_h, go_v), (out_h, out_v), (tg_h, tg_v)]
    loads = [pltpu.make_async_copy(a, b, lsem.at[i]) for i, (a, b) in enumerate(pairs)]
    for cp in loads:
        cp.start()
    stores = [
        pltpu.make_async_copy(a, b, ssem.at[i])
        for i, (a, b) in enumerate([(g_v, gg_f), (u_v, gu_f), (d_v, gd_f), (q_v, gq_f), (kv_v.at[0:kw], gk_f), (kv_v.at[kw:], gv_f),
                                    (o_v, go_f), (out_v, out_f), (tg_v, tg_f)])
    ]

    def widen(src, dst, width):
        def step(i, _):
            rows = pl.ds(pl.multiple_of(i * 32, 32), 32)
            dst[rows, :] = src[rows, 0:width].astype(F32)
            return 0

        lax.fori_loop(0, src.shape[0] // 32, step, 0)

    for i, (src, dst) in enumerate([(gg_v, g_v), (gu_v, u_v), (gd_v, d_v)]):
        loads[i].wait()
        widen(src, dst, src.shape[1])
        stores[i].start()
    loads[5].wait()
    stores[7].start()
    loads[6].wait()
    stores[8].start()
    loads[3].wait()
    widen(gw_v, q_v, nq)
    stores[3].start()
    for i in range(gw_v.shape[0] // PAD):
        kv_v[:, i * PAD : (i + 1) * PAD] = gw_v[i * PAD : (i + 1) * PAD, nq:].astype(F32).T
    stores[4].start()
    stores[5].start()
    loads[4].wait()
    widen(go_v, o_v, go_v.shape[1])
    stores[6].start()
    for cp in stores:
        cp.wait()


def fast(
    tokens, w_query, key_weight, value_weight, w_out, w_gate, w_up, w_down, gain_attn, gain_ffn, segments, positions, cotangent, n, nc
):
    _, rows, d = tokens.shape
    half = rows // 2
    runs = rows // RUN
    per = runs // 2
    prompt = segments.shape[1] // 2
    blocks = prompt // RUN
    dq, dk = w_query.shape[1], key_weight.shape[1]
    hq, hk = dq // HEAD_SIZE, dk // HEAD_SIZE
    nq, nk = hq * PAD, hk * PAD
    ff = w_gate.shape[1]
    dh = d // 2
    c = lax.axis_index("context")
    x = tokens.reshape(rows, d)
    dy = cotangent.reshape(rows, d)
    kbase = positions[0, 0 :: 2 * RUN]
    seg_here = lax.dynamic_slice_in_dim(segments[0], c * rows, rows, 0)
    pos_here = lax.dynamic_slice_in_dim(positions[0], c * rows, rows, 0)
    qbase = jnp.concatenate([pos_here[0 :: 2 * RUN], pos_here[1 :: 2 * RUN]])
    qlim = jnp.concatenate([pos_here[0 :: 2 * RUN], seg_here[1 :: 2 * RUN] * CLEN - 1])
    freq = np.exp(np.arange(HEAD_SIZE // 2, dtype=np.float32) * np.float32(-2.0 * math.log(rope_base) / HEAD_SIZE)).astype(np.float32)
    lanes = np.zeros((PAD,), np.float32)
    lanes[0:48] = freq
    lanes[64:112] = freq
    sign = np.where(np.arange(PAD) < 64, -1.0, 1.0).astype(np.float32)
    inner = np.arange(RUN, dtype=np.float64)[:, None] * lanes[None, :].astype(np.float64)
    cj = jnp.asarray(np.cos(inner).astype(np.float32))
    sj = jnp.asarray((np.sin(inner) * sign).astype(np.float32))
    angle = qbase.astype(F32)[:, None] * jnp.asarray(lanes)[None, :]
    cb = jnp.cos(angle)
    sb = jnp.sin(angle) * jnp.asarray(sign)[None, :]
    gains = jnp.concatenate([jnp.broadcast_to(g.astype(F32)[None, :], (8, dh)) for g in (gain_attn, gain_ffn)], axis=0)

    V = pl.BlockSpec(memory_space=pltpu.VMEM)
    S = pl.BlockSpec(memory_space=pltpu.SMEM)
    A = pl.BlockSpec(memory_space=pl.ANY)
    sds = jax.ShapeDtypeStruct
    DMA = pltpu.SemaphoreType.DMA

    def call(kernel, ins, outs, scratch, collective=None, flops=0):
        params = dict(vmem_limit_bytes=VLIM - 64 * 1024)
        if collective is not None:
            params.update(collective_id=collective, has_side_effects=True)
        args = [a for a, _ in ins]
        return pl.pallas_call(
            kernel,
            out_shape=[o for o, _ in outs],
            in_specs=[sp for _, sp in ins],
            out_specs=[sp for _, sp in outs],
            scratch_shapes=scratch,
            compiler_params=pltpu.CompilerParams(**params),
            cost_estimate=pl.CostEstimate(flops=flops, bytes_accessed=0, transcendentals=0),
        )(*args)

    rope_in = [(cb, V), (sb, V), (cj, V), (sj, V)]
    xp, dyp, n1, q, kvp, kvc, wp, gf, wo, wg, wu, wd = call(
        functools.partial(first_kernel, nc),
        [(x, V), (dy, A), (gains, A)] + rope_in + [(w_query, A), (key_weight.T, A), (value_weight.T, A), (w_out, A), (w_gate, A), (w_up, A), (w_down, A)],
        [
            (sds((rows, d), BF), V), (sds((rows, d), BF), V), (sds((rows, d), BF), V), (sds((rows, nq), BF), V),
            (sds((prompt, 2 * dk), BF), A), (sds((half, 2 * nk), BF), V), (sds((nq + 2 * nk, d), BF), V), (sds((16, d), F32), V),
            (sds((dq, d), BF), A), (sds((d, ff), BF), A), (sds((d, ff), BF), A), (sds((ff, d), BF), A),
        ],
        [
            pltpu.VMEM((rows, d), BF), pltpu.VMEM((d, dq), BF), pltpu.VMEM((dk, d), BF), pltpu.VMEM((dk, d), BF), pltpu.VMEM((16, d), F32),
            pltpu.VMEM((dq, dh), BF), pltpu.VMEM((dh, ff), BF), pltpu.VMEM((dh, ff), BF), pltpu.VMEM((ff, dh), BF),
            pltpu.VMEM((half, 2 * dk), BF),
            DMA((9,)), DMA((8,)), DMA((8,)), DMA((4,)), DMA((per, nc)), DMA((per, nc)),
        ],
        collective=0, flops=60 * 10**9,
    )

    chunk = 16
    count = 16 * (RUN // 2 // chunk)
    U = pltpu.VMEM((rows, d), BF)
    W = pltpu.VMEM((d, ff), BF)
    H = pltpu.VMEM((rows, ff), BF)
    KV = pltpu.VMEM((hk, prompt, PAD), BF)
    KVF = pltpu.VMEM((hk, prompt, PAD), F32)
    width = hq // hk * RUN
    out, tg, gg, gu, gd, go, gw, _, _, _, gains_grad = call(
        functools.partial(main_kernel, n, nc, chunk),
        [(kbase, S), (qlim, S)] + rope_in
        + [(gf, V), (q, V), (kvc, V), (wo, V), (kvp, A), (xp, A), (dyp, A), (wg, A), (wu, A), (wd, A), (n1, A), (wp, A)],
        [(sds((rows, d), BF), A), (sds((rows, d), BF), A), (sds((dh, ff), BF), A), (sds((dh, ff), BF), A), (sds((ff, dh), BF), A),
         (sds((dq, dh), BF), A), (sds((dh, dq + 2 * dk), BF), A), (sds((rows, d), F32), A), (sds((ff, d), BF), A), (sds((rows, d), BF), A),
         (sds((16, dh), F32), V)],
        [KV, KV, pltpu.VMEM((RUN, prompt + RUN), F32), pltpu.VMEM((rows, dq), BF), pltpu.VMEM((rows, nq), BF), pltpu.VMEM((runs * hq * 8, RUN), F32),
         U, U, U, U, pltpu.VMEM((3 * rows, d), BF), pltpu.VMEM((ff, d), BF), U, W, W, H, H, H, pltpu.VMEM((ff, dh), BF),
         KVF, KVF, pltpu.VMEM((rows, nq), BF), pltpu.VMEM((width, PAD), F32), pltpu.VMEM((8, width), F32), pltpu.VMEM((rows, nq), BF),
         pltpu.VMEM((rows, 2 * nk), BF), pltpu.VMEM((2, dq, dh), BF), pltpu.VMEM((RUN, d), BF), pltpu.VMEM((RUN, d), BF), pltpu.VMEM((RUN, d), BF),
         pltpu.VMEM((16, d), F32), pltpu.VMEM((2 * nc, 16, d), F32),
         DMA((7,)), DMA((blocks,)), DMA((3,)), DMA((runs,)), DMA((2,)), DMA, DMA((nc, per)), DMA((nc, per)), DMA((2 * nc - 1,)), DMA((2 * nc - 1,))]
        + [DMA((2, count))] * 4
        + [pltpu.SemaphoreType.REGULAR((6,)), DMA((5,)), DMA((5,)), DMA((5, 3, 2, 2)), DMA((5, 3, 2, 2)), DMA((5,))],
        collective=1, flops=300 * 10**9,
    )
    shapes = [(rows, d), (rows, d), (dh, dq + 2 * dk), (dq, dh), (dh, ff), (dh, ff), (ff, dh)]
    wide = [(dh, dq), (2 * dk, dh), (dq, dh), (dh, ff), (dh, ff), (ff, dh)]
    finals = [(dh, dq), (dk, dh), (dk, dh), (dq, dh), (dh, ff), (dh, ff), (ff, dh)]
    out, tg, gq, gk, gv, go, gg, gu, gd = call(
        finish_kernel,
        [(a, A) for a in (out, tg, gw, go, gg, gu, gd)],
        [(sds((rows, d), BF), A), (sds((rows, d), BF), A)] + [(sds(shape, F32), A) for shape in finals],
        [pltpu.VMEM(shape, BF) for shape in shapes] + [pltpu.VMEM(shape, F32) for shape in wide] + [DMA((7,)), DMA((9,))],
    )
    return out[None], tg[None], gq, gk.T, gv.T, go, gg, gu, gd, gains_grad[0], gains_grad[8]


def body(mesh, *args):
    tokens, w_query, segments = args[0], args[1], args[10]
    n, nc = mesh.shape["tensor"], mesh.shape["context"]
    rows = tokens.shape[1]
    if (tokens.shape[0] == 1 and rows % (4 * CLEN) == 0 and n == 4 and nc == 4 and mesh.shape["shard"] == 2
            and segments.shape[1] == rows * nc):
        return fast(*args, n, nc)
    return general(*args)


def solution(mesh):
    in_specs = (
        P("shard", "context", None),
        P("shard", "tensor"),
        P("shard", "tensor"),
        P("shard", "tensor"),
        P("tensor", "shard"),
        P("shard", "tensor"),
        P("shard", "tensor"),
        P("tensor", "shard"),
        P("shard"),
        P("shard"),
        P("shard", None),
        P("shard", None),
        P("shard", "context", None),
    )
    out_specs = (
        P("shard", "context", None),
        P("shard", "context", None),
        P("shard", "tensor"),
        P("shard", "tensor"),
        P("shard", "tensor"),
        P("tensor", "shard"),
        P("shard", "tensor"),
        P("shard", "tensor"),
        P("tensor", "shard"),
        P("shard"),
        P("shard"),
    )
    return jax.shard_map(functools.partial(body, mesh), mesh=mesh, in_specs=in_specs, out_specs=out_specs, check_vma=False)
```

```python
import functools
import math

import jax
import jax.numpy as jnp
import numpy as np
from jax import lax
from jax.experimental import pallas as pl
from jax.experimental.pallas import tpu as pltpu
from jax.sharding import PartitionSpec as P

HEAD_SIZE = 96
CLEN = 256


rope_base = 100000.0
norm_eps = 1e-05


def tables(positions):
    half_width = HEAD_SIZE // 2
    frequency = jnp.exp(
        jnp.arange(half_width, dtype=jnp.float32) * (-2.0 * math.log(rope_base) / HEAD_SIZE)
    )
    angles = positions.astype(jnp.float32)[:, None] * frequency[None, :]
    return (jnp.cos(angles)[:, None, :], jnp.sin(angles)[:, None, :])


def rotary_apply(heads, cosine_table, sine_values):
    half_width = HEAD_SIZE // 2
    front_half = heads[..., :half_width]
    back_half = heads[..., half_width:]
    return jnp.concatenate(
        [
            front_half * cosine_table - back_half * sine_values,
            back_half * cosine_table + front_half * sine_values,
        ],
        axis=-1,
    )


def rotate_back(heads, cosine_table, sine_values):
    half_width = HEAD_SIZE // 2
    front_half = heads[..., :half_width]
    back_half = heads[..., half_width:]
    return jnp.concatenate(
        [
            front_half * cosine_table + back_half * sine_values,
            back_half * cosine_table - front_half * sine_values,
        ],
        axis=-1,
    )


def contract_rows(left, right):
    return lax.dot_general(
        left, right, (((0,), (0,)), ((), ())), preferred_element_type=jnp.float32
    )


def contract_cols(left, right):
    return lax.dot_general(
        left, right, (((1,), (1,)), ((), ())), preferred_element_type=jnp.float32
    )


def norm_back(tok_rows, norm_scale, gain, grad_normed):
    weighted = gain * grad_normed
    inner = jnp.mean(weighted * tok_rows, axis=-1, keepdims=True)
    grad_rows = norm_scale * weighted - tok_rows * (norm_scale * norm_scale * norm_scale) * inner
    grad_gain = jnp.sum(grad_normed * tok_rows * norm_scale, axis=0)
    return (grad_rows, grad_gain)


def visible(seg_query, pos_query, seg_keys, pos_keys):
    own = (seg_keys[None, :] == seg_query[:, None]) & (pos_keys[None, :] <= pos_query[:, None])
    branch = (
        (seg_keys[None, :] == 0)
        & (seg_query[:, None] > 0)
        & (pos_keys[None, :] < seg_query[:, None] * CLEN)
    )
    return own | branch


def general(
    tokens,
    w_query,
    key_weight,
    value_weight,
    w_out,
    w_gate,
    w_up,
    w_down,
    gain_attn,
    gain_ffn,
    segments,
    positions,
    cotangent,
):
    groups, tok_local, model_width = tokens.shape
    token_count = groups * tok_local
    heads_here = w_query.shape[1] // HEAD_SIZE
    kv_here = key_weight.shape[1] // HEAD_SIZE
    per_kv = heads_here // kv_here
    kv_width = kv_here * HEAD_SIZE
    score_scale = 1.0 / math.sqrt(HEAD_SIZE)
    context_index = lax.axis_index("context")
    first_row = context_index * tok_local
    seg_here = lax.dynamic_slice_in_dim(segments, first_row, tok_local, 1)
    pos_here = lax.dynamic_slice_in_dim(positions, first_row, tok_local, 1)
    w_query, key_weight, value_weight, w_gate, w_up, gain_attn, gain_ffn = (
        lax.all_gather(w_query, "shard", axis=0, tiled=True),
        lax.all_gather(key_weight, "shard", axis=0, tiled=True),
        lax.all_gather(value_weight, "shard", axis=0, tiled=True),
        lax.all_gather(w_gate, "shard", axis=0, tiled=True),
        lax.all_gather(w_up, "shard", axis=0, tiled=True),
        lax.all_gather(gain_attn, "shard", axis=0, tiled=True),
        lax.all_gather(gain_ffn, "shard", axis=0, tiled=True),
    )
    w_out, w_down = (
        lax.all_gather(w_out, "shard", axis=1, tiled=True),
        lax.all_gather(w_down, "shard", axis=1, tiled=True),
    )
    gain_one = gain_attn.astype(jnp.float32)
    gain_two = gain_ffn.astype(jnp.float32)
    tok_rows = tokens.reshape(token_count, model_width).astype(jnp.float32)
    scale_one = lax.rsqrt(jnp.mean(tok_rows * tok_rows, axis=-1, keepdims=True) + norm_eps)
    normed_input = (tok_rows * scale_one * gain_one).astype(jnp.bfloat16)
    cosine_table, sine_values = tables(pos_here.reshape(token_count))
    query_heads_rows = rotary_apply(
        jnp.dot(normed_input, w_query, preferred_element_type=jnp.float32).reshape(
            token_count, heads_here, HEAD_SIZE
        ),
        cosine_table,
        sine_values,
    )
    query_heads_rows = query_heads_rows.astype(jnp.bfloat16).reshape(
        groups, tok_local, heads_here * HEAD_SIZE
    )
    key_rows = rotary_apply(
        jnp.dot(normed_input, key_weight, preferred_element_type=jnp.float32).reshape(
            token_count, kv_here, HEAD_SIZE
        ),
        cosine_table,
        sine_values,
    )
    key_rows = key_rows.astype(jnp.bfloat16).reshape(token_count, kv_width)
    value_rows = jnp.dot(normed_input, value_weight, preferred_element_type=jnp.float32).astype(
        jnp.bfloat16
    )
    keyval = jnp.concatenate([key_rows, value_rows], axis=-1).reshape(
        groups, tok_local, 2 * kv_width
    )
    gathered = lax.all_gather(keyval, "context", axis=1, tiled=True)

    def scores_of(group_queries, group_keyval, seg_query, pos_query, seg_keys, pos_keys):
        grouped_heads = group_queries.reshape(tok_local, kv_here, per_kv, HEAD_SIZE)
        key_head_rows = group_keyval[:, :kv_width].reshape(-1, kv_here, HEAD_SIZE)
        scores = (
            jnp.einsum(
                "bhgd,khd->hgbk", grouped_heads, key_head_rows, preferred_element_type=jnp.float32
            )
            * score_scale
        )
        allowed = visible(seg_query, pos_query, seg_keys, pos_keys)
        return (jnp.where(allowed[None, None], scores, -1e30), grouped_heads, key_head_rows)

    def attend_group(inputs):
        group_queries, group_keyval, seg_query, pos_query, seg_keys, pos_keys = inputs
        scores, grouped_heads, key_head_rows = scores_of(
            group_queries, group_keyval, seg_query, pos_query, seg_keys, pos_keys
        )
        top_score = jnp.max(scores, axis=-1, keepdims=True)
        exponent = jnp.exp(scores - top_score)
        totals = jnp.sum(exponent, axis=-1, keepdims=True)
        soft_weights = (exponent / totals).astype(jnp.bfloat16)
        value_head_rows = group_keyval[:, kv_width:].reshape(-1, kv_here, HEAD_SIZE)
        attended_output = jnp.einsum(
            "hgbk,khd->bhgd", soft_weights, value_head_rows, preferred_element_type=jnp.float32
        )
        return (
            attended_output.reshape(tok_local, heads_here * HEAD_SIZE),
            (top_score + jnp.log(totals))[..., 0],
        )

    attended_output, log_total = lax.map(
        attend_group, (query_heads_rows, gathered, seg_here, pos_here, segments, positions)
    )
    attended_low = attended_output.reshape(token_count, heads_here * HEAD_SIZE).astype(jnp.bfloat16)
    attn_sum = lax.psum(jnp.dot(attended_low, w_out, preferred_element_type=jnp.float32), "tensor")
    middle = tok_rows + attn_sum
    scale_two = lax.rsqrt(jnp.mean(middle * middle, axis=-1, keepdims=True) + norm_eps)
    normed_two = (middle * scale_two * gain_two).astype(jnp.bfloat16)
    gate_proj = jnp.dot(normed_two, w_gate, preferred_element_type=jnp.float32)
    up_proj = jnp.dot(normed_two, w_up, preferred_element_type=jnp.float32)
    sigmoid_gate = jax.nn.sigmoid(gate_proj)
    silu_gate = gate_proj * sigmoid_gate
    hidden = (silu_gate * up_proj).astype(jnp.bfloat16)
    ffn_sum = lax.psum(
        jnp.dot(hidden, w_down, preferred_element_type=jnp.float32).astype(jnp.bfloat16), "tensor"
    ).astype(jnp.float32)
    output = (middle + ffn_sum).astype(jnp.bfloat16).reshape(groups, tok_local, model_width)
    grad_low = cotangent.reshape(token_count, model_width)
    grad_out = grad_low.astype(jnp.float32)
    grad_hidden = contract_cols(grad_low, w_down)
    grad_w_down_t = contract_rows(grad_low, hidden)
    grad_gate = (
        grad_hidden * up_proj * sigmoid_gate * (1.0 + gate_proj * (1.0 - sigmoid_gate))
    ).astype(jnp.bfloat16)
    grad_up = (grad_hidden * silu_gate).astype(jnp.bfloat16)
    grad_w_gate = contract_rows(normed_two, grad_gate)
    grad_w_up = contract_rows(normed_two, grad_up)
    grad_normed_two = lax.psum(
        contract_cols(grad_gate, w_gate) + contract_cols(grad_up, w_up), "tensor"
    )
    back_two, grad_gain_two = norm_back(middle, scale_two, gain_two, grad_normed_two)
    grad_middle = grad_out + back_two
    grad_mid_low = grad_middle.astype(jnp.bfloat16)
    grad_w_out_t = contract_rows(grad_mid_low, attended_low)
    grad_attended = (
        contract_cols(grad_mid_low, w_out)
        .astype(jnp.bfloat16)
        .reshape(groups, tok_local, heads_here * HEAD_SIZE)
    )

    def attend_back(inputs):
        (
            group_queries,
            group_keyval,
            group_grad,
            group_total,
            seg_query,
            pos_query,
            seg_keys,
            pos_keys,
        ) = inputs
        scores, grouped_heads, key_head_rows = scores_of(
            group_queries, group_keyval, seg_query, pos_query, seg_keys, pos_keys
        )
        soft_weights = jnp.exp(scores - group_total[..., None])
        value_head_rows = group_keyval[:, kv_width:].reshape(-1, kv_here, HEAD_SIZE)
        grad_grouped = group_grad.reshape(tok_local, kv_here, per_kv, HEAD_SIZE)
        grad_weights = jnp.einsum(
            "bhgd,khd->hgbk", grad_grouped, value_head_rows, preferred_element_type=jnp.float32
        )
        inner = jnp.sum(soft_weights * grad_weights, axis=-1, keepdims=True)
        grad_scores = (soft_weights * (grad_weights - inner)).astype(jnp.bfloat16)
        grad_queries = (
            jnp.einsum(
                "hgbk,khd->bhgd", grad_scores, key_head_rows, preferred_element_type=jnp.float32
            )
            * score_scale
        )
        grad_keys = (
            jnp.einsum(
                "hgbk,bhgd->khd", grad_scores, grouped_heads, preferred_element_type=jnp.float32
            )
            * score_scale
        )
        grad_values = jnp.einsum(
            "hgbk,bhgd->khd",
            soft_weights.astype(jnp.bfloat16),
            grad_grouped,
            preferred_element_type=jnp.float32,
        )
        grad_keyval = jnp.concatenate(
            [grad_keys.reshape(-1, kv_width), grad_values.reshape(-1, kv_width)], axis=-1
        )
        return (grad_queries.reshape(tok_local, heads_here * HEAD_SIZE), grad_keyval)

    grad_queries, grad_keyval = lax.map(
        attend_back,
        (
            query_heads_rows,
            gathered,
            grad_attended,
            log_total,
            seg_here,
            pos_here,
            segments,
            positions,
        ),
    )
    grad_keyval = lax.psum_scatter(grad_keyval, "context", scatter_dimension=1, tiled=True)
    grad_query_rows = rotate_back(
        grad_queries.reshape(token_count, heads_here, HEAD_SIZE), cosine_table, sine_values
    )
    grad_query_rows = grad_query_rows.astype(jnp.bfloat16).reshape(
        token_count, heads_here * HEAD_SIZE
    )
    grad_key_rows = rotate_back(
        grad_keyval[..., :kv_width].reshape(token_count, kv_here, HEAD_SIZE),
        cosine_table,
        sine_values,
    )
    grad_key_rows = grad_key_rows.astype(jnp.bfloat16).reshape(token_count, kv_width)
    grad_value_rows = (
        grad_keyval[..., kv_width:].reshape(token_count, kv_width).astype(jnp.bfloat16)
    )
    grad_w_query = contract_rows(normed_input, grad_query_rows)
    grad_w_key = contract_rows(normed_input, grad_key_rows)
    grad_w_value = contract_rows(normed_input, grad_value_rows)
    partial_one = (
        contract_cols(grad_query_rows, w_query)
        + contract_cols(grad_key_rows, key_weight)
        + contract_cols(grad_value_rows, value_weight)
    )
    grad_normed = lax.psum(partial_one, "tensor")
    back_one, grad_gain_one = norm_back(tok_rows, scale_one, gain_one, grad_normed)
    tokens_grad = (
        (grad_middle + back_one).astype(jnp.bfloat16).reshape(groups, tok_local, model_width)
    )
    summed = (
        lax.psum_scatter(grad_w_query, ("shard", "context"), scatter_dimension=0, tiled=True),
        lax.psum_scatter(grad_w_key, ("shard", "context"), scatter_dimension=0, tiled=True),
        lax.psum_scatter(grad_w_value, ("shard", "context"), scatter_dimension=0, tiled=True),
        lax.psum_scatter(grad_w_out_t, ("shard", "context"), scatter_dimension=0, tiled=True),
        lax.psum_scatter(grad_w_gate, ("shard", "context"), scatter_dimension=0, tiled=True),
        lax.psum_scatter(grad_w_up, ("shard", "context"), scatter_dimension=0, tiled=True),
        lax.psum_scatter(grad_w_down_t, ("shard", "context"), scatter_dimension=0, tiled=True),
        lax.psum_scatter(grad_gain_one, ("shard", "context"), scatter_dimension=0, tiled=True),
        lax.psum_scatter(grad_gain_two, ("shard", "context"), scatter_dimension=0, tiled=True),
    )
    summed = (
        lax.all_gather(summed[0].astype(jnp.bfloat16), "context", axis=0, tiled=True).astype(
            jnp.float32
        ),
        lax.all_gather(summed[1].astype(jnp.bfloat16), "context", axis=0, tiled=True).astype(
            jnp.float32
        ),
        lax.all_gather(summed[2].astype(jnp.bfloat16), "context", axis=0, tiled=True).astype(
            jnp.float32
        ),
        lax.all_gather(summed[3].astype(jnp.bfloat16), "context", axis=0, tiled=True).astype(
            jnp.float32
        ),
        lax.all_gather(summed[4].astype(jnp.bfloat16), "context", axis=0, tiled=True).astype(
            jnp.float32
        ),
        lax.all_gather(summed[5].astype(jnp.bfloat16), "context", axis=0, tiled=True).astype(
            jnp.float32
        ),
        lax.all_gather(summed[6].astype(jnp.bfloat16), "context", axis=0, tiled=True).astype(
            jnp.float32
        ),
        lax.all_gather(summed[7].astype(jnp.bfloat16), "context", axis=0, tiled=True).astype(
            jnp.float32
        ),
        lax.all_gather(summed[8].astype(jnp.bfloat16), "context", axis=0, tiled=True).astype(
            jnp.float32
        ),
    )
    return (
        output,
        tokens_grad,
        summed[0],
        summed[1],
        summed[2],
        summed[3].T,
        summed[4],
        summed[5],
        summed[6].T,
        summed[7],
        summed[8],
    )


MESH = pl.DeviceIdType.MESH
RUN = 256
PAD = 128
NEG = -1e30
LOG2E = 1.4426950408889634
BF = jnp.bfloat16
F32 = jnp.float32
VLIM = 64 * 1024 * 1024


def mm(a, b):
    return lax.dot_general(a, b, (((1,), (0,)), ((), ())), preferred_element_type=F32)


def mm_nt(a, b):
    return lax.dot_general(a, b, (((1,), (1,)), ((), ())), preferred_element_type=F32)


def mm_tn(a, b):
    return lax.dot_general(a, b, (((0,), (0,)), ((), ())), preferred_element_type=F32)


def iota(shape, axis):
    return lax.broadcasted_iota(jnp.int32, shape, axis)


def one_hot(hit):
    return jnp.where(hit, 1.0, 0.0).astype(BF)


def pad_matrix(heads, flip=False):
    shape = (heads * HEAD_SIZE, heads * PAD)
    if flip:
        row, col = iota(shape[::-1], 1), iota(shape[::-1], 0)
    else:
        row, col = iota(shape, 0), iota(shape, 1)
    lane = col & 127
    part = jnp.where(lane < 64, lane, lane - 16)
    return one_hot((row == (col >> 7) * HEAD_SIZE + part) & ((lane & 63) < 48))


def split_matrix():
    row, col = iota((RUN, RUN), 0), iota((RUN, RUN), 1)
    return one_hot(col == jnp.where(row < 128, 2 * row, 2 * row - 255))


def merge_matrix():
    row, col = iota((RUN, RUN), 0), iota((RUN, RUN), 1)
    return one_hot(col == (row >> 1) + (row & 1) * 128)


def rope_tables(run, cb_ref, sb_ref, cj_ref, sj_ref):
    cb, sb = cb_ref[pl.ds(run, 1), :], sb_ref[pl.ds(run, 1), :]
    cj, sj = cj_ref[...], sj_ref[...]
    return cb * cj - sb * sj, sb * cj + cb * sj


def rope(u, c, s):
    return u * c + pltpu.roll(u, 64, 1) * s


def rope_back(u, c, s):
    return u * c - pltpu.roll(u, 64, 1) * s


def vmem(*shape_dtype):
    return pl.BlockSpec(memory_space=pltpu.VMEM)


def entry_barrier(targets):
    bar = pltpu.get_barrier_semaphore()
    for t in targets:
        pl.semaphore_signal(bar, inc=1, device_id=t, device_id_type=MESH)
    pl.semaphore_wait(bar, len(targets))


def remote(src, dst, send, recv, target):
    return pltpu.make_async_remote_copy(
        src_ref=src, dst_ref=dst, send_sem=send, recv_sem=recv, device_id=target, device_id_type=MESH
    )


def first_kernel(nc, x_ref, dy_h, g_ref, cb_ref, sb_ref, cj_ref, sj_ref, wq_h, wk_h, wv_h, wo_h, wg_h, wu_h, wd_h,
                 xp_ref, dyp_ref, n1_ref, q_ref, kvp_ref, kvc_ref, wp_ref, gf_ref, wo_f, wg_f, wu_f, wd_f,
                 dy_v, wq_s, wk_s, wv_s, g_s, wo_v, wg_v, wu_v, wd_v, kv_send,
                 lsem, ssem, rsem, osem, csem, crem):
    s = lax.axis_index("shard")
    c = lax.axis_index("context")
    dh = g_s.shape[1] // 2
    own = pl.ds(pl.multiple_of(s * dh, dh), dh)
    other = {"shard": 1 - s}
    loads = [
        pltpu.make_async_copy(wq_h, wq_s.at[own], lsem.at[0]),
        pltpu.make_async_copy(wk_h, wk_s.at[:, own], lsem.at[1]),
        pltpu.make_async_copy(wv_h, wv_s.at[:, own], lsem.at[2]),
        pltpu.make_async_copy(g_ref, g_s.at[:, own], lsem.at[3]),
        pltpu.make_async_copy(wo_h, wo_v, lsem.at[4]),
        pltpu.make_async_copy(wg_h, wg_v, lsem.at[5]),
        pltpu.make_async_copy(wu_h, wu_v, lsem.at[6]),
        pltpu.make_async_copy(wd_h, wd_v, lsem.at[7]),
        pltpu.make_async_copy(dy_h, dy_v, lsem.at[8]),
    ]
    for cp in loads:
        cp.start()
    entry_barrier([other] + [{"context": lax.rem(c + i, nc)} for i in range(1, nc)])
    sends = [
        remote(wq_s.at[own], wq_s.at[own], ssem.at[0], rsem.at[0], other),
        remote(wk_s.at[:, own], wk_s.at[:, own], ssem.at[1], rsem.at[1], other),
        remote(wv_s.at[:, own], wv_s.at[:, own], ssem.at[2], rsem.at[2], other),
        remote(g_s.at[:, own], g_s.at[:, own], ssem.at[3], rsem.at[3], other),
        remote(wo_v, wo_f.at[:, own], ssem.at[4], rsem.at[4], other),
        remote(wg_v, wg_f.at[own], ssem.at[5], rsem.at[5], other),
        remote(wu_v, wu_f.at[own], ssem.at[6], rsem.at[6], other),
        remote(wd_v, wd_f.at[:, own], ssem.at[7], rsem.at[7], other),
    ]
    keeps = [
        pltpu.make_async_copy(wo_v, wo_f.at[:, own], osem.at[0]),
        pltpu.make_async_copy(wg_v, wg_f.at[own], osem.at[1]),
        pltpu.make_async_copy(wu_v, wu_f.at[own], osem.at[2]),
        pltpu.make_async_copy(wd_v, wd_f.at[:, own], osem.at[3]),
    ]
    for i in (3, 0, 1, 2, 4, 5, 6, 7):
        loads[i].wait()
        sends[i].start()
        if i >= 4:
            keeps[i - 4].start()
    half = x_ref.shape[0] // 2
    split = split_matrix()
    for i in range(x_ref.shape[0] // RUN):
        xb = mm(split, x_ref[pl.ds(i * RUN, RUN), :])
        xp_ref[pl.ds(i * 128, 128), :] = xb[:128].astype(BF)
        xp_ref[pl.ds(half + i * 128, 128), :] = xb[128:].astype(BF)
        if i == 0:
            sends[3].wait_recv()
        r = lax.rsqrt(jnp.mean(xb * xb, axis=-1, keepdims=True) + norm_eps)
        nb = (xb * r * g_s[0:1, :]).astype(BF)
        n1_ref[pl.ds(i * 128, 128), :] = nb[:128]
        n1_ref[pl.ds(half + i * 128, 128), :] = nb[128:]
    gf_ref[...] = g_s[...]
    hq, hk = wq_s.shape[1] // HEAD_SIZE, wk_s.shape[0] // HEAD_SIZE
    selq, selk = pad_matrix(hq, True), pad_matrix(hk, True)
    nq, nk = hq * PAD, hk * PAD
    for i in range(3):
        sends[i].wait_recv()
    wp_ref[0:nq, :] = mm_nt(selq, wq_s[...]).astype(BF)
    wp_ref[nq : nq + nk, :] = mm(selk, wk_s[...]).astype(BF)
    wp_ref[nq + nk :, :] = mm(selk, wv_s[...]).astype(BF)
    selkv = pad_matrix(2 * hk)
    runs = x_ref.shape[0] // RUN
    per = runs // 2
    kv_copies = []
    for run in range(runs):
        rows = pl.ds(run * RUN, RUN)
        y = mm_nt(n1_ref[rows, :], wp_ref[...])
        ct, st = rope_tables(run, cb_ref, sb_ref, cj_ref, sj_ref)
        for h in range(hq):
            q_ref[rows, h * PAD : (h + 1) * PAD] = rope(y[:, h * PAD : (h + 1) * PAD], ct, st).astype(BF)
        kv = [rope(y[:, nq + h * PAD : nq + (h + 1) * PAD], ct, st).astype(BF) for h in range(hk)]
        kv = jnp.concatenate(kv + [y[:, nq + nk :].astype(BF)], axis=1)
        if run < per:
            kv_send[pl.ds(run * RUN, RUN), :] = mm_nt(kv, selkv).astype(BF)
            mine = pl.ds(pl.multiple_of((c * per + run) * RUN, RUN), RUN)
            for i in range(1, nc):
                cp = remote(kv_send.at[pl.ds(run * RUN, RUN)], kvp_ref.at[mine], csem.at[run, i], crem.at[run, i],
                            {"context": lax.rem(c + i, nc)})
                cp.start()
                kv_copies.append(cp)
            cp = pltpu.make_async_copy(kv_send.at[pl.ds(run * RUN, RUN)], kvp_ref.at[mine], csem.at[run, 0])
            cp.start()
            kv_copies.append(cp)
        else:
            kvc_ref[pl.ds((run - per) * RUN, RUN), :] = kv
    loads[8].wait()
    for i in range(x_ref.shape[0] // RUN):
        b = mm(split, dy_v[pl.ds(i * RUN, RUN), :]).astype(BF)
        dyp_ref[pl.ds(i * 128, 128), :] = b[:128]
        dyp_ref[pl.ds(half + i * 128, 128), :] = b[128:]
    for cp in kv_copies:
        cp.wait()
    for i in range(4):
        keeps[i].wait()
        sends[4 + i].wait_recv()
    for cp in sends:
        cp.wait_send()


class Line:
    F_AT = (8, 9, 10, 12)
    D_AT = (11, 13, 14, 15)

    def __init__(self, n, chunk, pbuf, rbuf, obuf, sems):
        self.n, self.chunk, self.per = n, chunk, RUN // 2 // chunk
        self.count = 16 * self.per
        self.pbuf, self.rbuf, self.obuf = pbuf, rbuf, obuf
        self.rs, self.rr, self.bs, self.br = sems
        self.ticks = 32 // chunk
        self.hop = 3
        self.turn = 2 * (n - 1) * self.hop
        self.slots = self.count + self.turn

    def pieces(self, h, i):
        n, chunk = self.n, self.chunk
        z = lax.axis_index("tensor")
        job = i // self.per
        late = jnp.where((job == 11) | (job > 12), 1, 0)
        row = jnp.where(job < 8, lax.rem(job, 4), jnp.where(late == 1, jnp.maximum(job - 12, 0), jnp.minimum(job - 8, 3)))
        part = jnp.where(job < 8, job // 4, 2 - late)
        off = row * RUN + h * (RUN // 2) + lax.rem(i, self.per) * chunk
        rows = pl.ds(pl.multiple_of(off, chunk), chunk)
        orows = pl.ds(pl.multiple_of(part * (4 * RUN) + off, chunk), chunk)
        place = z if h == 0 else n - 1 - z
        up, down = jnp.minimum(z + 1, n - 1), jnp.maximum(z - 1, 0)
        ahead = {"tensor": up if h == 0 else down}
        back = {"tensor": down if h == 0 else up}
        fwd = remote(self.pbuf.at[rows], self.rbuf.at[rows], self.rs.at[h, i], self.rr.at[h, i], ahead)
        ret = remote(self.obuf.at[orows], self.obuf.at[orows], self.bs.at[h, i], self.br.at[h, i], back)
        return rows, orows, place, fwd, ret

    def reduce_step(self, h, i):
        rows, orows, place, fwd, ret = self.pieces(h, i)
        n = self.n

        @pl.when(place == 0)
        def _():
            fwd.start()

        @pl.when(place > 0)
        def _():
            fwd.wait_recv()
            total = (self.rbuf[rows, :].astype(F32) + self.pbuf[rows, :].astype(F32)).astype(BF)

            @pl.when(place < n - 1)
            def _():
                self.pbuf[rows, :] = total
                fwd.start()

            @pl.when(place == n - 1)
            def _():
                self.obuf[orows, :] = total
                ret.start()

    def spread_step(self, h, i):
        rows, orows, place, fwd, ret = self.pieces(h, i)

        @pl.when(place < self.n - 1)
        def _():
            ret.wait_recv()

        @pl.when((place < self.n - 1) & (place > 0))
        def _():
            ret.start()

    def serve(self, t):
        n = self.n
        z = lax.axis_index("tensor")
        for h in range(2):
            place = z if h == 0 else n - 1 - z
            i = t - place * self.hop

            @pl.when((i >= 0) & (i < self.count))
            def _():
                self.reduce_step(h, i)

            j = t - (2 * (n - 1) - place) * self.hop

            @pl.when((j >= 0) & (j < self.count))
            def _():
                self.spread_step(h, j)

    def sent(self, job, fwd=True, ret=False):
        def step(i, _):
            for h in range(2):
                rows, orows, place, f, r = self.pieces(h, job * self.per + i)
                if fwd:

                    @pl.when(place < self.n - 1)
                    def _():
                        f.wait_send()

                if ret:

                    @pl.when(place > 0)
                    def _():
                        r.wait_send()

            return 0

        lax.fori_loop(0, self.per, step, 0)


def run_items(items, serve):
    total = max(e for spans, _ in items for _, e in spans)

    def step(k, _):
        for spans, body in items:
            hit = functools.reduce(jnp.logical_or, [(k >= lo) & (k < hi) for lo, hi in spans])
            pl.when(hit)(functools.partial(body, k))
        serve(k)
        return 0

    lax.fori_loop(0, total, step, 0)


class Square:
    def __init__(self, rows, cols, src, mine, theirs, spare, out, credit, shard_send, shard_recv, send, recv, store):
        self.src, self.mine, self.theirs, self.res, self.out = src, mine, theirs, theirs, out
        self.r1, self.r2 = [spare[0:2], spare[2:4]], spare[4:6]
        self.credit, self.shard_sems, self.shard_recv, self.send, self.recv, self.store_sem = credit, shard_send, shard_recv, send, recv, store
        self.rows, self.qr, self.cols = rows, rows // 4, cols
        c = lax.axis_index("context")
        self.cy, self.cx = c // 2, lax.rem(c, 2)

    def at(self, y, x, half):
        w = self.cols // 2
        return (pl.ds(pl.multiple_of((2 * y + x) * self.qr, self.qr), self.qr), pl.ds(half * w, w))

    def peer(self, half, first):
        if (half == 0) == first:
            return {"context": 2 * self.cy + 1 - self.cx}
        return {"context": 2 * (1 - self.cy) + self.cx}

    def shard_copy(self):
        return remote(self.src, self.theirs, self.shard_sems, self.shard_recv, {"shard": 1 - lax.axis_index("shard")})

    def outer(self, half):
        if half == 0:
            return [(y, 1 - self.cx) for y in range(2)], [(y, self.cx) for y in range(2)]
        return [(1 - self.cy, x) for x in range(2)], [(self.cy, x) for x in range(2)]

    def p1(self, half, j):
        return remote(self.mine.at[self.at(*self.outer(half)[0][j], half)], self.r1[half][j],
                      self.send.at[0, half, j], self.recv.at[0, half, j], self.peer(half, True))

    def p2(self, half):
        q = (1 - self.cy, self.cx) if half == 0 else (self.cy, 1 - self.cx)
        return remote(self.mine.at[self.at(*q, half)], self.r2[half],
                      self.send.at[1, half, 0], self.recv.at[1, half, 0], self.peer(half, False))

    def p3(self, half):
        at = self.at(self.cy, self.cx, half)
        return remote(self.res.at[at], self.res.at[at], self.send.at[1, half, 1], self.recv.at[1, half, 1], self.peer(half, False))

    def p4(self, half, j):
        at = self.at(*self.outer(half)[1][j], half)
        return remote(self.res.at[at], self.res.at[at], self.send.at[2, half, j], self.recv.at[2, half, j], self.peer(half, True))

    def free(self):
        for t in ({"shard": 1 - lax.axis_index("shard")}, self.peer(0, True), self.peer(0, False)):
            pl.semaphore_signal(self.credit, inc=1, device_id=t, device_id_type=MESH)

    def e0(self):
        pl.semaphore_wait(self.credit, 3)
        self.shard_copy().start()

    def e1(self):
        self.shard_copy().wait_recv()
        step = self.qr

        def add(i, _):
            rows = pl.ds(pl.multiple_of(i * step, step), step)
            self.mine[rows, :] = (self.mine[rows, :].astype(F32) + self.theirs[rows, :].astype(F32)).astype(BF)
            return 0

        lax.fori_loop(0, self.rows // step, add, 0)
        for j in range(2):
            for half in range(2):
                self.p1(half, j).start()

    def e2(self):
        for half in range(2):
            for j in range(2):
                self.p1(half, j).wait_recv()
                at = self.at(*self.outer(half)[1][j], half)
                self.mine[at] = (self.mine[at].astype(F32) + self.r1[half][j][...].astype(F32)).astype(BF)
            self.p2(half).start()

    def e3(self):
        for half in range(2):
            self.p2(half).wait_recv()
            at = self.at(self.cy, self.cx, half)
            self.res[at] = (self.mine[at].astype(F32) + self.r2[half][...].astype(F32)).astype(BF)
            self.p3(half).start()

    def e4(self):
        for half in range(2):
            self.p3(half).wait_recv()
            for j in range(2):
                self.p4(half, j).start()

    def e5(self):
        for half in range(2):
            for j in range(2):
                self.p4(half, j).wait_recv()

    def store(self):
        return pltpu.make_async_copy(self.res, self.out, self.store_sem)

    def done(self):
        self.shard_copy().wait_send()
        for half in range(2):
            for j in range(2):
                self.p1(half, j).wait_send()
                self.p4(half, j).wait_send()
            self.p2(half).wait_send()
            self.p3(half).wait_send()


def line_barrier(n, peers=()):
    z = lax.axis_index("tensor")
    bar = pltpu.get_barrier_semaphore()
    for t in peers:
        pl.semaphore_signal(bar, inc=1, device_id=t, device_id_type=MESH)

    @pl.when(z > 0)
    def _():
        pl.semaphore_signal(bar, inc=1, device_id={"tensor": jnp.maximum(z - 1, 0)}, device_id_type=MESH)

    @pl.when(z < n - 1)
    def _():
        pl.semaphore_signal(bar, inc=1, device_id={"tensor": jnp.minimum(z + 1, n - 1)}, device_id_type=MESH)

    pl.semaphore_wait(bar, len(peers) + jnp.minimum(z, 1) + jnp.minimum(n - 1 - z, 1))


def main_kernel(n, nc, chunk, kbase, qlim, cb_ref, sb_ref, cj_ref, sj_ref, gf_ref, q_ref, kvc_ref, wo_ref,
                kvp_h, xp_h, dyp_h, wg_h, wu_h, wd_h, n1_h, wp_h,
                out_h, tg_h, gg_h, gu_h, gd_h, go_h, gw_h, dm_h, gds_h, fp_h, gains_ref,
                k_s, v_s, s_s, o_v, op_v, lse_v, xs, ys, pbuf, rbuf, obuf, wd, n2, wg, wu, hid, dg, du, gt,
                dk_s, dv_s, do_v, dq_s, delta_s, dqp, dkv_s, go_v, st_o, st_t, st_p, gpart, grecv,
                lsem, ksem, osem, fsem, msem, nsem, qsend, qrecv, gs, gr, rs, rr, bs, br, credits, shard_send, shard_recv, send, recv, store):
    s = lax.axis_index("shard")
    c = lax.axis_index("context")
    rows_here, d = xs.shape
    runs = rows_here // RUN
    per = runs // 2
    half = rows_here // 2
    hk = k_s.shape[0]
    hq = q_ref.shape[1] // PAD
    rep = hq // hk
    blocks = k_s.shape[1] // RUN
    ff = wg.shape[1]
    dh = d // 2
    nq, nk = hq * PAD, hk * PAD
    score = 1.0 / math.sqrt(HEAD_SIZE)
    scale = LOG2E * score
    own = pl.ds(pl.multiple_of(s * dh, dh), dh)
    yours = pl.ds(pl.multiple_of((1 - s) * dh, dh), dh)
    wide = 2 * hk * HEAD_SIZE

    def at(i, size=RUN):
        return pl.ds(pl.multiple_of(i * size, size), size)

    kv_in = [dg.at[pl.ds((b % 4) * RUN, RUN), pl.ds(b // 4 * wide, wide)] for b in range(blocks)]
    key_loads = [pltpu.make_async_copy(kvp_h.at[pl.ds(b * RUN, RUN)], kv_in[b], ksem.at[b]) for b in range(blocks)]
    for cp in key_loads:
        cp.start()
    pairs = [(xp_h, xs), (wg_h, wg), (wu_h, wu), (dyp_h, ys), (wd_h, wd)]
    loads = [pltpu.make_async_copy(a, b, lsem.at[i]) for i, (a, b) in enumerate(pairs)]
    for cp in loads:
        cp.start()
    peers = [{"shard": lax.rem(s + i // nc, 2), "context": lax.rem(c + lax.rem(i, nc), nc)} for i in range(1, 2 * nc)]
    line_barrier(n, peers)
    line = Line(n, chunk, pbuf, rbuf, obuf, (rs, rr, bs, br))
    a_of = lambda job: at(job)
    b_of = lambda job: at(runs + job)
    lane = iota((RUN, PAD), 1)
    for b in range(blocks):
        key_loads[b].wait()
        kv = mm(kv_in[b][...], pad_matrix(2 * hk))
        rows = pl.ds(b * RUN, RUN)
        for g in range(hk):
            k_s[g, rows, :] = kv[:, g * PAD : (g + 1) * PAD].astype(BF)
            v_s[g, rows, :] = jnp.where(lane == 48, 1.0, kv[:, (hk + g) * PAD : (hk + g + 1) * PAD]).astype(BF)
    dk_s[...] = jnp.zeros_like(dk_s)
    dv_s[...] = jnp.zeros_like(dv_s)
    gpart[...] = jnp.zeros_like(gpart)

    def across(total, width, body):
        def step(i, _):
            body(at(i, width))
            return 0

        lax.fori_loop(0, total // width, step, 0)

    def down_rows(start, count, size, body):
        def step(i, _):
            body(pl.ds(pl.multiple_of(start + i * size, size), size), pl.ds(pl.multiple_of(i * size, size), size))
            return 0

        lax.fori_loop(0, count // size, step, 0)

    def head(k, mixed):
        job, h = k // hq, lax.rem(k, hq)
        run = job + per if mixed else job - per
        diff = iota((RUN, RUN), 1) - iota((RUN, RUN), 0)
        rows, cols = at(run), at(h, PAD)
        g = h // rep
        q = q_ref[rows, cols]
        lim = qlim[run]
        top = None
        for b in range(blocks):
            t = mm_nt(q, k_s[g, pl.ds(b * RUN, RUN), :]) * scale
            room = lim - kbase[b]
            if mixed:
                t = t + jnp.where(room >= 0, 0.0, NEG)
            else:
                t = jnp.where(diff <= room, t, NEG)
            s_s[:, b * RUN : (b + 1) * RUN] = t
            top = t if top is None else jnp.maximum(top, t)
        if mixed:
            crow = at(run - per)
            kc = kvc_ref[crow, at(g, PAD)]
            vc = kvc_ref[crow, at(hk + g, PAD)]
            vc = jnp.where(lane == 48, 1.0, vc.astype(F32)).astype(BF)
            t = jnp.where(diff <= 0, mm_nt(q, kc) * scale, NEG)
            s_s[:, blocks * RUN :] = t
            top = jnp.maximum(top, t)
        m = jnp.max(top, axis=1, keepdims=True)
        acc = None
        for b in range(blocks):
            p = jnp.exp2(s_s[:, b * RUN : (b + 1) * RUN] - m).astype(BF)
            o = mm(p, v_s[g, pl.ds(b * RUN, RUN), :])
            acc = o if acc is None else acc + o
        if mixed:
            p = jnp.exp2(s_s[:, blocks * RUN :] - m).astype(BF)
            acc = acc + mm(p, vc)
        total = acc[:, 48:49]
        op_v[rows, cols] = (acc / total).astype(BF)
        lse = jnp.broadcast_to(m + jnp.log2(total), (RUN, PAD)).T
        lse_v[at(run * hq + h, 8), :] = lse[0:8, :]

        @pl.when(h == hq - 1)
        def _():
            o = mm_nt(op_v[rows, :], pad_matrix(hq)).astype(BF)
            o_v[rows, :] = o


            def out(cols):
                pbuf[at(job), cols] = mm(o, wo_ref[:, cols]).astype(BF)

            across(d, 512, out)

    first = runs * hq

    def ffn(k):
        job = (k - first) // 4
        part = lax.rem(k - first, 4)
        run = lax.rem(job + per, runs)
        rows = at(run)

        @pl.when(k == first)
        def _():
            for cp in loads:
                cp.wait()

        @pl.when(part == 0)
        def _():
            def norm(to, sub):
                srows = pl.ds(pl.multiple_of(job * RUN + sub.start, 32), 32)
                mid = xs[to, :].astype(F32) + obuf[srows, :].astype(F32)
                r = lax.rsqrt(jnp.mean(mid * mid, axis=-1, keepdims=True) + norm_eps)
                n2[to, :] = (mid * r * gf_ref[8:9, :]).astype(BF)

            down_rows(run * RUN, RUN, 32, norm)

            def gate(cols):
                s_s[:, cols] = mm(n2[rows, :], wg[:, cols])

            across(ff, 512, gate)

        @pl.when(part == 1)
        def _():
            def up(i, _):
                s_s[:, pl.ds(pl.multiple_of(ff + i * 512, 512), 512)] = mm(n2[rows, :], wu[:, at(i, 512)])
                return 0

            lax.fori_loop(0, ff // 512, up, 0)

        @pl.when(part == 2)
        def _():
            def gated(i, _):
                cols = at(i)
                dhid = mm_nt(ys[rows, :], wd[cols, :])
                gate, up = s_s[:, cols], s_s[:, pl.ds(pl.multiple_of(ff + i * RUN, RUN), RUN)]
                sig = jax.nn.sigmoid(gate)
                silu = gate * sig
                hid[rows, cols] = (silu * up).astype(BF)
                dg[rows, cols] = (dhid * up * sig * (1.0 + gate * (1.0 - sig))).astype(BF)
                du[rows, cols] = (dhid * silu).astype(BF)
                return 0

            lax.fori_loop(0, ff // RUN, gated, 0)

        @pl.when(part == 3)
        def _():
            line.sent(job)

            def normed_two(cols):
                pbuf[at(job), cols] = (mm_nt(dg[rows, :], wg[cols, :]) + mm_nt(du[rows, :], wu[cols, :])).astype(BF)

            across(d, 512, normed_two)
            cp = pltpu.make_async_copy(st_o, fp_h.at[at(job)], osem.at[0])

            @pl.when(job > 0)
            def _():
                cp.wait()

            def project(cols):
                st_o[:, cols] = mm(hid[rows, :], wd[:, cols]).astype(BF)

            across(d, 512, project)
            cp.start()

    second = first + 4 * runs

    def stage(st, sem, dst, value, busy=True):
        cp = pltpu.make_async_copy(st, dst, sem)
        if busy is True:
            cp.wait()
        else:
            pl.when(busy)(cp.wait)

        def fill(cols):
            st[:, cols] = value(cols)

        across(d, 512, fill)
        cp.start()

    def grads_down(k):
        i = k - second
        for j in range(2):
            cols = at(2 * i + j)
            ht = hid[:, cols].T
            stage(st_o, osem.at[0], gds_h.at[cols], lambda to: mm(ht, ys[:, to]).astype(BF))

    def grads_up(k):
        i = k - second - 2
        for j in range(2):
            cols = at(2 * i + j)
            nt = n2[:, cols].T


            def both(to):
                wg[cols, to] = mm(nt, dg[:, to]).astype(BF)
                wu[cols, to] = mm(nt, du[:, to]).astype(BF)

            across(ff, 512, both)

    back = second + 5

    def middle(k):
        job = (k - back) // 5
        run = lax.rem(job + per, runs)
        rows = at(run)
        cp = pltpu.make_async_copy(s_s.at[:, pl.ds(0, d)], dm_h.at[rows], osem.at[1])

        @pl.when(job > 0)
        def _():
            cp.wait()

        def one(to, sub):
            def there(base):
                return pl.ds(pl.multiple_of(base + sub.start, 32), 32)

            mid = xs[to, :].astype(F32) + obuf[there(job * RUN), :].astype(F32)
            r = lax.rsqrt(jnp.mean(mid * mid, axis=-1, keepdims=True) + norm_eps)
            dn = obuf[there((runs + job) * RUN), :].astype(F32)
            w = gf_ref[8:9, :] * dn
            inner = jnp.mean(w * mid, axis=-1, keepdims=True)
            dm = ys[to, :].astype(F32) + r * w - mid * (r * r * r) * inner
            s_s[sub, 0:d] = dm
            gpart[8:16, :] += jnp.sum((dn * mid * r).reshape(4, 8, d), axis=0)
            ys[to, :] = dm.astype(BF)

        down_rows(run * RUN, RUN, 32, one)
        cp.start()
        do = mm_nt(ys[rows, :], wo_ref[...]).astype(BF)
        do_v[rows, :] = mm(do, pad_matrix(hq)).astype(BF)

    width = rep * RUN

    def pair(k, mixed):
        job = (k - back) // 5
        idx = lax.rem(k - back, 5) - 1
        g, part = idx // 2, lax.rem(idx, 2)
        run = lax.rem(job + per, runs)
        rows = at(run)
        diff = iota((RUN, width), 0) - (iota((RUN, width), 1) & (RUN - 1))

        def stack(ref):
            return jnp.concatenate([ref[rows, at(g * rep + j, PAD)] for j in range(rep)], axis=0)

        q, do = stack(q_ref), stack(do_v)

        @pl.when(part == 0)
        def _():
            op = stack(op_v)
            delta_s[0:1, :] = jnp.sum((do.astype(F32) * op.astype(F32)).T, axis=0, keepdims=True)
            dq_s[...] = jnp.zeros_like(dq_s)

        delta = delta_s[0:1, :]
        lse = jnp.concatenate(
            [lse_v[pl.ds(pl.multiple_of((run * hq + g * rep + j) * 8, 8), 1), :] for j in range(rep)], axis=1
        )
        lim = qlim[run]

        def tile(kk, vv, hide):
            p = jnp.exp2(hide(mm_nt(kk, q) * scale - lse))
            ds = (p * (mm_nt(vv, do) - delta)).astype(BF)
            return mm(ds, q), mm(p.astype(BF), do), mm_tn(ds, kk)

        dq = dq_s[...]
        for bb in range(blocks // 2):
            b = part * (blocks // 2) + bb
            room = lim - kbase[b]
            if mixed:
                hide = lambda t: t + jnp.where(room >= 0, 0.0, NEG)
            else:
                hide = lambda t: jnp.where(diff <= room, t, NEG)
            dk, dv, dd = tile(k_s[g, at(b), :], v_s[g, at(b), :], hide)
            dk_s[g, at(b), :] += dk
            dv_s[g, at(b), :] += dv
            dq = dq + dd
        dq_s[...] = dq

        @pl.when(part == 1)
        def _():
            total = dq_s[...]
            ct, st = rope_tables(run, cb_ref, sb_ref, cj_ref, sj_ref)
            if mixed:
                crow = at(run - per)
                dk, dv, dd = tile(kvc_ref[crow, at(g, PAD)], kvc_ref[crow, at(hk + g, PAD)], lambda t: jnp.where(diff <= 0, t, NEG))
                total = total + dd
                dkv_s[rows, at(g, PAD)] = rope_back(dk * score, ct, st).astype(BF)
                dkv_s[rows, at(hk + g, PAD)] = dv.astype(BF)
            for j in range(rep):
                dqp[rows, at(g * rep + j, PAD)] = rope_back(total[j * RUN : (j + 1) * RUN] * score, ct, st).astype(BF)

    def spare(ref, r0, c0, rows, cols, across, count):
        return [ref.at[pl.ds(r0 + i // across * rows, rows), pl.ds(c0 + i % across * cols, cols)] for i in range(count)]

    def square(i, rows, cols, src, mine, theirs, views, out):
        return Square(rows, cols, src, mine, theirs, views, out, credits.at[i], shard_send.at[i], shard_recv.at[i], send.at[i], recv.at[i], store.at[i])

    q4, w4 = dh // 4, ff // 2
    sq_g = square(0, dh, ff, wg.at[yours], wg.at[own], dg.at[pl.ds(0, dh)], spare(n2, 0, 0, q4, w4, 2, 6), gg_h)
    left = spare(n2, 0, 2 * w4, q4, w4, 1, 3) + spare(n2, 3 * q4, 0, q4, w4, 3, 3)
    sq_u = square(1, dh, ff, wu.at[yours], wu.at[own], du.at[pl.ds(0, dh)], left, gu_h)
    f4, d4 = ff // 4, dh // 2
    sq_d = square(2, ff, dh, gds_h.at[:, yours], hid.at[:, pl.ds(0, dh)], gt,
                  spare(n2, dh, 0, f4, d4, 4, 4) + spare(dg, dh, 0, f4, d4, 2, 2), gd_h)
    dq_cols = hq * HEAD_SIZE
    sq_o = square(3, dq_cols, dh, go_v.at[1 - s], go_v.at[s], wg.at[pl.ds(0, dq_cols), pl.ds(0, dh)],
                  spare(wg, dq_cols, 0, dq_cols // 4, d4, 2, 6), go_h)
    gw_cols = dq_cols + wide
    sq_w = square(4, dh, gw_cols, wu.at[yours, pl.ds(0, gw_cols)], wu.at[own, pl.ds(0, gw_cols)], hid.at[pl.ds(0, dh), pl.ds(0, gw_cols)],
                  spare(gt, 0, 0, q4, gw_cols // 2, 2, 6), gw_h)
    down_load = pltpu.make_async_copy(gds_h.at[:, own], hid.at[:, pl.ds(0, dh)], lsem.at[5])
    wp_load = pltpu.make_async_copy(wp_h, wd, lsem.at[6])

    def f_load(job):
        return pltpu.make_async_copy(fp_h.at[at(job)], pbuf.at[at(job)], fsem.at[job])

    def f_start(job):
        line.sent(4 + job)
        f_load(job).start()

    def key_piece(b):
        return ys.at[pl.ds(pl.multiple_of(lax.rem(b, 4) * RUN, RUN), RUN), pl.ds(pl.multiple_of(b // 4 * wide, wide), wide)]

    def key_recv(i, run):
        m = (i - 1) * per + run
        return ys.at[pl.ds(m % 4 * RUN, RUN), pl.ds(dh + m // 4 * wide, wide)]

    def key_copy(i, run):
        to = lax.rem(c + i, nc)
        return remote(key_piece(to * per + run), key_recv(i, run), qsend.at[i, run], qrecv.at[i, run], {"context": to})

    def pack():
        ot = o_v[...].T
        for j in range(2):


            def part(cols, j=j):
                go_v[j, :, cols] = mm(ot, ys[:, pl.ds(pl.multiple_of(j * dh + cols.start, RUN), RUN)]).astype(BF)

            across(dh, RUN, part)
        for i in range(1, nc):
            pl.semaphore_signal(credits.at[5], inc=1, device_id={"context": lax.rem(c + i, nc)}, device_id_type=MESH)

        def one(b, _):
            rows = at(b)
            parts = [(dk_s[g, rows, :] * score).astype(BF) for g in range(hk)]
            parts += [dv_s[g, rows, :].astype(BF) for g in range(hk)]
            value = mm_nt(jnp.concatenate(parts, axis=1), pad_matrix(2 * hk)).astype(BF)
            key_piece(b)[...] = value
            return 0

        lax.fori_loop(0, blocks, one, 0)
        pl.semaphore_wait(credits.at[5], nc - 1)
        for i in range(1, nc):
            for run in range(per):
                key_copy(i, run).start()

    def normed(job):
        rows = at(lax.rem(job + per, runs))
        line.sent(8 + job + jnp.where(job == 3, 1, 0))
        line.sent(4 + job, fwd=False, ret=True)

        def part(cols):
            dn = mm(dqp[rows, :], wd[0:nq, cols]) + mm(dkv_s[rows, :], wd[nq:, cols])
            pbuf[at(job), cols] = dn.astype(BF)

        across(d, 512, part)

    def keys():
        for i in range(1, nc):
            for run in range(per):
                key_copy(i, run).wait_recv()
        selkv = pad_matrix(2 * hk)
        for run in range(per):
            rows = pl.ds(run * RUN, RUN)
            total = mm(key_piece(c * per + run)[...], selkv)
            for i in range(1, nc):
                total = total + mm(key_recv(i, run)[...], selkv)
            ct, st = rope_tables(run, cb_ref, sb_ref, cj_ref, sj_ref)
            for g in range(hk):
                dkv_s[rows, g * PAD : (g + 1) * PAD] = rope_back(total[:, g * PAD : (g + 1) * PAD], ct, st).astype(BF)
            dkv_s[rows, hk * PAD :] = total[:, hk * PAD :].astype(BF)

    tile_v = hid.at[:, pl.ds(dh, RUN)]

    def tile_load(i):
        return pltpu.make_async_copy(n1_h.at[:, at(i)], tile_v, nsem)

    def grads_in(k):
        i = k - into

        @pl.when(i == 0)
        def _():
            def pack_rows(to, sub):
                du[to, 0:dq_cols] = mm_nt(dqp[to, :], pad_matrix(hq)).astype(BF)
                du[to, dq_cols:gw_cols] = mm_nt(dkv_s[to, :], pad_matrix(2 * hk)).astype(BF)

            down_rows(0, rows_here, RUN, pack_rows)

        for j in range(2):
            tile_load(2 * i + j).wait()
            nt = tile_v[...].T


            def part(cols, j=j):
                wu[at(2 * i + j), cols] = mm(nt, du[:, cols]).astype(BF)

            across(gw_cols, gw_cols // 2, part)

            @pl.when(2 * i + j + 1 < d // RUN)
            def _():
                tile_load(2 * i + j + 1).start()

    def halves(i, body):
        for j in range(2):

            def step(m, _, j=j):
                natural = pl.ds(pl.multiple_of(j * half + i * 128 + m * 32, 32), 32)
                by_job = lambda part: pl.ds(pl.multiple_of(part * rows_here + (1 - j) * half + i * 128 + m * 32, 32), 32)
                body(natural, by_job, pl.ds(pl.multiple_of(j * 128 + m * 32, 32), 32))
                return 0

            lax.fori_loop(0, 4, step, 0)

    def output(k):
        i = k - outs

        def one(natural, by_job, to):
            total = xs[natural, :].astype(F32) + obuf[by_job(0), :].astype(F32)
            st_p[to, :] = (total + obuf[by_job(2), :].astype(F32)).astype(BF)

        halves(i, one)
        stage(st_o, osem.at[0], out_h.at[at(i)], lambda cols: mm(merge_matrix(), st_p[:, cols]).astype(BF), i > 0)

    def m_load(i, j):
        src = dm_h.at[pl.ds(pl.multiple_of(j * half + i * 128, 128), 128)]
        return pltpu.make_async_copy(src, s_s.at[pl.ds(j * 128, 128), pl.ds(0, d)], msem.at[j])

    def finals(i):
        for j in range(2):
            m_load(i, j).wait()

        def one(natural, by_job, to):
            x = xs[natural, :].astype(F32)
            dn = obuf[by_job(1), :].astype(F32)
            r = lax.rsqrt(jnp.mean(x * x, axis=-1, keepdims=True) + norm_eps)
            w = gf_ref[0:1, :] * dn
            inner = jnp.mean(w * x, axis=-1, keepdims=True)
            st_p[to, :] = (s_s[to, 0:d] + (r * w - x * (r * r * r) * inner)).astype(BF)
            gpart[0:8, :] += jnp.sum((dn * x * r).reshape(4, 8, d), axis=0)

        halves(i, one)

        @pl.when(i + 1 < runs)
        def _():
            for j in range(2):
                m_load(i + 1, j).start()

        cp = pltpu.make_async_copy(st_t, tg_h.at[at(i)], osem.at[2])

        @pl.when(i > 0)
        def _():
            cp.wait()

        def fill(cols):
            st_t[:, cols] = mm(merge_matrix(), st_p[:, cols]).astype(BF)

        across(d, 512, fill)
        cp.start()

    packed = back + 5 * runs
    into = packed + 3
    outs = into + 4
    lag = hq - 1

    def due(job):
        return (line.per * (job + 1) - 1 + line.turn) // line.ticks + lag + 1

    begins = [back + 5 * job for job in range(runs)]
    items = [([(0, per * hq)], lambda k: head(k, True)), ([(per * hq, first)], lambda k: head(k, False)), ([(first, second)], ffn),
             ([(second, second + 2)], grads_down), ([(second + 2, back)], grads_up), ([(b, b + 1) for b in begins], middle),
             ([(b + 1, b + 5) for b in begins[:per]], lambda k: pair(k, True)),
             ([(b + 1, b + 5) for b in begins[per:]], lambda k: pair(k, False)),
             ([(into, into + 3)], grads_in), ([(outs, outs + runs)], output)]
    fin = due(Line.D_AT[per])

    def begin_down():
        pltpu.make_async_copy(st_o, gds_h.at[pl.ds(0, RUN)], osem.at[0]).wait()
        down_load.start()
        wp_load.start()

    def free_three():
        for sq in (sq_g, sq_u, sq_d):
            sq.free()
        for sq in (sq_d, sq_g, sq_u):
            sq.e0()

    def store_start(sq):
        def body():
            sq.e5()
            sq.store().start()

        return body

    def dm_begin():
        pltpu.make_async_copy(s_s.at[:, pl.ds(0, d)], dm_h.at[pl.ds(0, RUN)], osem.at[1]).wait()
        for j in range(2):
            m_load(0, j).start()

    def first_e1():
        down_load.wait()
        sq_d.e1()

    def give_o():
        sq_g.store().wait()
        sq_g.done()
        sq_o.free()

    def give_w():
        sq_d.store().wait()
        sq_d.done()
        sq_w.free()

    def release_u():
        sq_u.store().wait()
        sq_u.done()

    def number(k, steps):
        return sum(jnp.where(k >= step, 1, 0) for step in steps[1:])

    events = [(second + 2, begin_down), (second + 4, free_three)]
    at_f = [4 * Line.F_AT[job] + lag - 2 for job in range(runs)]
    events += [
        (38, first_e1), (40, sq_g.e1), (41, sq_d.e2), (42, sq_u.e1), (43, sq_g.e2), (44, sq_d.e3), (45, wp_load.wait), (46, sq_u.e2), (47, sq_g.e3),
        (48, sq_d.e4), (49, sq_u.e3), (50, sq_g.e4), (52, store_start(sq_d)), (53, sq_u.e4), (54, give_w), (55, store_start(sq_g)),
        (57, store_start(sq_u)), (57, give_o), (59, release_u),
        (packed, pack), (packed, lambda: tile_load(0).start()), (packed, dm_begin), (packed + 2, keys), (packed + 2, sq_o.e0),
        (61, sq_o.e1), (62, sq_w.e0), (63, sq_o.e2), (64, sq_w.e1), (65, sq_o.e3), (66, sq_w.e2), (67, sq_o.e4), (68, sq_w.e3),
        (69, store_start(sq_o)), (70, sq_w.e4), (73, store_start(sq_w)),
    ]
    items += [([(k, k + 1)], functools.partial(lambda e, k: e(), e)) for k, e in events]
    at_normed = (45, 50, packed + 2, packed + 3)
    items.append(([(k, k + 1) for k in at_f], lambda k: f_start(number(k, at_f))))
    items.append(([(k + 1, k + 2) for k in at_f], lambda k: f_load(number(k, at_f)).wait()))
    items.append(([(k, k + 1) for k in at_normed], lambda k: normed(number(k, at_normed))))
    end = -(-line.slots // line.ticks) + lag
    items.append(([(fin, fin + 2), (end, end + 2)], lambda k: finals(jnp.where(k < end, k - fin, k - end + 2))))

    def serve(k):
        def tick(j, _):
            line.serve(line.ticks * (k - lag) + j)
            return 0

        lax.fori_loop(0, line.ticks, tick, 0)

    run_items(items, serve)
    me = s * nc + c
    sums = jnp.concatenate(
        [jnp.broadcast_to(jnp.sum(gpart[k * 8 : (k + 1) * 8, :], axis=0, keepdims=True), (8, d)) for k in range(2)], axis=0
    )
    grecv[me] = sums
    gcopies = []
    for i, t in enumerate(peers):
        cp = remote(grecv.at[me], grecv.at[me], gs.at[i], gr.at[i], t)
        cp.start()
        gcopies.append(cp)

    def rest(job, _):
        line.sent(jnp.where(job < runs, job, job + runs), fwd=False, ret=True)
        return 0

    lax.fori_loop(0, 3 * runs, rest, 0)
    for job in Line.D_AT:
        line.sent(job)
    for sq in (sq_o, sq_w):
        sq.store().wait()
        sq.done()
    for i in range(1, nc):
        for run in range(per):
            key_copy(i, run).wait_send()
    pltpu.make_async_copy(st_o, out_h.at[pl.ds(0, RUN)], osem.at[0]).wait()
    pltpu.make_async_copy(st_t, tg_h.at[pl.ds(0, RUN)], osem.at[2]).wait()
    for cp in gcopies:
        cp.wait()
    total = grecv[0]
    for i in range(1, 2 * nc):
        total = total + grecv[i]
    gpart[...] = total
    gains_ref[...] = gpart[:, own]


def finish_kernel(out_h, tg_h, gw_h, go_h, gg_h, gu_h, gd_h, out_f, tg_f, gq_f, gk_f, gv_f, go_f, gg_f, gu_f, gd_f,
                  out_v, tg_v, gw_v, go_v, gg_v, gu_v, gd_v, q_v, kv_v, o_v, g_v, u_v, d_v, lsem, ssem):
    kw = gk_f.shape[0]
    nq = gw_h.shape[1] - 2 * kw
    pairs = [(gg_h, gg_v), (gu_h, gu_v), (gd_h, gd_v), (gw_h, gw_v), (go_h, go_v), (out_h, out_v), (tg_h, tg_v)]
    loads = [pltpu.make_async_copy(a, b, lsem.at[i]) for i, (a, b) in enumerate(pairs)]
    for cp in loads:
        cp.start()
    stores = [
        pltpu.make_async_copy(a, b, ssem.at[i])
        for i, (a, b) in enumerate([(g_v, gg_f), (u_v, gu_f), (d_v, gd_f), (q_v, gq_f), (kv_v.at[0:kw], gk_f), (kv_v.at[kw:], gv_f),
                                    (o_v, go_f), (out_v, out_f), (tg_v, tg_f)])
    ]

    def widen(src, dst, width):
        def step(i, _):
            rows = pl.ds(pl.multiple_of(i * 32, 32), 32)
            dst[rows, :] = src[rows, 0:width].astype(F32)
            return 0

        lax.fori_loop(0, src.shape[0] // 32, step, 0)

    for i, (src, dst) in enumerate([(gg_v, g_v), (gu_v, u_v), (gd_v, d_v)]):
        loads[i].wait()
        widen(src, dst, src.shape[1])
        stores[i].start()
    loads[5].wait()
    stores[7].start()
    loads[6].wait()
    stores[8].start()
    loads[3].wait()
    widen(gw_v, q_v, nq)
    stores[3].start()
    for i in range(gw_v.shape[0] // PAD):
        kv_v[:, i * PAD : (i + 1) * PAD] = gw_v[i * PAD : (i + 1) * PAD, nq:].astype(F32).T
    stores[4].start()
    stores[5].start()
    loads[4].wait()
    widen(go_v, o_v, go_v.shape[1])
    stores[6].start()
    for cp in stores:
        cp.wait()


def fast(
    tokens, w_query, key_weight, value_weight, w_out, w_gate, w_up, w_down, gain_attn, gain_ffn, segments, positions, cotangent, n, nc
):
    _, rows, d = tokens.shape
    half = rows // 2
    runs = rows // RUN
    per = runs // 2
    prompt = segments.shape[1] // 2
    blocks = prompt // RUN
    dq, dk = w_query.shape[1], key_weight.shape[1]
    hq, hk = dq // HEAD_SIZE, dk // HEAD_SIZE
    nq, nk = hq * PAD, hk * PAD
    ff = w_gate.shape[1]
    dh = d // 2
    c = lax.axis_index("context")
    x = tokens.reshape(rows, d)
    dy = cotangent.reshape(rows, d)
    kbase = positions[0, 0 :: 2 * RUN]
    seg_here = lax.dynamic_slice_in_dim(segments[0], c * rows, rows, 0)
    pos_here = lax.dynamic_slice_in_dim(positions[0], c * rows, rows, 0)
    qbase = jnp.concatenate([pos_here[0 :: 2 * RUN], pos_here[1 :: 2 * RUN]])
    qlim = jnp.concatenate([pos_here[0 :: 2 * RUN], seg_here[1 :: 2 * RUN] * CLEN - 1])
    freq = np.exp(np.arange(HEAD_SIZE // 2, dtype=np.float32) * np.float32(-2.0 * math.log(rope_base) / HEAD_SIZE)).astype(np.float32)
    lanes = np.zeros((PAD,), np.float32)
    lanes[0:48] = freq
    lanes[64:112] = freq
    sign = np.where(np.arange(PAD) < 64, -1.0, 1.0).astype(np.float32)
    inner = np.arange(RUN, dtype=np.float64)[:, None] * lanes[None, :].astype(np.float64)
    cj = jnp.asarray(np.cos(inner).astype(np.float32))
    sj = jnp.asarray((np.sin(inner) * sign).astype(np.float32))
    angle = qbase.astype(F32)[:, None] * jnp.asarray(lanes)[None, :]
    cb = jnp.cos(angle)
    sb = jnp.sin(angle) * jnp.asarray(sign)[None, :]
    gains = jnp.concatenate([jnp.broadcast_to(g.astype(F32)[None, :], (8, dh)) for g in (gain_attn, gain_ffn)], axis=0)

    V = pl.BlockSpec(memory_space=pltpu.VMEM)
    S = pl.BlockSpec(memory_space=pltpu.SMEM)
    A = pl.BlockSpec(memory_space=pl.ANY)
    sds = jax.ShapeDtypeStruct
    DMA = pltpu.SemaphoreType.DMA

    def call(kernel, ins, outs, scratch, collective=None, flops=0):
        params = dict(vmem_limit_bytes=VLIM - 64 * 1024)
        if collective is not None:
            params.update(collective_id=collective, has_side_effects=True)
        args = [a for a, _ in ins]
        return pl.pallas_call(
            kernel,
            out_shape=[o for o, _ in outs],
            in_specs=[sp for _, sp in ins],
            out_specs=[sp for _, sp in outs],
            scratch_shapes=scratch,
            compiler_params=pltpu.CompilerParams(**params),
            cost_estimate=pl.CostEstimate(flops=flops, bytes_accessed=0, transcendentals=0),
        )(*args)

    rope_in = [(cb, V), (sb, V), (cj, V), (sj, V)]
    xp, dyp, n1, q, kvp, kvc, wp, gf, wo, wg, wu, wd = call(
        functools.partial(first_kernel, nc),
        [(x, V), (dy, A), (gains, A)] + rope_in + [(w_query, A), (key_weight.T, A), (value_weight.T, A), (w_out, A), (w_gate, A), (w_up, A), (w_down, A)],
        [
            (sds((rows, d), BF), V), (sds((rows, d), BF), V), (sds((rows, d), BF), V), (sds((rows, nq), BF), V),
            (sds((prompt, 2 * dk), BF), A), (sds((half, 2 * nk), BF), V), (sds((nq + 2 * nk, d), BF), V), (sds((16, d), F32), V),
            (sds((dq, d), BF), A), (sds((d, ff), BF), A), (sds((d, ff), BF), A), (sds((ff, d), BF), A),
        ],
        [
            pltpu.VMEM((rows, d), BF), pltpu.VMEM((d, dq), BF), pltpu.VMEM((dk, d), BF), pltpu.VMEM((dk, d), BF), pltpu.VMEM((16, d), F32),
            pltpu.VMEM((dq, dh), BF), pltpu.VMEM((dh, ff), BF), pltpu.VMEM((dh, ff), BF), pltpu.VMEM((ff, dh), BF),
            pltpu.VMEM((half, 2 * dk), BF),
            DMA((9,)), DMA((8,)), DMA((8,)), DMA((4,)), DMA((per, nc)), DMA((per, nc)),
        ],
        collective=0, flops=60 * 10**9,
    )

    chunk = 16
    count = 16 * (RUN // 2 // chunk)
    U = pltpu.VMEM((rows, d), BF)
    W = pltpu.VMEM((d, ff), BF)
    H = pltpu.VMEM((rows, ff), BF)
    KV = pltpu.VMEM((hk, prompt, PAD), BF)
    KVF = pltpu.VMEM((hk, prompt, PAD), F32)
    width = hq // hk * RUN
    out, tg, gg, gu, gd, go, gw, _, _, _, gains_grad = call(
        functools.partial(main_kernel, n, nc, chunk),
        [(kbase, S), (qlim, S)] + rope_in
        + [(gf, V), (q, V), (kvc, V), (wo, V), (kvp, A), (xp, A), (dyp, A), (wg, A), (wu, A), (wd, A), (n1, A), (wp, A)],
        [(sds((rows, d), BF), A), (sds((rows, d), BF), A), (sds((dh, ff), BF), A), (sds((dh, ff), BF), A), (sds((ff, dh), BF), A),
         (sds((dq, dh), BF), A), (sds((dh, dq + 2 * dk), BF), A), (sds((rows, d), F32), A), (sds((ff, d), BF), A), (sds((rows, d), BF), A),
         (sds((16, dh), F32), V)],
        [KV, KV, pltpu.VMEM((RUN, prompt + RUN), F32), pltpu.VMEM((rows, dq), BF), pltpu.VMEM((rows, nq), BF), pltpu.VMEM((runs * hq * 8, RUN), F32),
         U, U, U, U, pltpu.VMEM((3 * rows, d), BF), pltpu.VMEM((ff, d), BF), U, W, W, H, H, H, pltpu.VMEM((ff, dh), BF),
         KVF, KVF, pltpu.VMEM((rows, nq), BF), pltpu.VMEM((width, PAD), F32), pltpu.VMEM((8, width), F32), pltpu.VMEM((rows, nq), BF),
         pltpu.VMEM((rows, 2 * nk), BF), pltpu.VMEM((2, dq, dh), BF), pltpu.VMEM((RUN, d), BF), pltpu.VMEM((RUN, d), BF), pltpu.VMEM((RUN, d), BF),
         pltpu.VMEM((16, d), F32), pltpu.VMEM((2 * nc, 16, d), F32),
         DMA((7,)), DMA((blocks,)), DMA((3,)), DMA((runs,)), DMA((2,)), DMA, DMA((nc, per)), DMA((nc, per)), DMA((2 * nc - 1,)), DMA((2 * nc - 1,))]
        + [DMA((2, count))] * 4
        + [pltpu.SemaphoreType.REGULAR((6,)), DMA((5,)), DMA((5,)), DMA((5, 3, 2, 2)), DMA((5, 3, 2, 2)), DMA((5,))],
        collective=1, flops=300 * 10**9,
    )
    shapes = [(rows, d), (rows, d), (dh, dq + 2 * dk), (dq, dh), (dh, ff), (dh, ff), (ff, dh)]
    wide = [(dh, dq), (2 * dk, dh), (dq, dh), (dh, ff), (dh, ff), (ff, dh)]
    finals = [(dh, dq), (dk, dh), (dk, dh), (dq, dh), (dh, ff), (dh, ff), (ff, dh)]
    out, tg, gq, gk, gv, go, gg, gu, gd = call(
        finish_kernel,
        [(a, A) for a in (out, tg, gw, go, gg, gu, gd)],
        [(sds((rows, d), BF), A), (sds((rows, d), BF), A)] + [(sds(shape, F32), A) for shape in finals],
        [pltpu.VMEM(shape, BF) for shape in shapes] + [pltpu.VMEM(shape, F32) for shape in wide] + [DMA((7,)), DMA((9,))],
    )
    return out[None], tg[None], gq, gk.T, gv.T, go, gg, gu, gd, gains_grad[0], gains_grad[8]


def body(mesh, *args):
    tokens, w_query, segments = args[0], args[1], args[10]
    n, nc = mesh.shape["tensor"], mesh.shape["context"]
    rows = tokens.shape[1]
    if (tokens.shape[0] == 1 and rows % (4 * CLEN) == 0 and n == 4 and nc == 4 and mesh.shape["shard"] == 2
            and segments.shape[1] == rows * nc):
        return fast(*args, n, nc)
    return general(*args)


def solution(mesh):
    in_specs = (
        P("shard", "context", None),
        P("shard", "tensor"),
        P("shard", "tensor"),
        P("shard", "tensor"),
        P("tensor", "shard"),
        P("shard", "tensor"),
        P("shard", "tensor"),
        P("tensor", "shard"),
        P("shard"),
        P("shard"),
        P("shard", None),
        P("shard", None),
        P("shard", "context", None),
    )
    out_specs = (
        P("shard", "context", None),
        P("shard", "context", None),
        P("shard", "tensor"),
        P("shard", "tensor"),
        P("shard", "tensor"),
        P("tensor", "shard"),
        P("shard", "tensor"),
        P("shard", "tensor"),
        P("tensor", "shard"),
        P("shard"),
        P("shard"),
    )
    return jax.shard_map(functools.partial(body, mesh), mesh=mesh, in_specs=in_specs, out_specs=out_specs, check_vma=False)
```

```python
import functools
import math

import jax
import jax.numpy as jnp
import numpy as np
from jax import lax
from jax.experimental import pallas as pl
from jax.experimental.pallas import tpu as pltpu
from jax.sharding import PartitionSpec as P

HEAD_SIZE = 96
CLEN = 256


rope_base = 100000.0
norm_eps = 1e-05


def tables(positions):
    half_width = HEAD_SIZE // 2
    frequency = jnp.exp(
        jnp.arange(half_width, dtype=jnp.float32) * (-2.0 * math.log(rope_base) / HEAD_SIZE)
    )
    angles = positions.astype(jnp.float32)[:, None] * frequency[None, :]
    return (jnp.cos(angles)[:, None, :], jnp.sin(angles)[:, None, :])


def rotary_apply(heads, cosine_table, sine_values):
    half_width = HEAD_SIZE // 2
    front_half = heads[..., :half_width]
    back_half = heads[..., half_width:]
    return jnp.concatenate(
        [
            front_half * cosine_table - back_half * sine_values,
            back_half * cosine_table + front_half * sine_values,
        ],
        axis=-1,
    )


def rotate_back(heads, cosine_table, sine_values):
    half_width = HEAD_SIZE // 2
    front_half = heads[..., :half_width]
    back_half = heads[..., half_width:]
    return jnp.concatenate(
        [
            front_half * cosine_table + back_half * sine_values,
            back_half * cosine_table - front_half * sine_values,
        ],
        axis=-1,
    )


def contract_rows(left, right):
    return lax.dot_general(
        left, right, (((0,), (0,)), ((), ())), preferred_element_type=jnp.float32
    )


def contract_cols(left, right):
    return lax.dot_general(
        left, right, (((1,), (1,)), ((), ())), preferred_element_type=jnp.float32
    )


def norm_back(tok_rows, norm_scale, gain, grad_normed):
    weighted = gain * grad_normed
    inner = jnp.mean(weighted * tok_rows, axis=-1, keepdims=True)
    grad_rows = norm_scale * weighted - tok_rows * (norm_scale * norm_scale * norm_scale) * inner
    grad_gain = jnp.sum(grad_normed * tok_rows * norm_scale, axis=0)
    return (grad_rows, grad_gain)


def visible(seg_query, pos_query, seg_keys, pos_keys):
    own = (seg_keys[None, :] == seg_query[:, None]) & (pos_keys[None, :] <= pos_query[:, None])
    branch = (
        (seg_keys[None, :] == 0)
        & (seg_query[:, None] > 0)
        & (pos_keys[None, :] < seg_query[:, None] * CLEN)
    )
    return own | branch


def general(
    tokens,
    w_query,
    key_weight,
    value_weight,
    w_out,
    w_gate,
    w_up,
    w_down,
    gain_attn,
    gain_ffn,
    segments,
    positions,
    cotangent,
):
    groups, tok_local, model_width = tokens.shape
    token_count = groups * tok_local
    heads_here = w_query.shape[1] // HEAD_SIZE
    kv_here = key_weight.shape[1] // HEAD_SIZE
    per_kv = heads_here // kv_here
    kv_width = kv_here * HEAD_SIZE
    score_scale = 1.0 / math.sqrt(HEAD_SIZE)
    context_index = lax.axis_index("context")
    first_row = context_index * tok_local
    seg_here = lax.dynamic_slice_in_dim(segments, first_row, tok_local, 1)
    pos_here = lax.dynamic_slice_in_dim(positions, first_row, tok_local, 1)
    w_query, key_weight, value_weight, w_gate, w_up, gain_attn, gain_ffn = (
        lax.all_gather(w_query, "shard", axis=0, tiled=True),
        lax.all_gather(key_weight, "shard", axis=0, tiled=True),
        lax.all_gather(value_weight, "shard", axis=0, tiled=True),
        lax.all_gather(w_gate, "shard", axis=0, tiled=True),
        lax.all_gather(w_up, "shard", axis=0, tiled=True),
        lax.all_gather(gain_attn, "shard", axis=0, tiled=True),
        lax.all_gather(gain_ffn, "shard", axis=0, tiled=True),
    )
    w_out, w_down = (
        lax.all_gather(w_out, "shard", axis=1, tiled=True),
        lax.all_gather(w_down, "shard", axis=1, tiled=True),
    )
    gain_one = gain_attn.astype(jnp.float32)
    gain_two = gain_ffn.astype(jnp.float32)
    tok_rows = tokens.reshape(token_count, model_width).astype(jnp.float32)
    scale_one = lax.rsqrt(jnp.mean(tok_rows * tok_rows, axis=-1, keepdims=True) + norm_eps)
    normed_input = (tok_rows * scale_one * gain_one).astype(jnp.bfloat16)
    cosine_table, sine_values = tables(pos_here.reshape(token_count))
    query_heads_rows = rotary_apply(
        jnp.dot(normed_input, w_query, preferred_element_type=jnp.float32).reshape(
            token_count, heads_here, HEAD_SIZE
        ),
        cosine_table,
        sine_values,
    )
    query_heads_rows = query_heads_rows.astype(jnp.bfloat16).reshape(
        groups, tok_local, heads_here * HEAD_SIZE
    )
    key_rows = rotary_apply(
        jnp.dot(normed_input, key_weight, preferred_element_type=jnp.float32).reshape(
            token_count, kv_here, HEAD_SIZE
        ),
        cosine_table,
        sine_values,
    )
    key_rows = key_rows.astype(jnp.bfloat16).reshape(token_count, kv_width)
    value_rows = jnp.dot(normed_input, value_weight, preferred_element_type=jnp.float32).astype(
        jnp.bfloat16
    )
    keyval = jnp.concatenate([key_rows, value_rows], axis=-1).reshape(
        groups, tok_local, 2 * kv_width
    )
    gathered = lax.all_gather(keyval, "context", axis=1, tiled=True)

    def scores_of(group_queries, group_keyval, seg_query, pos_query, seg_keys, pos_keys):
        grouped_heads = group_queries.reshape(tok_local, kv_here, per_kv, HEAD_SIZE)
        key_head_rows = group_keyval[:, :kv_width].reshape(-1, kv_here, HEAD_SIZE)
        scores = (
            jnp.einsum(
                "bhgd,khd->hgbk", grouped_heads, key_head_rows, preferred_element_type=jnp.float32
            )
            * score_scale
        )
        allowed = visible(seg_query, pos_query, seg_keys, pos_keys)
        return (jnp.where(allowed[None, None], scores, -1e30), grouped_heads, key_head_rows)

    def attend_group(inputs):
        group_queries, group_keyval, seg_query, pos_query, seg_keys, pos_keys = inputs
        scores, grouped_heads, key_head_rows = scores_of(
            group_queries, group_keyval, seg_query, pos_query, seg_keys, pos_keys
        )
        top_score = jnp.max(scores, axis=-1, keepdims=True)
        exponent = jnp.exp(scores - top_score)
        totals = jnp.sum(exponent, axis=-1, keepdims=True)
        soft_weights = (exponent / totals).astype(jnp.bfloat16)
        value_head_rows = group_keyval[:, kv_width:].reshape(-1, kv_here, HEAD_SIZE)
        attended_output = jnp.einsum(
            "hgbk,khd->bhgd", soft_weights, value_head_rows, preferred_element_type=jnp.float32
        )
        return (
            attended_output.reshape(tok_local, heads_here * HEAD_SIZE),
            (top_score + jnp.log(totals))[..., 0],
        )

    attended_output, log_total = lax.map(
        attend_group, (query_heads_rows, gathered, seg_here, pos_here, segments, positions)
    )
    attended_low = attended_output.reshape(token_count, heads_here * HEAD_SIZE).astype(jnp.bfloat16)
    attn_sum = lax.psum(jnp.dot(attended_low, w_out, preferred_element_type=jnp.float32), "tensor")
    middle = tok_rows + attn_sum
    scale_two = lax.rsqrt(jnp.mean(middle * middle, axis=-1, keepdims=True) + norm_eps)
    normed_two = (middle * scale_two * gain_two).astype(jnp.bfloat16)
    gate_proj = jnp.dot(normed_two, w_gate, preferred_element_type=jnp.float32)
    up_proj = jnp.dot(normed_two, w_up, preferred_element_type=jnp.float32)
    sigmoid_gate = jax.nn.sigmoid(gate_proj)
    silu_gate = gate_proj * sigmoid_gate
    hidden = (silu_gate * up_proj).astype(jnp.bfloat16)
    ffn_sum = lax.psum(
        jnp.dot(hidden, w_down, preferred_element_type=jnp.float32).astype(jnp.bfloat16), "tensor"
    ).astype(jnp.float32)
    output = (middle + ffn_sum).astype(jnp.bfloat16).reshape(groups, tok_local, model_width)
    grad_low = cotangent.reshape(token_count, model_width)
    grad_out = grad_low.astype(jnp.float32)
    grad_hidden = contract_cols(grad_low, w_down)
    grad_w_down_t = contract_rows(grad_low, hidden)
    grad_gate = (
        grad_hidden * up_proj * sigmoid_gate * (1.0 + gate_proj * (1.0 - sigmoid_gate))
    ).astype(jnp.bfloat16)
    grad_up = (grad_hidden * silu_gate).astype(jnp.bfloat16)
    grad_w_gate = contract_rows(normed_two, grad_gate)
    grad_w_up = contract_rows(normed_two, grad_up)
    grad_normed_two = lax.psum(
        contract_cols(grad_gate, w_gate) + contract_cols(grad_up, w_up), "tensor"
    )
    back_two, grad_gain_two = norm_back(middle, scale_two, gain_two, grad_normed_two)
    grad_middle = grad_out + back_two
    grad_mid_low = grad_middle.astype(jnp.bfloat16)
    grad_w_out_t = contract_rows(grad_mid_low, attended_low)
    grad_attended = (
        contract_cols(grad_mid_low, w_out)
        .astype(jnp.bfloat16)
        .reshape(groups, tok_local, heads_here * HEAD_SIZE)
    )

    def attend_back(inputs):
        (
            group_queries,
            group_keyval,
            group_grad,
            group_total,
            seg_query,
            pos_query,
            seg_keys,
            pos_keys,
        ) = inputs
        scores, grouped_heads, key_head_rows = scores_of(
            group_queries, group_keyval, seg_query, pos_query, seg_keys, pos_keys
        )
        soft_weights = jnp.exp(scores - group_total[..., None])
        value_head_rows = group_keyval[:, kv_width:].reshape(-1, kv_here, HEAD_SIZE)
        grad_grouped = group_grad.reshape(tok_local, kv_here, per_kv, HEAD_SIZE)
        grad_weights = jnp.einsum(
            "bhgd,khd->hgbk", grad_grouped, value_head_rows, preferred_element_type=jnp.float32
        )
        inner = jnp.sum(soft_weights * grad_weights, axis=-1, keepdims=True)
        grad_scores = (soft_weights * (grad_weights - inner)).astype(jnp.bfloat16)
        grad_queries = (
            jnp.einsum(
                "hgbk,khd->bhgd", grad_scores, key_head_rows, preferred_element_type=jnp.float32
            )
            * score_scale
        )
        grad_keys = (
            jnp.einsum(
                "hgbk,bhgd->khd", grad_scores, grouped_heads, preferred_element_type=jnp.float32
            )
            * score_scale
        )
        grad_values = jnp.einsum(
            "hgbk,bhgd->khd",
            soft_weights.astype(jnp.bfloat16),
            grad_grouped,
            preferred_element_type=jnp.float32,
        )
        grad_keyval = jnp.concatenate(
            [grad_keys.reshape(-1, kv_width), grad_values.reshape(-1, kv_width)], axis=-1
        )
        return (grad_queries.reshape(tok_local, heads_here * HEAD_SIZE), grad_keyval)

    grad_queries, grad_keyval = lax.map(
        attend_back,
        (
            query_heads_rows,
            gathered,
            grad_attended,
            log_total,
            seg_here,
            pos_here,
            segments,
            positions,
        ),
    )
    grad_keyval = lax.psum_scatter(grad_keyval, "context", scatter_dimension=1, tiled=True)
    grad_query_rows = rotate_back(
        grad_queries.reshape(token_count, heads_here, HEAD_SIZE), cosine_table, sine_values
    )
    grad_query_rows = grad_query_rows.astype(jnp.bfloat16).reshape(
        token_count, heads_here * HEAD_SIZE
    )
    grad_key_rows = rotate_back(
        grad_keyval[..., :kv_width].reshape(token_count, kv_here, HEAD_SIZE),
        cosine_table,
        sine_values,
    )
    grad_key_rows = grad_key_rows.astype(jnp.bfloat16).reshape(token_count, kv_width)
    grad_value_rows = (
        grad_keyval[..., kv_width:].reshape(token_count, kv_width).astype(jnp.bfloat16)
    )
    grad_w_query = contract_rows(normed_input, grad_query_rows)
    grad_w_key = contract_rows(normed_input, grad_key_rows)
    grad_w_value = contract_rows(normed_input, grad_value_rows)
    partial_one = (
        contract_cols(grad_query_rows, w_query)
        + contract_cols(grad_key_rows, key_weight)
        + contract_cols(grad_value_rows, value_weight)
    )
    grad_normed = lax.psum(partial_one, "tensor")
    back_one, grad_gain_one = norm_back(tok_rows, scale_one, gain_one, grad_normed)
    tokens_grad = (
        (grad_middle + back_one).astype(jnp.bfloat16).reshape(groups, tok_local, model_width)
    )
    summed = (
        lax.psum_scatter(grad_w_query, ("shard", "context"), scatter_dimension=0, tiled=True),
        lax.psum_scatter(grad_w_key, ("shard", "context"), scatter_dimension=0, tiled=True),
        lax.psum_scatter(grad_w_value, ("shard", "context"), scatter_dimension=0, tiled=True),
        lax.psum_scatter(grad_w_out_t, ("shard", "context"), scatter_dimension=0, tiled=True),
        lax.psum_scatter(grad_w_gate, ("shard", "context"), scatter_dimension=0, tiled=True),
        lax.psum_scatter(grad_w_up, ("shard", "context"), scatter_dimension=0, tiled=True),
        lax.psum_scatter(grad_w_down_t, ("shard", "context"), scatter_dimension=0, tiled=True),
        lax.psum_scatter(grad_gain_one, ("shard", "context"), scatter_dimension=0, tiled=True),
        lax.psum_scatter(grad_gain_two, ("shard", "context"), scatter_dimension=0, tiled=True),
    )
    summed = (
        lax.all_gather(summed[0].astype(jnp.bfloat16), "context", axis=0, tiled=True).astype(
            jnp.float32
        ),
        lax.all_gather(summed[1].astype(jnp.bfloat16), "context", axis=0, tiled=True).astype(
            jnp.float32
        ),
        lax.all_gather(summed[2].astype(jnp.bfloat16), "context", axis=0, tiled=True).astype(
            jnp.float32
        ),
        lax.all_gather(summed[3].astype(jnp.bfloat16), "context", axis=0, tiled=True).astype(
            jnp.float32
        ),
        lax.all_gather(summed[4].astype(jnp.bfloat16), "context", axis=0, tiled=True).astype(
            jnp.float32
        ),
        lax.all_gather(summed[5].astype(jnp.bfloat16), "context", axis=0, tiled=True).astype(
            jnp.float32
        ),
        lax.all_gather(summed[6].astype(jnp.bfloat16), "context", axis=0, tiled=True).astype(
            jnp.float32
        ),
        lax.all_gather(summed[7].astype(jnp.bfloat16), "context", axis=0, tiled=True).astype(
            jnp.float32
        ),
        lax.all_gather(summed[8].astype(jnp.bfloat16), "context", axis=0, tiled=True).astype(
            jnp.float32
        ),
    )
    return (
        output,
        tokens_grad,
        summed[0],
        summed[1],
        summed[2],
        summed[3].T,
        summed[4],
        summed[5],
        summed[6].T,
        summed[7],
        summed[8],
    )


MESH = pl.DeviceIdType.MESH
RUN = 256
PAD = 128
NEG = -1e30
LOG2E = 1.4426950408889634
BF = jnp.bfloat16
F32 = jnp.float32
VLIM = 64 * 1024 * 1024


def mm(a, b):
    return lax.dot_general(a, b, (((1,), (0,)), ((), ())), preferred_element_type=F32)


def mm_nt(a, b):
    return lax.dot_general(a, b, (((1,), (1,)), ((), ())), preferred_element_type=F32)


def mm_tn(a, b):
    return lax.dot_general(a, b, (((0,), (0,)), ((), ())), preferred_element_type=F32)


def iota(shape, axis):
    return lax.broadcasted_iota(jnp.int32, shape, axis)


def one_hot(hit):
    return jnp.where(hit, 1.0, 0.0).astype(BF)


def pad_matrix(heads, flip=False):
    shape = (heads * HEAD_SIZE, heads * PAD)
    if flip:
        row, col = iota(shape[::-1], 1), iota(shape[::-1], 0)
    else:
        row, col = iota(shape, 0), iota(shape, 1)
    lane = col & 127
    part = jnp.where(lane < 64, lane, lane - 16)
    return one_hot((row == (col >> 7) * HEAD_SIZE + part) & ((lane & 63) < 48))


def split_matrix():
    row, col = iota((RUN, RUN), 0), iota((RUN, RUN), 1)
    return one_hot(col == jnp.where(row < 128, 2 * row, 2 * row - 255))


def merge_matrix():
    row, col = iota((RUN, RUN), 0), iota((RUN, RUN), 1)
    return one_hot(col == (row >> 1) + (row & 1) * 128)


def rope_tables(run, cb_ref, sb_ref, cj_ref, sj_ref):
    cb, sb = cb_ref[pl.ds(run, 1), :], sb_ref[pl.ds(run, 1), :]
    cj, sj = cj_ref[...], sj_ref[...]
    return cb * cj - sb * sj, sb * cj + cb * sj


def rope(u, c, s):
    return u * c + pltpu.roll(u, 64, 1) * s


def rope_back(u, c, s):
    return u * c - pltpu.roll(u, 64, 1) * s


def vmem(*shape_dtype):
    return pl.BlockSpec(memory_space=pltpu.VMEM)


def entry_barrier(targets):
    bar = pltpu.get_barrier_semaphore()
    for t in targets:
        pl.semaphore_signal(bar, inc=1, device_id=t, device_id_type=MESH)
    pl.semaphore_wait(bar, len(targets))


def remote(src, dst, send, recv, target):
    return pltpu.make_async_remote_copy(
        src_ref=src, dst_ref=dst, send_sem=send, recv_sem=recv, device_id=target, device_id_type=MESH
    )


def first_kernel(nc, x_ref, dy_h, g_ref, cb_ref, sb_ref, cj_ref, sj_ref, wq_h, wk_h, wv_h, wo_h, wg_h, wu_h, wd_h,
                 xp_ref, dyp_ref, n1_ref, q_ref, kvp_ref, kvc_ref, wp_ref, gf_ref, wo_f, wg_f, wu_f, wd_f,
                 dy_v, wq_s, wk_s, wv_s, g_s, wo_v, wg_v, wu_v, wd_v, kv_send,
                 lsem, ssem, rsem, osem, csem, crem):
    s = lax.axis_index("shard")
    c = lax.axis_index("context")
    dh = g_s.shape[1] // 2
    own = pl.ds(pl.multiple_of(s * dh, dh), dh)
    other = {"shard": 1 - s}
    loads = [
        pltpu.make_async_copy(wq_h, wq_s.at[own], lsem.at[0]),
        pltpu.make_async_copy(wk_h, wk_s.at[:, own], lsem.at[1]),
        pltpu.make_async_copy(wv_h, wv_s.at[:, own], lsem.at[2]),
        None,
        pltpu.make_async_copy(wo_h, wo_v, lsem.at[4]),
        pltpu.make_async_copy(wg_h, wg_v, lsem.at[5]),
        pltpu.make_async_copy(wu_h, wu_v, lsem.at[6]),
        pltpu.make_async_copy(wd_h, wd_v, lsem.at[7]),
        pltpu.make_async_copy(dy_h, dy_v, lsem.at[8]),
    ]
    for cp in loads[:3] + loads[4:]:
        cp.start()
    for i in range(2):
        g_s[8 * i : 8 * i + 8, own] = jnp.broadcast_to(g_ref[i : i + 1, :], (8, dh))
    entry_barrier([other] + [{"context": lax.rem(c + i, nc)} for i in range(1, nc)])
    sends = [
        remote(wq_s.at[own], wq_s.at[own], ssem.at[0], rsem.at[0], other),
        remote(wk_s.at[:, own], wk_s.at[:, own], ssem.at[1], rsem.at[1], other),
        remote(wv_s.at[:, own], wv_s.at[:, own], ssem.at[2], rsem.at[2], other),
        remote(g_s.at[:, own], g_s.at[:, own], ssem.at[3], rsem.at[3], other),
        remote(wo_v, wo_f.at[:, own], ssem.at[4], rsem.at[4], other),
        remote(wg_v, wg_f.at[own], ssem.at[5], rsem.at[5], other),
        remote(wu_v, wu_f.at[own], ssem.at[6], rsem.at[6], other),
        remote(wd_v, wd_f.at[:, own], ssem.at[7], rsem.at[7], other),
    ]
    keeps = [
        pltpu.make_async_copy(wo_v, wo_f.at[:, own], osem.at[0]),
        pltpu.make_async_copy(wg_v, wg_f.at[own], osem.at[1]),
        pltpu.make_async_copy(wu_v, wu_f.at[own], osem.at[2]),
        pltpu.make_async_copy(wd_v, wd_f.at[:, own], osem.at[3]),
    ]
    for i in (3, 0, 1, 2, 4, 5, 6, 7):
        if i != 3:
            loads[i].wait()
        sends[i].start()
        if i >= 4:
            keeps[i - 4].start()
    half = x_ref.shape[0] // 2
    split = split_matrix()
    for i in range(x_ref.shape[0] // RUN):
        xb = mm(split, x_ref[pl.ds(i * RUN, RUN), :])
        xp_ref[pl.ds(i * 128, 128), :] = xb[:128].astype(BF)
        xp_ref[pl.ds(half + i * 128, 128), :] = xb[128:].astype(BF)
        if i == 0:
            sends[3].wait_recv()
        r = lax.rsqrt(jnp.mean(xb * xb, axis=-1, keepdims=True) + norm_eps)
        nb = (xb * r * g_s[0:1, :]).astype(BF)
        n1_ref[pl.ds(i * 128, 128), :] = nb[:128]
        n1_ref[pl.ds(half + i * 128, 128), :] = nb[128:]
    gf_ref[...] = g_s[...]
    hq, hk = wq_s.shape[1] // HEAD_SIZE, wk_s.shape[0] // HEAD_SIZE
    selq, selk = pad_matrix(hq, True), pad_matrix(hk, True)
    nq, nk = hq * PAD, hk * PAD
    for i in range(3):
        sends[i].wait_recv()
    wp_ref[0:nq, :] = mm_nt(selq, wq_s[...]).astype(BF)
    wp_ref[nq : nq + nk, :] = mm(selk, wk_s[...]).astype(BF)
    wp_ref[nq + nk :, :] = mm(selk, wv_s[...]).astype(BF)
    selkv = pad_matrix(2 * hk)
    runs = x_ref.shape[0] // RUN
    per = runs // 2
    kv_copies = []
    for run in range(runs):
        rows = pl.ds(run * RUN, RUN)
        y = mm_nt(n1_ref[rows, :], wp_ref[nq:, :])
        ct, st = rope_tables(run, cb_ref, sb_ref, cj_ref, sj_ref)
        kv = [rope(y[:, h * PAD : (h + 1) * PAD], ct, st).astype(BF) for h in range(hk)]
        kv = jnp.concatenate(kv + [y[:, nk:].astype(BF)], axis=1)
        if run < per:
            kv_send[pl.ds(run * RUN, RUN), :] = mm_nt(kv, selkv).astype(BF)
            mine = pl.ds(pl.multiple_of((c * per + run) * RUN, RUN), RUN)
            for i in range(1, nc):
                cp = remote(kv_send.at[pl.ds(run * RUN, RUN)], kvp_ref.at[mine], csem.at[run, i], crem.at[run, i],
                            {"context": lax.rem(c + i, nc)})
                cp.start()
                kv_copies.append(cp)
            cp = pltpu.make_async_copy(kv_send.at[pl.ds(run * RUN, RUN)], kvp_ref.at[mine], csem.at[run, 0])
            cp.start()
            kv_copies.append(cp)
        else:
            kvc_ref[pl.ds((run - per) * RUN, RUN), :] = kv
    for run in range(runs):
        rows = pl.ds(run * RUN, RUN)
        y = mm_nt(n1_ref[rows, :], wp_ref[0:nq, :])
        ct, st = rope_tables(run, cb_ref, sb_ref, cj_ref, sj_ref)
        for h in range(hq):
            q_ref[rows, h * PAD : (h + 1) * PAD] = rope(y[:, h * PAD : (h + 1) * PAD], ct, st).astype(BF)
    loads[8].wait()
    for i in range(x_ref.shape[0] // RUN):
        b = mm(split, dy_v[pl.ds(i * RUN, RUN), :]).astype(BF)
        dyp_ref[pl.ds(i * 128, 128), :] = b[:128]
        dyp_ref[pl.ds(half + i * 128, 128), :] = b[128:]
    for cp in kv_copies:
        cp.wait()
    for i in range(4):
        keeps[i].wait()
        sends[4 + i].wait_recv()
    for cp in sends:
        cp.wait_send()


class Line:
    F_AT = (8, 9, 10, 12)
    D_AT = (11, 13, 14, 15)

    def __init__(self, n, chunk, pbuf, rbuf, obuf, sems):
        self.n, self.chunk, self.per = n, chunk, RUN // 2 // chunk
        self.count = 16 * self.per
        self.pbuf, self.rbuf, self.obuf = pbuf, rbuf, obuf
        self.rs, self.rr, self.bs, self.br = sems
        self.ticks = 32 // chunk
        self.hop = 3
        self.turn = 2 * (n - 1) * self.hop
        self.slots = self.count + self.turn

    def pieces(self, h, i):
        n, chunk = self.n, self.chunk
        z = lax.axis_index("tensor")
        job = i // self.per
        late = jnp.where((job == 11) | (job > 12), 1, 0)
        row = jnp.where(job < 8, lax.rem(job, 4), jnp.where(late == 1, jnp.maximum(job - 12, 0), jnp.minimum(job - 8, 3)))
        part = jnp.where(job < 8, job // 4, 2 - late)
        off = row * RUN + h * (RUN // 2) + lax.rem(i, self.per) * chunk
        rows = pl.ds(pl.multiple_of(off, chunk), chunk)
        orows = pl.ds(pl.multiple_of(part * (4 * RUN) + off, chunk), chunk)
        place = z if h == 0 else n - 1 - z
        up, down = jnp.minimum(z + 1, n - 1), jnp.maximum(z - 1, 0)
        ahead = {"tensor": up if h == 0 else down}
        back = {"tensor": down if h == 0 else up}
        fwd = remote(self.pbuf.at[rows], self.rbuf.at[rows], self.rs.at[h, i], self.rr.at[h, i], ahead)
        ret = remote(self.obuf.at[orows], self.obuf.at[orows], self.bs.at[h, i], self.br.at[h, i], back)
        return rows, orows, place, fwd, ret

    def reduce_step(self, h, i):
        rows, orows, place, fwd, ret = self.pieces(h, i)
        n = self.n

        @pl.when(place == 0)
        def _():
            fwd.start()

        @pl.when(place > 0)
        def _():
            fwd.wait_recv()
            total = (self.rbuf[rows, :].astype(F32) + self.pbuf[rows, :].astype(F32)).astype(BF)

            @pl.when(place < n - 1)
            def _():
                self.pbuf[rows, :] = total
                fwd.start()

            @pl.when(place == n - 1)
            def _():
                self.obuf[orows, :] = total
                ret.start()

    def spread_step(self, h, i):
        rows, orows, place, fwd, ret = self.pieces(h, i)

        @pl.when(place < self.n - 1)
        def _():
            ret.wait_recv()

        @pl.when((place < self.n - 1) & (place > 0))
        def _():
            ret.start()

    def serve(self, t):
        n = self.n
        z = lax.axis_index("tensor")
        for h in range(2):
            place = z if h == 0 else n - 1 - z
            i = t - place * self.hop

            @pl.when((i >= 0) & (i < self.count))
            def _():
                self.reduce_step(h, i)

            j = t - (2 * (n - 1) - place) * self.hop

            @pl.when((j >= 0) & (j < self.count))
            def _():
                self.spread_step(h, j)

    def sent(self, job, fwd=True, ret=False):
        def step(i, _):
            for h in range(2):
                rows, orows, place, f, r = self.pieces(h, job * self.per + i)
                if fwd:

                    @pl.when(place < self.n - 1)
                    def _():
                        f.wait_send()

                if ret:

                    @pl.when(place > 0)
                    def _():
                        r.wait_send()

            return 0

        lax.fori_loop(0, self.per, step, 0)


def run_items(items, serve):
    total = max(e for spans, _ in items for _, e in spans)

    def step(k, _):
        for spans, body in items:
            hit = functools.reduce(jnp.logical_or, [(k >= lo) & (k < hi) for lo, hi in spans])
            pl.when(hit)(functools.partial(body, k))
        serve(k)
        return 0

    lax.fori_loop(0, total, step, 0)


class Square:
    def __init__(self, rows, cols, src, mine, theirs, spare, out, credit, shard_send, shard_recv, send, recv, store):
        self.src, self.mine, self.theirs, self.res, self.out = src, mine, theirs, theirs, out
        self.r1, self.r2 = [spare[0:2], spare[2:4]], spare[4:6]
        self.credit, self.shard_sems, self.shard_recv, self.send, self.recv, self.store_sem = credit, shard_send, shard_recv, send, recv, store
        self.rows, self.qr, self.cols = rows, rows // 4, cols
        c = lax.axis_index("context")
        self.cy, self.cx = c // 2, lax.rem(c, 2)

    def at(self, y, x, half):
        w = self.cols // 2
        return (pl.ds(pl.multiple_of((2 * y + x) * self.qr, self.qr), self.qr), pl.ds(half * w, w))

    def peer(self, half, first):
        if (half == 0) == first:
            return {"context": 2 * self.cy + 1 - self.cx}
        return {"context": 2 * (1 - self.cy) + self.cx}

    def shard_copy(self):
        return remote(self.src, self.theirs, self.shard_sems, self.shard_recv, {"shard": 1 - lax.axis_index("shard")})

    def outer(self, half):
        if half == 0:
            return [(y, 1 - self.cx) for y in range(2)], [(y, self.cx) for y in range(2)]
        return [(1 - self.cy, x) for x in range(2)], [(self.cy, x) for x in range(2)]

    def p1(self, half, j):
        return remote(self.mine.at[self.at(*self.outer(half)[0][j], half)], self.r1[half][j],
                      self.send.at[0, half, j], self.recv.at[0, half, j], self.peer(half, True))

    def p2(self, half):
        q = (1 - self.cy, self.cx) if half == 0 else (self.cy, 1 - self.cx)
        return remote(self.mine.at[self.at(*q, half)], self.r2[half],
                      self.send.at[1, half, 0], self.recv.at[1, half, 0], self.peer(half, False))

    def p3(self, half):
        at = self.at(self.cy, self.cx, half)
        return remote(self.res.at[at], self.res.at[at], self.send.at[1, half, 1], self.recv.at[1, half, 1], self.peer(half, False))

    def p4(self, half, j):
        at = self.at(*self.outer(half)[1][j], half)
        return remote(self.res.at[at], self.res.at[at], self.send.at[2, half, j], self.recv.at[2, half, j], self.peer(half, True))

    def free(self):
        for t in ({"shard": 1 - lax.axis_index("shard")}, self.peer(0, True), self.peer(0, False)):
            pl.semaphore_signal(self.credit, inc=1, device_id=t, device_id_type=MESH)

    def e0(self):
        pl.semaphore_wait(self.credit, 3)
        self.shard_copy().start()

    def e1(self):
        self.shard_copy().wait_recv()
        step = self.qr

        def add(i, _):
            rows = pl.ds(pl.multiple_of(i * step, step), step)
            self.mine[rows, :] = (self.mine[rows, :].astype(F32) + self.theirs[rows, :].astype(F32)).astype(BF)
            return 0

        lax.fori_loop(0, self.rows // step, add, 0)
        for j in range(2):
            for half in range(2):
                self.p1(half, j).start()

    def e2(self):
        for half in range(2):
            for j in range(2):
                self.p1(half, j).wait_recv()
                at = self.at(*self.outer(half)[1][j], half)
                self.mine[at] = (self.mine[at].astype(F32) + self.r1[half][j][...].astype(F32)).astype(BF)
            self.p2(half).start()

    def e3(self):
        for half in range(2):
            self.p2(half).wait_recv()
            at = self.at(self.cy, self.cx, half)
            self.res[at] = (self.mine[at].astype(F32) + self.r2[half][...].astype(F32)).astype(BF)
            self.p3(half).start()

    def e4(self):
        for half in range(2):
            self.p3(half).wait_recv()
            for j in range(2):
                self.p4(half, j).start()

    def e5(self):
        for half in range(2):
            for j in range(2):
                self.p4(half, j).wait_recv()

    def store(self):
        return pltpu.make_async_copy(self.res, self.out, self.store_sem)

    def done(self):
        self.shard_copy().wait_send()
        for half in range(2):
            for j in range(2):
                self.p1(half, j).wait_send()
                self.p4(half, j).wait_send()
            self.p2(half).wait_send()
            self.p3(half).wait_send()


def line_barrier(n, peers=()):
    z = lax.axis_index("tensor")
    bar = pltpu.get_barrier_semaphore()
    for t in peers:
        pl.semaphore_signal(bar, inc=1, device_id=t, device_id_type=MESH)

    @pl.when(z > 0)
    def _():
        pl.semaphore_signal(bar, inc=1, device_id={"tensor": jnp.maximum(z - 1, 0)}, device_id_type=MESH)

    @pl.when(z < n - 1)
    def _():
        pl.semaphore_signal(bar, inc=1, device_id={"tensor": jnp.minimum(z + 1, n - 1)}, device_id_type=MESH)

    pl.semaphore_wait(bar, len(peers) + jnp.minimum(z, 1) + jnp.minimum(n - 1 - z, 1))


def main_kernel(n, nc, chunk, kbase, qlim, cb_ref, sb_ref, cj_ref, sj_ref, gf_ref, q_ref, kvc_ref, wo_ref,
                kvp_h, xp_h, dyp_h, wg_h, wu_h, wd_h, n1_h, wp_h,
                out_h, tg_h, gg_h, gu_h, gd_h, go_h, gw_h, dm_h, gds_h, fp_h, gains_ref,
                k_s, v_s, s_s, o_v, op_v, lse_v, xs, ys, pbuf, rbuf, obuf, wd, n2, wg, wu, hid, dg, du, gt,
                dk_s, dv_s, do_v, dq_s, delta_s, dqp, dkv_s, go_v, st_o, st_t, st_p, gpart, grecv,
                lsem, ksem, osem, fsem, msem, nsem, qsend, qrecv, gs, gr, rs, rr, bs, br, credits, shard_send, shard_recv, send, recv, store):
    s = lax.axis_index("shard")
    c = lax.axis_index("context")
    rows_here, d = xs.shape
    runs = rows_here // RUN
    per = runs // 2
    half = rows_here // 2
    hk = k_s.shape[0]
    hq = q_ref.shape[1] // PAD
    rep = hq // hk
    blocks = k_s.shape[1] // RUN
    ff = wg.shape[1]
    dh = d // 2
    nq, nk = hq * PAD, hk * PAD
    score = 1.0 / math.sqrt(HEAD_SIZE)
    scale = LOG2E * score
    own = pl.ds(pl.multiple_of(s * dh, dh), dh)
    yours = pl.ds(pl.multiple_of((1 - s) * dh, dh), dh)
    wide = 2 * hk * HEAD_SIZE

    def at(i, size=RUN):
        return pl.ds(pl.multiple_of(i * size, size), size)

    kv_in = [dg.at[pl.ds((b % 4) * RUN, RUN), pl.ds(b // 4 * wide, wide)] for b in range(blocks)]
    key_loads = [pltpu.make_async_copy(kvp_h.at[pl.ds(b * RUN, RUN)], kv_in[b], ksem.at[b]) for b in range(blocks)]
    for cp in key_loads:
        cp.start()
    pairs = [(xp_h, xs), (wg_h, wg), (wu_h, wu), (dyp_h, ys), (wd_h, wd)]
    loads = [pltpu.make_async_copy(a, b, lsem.at[i]) for i, (a, b) in enumerate(pairs)]
    for cp in loads:
        cp.start()
    peers = [{"shard": lax.rem(s + i // nc, 2), "context": lax.rem(c + lax.rem(i, nc), nc)} for i in range(1, 2 * nc)]
    line_barrier(n, peers)
    line = Line(n, chunk, pbuf, rbuf, obuf, (rs, rr, bs, br))
    a_of = lambda job: at(job)
    b_of = lambda job: at(runs + job)
    lane = iota((RUN, PAD), 1)
    for b in range(blocks):
        key_loads[b].wait()
        kv = mm(kv_in[b][...], pad_matrix(2 * hk))
        rows = pl.ds(b * RUN, RUN)
        for g in range(hk):
            k_s[g, rows, :] = kv[:, g * PAD : (g + 1) * PAD].astype(BF)
            v_s[g, rows, :] = jnp.where(lane == 48, 1.0, kv[:, (hk + g) * PAD : (hk + g + 1) * PAD]).astype(BF)
    dk_s[...] = jnp.zeros_like(dk_s)
    dv_s[...] = jnp.zeros_like(dv_s)
    gpart[...] = jnp.zeros_like(gpart)

    def across(total, width, body):
        def step(i, _):
            body(at(i, width))
            return 0

        lax.fori_loop(0, total // width, step, 0)

    def down_rows(start, count, size, body):
        def step(i, _):
            body(pl.ds(pl.multiple_of(start + i * size, size), size), pl.ds(pl.multiple_of(i * size, size), size))
            return 0

        lax.fori_loop(0, count // size, step, 0)

    def head(k, mixed):
        job, h = k // hq, lax.rem(k, hq)
        run = job + per if mixed else job - per
        diff = iota((RUN, RUN), 1) - iota((RUN, RUN), 0)
        rows, cols = at(run), at(h, PAD)
        g = h // rep
        q = q_ref[rows, cols]
        lim = qlim[run]
        top = None
        for b in range(blocks):
            t = mm_nt(q, k_s[g, pl.ds(b * RUN, RUN), :]) * scale
            room = lim - kbase[b]
            if mixed:
                t = t + jnp.where(room >= 0, 0.0, NEG)
            else:
                t = jnp.where(diff <= room, t, NEG)
            s_s[:, b * RUN : (b + 1) * RUN] = t
            top = t if top is None else jnp.maximum(top, t)
        if mixed:
            crow = at(run - per)
            kc = kvc_ref[crow, at(g, PAD)]
            vc = kvc_ref[crow, at(hk + g, PAD)]
            vc = jnp.where(lane == 48, 1.0, vc.astype(F32)).astype(BF)
            t = jnp.where(diff <= 0, mm_nt(q, kc) * scale, NEG)
            s_s[:, blocks * RUN :] = t
            top = jnp.maximum(top, t)
        m = jnp.max(top, axis=1, keepdims=True)
        acc = None
        for b in range(blocks):
            p = jnp.exp2(s_s[:, b * RUN : (b + 1) * RUN] - m).astype(BF)
            o = mm(p, v_s[g, pl.ds(b * RUN, RUN), :])
            acc = o if acc is None else acc + o
        if mixed:
            p = jnp.exp2(s_s[:, blocks * RUN :] - m).astype(BF)
            acc = acc + mm(p, vc)
        total = acc[:, 48:49]
        op_v[rows, cols] = (acc / total).astype(BF)
        lse = jnp.broadcast_to(m + jnp.log2(total), (RUN, PAD)).T
        lse_v[at(run * hq + h, 8), :] = lse[0:8, :]

        @pl.when(h == hq - 1)
        def _():
            o = mm_nt(op_v[rows, :], pad_matrix(hq)).astype(BF)
            o_v[rows, :] = o


            def out(cols):
                pbuf[at(job), cols] = mm(o, wo_ref[:, cols]).astype(BF)

            across(d, 512, out)

    first = runs * hq

    def ffn(k):
        job = (k - first) // 4
        part = lax.rem(k - first, 4)
        run = lax.rem(job + per, runs)
        rows = at(run)

        @pl.when(k == first)
        def _():
            for cp in loads:
                cp.wait()

        @pl.when(part == 0)
        def _():
            def norm(to, sub):
                srows = pl.ds(pl.multiple_of(job * RUN + sub.start, 32), 32)
                mid = xs[to, :].astype(F32) + obuf[srows, :].astype(F32)
                r = lax.rsqrt(jnp.mean(mid * mid, axis=-1, keepdims=True) + norm_eps)
                n2[to, :] = (mid * r * gf_ref[8:9, :]).astype(BF)

            down_rows(run * RUN, RUN, 32, norm)

            def gate(cols):
                s_s[:, cols] = mm(n2[rows, :], wg[:, cols])

            across(ff, 512, gate)

        @pl.when(part == 1)
        def _():
            def up(i, _):
                s_s[:, pl.ds(pl.multiple_of(ff + i * 512, 512), 512)] = mm(n2[rows, :], wu[:, at(i, 512)])
                return 0

            lax.fori_loop(0, ff // 512, up, 0)

        @pl.when(part == 2)
        def _():
            def gated(i, _):
                cols = at(i)
                dhid = mm_nt(ys[rows, :], wd[cols, :])
                gate, up = s_s[:, cols], s_s[:, pl.ds(pl.multiple_of(ff + i * RUN, RUN), RUN)]
                sig = jax.nn.sigmoid(gate)
                silu = gate * sig
                hid[rows, cols] = (silu * up).astype(BF)
                dg[rows, cols] = (dhid * up * sig * (1.0 + gate * (1.0 - sig))).astype(BF)
                du[rows, cols] = (dhid * silu).astype(BF)
                return 0

            lax.fori_loop(0, ff // RUN, gated, 0)

        @pl.when(part == 3)
        def _():
            line.sent(job)

            def normed_two(cols):
                pbuf[at(job), cols] = (mm_nt(dg[rows, :], wg[cols, :]) + mm_nt(du[rows, :], wu[cols, :])).astype(BF)

            across(d, 512, normed_two)
            cp = pltpu.make_async_copy(st_o, fp_h.at[at(job)], osem.at[0])

            @pl.when(job > 0)
            def _():
                cp.wait()

            def project(cols):
                st_o[:, cols] = mm(hid[rows, :], wd[:, cols]).astype(BF)

            across(d, 512, project)
            cp.start()

    second = first + 4 * runs

    def stage(st, sem, dst, value, busy=True):
        cp = pltpu.make_async_copy(st, dst, sem)
        if busy is True:
            cp.wait()
        else:
            pl.when(busy)(cp.wait)

        def fill(cols):
            st[:, cols] = value(cols)

        across(d, 512, fill)
        cp.start()

    def grads_down(k):
        i = k - second
        for j in range(2):
            cols = at(2 * i + j)
            ht = hid[:, cols].T
            stage(st_o, osem.at[0], gds_h.at[cols], lambda to: mm(ht, ys[:, to]).astype(BF))

    def grads_up(k):
        i = k - second - 2
        for j in range(2):
            cols = at(2 * i + j)
            nt = n2[:, cols].T


            def both(to):
                wg[cols, to] = mm(nt, dg[:, to]).astype(BF)
                wu[cols, to] = mm(nt, du[:, to]).astype(BF)

            across(ff, 512, both)

    back = second + 5

    def middle(k):
        job = (k - back) // 5
        run = lax.rem(job + per, runs)
        rows = at(run)
        cp = pltpu.make_async_copy(s_s.at[:, pl.ds(0, d)], dm_h.at[rows], osem.at[1])

        @pl.when(job > 0)
        def _():
            cp.wait()

        def one(to, sub):
            def there(base):
                return pl.ds(pl.multiple_of(base + sub.start, 32), 32)

            mid = xs[to, :].astype(F32) + obuf[there(job * RUN), :].astype(F32)
            r = lax.rsqrt(jnp.mean(mid * mid, axis=-1, keepdims=True) + norm_eps)
            dn = obuf[there((runs + job) * RUN), :].astype(F32)
            w = gf_ref[8:9, :] * dn
            inner = jnp.mean(w * mid, axis=-1, keepdims=True)
            dm = ys[to, :].astype(F32) + r * w - mid * (r * r * r) * inner
            s_s[sub, 0:d] = dm
            gpart[8:16, :] += jnp.sum((dn * mid * r).reshape(4, 8, d), axis=0)
            ys[to, :] = dm.astype(BF)

        down_rows(run * RUN, RUN, 32, one)
        cp.start()
        do = mm_nt(ys[rows, :], wo_ref[...]).astype(BF)
        do_v[rows, :] = mm(do, pad_matrix(hq)).astype(BF)

    width = rep * RUN

    def pair(k, mixed):
        job = (k - back) // 5
        idx = lax.rem(k - back, 5) - 1
        g, part = idx // 2, lax.rem(idx, 2)
        run = lax.rem(job + per, runs)
        rows = at(run)
        diff = iota((RUN, width), 0) - (iota((RUN, width), 1) & (RUN - 1))

        def stack(ref):
            return jnp.concatenate([ref[rows, at(g * rep + j, PAD)] for j in range(rep)], axis=0)

        q, do = stack(q_ref), stack(do_v)

        @pl.when(part == 0)
        def _():
            op = stack(op_v)
            delta_s[0:1, :] = jnp.sum((do.astype(F32) * op.astype(F32)).T, axis=0, keepdims=True)
            dq_s[...] = jnp.zeros_like(dq_s)

        delta = delta_s[0:1, :]
        lse = jnp.concatenate(
            [lse_v[pl.ds(pl.multiple_of((run * hq + g * rep + j) * 8, 8), 1), :] for j in range(rep)], axis=1
        )
        lim = qlim[run]

        def tile(kk, vv, hide):
            p = jnp.exp2(hide(mm_nt(kk, q) * scale - lse))
            ds = (p * (mm_nt(vv, do) - delta)).astype(BF)
            return mm(ds, q), mm(p.astype(BF), do), mm_tn(ds, kk)

        dq = dq_s[...]
        for bb in range(blocks // 2):
            b = part * (blocks // 2) + bb
            room = lim - kbase[b]
            if mixed:
                hide = lambda t: t + jnp.where(room >= 0, 0.0, NEG)
            else:
                hide = lambda t: jnp.where(diff <= room, t, NEG)
            dk, dv, dd = tile(k_s[g, at(b), :], v_s[g, at(b), :], hide)
            dk_s[g, at(b), :] += dk
            dv_s[g, at(b), :] += dv
            dq = dq + dd
        dq_s[...] = dq

        @pl.when(part == 1)
        def _():
            total = dq_s[...]
            ct, st = rope_tables(run, cb_ref, sb_ref, cj_ref, sj_ref)
            if mixed:
                crow = at(run - per)
                dk, dv, dd = tile(kvc_ref[crow, at(g, PAD)], kvc_ref[crow, at(hk + g, PAD)], lambda t: jnp.where(diff <= 0, t, NEG))
                total = total + dd
                dkv_s[rows, at(g, PAD)] = rope_back(dk * score, ct, st).astype(BF)
                dkv_s[rows, at(hk + g, PAD)] = dv.astype(BF)
            for j in range(rep):
                dqp[rows, at(g * rep + j, PAD)] = rope_back(total[j * RUN : (j + 1) * RUN] * score, ct, st).astype(BF)

    def spare(ref, r0, c0, rows, cols, across, count):
        return [ref.at[pl.ds(r0 + i // across * rows, rows), pl.ds(c0 + i % across * cols, cols)] for i in range(count)]

    def square(i, rows, cols, src, mine, theirs, views, out):
        return Square(rows, cols, src, mine, theirs, views, out, credits.at[i], shard_send.at[i], shard_recv.at[i], send.at[i], recv.at[i], store.at[i])

    q4, w4 = dh // 4, ff // 2
    sq_g = square(0, dh, ff, wg.at[yours], wg.at[own], dg.at[pl.ds(0, dh)], spare(n2, 0, 0, q4, w4, 2, 6), gg_h)
    left = spare(n2, 0, 2 * w4, q4, w4, 1, 3) + spare(n2, 3 * q4, 0, q4, w4, 3, 3)
    sq_u = square(1, dh, ff, wu.at[yours], wu.at[own], du.at[pl.ds(0, dh)], left, gu_h)
    f4, d4 = ff // 4, dh // 2
    sq_d = square(2, ff, dh, gds_h.at[:, yours], hid.at[:, pl.ds(0, dh)], gt,
                  spare(n2, dh, 0, f4, d4, 4, 4) + spare(dg, dh, 0, f4, d4, 2, 2), gd_h)
    dq_cols = hq * HEAD_SIZE
    sq_o = square(3, dq_cols, dh, go_v.at[1 - s], go_v.at[s], wg.at[pl.ds(0, dq_cols), pl.ds(0, dh)],
                  spare(wg, dq_cols, 0, dq_cols // 4, d4, 2, 6), go_h)
    gw_cols = dq_cols + wide
    sq_w = square(4, dh, gw_cols, wu.at[yours, pl.ds(0, gw_cols)], wu.at[own, pl.ds(0, gw_cols)], hid.at[pl.ds(0, dh), pl.ds(0, gw_cols)],
                  spare(gt, 0, 0, q4, gw_cols // 2, 2, 6), gw_h)
    down_load = pltpu.make_async_copy(gds_h.at[:, own], hid.at[:, pl.ds(0, dh)], lsem.at[5])
    wp_load = pltpu.make_async_copy(wp_h, wd, lsem.at[6])

    def f_load(job):
        return pltpu.make_async_copy(fp_h.at[at(job)], pbuf.at[at(job)], fsem.at[job])

    def f_start(job):
        line.sent(4 + job)
        f_load(job).start()

    def key_piece(b):
        return ys.at[pl.ds(pl.multiple_of(lax.rem(b, 4) * RUN, RUN), RUN), pl.ds(pl.multiple_of(b // 4 * wide, wide), wide)]

    def key_recv(i, run):
        m = (i - 1) * per + run
        return ys.at[pl.ds(m % 4 * RUN, RUN), pl.ds(dh + m // 4 * wide, wide)]

    def key_copy(i, run):
        to = lax.rem(c + i, nc)
        return remote(key_piece(to * per + run), key_recv(i, run), qsend.at[i, run], qrecv.at[i, run], {"context": to})

    def grad_out(j):
        ot = o_v[...].T

        def part(cols):
            go_v[j, :, cols] = mm(ot, ys[:, pl.ds(pl.multiple_of(j * dh + cols.start, RUN), RUN)]).astype(BF)

        across(dh, RUN, part)

    def pack():
        for i in range(1, nc):
            pl.semaphore_signal(credits.at[5], inc=1, device_id={"context": lax.rem(c + i, nc)}, device_id_type=MESH)

        def one(b, _):
            rows = at(b)
            parts = [(dk_s[g, rows, :] * score).astype(BF) for g in range(hk)]
            parts += [dv_s[g, rows, :].astype(BF) for g in range(hk)]
            value = mm_nt(jnp.concatenate(parts, axis=1), pad_matrix(2 * hk)).astype(BF)
            key_piece(b)[...] = value
            return 0

        lax.fori_loop(0, blocks, one, 0)
        pl.semaphore_wait(credits.at[5], nc - 1)
        for run in range(per):
            for i in range(1, nc):
                key_copy(i, run).start()

    def normed(job):
        rows = at(lax.rem(job + per, runs))
        line.sent(8 + job + jnp.where(job == 3, 1, 0))
        line.sent(4 + job, fwd=False, ret=True)

        def part(cols):
            dn = mm(dqp[rows, :], wd[0:nq, cols]) + mm(dkv_s[rows, :], wd[nq:, cols])
            pbuf[at(job), cols] = dn.astype(BF)

        across(d, 512, part)

    def keys(run):
        for i in range(1, nc):
            key_copy(i, run).wait_recv()
        selkv = pad_matrix(2 * hk)
        rows = pl.ds(run * RUN, RUN)
        total = mm(key_piece(c * per + run)[...], selkv)
        for i in range(1, nc):
            total = total + mm(key_recv(i, run)[...], selkv)
        ct, st = rope_tables(run, cb_ref, sb_ref, cj_ref, sj_ref)
        for g in range(hk):
            dkv_s[rows, g * PAD : (g + 1) * PAD] = rope_back(total[:, g * PAD : (g + 1) * PAD], ct, st).astype(BF)
        dkv_s[rows, hk * PAD :] = total[:, hk * PAD :].astype(BF)

    tile_v = hid.at[:, pl.ds(dh, RUN)]

    def tile_load(i):
        return pltpu.make_async_copy(n1_h.at[:, at(i)], tile_v, nsem)

    def grads_in(k):
        i = k - into

        @pl.when(i == 0)
        def _():
            def pack_rows(to, sub):
                du[to, 0:dq_cols] = mm_nt(dqp[to, :], pad_matrix(hq)).astype(BF)
                du[to, dq_cols:gw_cols] = mm_nt(dkv_s[to, :], pad_matrix(2 * hk)).astype(BF)

            down_rows(0, rows_here, RUN, pack_rows)

        for j in range(2):
            tile_load(2 * i + j).wait()
            nt = tile_v[...].T


            def part(cols, j=j):
                wu[at(2 * i + j), cols] = mm(nt, du[:, cols]).astype(BF)

            across(gw_cols, gw_cols // 2, part)

            @pl.when(2 * i + j + 1 < d // RUN)
            def _():
                tile_load(2 * i + j + 1).start()

    def halves(i, body):
        for j in range(2):

            def step(m, _, j=j):
                natural = pl.ds(pl.multiple_of(j * half + i * 128 + m * 32, 32), 32)
                by_job = lambda part: pl.ds(pl.multiple_of(part * rows_here + (1 - j) * half + i * 128 + m * 32, 32), 32)
                body(natural, by_job, pl.ds(pl.multiple_of(j * 128 + m * 32, 32), 32))
                return 0

            lax.fori_loop(0, 4, step, 0)

    def output(k):
        i = k - outs

        def one(natural, by_job, to):
            total = xs[natural, :].astype(F32) + obuf[by_job(0), :].astype(F32)
            st_p[to, :] = (total + obuf[by_job(2), :].astype(F32)).astype(BF)

        halves(i, one)
        stage(st_o, osem.at[0], out_h.at[at(i)], lambda cols: mm(merge_matrix(), st_p[:, cols]).astype(BF), i > 0)

    def m_load(i, j):
        src = dm_h.at[pl.ds(pl.multiple_of(j * half + i * 128, 128), 128)]
        return pltpu.make_async_copy(src, s_s.at[pl.ds(j * 128, 128), pl.ds(0, d)], msem.at[j])

    def finals(i):
        for j in range(2):
            m_load(i, j).wait()

        def one(natural, by_job, to):
            x = xs[natural, :].astype(F32)
            dn = obuf[by_job(1), :].astype(F32)
            r = lax.rsqrt(jnp.mean(x * x, axis=-1, keepdims=True) + norm_eps)
            w = gf_ref[0:1, :] * dn
            inner = jnp.mean(w * x, axis=-1, keepdims=True)
            st_p[to, :] = (s_s[to, 0:d] + (r * w - x * (r * r * r) * inner)).astype(BF)
            gpart[0:8, :] += jnp.sum((dn * x * r).reshape(4, 8, d), axis=0)

        halves(i, one)

        @pl.when(i + 1 < runs)
        def _():
            for j in range(2):
                m_load(i + 1, j).start()

        cp = pltpu.make_async_copy(st_t, tg_h.at[at(i)], osem.at[2])

        @pl.when(i > 0)
        def _():
            cp.wait()

        def fill(cols):
            st_t[:, cols] = mm(merge_matrix(), st_p[:, cols]).astype(BF)

        across(d, 512, fill)
        cp.start()

    packed = back + 5 * runs
    into = packed + 4
    outs = into + 4
    lag = hq - 1

    def due(job):
        return (line.per * (job + 1) - 1 + line.turn) // line.ticks + lag + 1

    begins = [back + 5 * job for job in range(runs)]
    items = [([(0, per * hq)], lambda k: head(k, True)), ([(per * hq, first)], lambda k: head(k, False)), ([(first, second)], ffn),
             ([(second, second + 2)], grads_down), ([(second + 2, back)], grads_up), ([(b, b + 1) for b in begins], middle),
             ([(b + 1, b + 5) for b in begins[:per]], lambda k: pair(k, True)),
             ([(b + 1, b + 5) for b in begins[per:]], lambda k: pair(k, False)),
             ([(into, into + 3)], grads_in), ([(outs, outs + runs)], output)]
    fin = due(Line.D_AT[per])

    def begin_down():
        pltpu.make_async_copy(st_o, gds_h.at[pl.ds(0, RUN)], osem.at[0]).wait()
        down_load.start()
        wp_load.start()

    def free_three():
        for sq in (sq_g, sq_u, sq_d):
            sq.free()
        for sq in (sq_d, sq_g, sq_u):
            sq.e0()

    def store_start(sq):
        def body():
            sq.e5()
            sq.store().start()

        return body

    def dm_begin():
        pltpu.make_async_copy(s_s.at[:, pl.ds(0, d)], dm_h.at[pl.ds(0, RUN)], osem.at[1]).wait()
        for j in range(2):
            m_load(0, j).start()

    def first_e1():
        down_load.wait()
        sq_d.e1()

    def give_o():
        sq_g.store().wait()
        sq_g.done()
        sq_o.free()

    def give_w():
        sq_d.store().wait()
        sq_d.done()
        sq_w.free()

    def release_u():
        sq_u.store().wait()
        sq_u.done()

    def number(k, steps):
        return sum(jnp.where(k >= step, 1, 0) for step in steps[1:])

    events = [(second + 2, begin_down), (second + 4, free_three)]
    at_f = [4 * Line.F_AT[job] + lag - 2 for job in range(runs)]
    events += [
        (38, first_e1), (40, sq_g.e1), (41, sq_d.e2), (42, sq_u.e1), (43, sq_g.e2), (44, sq_d.e3), (45, wp_load.wait), (46, sq_u.e2), (47, sq_g.e3),
        (48, sq_d.e4), (49, sq_u.e3), (50, sq_g.e4), (52, store_start(sq_d)), (53, sq_u.e4), (54, give_w), (55, store_start(sq_g)),
        (57, store_start(sq_u)), (57, give_o), (59, release_u),
        (53, lambda: grad_out(0)), (54, lambda: grad_out(1)), (packed, pack), (packed, lambda: tile_load(0).start()), (packed, dm_begin), (packed + 2, lambda: keys(0)), (packed + 2, sq_o.e0), (packed + 3, lambda: keys(1)),
        (61, sq_o.e1), (63, sq_o.e2), (64, sq_w.e0), (65, sq_w.e1), (65, sq_o.e3), (67, sq_w.e2), (67, sq_o.e4), (68, sq_w.e3),
        (69, store_start(sq_o)), (70, sq_w.e4), (73, store_start(sq_w)),
    ]
    items += [([(k, k + 1)], functools.partial(lambda e, k: e(), e)) for k, e in events]
    at_normed = (45, 50, packed + 2, packed + 4)
    items.append(([(k, k + 1) for k in at_f], lambda k: f_start(number(k, at_f))))
    items.append(([(k + 1, k + 2) for k in at_f], lambda k: f_load(number(k, at_f)).wait()))
    items.append(([(k, k + 1) for k in at_normed], lambda k: normed(number(k, at_normed))))
    end = -(-line.slots // line.ticks) + lag
    items.append(([(fin, fin + 2), (end, end + 2)], lambda k: finals(jnp.where(k < end, k - fin, k - end + 2))))

    def serve(k):
        def tick(j, _):
            line.serve(line.ticks * (k - lag) + j)
            return 0

        lax.fori_loop(0, line.ticks, tick, 0)

    run_items(items, serve)
    me = s * nc + c
    sums = jnp.concatenate(
        [jnp.broadcast_to(jnp.sum(gpart[k * 8 : (k + 1) * 8, :], axis=0, keepdims=True), (8, d)) for k in range(2)], axis=0
    )
    grecv[me] = sums
    gcopies = []
    for i, t in enumerate(peers):
        cp = remote(grecv.at[me], grecv.at[me], gs.at[i], gr.at[i], t)
        cp.start()
        gcopies.append(cp)

    def rest(job, _):
        line.sent(jnp.where(job < runs, job, job + runs), fwd=False, ret=True)
        return 0

    lax.fori_loop(0, 3 * runs, rest, 0)
    for job in Line.D_AT:
        line.sent(job)
    for sq in (sq_o, sq_w):
        sq.store().wait()
        sq.done()
    for i in range(1, nc):
        for run in range(per):
            key_copy(i, run).wait_send()
    pltpu.make_async_copy(st_o, out_h.at[pl.ds(0, RUN)], osem.at[0]).wait()
    pltpu.make_async_copy(st_t, tg_h.at[pl.ds(0, RUN)], osem.at[2]).wait()
    for cp in gcopies:
        cp.wait()
    total = grecv[0]
    for i in range(1, 2 * nc):
        total = total + grecv[i]
    gpart[...] = total
    gains_ref[...] = gpart[:, own]


def finish_kernel(out_h, tg_h, gw_h, go_h, gg_h, gu_h, gd_h, out_f, tg_f, gq_f, gk_f, gv_f, go_f, gg_f, gu_f, gd_f,
                  out_v, tg_v, gw_v, go_v, gg_v, gu_v, gd_v, q_v, kv_v, o_v, g_v, u_v, d_v, lsem, ssem):
    kw = gk_f.shape[0]
    nq = gw_h.shape[1] - 2 * kw
    pairs = [(gg_h, gg_v), (gu_h, gu_v), (gd_h, gd_v), (gw_h, gw_v), (go_h, go_v), (out_h, out_v), (tg_h, tg_v)]
    loads = [pltpu.make_async_copy(a, b, lsem.at[i]) for i, (a, b) in enumerate(pairs)]
    for cp in loads:
        cp.start()
    stores = [
        pltpu.make_async_copy(a, b, ssem.at[i])
        for i, (a, b) in enumerate([(g_v, gg_f), (u_v, gu_f), (d_v, gd_f), (q_v, gq_f), (kv_v.at[0:kw], gk_f), (kv_v.at[kw:], gv_f),
                                    (o_v, go_f), (out_v, out_f), (tg_v, tg_f)])
    ]

    def widen(src, dst, width):
        def step(i, _):
            rows = pl.ds(pl.multiple_of(i * 32, 32), 32)
            dst[rows, :] = src[rows, 0:width].astype(F32)
            return 0

        lax.fori_loop(0, src.shape[0] // 32, step, 0)

    for i, (src, dst) in enumerate([(gg_v, g_v), (gu_v, u_v), (gd_v, d_v)]):
        loads[i].wait()
        widen(src, dst, src.shape[1])
        stores[i].start()
    loads[5].wait()
    stores[7].start()
    loads[6].wait()
    stores[8].start()
    loads[3].wait()
    widen(gw_v, q_v, nq)
    stores[3].start()
    for i in range(gw_v.shape[0] // PAD):
        kv_v[:, i * PAD : (i + 1) * PAD] = gw_v[i * PAD : (i + 1) * PAD, nq:].astype(F32).T
    stores[4].start()
    stores[5].start()
    loads[4].wait()
    widen(go_v, o_v, go_v.shape[1])
    stores[6].start()
    for cp in stores:
        cp.wait()


def fast(
    tokens, w_query, key_weight, value_weight, w_out, w_gate, w_up, w_down, gain_attn, gain_ffn, segments, positions, cotangent, n, nc
):
    _, rows, d = tokens.shape
    half = rows // 2
    runs = rows // RUN
    per = runs // 2
    prompt = segments.shape[1] // 2
    blocks = prompt // RUN
    dq, dk = w_query.shape[1], key_weight.shape[1]
    hq, hk = dq // HEAD_SIZE, dk // HEAD_SIZE
    nq, nk = hq * PAD, hk * PAD
    ff = w_gate.shape[1]
    dh = d // 2
    c = lax.axis_index("context")
    x = tokens.reshape(rows, d)
    dy = cotangent.reshape(rows, d)
    kbase = positions[0, 0 :: 2 * RUN]
    seg_here = lax.dynamic_slice_in_dim(segments[0], c * rows, rows, 0)
    pos_here = lax.dynamic_slice_in_dim(positions[0], c * rows, rows, 0)
    qbase = jnp.concatenate([pos_here[0 :: 2 * RUN], pos_here[1 :: 2 * RUN]])
    qlim = jnp.concatenate([pos_here[0 :: 2 * RUN], seg_here[1 :: 2 * RUN] * CLEN - 1])
    freq = np.exp(np.arange(HEAD_SIZE // 2, dtype=np.float32) * np.float32(-2.0 * math.log(rope_base) / HEAD_SIZE)).astype(np.float32)
    lanes = np.zeros((PAD,), np.float32)
    lanes[0:48] = freq
    lanes[64:112] = freq
    sign = np.where(np.arange(PAD) < 64, -1.0, 1.0).astype(np.float32)
    inner = np.arange(RUN, dtype=np.float64)[:, None] * lanes[None, :].astype(np.float64)
    cj = jnp.asarray(np.cos(inner).astype(np.float32))
    sj = jnp.asarray((np.sin(inner) * sign).astype(np.float32))
    angle = qbase.astype(F32)[:, None] * jnp.asarray(lanes)[None, :]
    cb = jnp.cos(angle)
    sb = jnp.sin(angle) * jnp.asarray(sign)[None, :]
    gains = jnp.stack([gain_attn, gain_ffn]).astype(F32)

    V = pl.BlockSpec(memory_space=pltpu.VMEM)
    S = pl.BlockSpec(memory_space=pltpu.SMEM)
    A = pl.BlockSpec(memory_space=pl.ANY)
    sds = jax.ShapeDtypeStruct
    DMA = pltpu.SemaphoreType.DMA

    def call(kernel, ins, outs, scratch, collective=None, flops=0):
        params = dict(vmem_limit_bytes=VLIM - 64 * 1024)
        if collective is not None:
            params.update(collective_id=collective, has_side_effects=True)
        args = [a for a, _ in ins]
        return pl.pallas_call(
            kernel,
            out_shape=[o for o, _ in outs],
            in_specs=[sp for _, sp in ins],
            out_specs=[sp for _, sp in outs],
            scratch_shapes=scratch,
            compiler_params=pltpu.CompilerParams(**params),
            cost_estimate=pl.CostEstimate(flops=flops, bytes_accessed=0, transcendentals=0),
        )(*args)

    rope_in = [(cb, V), (sb, V), (cj, V), (sj, V)]
    xp, dyp, n1, q, kvp, kvc, wp, gf, wo, wg, wu, wd = call(
        functools.partial(first_kernel, nc),
        [(x, V), (dy, A), (gains, V)] + rope_in + [(w_query, A), (key_weight.T, A), (value_weight.T, A), (w_out, A), (w_gate, A), (w_up, A), (w_down, A)],
        [
            (sds((rows, d), BF), V), (sds((rows, d), BF), V), (sds((rows, d), BF), V), (sds((rows, nq), BF), V),
            (sds((prompt, 2 * dk), BF), A), (sds((half, 2 * nk), BF), V), (sds((nq + 2 * nk, d), BF), V), (sds((16, d), F32), V),
            (sds((dq, d), BF), A), (sds((d, ff), BF), A), (sds((d, ff), BF), A), (sds((ff, d), BF), A),
        ],
        [
            pltpu.VMEM((rows, d), BF), pltpu.VMEM((d, dq), BF), pltpu.VMEM((dk, d), BF), pltpu.VMEM((dk, d), BF), pltpu.VMEM((16, d), F32),
            pltpu.VMEM((dq, dh), BF), pltpu.VMEM((dh, ff), BF), pltpu.VMEM((dh, ff), BF), pltpu.VMEM((ff, dh), BF),
            pltpu.VMEM((half, 2 * dk), BF),
            DMA((9,)), DMA((8,)), DMA((8,)), DMA((4,)), DMA((per, nc)), DMA((per, nc)),
        ],
        collective=0, flops=60 * 10**9,
    )

    chunk = 16
    count = 16 * (RUN // 2 // chunk)
    U = pltpu.VMEM((rows, d), BF)
    W = pltpu.VMEM((d, ff), BF)
    H = pltpu.VMEM((rows, ff), BF)
    KV = pltpu.VMEM((hk, prompt, PAD), BF)
    KVF = pltpu.VMEM((hk, prompt, PAD), F32)
    width = hq // hk * RUN
    out, tg, gg, gu, gd, go, gw, _, _, _, gains_grad = call(
        functools.partial(main_kernel, n, nc, chunk),
        [(kbase, S), (qlim, S)] + rope_in
        + [(gf, V), (q, V), (kvc, V), (wo, V), (kvp, A), (xp, A), (dyp, A), (wg, A), (wu, A), (wd, A), (n1, A), (wp, A)],
        [(sds((rows, d), BF), A), (sds((rows, d), BF), A), (sds((dh, ff), BF), A), (sds((dh, ff), BF), A), (sds((ff, dh), BF), A),
         (sds((dq, dh), BF), A), (sds((dh, dq + 2 * dk), BF), A), (sds((rows, d), F32), A), (sds((ff, d), BF), A), (sds((rows, d), BF), A),
         (sds((16, dh), F32), V)],
        [KV, KV, pltpu.VMEM((RUN, prompt + RUN), F32), pltpu.VMEM((rows, dq), BF), pltpu.VMEM((rows, nq), BF), pltpu.VMEM((runs * hq * 8, RUN), F32),
         U, U, U, U, pltpu.VMEM((3 * rows, d), BF), pltpu.VMEM((ff, d), BF), U, W, W, H, H, H, pltpu.VMEM((ff, dh), BF),
         KVF, KVF, pltpu.VMEM((rows, nq), BF), pltpu.VMEM((width, PAD), F32), pltpu.VMEM((8, width), F32), pltpu.VMEM((rows, nq), BF),
         pltpu.VMEM((rows, 2 * nk), BF), pltpu.VMEM((2, dq, dh), BF), pltpu.VMEM((RUN, d), BF), pltpu.VMEM((RUN, d), BF), pltpu.VMEM((RUN, d), BF),
         pltpu.VMEM((16, d), F32), pltpu.VMEM((2 * nc, 16, d), F32),
         DMA((7,)), DMA((blocks,)), DMA((3,)), DMA((runs,)), DMA((2,)), DMA, DMA((nc, per)), DMA((nc, per)), DMA((2 * nc - 1,)), DMA((2 * nc - 1,))]
        + [DMA((2, count))] * 4
        + [pltpu.SemaphoreType.REGULAR((6,)), DMA((5,)), DMA((5,)), DMA((5, 3, 2, 2)), DMA((5, 3, 2, 2)), DMA((5,))],
        collective=1, flops=300 * 10**9,
    )
    shapes = [(rows, d), (rows, d), (dh, dq + 2 * dk), (dq, dh), (dh, ff), (dh, ff), (ff, dh)]
    wide = [(dh, dq), (2 * dk, dh), (dq, dh), (dh, ff), (dh, ff), (ff, dh)]
    finals = [(dh, dq), (dk, dh), (dk, dh), (dq, dh), (dh, ff), (dh, ff), (ff, dh)]
    out, tg, gq, gk, gv, go, gg, gu, gd = call(
        finish_kernel,
        [(a, A) for a in (out, tg, gw, go, gg, gu, gd)],
        [(sds((rows, d), BF), A), (sds((rows, d), BF), A)] + [(sds(shape, F32), A) for shape in finals],
        [pltpu.VMEM(shape, BF) for shape in shapes] + [pltpu.VMEM(shape, F32) for shape in wide] + [DMA((7,)), DMA((9,))],
    )
    return out[None], tg[None], gq, gk.T, gv.T, go, gg, gu, gd, gains_grad[0], gains_grad[8]


def body(mesh, *args):
    tokens, w_query, segments = args[0], args[1], args[10]
    n, nc = mesh.shape["tensor"], mesh.shape["context"]
    rows = tokens.shape[1]
    if (tokens.shape[0] == 1 and rows % (4 * CLEN) == 0 and n == 4 and nc == 4 and mesh.shape["shard"] == 2
            and segments.shape[1] == rows * nc):
        return fast(*args, n, nc)
    return general(*args)


def solution(mesh):
    in_specs = (
        P("shard", "context", None),
        P("shard", "tensor"),
        P("shard", "tensor"),
        P("shard", "tensor"),
        P("tensor", "shard"),
        P("shard", "tensor"),
        P("shard", "tensor"),
        P("tensor", "shard"),
        P("shard"),
        P("shard"),
        P("shard", None),
        P("shard", None),
        P("shard", "context", None),
    )
    out_specs = (
        P("shard", "context", None),
        P("shard", "context", None),
        P("shard", "tensor"),
        P("shard", "tensor"),
        P("shard", "tensor"),
        P("tensor", "shard"),
        P("shard", "tensor"),
        P("shard", "tensor"),
        P("tensor", "shard"),
        P("shard"),
        P("shard"),
    )
    return jax.shard_map(functools.partial(body, mesh), mesh=mesh, in_specs=in_specs, out_specs=out_specs, check_vma=False)
```

```python
import functools
import math

import jax
import jax.numpy as jnp
import numpy as np
from jax import lax
from jax.experimental import pallas as pl
from jax.experimental.pallas import tpu as pltpu
from jax.sharding import PartitionSpec as P

HEAD_SIZE = 96
CLEN = 256


rope_base = 100000.0
norm_eps = 1e-05


def tables(positions):
    half_width = HEAD_SIZE // 2
    frequency = jnp.exp(
        jnp.arange(half_width, dtype=jnp.float32) * (-2.0 * math.log(rope_base) / HEAD_SIZE)
    )
    angles = positions.astype(jnp.float32)[:, None] * frequency[None, :]
    return (jnp.cos(angles)[:, None, :], jnp.sin(angles)[:, None, :])


def rotary_apply(heads, cosine_table, sine_values):
    half_width = HEAD_SIZE // 2
    front_half = heads[..., :half_width]
    back_half = heads[..., half_width:]
    return jnp.concatenate(
        [
            front_half * cosine_table - back_half * sine_values,
            back_half * cosine_table + front_half * sine_values,
        ],
        axis=-1,
    )


def rotate_back(heads, cosine_table, sine_values):
    half_width = HEAD_SIZE // 2
    front_half = heads[..., :half_width]
    back_half = heads[..., half_width:]
    return jnp.concatenate(
        [
            front_half * cosine_table + back_half * sine_values,
            back_half * cosine_table - front_half * sine_values,
        ],
        axis=-1,
    )


def contract_rows(left, right):
    return lax.dot_general(
        left, right, (((0,), (0,)), ((), ())), preferred_element_type=jnp.float32
    )


def contract_cols(left, right):
    return lax.dot_general(
        left, right, (((1,), (1,)), ((), ())), preferred_element_type=jnp.float32
    )


def norm_back(tok_rows, norm_scale, gain, grad_normed):
    weighted = gain * grad_normed
    inner = jnp.mean(weighted * tok_rows, axis=-1, keepdims=True)
    grad_rows = norm_scale * weighted - tok_rows * (norm_scale * norm_scale * norm_scale) * inner
    grad_gain = jnp.sum(grad_normed * tok_rows * norm_scale, axis=0)
    return (grad_rows, grad_gain)


def visible(seg_query, pos_query, seg_keys, pos_keys):
    own = (seg_keys[None, :] == seg_query[:, None]) & (pos_keys[None, :] <= pos_query[:, None])
    branch = (
        (seg_keys[None, :] == 0)
        & (seg_query[:, None] > 0)
        & (pos_keys[None, :] < seg_query[:, None] * CLEN)
    )
    return own | branch


def general(
    tokens,
    w_query,
    key_weight,
    value_weight,
    w_out,
    w_gate,
    w_up,
    w_down,
    gain_attn,
    gain_ffn,
    segments,
    positions,
    cotangent,
):
    groups, tok_local, model_width = tokens.shape
    token_count = groups * tok_local
    heads_here = w_query.shape[1] // HEAD_SIZE
    kv_here = key_weight.shape[1] // HEAD_SIZE
    per_kv = heads_here // kv_here
    kv_width = kv_here * HEAD_SIZE
    score_scale = 1.0 / math.sqrt(HEAD_SIZE)
    context_index = lax.axis_index("context")
    first_row = context_index * tok_local
    seg_here = lax.dynamic_slice_in_dim(segments, first_row, tok_local, 1)
    pos_here = lax.dynamic_slice_in_dim(positions, first_row, tok_local, 1)
    w_query, key_weight, value_weight, w_gate, w_up, gain_attn, gain_ffn = (
        lax.all_gather(w_query, "shard", axis=0, tiled=True),
        lax.all_gather(key_weight, "shard", axis=0, tiled=True),
        lax.all_gather(value_weight, "shard", axis=0, tiled=True),
        lax.all_gather(w_gate, "shard", axis=0, tiled=True),
        lax.all_gather(w_up, "shard", axis=0, tiled=True),
        lax.all_gather(gain_attn, "shard", axis=0, tiled=True),
        lax.all_gather(gain_ffn, "shard", axis=0, tiled=True),
    )
    w_out, w_down = (
        lax.all_gather(w_out, "shard", axis=1, tiled=True),
        lax.all_gather(w_down, "shard", axis=1, tiled=True),
    )
    gain_one = gain_attn.astype(jnp.float32)
    gain_two = gain_ffn.astype(jnp.float32)
    tok_rows = tokens.reshape(token_count, model_width).astype(jnp.float32)
    scale_one = lax.rsqrt(jnp.mean(tok_rows * tok_rows, axis=-1, keepdims=True) + norm_eps)
    normed_input = (tok_rows * scale_one * gain_one).astype(jnp.bfloat16)
    cosine_table, sine_values = tables(pos_here.reshape(token_count))
    query_heads_rows = rotary_apply(
        jnp.dot(normed_input, w_query, preferred_element_type=jnp.float32).reshape(
            token_count, heads_here, HEAD_SIZE
        ),
        cosine_table,
        sine_values,
    )
    query_heads_rows = query_heads_rows.astype(jnp.bfloat16).reshape(
        groups, tok_local, heads_here * HEAD_SIZE
    )
    key_rows = rotary_apply(
        jnp.dot(normed_input, key_weight, preferred_element_type=jnp.float32).reshape(
            token_count, kv_here, HEAD_SIZE
        ),
        cosine_table,
        sine_values,
    )
    key_rows = key_rows.astype(jnp.bfloat16).reshape(token_count, kv_width)
    value_rows = jnp.dot(normed_input, value_weight, preferred_element_type=jnp.float32).astype(
        jnp.bfloat16
    )
    keyval = jnp.concatenate([key_rows, value_rows], axis=-1).reshape(
        groups, tok_local, 2 * kv_width
    )
    gathered = lax.all_gather(keyval, "context", axis=1, tiled=True)

    def scores_of(group_queries, group_keyval, seg_query, pos_query, seg_keys, pos_keys):
        grouped_heads = group_queries.reshape(tok_local, kv_here, per_kv, HEAD_SIZE)
        key_head_rows = group_keyval[:, :kv_width].reshape(-1, kv_here, HEAD_SIZE)
        scores = (
            jnp.einsum(
                "bhgd,khd->hgbk", grouped_heads, key_head_rows, preferred_element_type=jnp.float32
            )
            * score_scale
        )
        allowed = visible(seg_query, pos_query, seg_keys, pos_keys)
        return (jnp.where(allowed[None, None], scores, -1e30), grouped_heads, key_head_rows)

    def attend_group(inputs):
        group_queries, group_keyval, seg_query, pos_query, seg_keys, pos_keys = inputs
        scores, grouped_heads, key_head_rows = scores_of(
            group_queries, group_keyval, seg_query, pos_query, seg_keys, pos_keys
        )
        top_score = jnp.max(scores, axis=-1, keepdims=True)
        exponent = jnp.exp(scores - top_score)
        totals = jnp.sum(exponent, axis=-1, keepdims=True)
        soft_weights = (exponent / totals).astype(jnp.bfloat16)
        value_head_rows = group_keyval[:, kv_width:].reshape(-1, kv_here, HEAD_SIZE)
        attended_output = jnp.einsum(
            "hgbk,khd->bhgd", soft_weights, value_head_rows, preferred_element_type=jnp.float32
        )
        return (
            attended_output.reshape(tok_local, heads_here * HEAD_SIZE),
            (top_score + jnp.log(totals))[..., 0],
        )

    attended_output, log_total = lax.map(
        attend_group, (query_heads_rows, gathered, seg_here, pos_here, segments, positions)
    )
    attended_low = attended_output.reshape(token_count, heads_here * HEAD_SIZE).astype(jnp.bfloat16)
    attn_sum = lax.psum(jnp.dot(attended_low, w_out, preferred_element_type=jnp.float32), "tensor")
    middle = tok_rows + attn_sum
    scale_two = lax.rsqrt(jnp.mean(middle * middle, axis=-1, keepdims=True) + norm_eps)
    normed_two = (middle * scale_two * gain_two).astype(jnp.bfloat16)
    gate_proj = jnp.dot(normed_two, w_gate, preferred_element_type=jnp.float32)
    up_proj = jnp.dot(normed_two, w_up, preferred_element_type=jnp.float32)
    sigmoid_gate = jax.nn.sigmoid(gate_proj)
    silu_gate = gate_proj * sigmoid_gate
    hidden = (silu_gate * up_proj).astype(jnp.bfloat16)
    ffn_sum = lax.psum(
        jnp.dot(hidden, w_down, preferred_element_type=jnp.float32).astype(jnp.bfloat16), "tensor"
    ).astype(jnp.float32)
    output = (middle + ffn_sum).astype(jnp.bfloat16).reshape(groups, tok_local, model_width)
    grad_low = cotangent.reshape(token_count, model_width)
    grad_out = grad_low.astype(jnp.float32)
    grad_hidden = contract_cols(grad_low, w_down)
    grad_w_down_t = contract_rows(grad_low, hidden)
    grad_gate = (
        grad_hidden * up_proj * sigmoid_gate * (1.0 + gate_proj * (1.0 - sigmoid_gate))
    ).astype(jnp.bfloat16)
    grad_up = (grad_hidden * silu_gate).astype(jnp.bfloat16)
    grad_w_gate = contract_rows(normed_two, grad_gate)
    grad_w_up = contract_rows(normed_two, grad_up)
    grad_normed_two = lax.psum(
        contract_cols(grad_gate, w_gate) + contract_cols(grad_up, w_up), "tensor"
    )
    back_two, grad_gain_two = norm_back(middle, scale_two, gain_two, grad_normed_two)
    grad_middle = grad_out + back_two
    grad_mid_low = grad_middle.astype(jnp.bfloat16)
    grad_w_out_t = contract_rows(grad_mid_low, attended_low)
    grad_attended = (
        contract_cols(grad_mid_low, w_out)
        .astype(jnp.bfloat16)
        .reshape(groups, tok_local, heads_here * HEAD_SIZE)
    )

    def attend_back(inputs):
        (
            group_queries,
            group_keyval,
            group_grad,
            group_total,
            seg_query,
            pos_query,
            seg_keys,
            pos_keys,
        ) = inputs
        scores, grouped_heads, key_head_rows = scores_of(
            group_queries, group_keyval, seg_query, pos_query, seg_keys, pos_keys
        )
        soft_weights = jnp.exp(scores - group_total[..., None])
        value_head_rows = group_keyval[:, kv_width:].reshape(-1, kv_here, HEAD_SIZE)
        grad_grouped = group_grad.reshape(tok_local, kv_here, per_kv, HEAD_SIZE)
        grad_weights = jnp.einsum(
            "bhgd,khd->hgbk", grad_grouped, value_head_rows, preferred_element_type=jnp.float32
        )
        inner = jnp.sum(soft_weights * grad_weights, axis=-1, keepdims=True)
        grad_scores = (soft_weights * (grad_weights - inner)).astype(jnp.bfloat16)
        grad_queries = (
            jnp.einsum(
                "hgbk,khd->bhgd", grad_scores, key_head_rows, preferred_element_type=jnp.float32
            )
            * score_scale
        )
        grad_keys = (
            jnp.einsum(
                "hgbk,bhgd->khd", grad_scores, grouped_heads, preferred_element_type=jnp.float32
            )
            * score_scale
        )
        grad_values = jnp.einsum(
            "hgbk,bhgd->khd",
            soft_weights.astype(jnp.bfloat16),
            grad_grouped,
            preferred_element_type=jnp.float32,
        )
        grad_keyval = jnp.concatenate(
            [grad_keys.reshape(-1, kv_width), grad_values.reshape(-1, kv_width)], axis=-1
        )
        return (grad_queries.reshape(tok_local, heads_here * HEAD_SIZE), grad_keyval)

    grad_queries, grad_keyval = lax.map(
        attend_back,
        (
            query_heads_rows,
            gathered,
            grad_attended,
            log_total,
            seg_here,
            pos_here,
            segments,
            positions,
        ),
    )
    grad_keyval = lax.psum_scatter(grad_keyval, "context", scatter_dimension=1, tiled=True)
    grad_query_rows = rotate_back(
        grad_queries.reshape(token_count, heads_here, HEAD_SIZE), cosine_table, sine_values
    )
    grad_query_rows = grad_query_rows.astype(jnp.bfloat16).reshape(
        token_count, heads_here * HEAD_SIZE
    )
    grad_key_rows = rotate_back(
        grad_keyval[..., :kv_width].reshape(token_count, kv_here, HEAD_SIZE),
        cosine_table,
        sine_values,
    )
    grad_key_rows = grad_key_rows.astype(jnp.bfloat16).reshape(token_count, kv_width)
    grad_value_rows = (
        grad_keyval[..., kv_width:].reshape(token_count, kv_width).astype(jnp.bfloat16)
    )
    grad_w_query = contract_rows(normed_input, grad_query_rows)
    grad_w_key = contract_rows(normed_input, grad_key_rows)
    grad_w_value = contract_rows(normed_input, grad_value_rows)
    partial_one = (
        contract_cols(grad_query_rows, w_query)
        + contract_cols(grad_key_rows, key_weight)
        + contract_cols(grad_value_rows, value_weight)
    )
    grad_normed = lax.psum(partial_one, "tensor")
    back_one, grad_gain_one = norm_back(tok_rows, scale_one, gain_one, grad_normed)
    tokens_grad = (
        (grad_middle + back_one).astype(jnp.bfloat16).reshape(groups, tok_local, model_width)
    )
    summed = (
        lax.psum_scatter(grad_w_query, ("shard", "context"), scatter_dimension=0, tiled=True),
        lax.psum_scatter(grad_w_key, ("shard", "context"), scatter_dimension=0, tiled=True),
        lax.psum_scatter(grad_w_value, ("shard", "context"), scatter_dimension=0, tiled=True),
        lax.psum_scatter(grad_w_out_t, ("shard", "context"), scatter_dimension=0, tiled=True),
        lax.psum_scatter(grad_w_gate, ("shard", "context"), scatter_dimension=0, tiled=True),
        lax.psum_scatter(grad_w_up, ("shard", "context"), scatter_dimension=0, tiled=True),
        lax.psum_scatter(grad_w_down_t, ("shard", "context"), scatter_dimension=0, tiled=True),
        lax.psum_scatter(grad_gain_one, ("shard", "context"), scatter_dimension=0, tiled=True),
        lax.psum_scatter(grad_gain_two, ("shard", "context"), scatter_dimension=0, tiled=True),
    )
    summed = (
        lax.all_gather(summed[0].astype(jnp.bfloat16), "context", axis=0, tiled=True).astype(
            jnp.float32
        ),
        lax.all_gather(summed[1].astype(jnp.bfloat16), "context", axis=0, tiled=True).astype(
            jnp.float32
        ),
        lax.all_gather(summed[2].astype(jnp.bfloat16), "context", axis=0, tiled=True).astype(
            jnp.float32
        ),
        lax.all_gather(summed[3].astype(jnp.bfloat16), "context", axis=0, tiled=True).astype(
            jnp.float32
        ),
        lax.all_gather(summed[4].astype(jnp.bfloat16), "context", axis=0, tiled=True).astype(
            jnp.float32
        ),
        lax.all_gather(summed[5].astype(jnp.bfloat16), "context", axis=0, tiled=True).astype(
            jnp.float32
        ),
        lax.all_gather(summed[6].astype(jnp.bfloat16), "context", axis=0, tiled=True).astype(
            jnp.float32
        ),
        lax.all_gather(summed[7].astype(jnp.bfloat16), "context", axis=0, tiled=True).astype(
            jnp.float32
        ),
        lax.all_gather(summed[8].astype(jnp.bfloat16), "context", axis=0, tiled=True).astype(
            jnp.float32
        ),
    )
    return (
        output,
        tokens_grad,
        summed[0],
        summed[1],
        summed[2],
        summed[3].T,
        summed[4],
        summed[5],
        summed[6].T,
        summed[7],
        summed[8],
    )


MESH = pl.DeviceIdType.MESH
RUN = 256
PAD = 128
NEG = -1e30
LOG2E = 1.4426950408889634
BF = jnp.bfloat16
F32 = jnp.float32
VLIM = 64 * 1024 * 1024


def mm(a, b):
    return lax.dot_general(a, b, (((1,), (0,)), ((), ())), preferred_element_type=F32)


def mm_nt(a, b):
    return lax.dot_general(a, b, (((1,), (1,)), ((), ())), preferred_element_type=F32)


def mm_tn(a, b):
    return lax.dot_general(a, b, (((0,), (0,)), ((), ())), preferred_element_type=F32)


def iota(shape, axis):
    return lax.broadcasted_iota(jnp.int32, shape, axis)


def one_hot(hit):
    return jnp.where(hit, 1.0, 0.0).astype(BF)


def pad_matrix(heads, flip=False):
    shape = (heads * HEAD_SIZE, heads * PAD)
    if flip:
        row, col = iota(shape[::-1], 1), iota(shape[::-1], 0)
    else:
        row, col = iota(shape, 0), iota(shape, 1)
    lane = col & 127
    part = jnp.where(lane < 64, lane, lane - 16)
    return one_hot((row == (col >> 7) * HEAD_SIZE + part) & ((lane & 63) < 48))


def split_matrix():
    row, col = iota((RUN, RUN), 0), iota((RUN, RUN), 1)
    return one_hot(col == jnp.where(row < 128, 2 * row, 2 * row - 255))


def merge_matrix():
    row, col = iota((RUN, RUN), 0), iota((RUN, RUN), 1)
    return one_hot(col == (row >> 1) + (row & 1) * 128)


def first_of(ref, run, per):
    start = lax.axis_index("context") * (2 * per * RUN)
    return ref[0, start + run % per * (2 * RUN) + run // per]


def rope_tables(run, per, pos_ref, cb_ref, sb_ref, cj_ref, sj_ref):
    base = first_of(pos_ref, run, per) // RUN
    cb, sb = cb_ref[pl.ds(base, 1), :], sb_ref[pl.ds(base, 1), :]
    cj, sj = cj_ref[...], sj_ref[...]
    return cb * cj - sb * sj, sb * cj + cb * sj


def rope(u, c, s):
    return u * c + pltpu.roll(u, 64, 1) * s


def rope_back(u, c, s):
    return u * c - pltpu.roll(u, 64, 1) * s


def vmem(*shape_dtype):
    return pl.BlockSpec(memory_space=pltpu.VMEM)


def entry_barrier(targets):
    bar = pltpu.get_barrier_semaphore()
    for t in targets:
        pl.semaphore_signal(bar, inc=1, device_id=t, device_id_type=MESH)
    pl.semaphore_wait(bar, len(targets))


def remote(src, dst, send, recv, target):
    return pltpu.make_async_remote_copy(
        src_ref=src, dst_ref=dst, send_sem=send, recv_sem=recv, device_id=target, device_id_type=MESH
    )


def first_kernel(nc, x_ref, dy_h, g_ref, pos_ref, cb_ref, sb_ref, cj_ref, sj_ref, wq_h, wk_h, wv_h, wo_h, wg_h, wu_h, wd_h,
                 xp_h, dyp_h, n1_h, q_ref, kvp_ref, kvc_ref, wp_h, gf_ref, wo_f, wg_f, wu_f, wd_f,
                 xp_ref, dyp_ref, n1_ref, wp_ref, dy_v, wq_s, wk_s, wv_s, g_s, wo_v, wg_v, wu_v, wd_v, kv_send,
                 lsem, ssem, rsem, osem, csem, crem, esem):
    s = lax.axis_index("shard")
    c = lax.axis_index("context")
    dh = g_s.shape[1] // 2
    own = pl.ds(pl.multiple_of(s * dh, dh), dh)
    other = {"shard": 1 - s}
    loads = [
        pltpu.make_async_copy(wq_h, wq_s.at[own], lsem.at[0]),
        pltpu.make_async_copy(wk_h, wk_s.at[:, own], lsem.at[1]),
        pltpu.make_async_copy(wv_h, wv_s.at[:, own], lsem.at[2]),
        None,
        pltpu.make_async_copy(wo_h, wo_v, lsem.at[4]),
        pltpu.make_async_copy(wg_h, wg_v, lsem.at[5]),
        pltpu.make_async_copy(wu_h, wu_v, lsem.at[6]),
        pltpu.make_async_copy(wd_h, wd_v, lsem.at[7]),
        pltpu.make_async_copy(dy_h, dy_v, lsem.at[8]),
    ]
    for cp in loads[:3] + loads[4:]:
        cp.start()
    for i in range(2):
        g_s[8 * i : 8 * i + 8, own] = jnp.broadcast_to(g_ref[i : i + 1, :], (8, dh))
    entry_barrier([other] + [{"context": lax.rem(c + i, nc)} for i in range(1, nc)])
    sends = [
        remote(wq_s.at[own], wq_s.at[own], ssem.at[0], rsem.at[0], other),
        remote(wk_s.at[:, own], wk_s.at[:, own], ssem.at[1], rsem.at[1], other),
        remote(wv_s.at[:, own], wv_s.at[:, own], ssem.at[2], rsem.at[2], other),
        remote(g_s.at[:, own], g_s.at[:, own], ssem.at[3], rsem.at[3], other),
        remote(wo_v, wo_f.at[:, own], ssem.at[4], rsem.at[4], other),
        remote(wg_v, wg_f.at[own], ssem.at[5], rsem.at[5], other),
        remote(wu_v, wu_f.at[own], ssem.at[6], rsem.at[6], other),
        remote(wd_v, wd_f.at[:, own], ssem.at[7], rsem.at[7], other),
    ]
    keeps = [
        pltpu.make_async_copy(wo_v, wo_f.at[:, own], osem.at[0]),
        pltpu.make_async_copy(wg_v, wg_f.at[own], osem.at[1]),
        pltpu.make_async_copy(wu_v, wu_f.at[own], osem.at[2]),
        pltpu.make_async_copy(wd_v, wd_f.at[:, own], osem.at[3]),
    ]
    for i in (3, 0, 1, 2, 4, 5, 6, 7):
        if i != 3:
            loads[i].wait()
        sends[i].start()
        if i >= 4:
            keeps[i - 4].start()
    half = x_ref.shape[0] // 2
    split = split_matrix()
    for i in range(x_ref.shape[0] // RUN):
        xb = mm(split, x_ref[pl.ds(i * RUN, RUN), :])
        xp_ref[pl.ds(i * 128, 128), :] = xb[:128].astype(BF)
        xp_ref[pl.ds(half + i * 128, 128), :] = xb[128:].astype(BF)
        if i == 0:
            sends[3].wait_recv()
        r = lax.rsqrt(jnp.mean(xb * xb, axis=-1, keepdims=True) + norm_eps)
        nb = (xb * r * g_s[0:1, :]).astype(BF)
        n1_ref[pl.ds(i * 128, 128), :] = nb[:128]
        n1_ref[pl.ds(half + i * 128, 128), :] = nb[128:]
    gf_ref[...] = g_s[...]
    exits = [pltpu.make_async_copy(a, b, esem.at[i]) for i, (a, b) in enumerate([(xp_ref, xp_h), (n1_ref, n1_h), (wp_ref, wp_h), (dyp_ref, dyp_h)])]
    exits[0].start()
    exits[1].start()
    hq, hk = wq_s.shape[1] // HEAD_SIZE, wk_s.shape[0] // HEAD_SIZE
    selq, selk = pad_matrix(hq, True), pad_matrix(hk, True)
    nq, nk = hq * PAD, hk * PAD
    for i in range(3):
        sends[i].wait_recv()
    wp_ref[0:nq, :] = mm_nt(selq, wq_s[...]).astype(BF)
    wp_ref[nq : nq + nk, :] = mm(selk, wk_s[...]).astype(BF)
    wp_ref[nq + nk :, :] = mm(selk, wv_s[...]).astype(BF)
    exits[2].start()
    selkv = pad_matrix(2 * hk)
    runs = x_ref.shape[0] // RUN
    per = runs // 2
    kv_copies = []
    for run in range(runs):
        rows = pl.ds(run * RUN, RUN)
        y = mm_nt(n1_ref[rows, :], wp_ref[nq:, :])
        ct, st = rope_tables(run, per, pos_ref, cb_ref, sb_ref, cj_ref, sj_ref)
        kv = [rope(y[:, h * PAD : (h + 1) * PAD], ct, st).astype(BF) for h in range(hk)]
        kv = jnp.concatenate(kv + [y[:, nk:].astype(BF)], axis=1)
        if run < per:
            kv_send[pl.ds(run * RUN, RUN), :] = mm_nt(kv, selkv).astype(BF)
            mine = pl.ds(pl.multiple_of((c * per + run) * RUN, RUN), RUN)
            for i in range(1, nc):
                cp = remote(kv_send.at[pl.ds(run * RUN, RUN)], kvp_ref.at[mine], csem.at[run, i], crem.at[run, i],
                            {"context": lax.rem(c + i, nc)})
                cp.start()
                kv_copies.append(cp)
            cp = pltpu.make_async_copy(kv_send.at[pl.ds(run * RUN, RUN)], kvp_ref.at[mine], csem.at[run, 0])
            cp.start()
            kv_copies.append(cp)
        else:
            kvc_ref[pl.ds((run - per) * RUN, RUN), :] = kv
    for run in range(runs):
        rows = pl.ds(run * RUN, RUN)
        y = mm_nt(n1_ref[rows, :], wp_ref[0:nq, :])
        ct, st = rope_tables(run, per, pos_ref, cb_ref, sb_ref, cj_ref, sj_ref)
        for h in range(hq):
            q_ref[rows, h * PAD : (h + 1) * PAD] = rope(y[:, h * PAD : (h + 1) * PAD], ct, st).astype(BF)
    loads[8].wait()
    for i in range(x_ref.shape[0] // RUN):
        b = mm(split, dy_v[pl.ds(i * RUN, RUN), :]).astype(BF)
        dyp_ref[pl.ds(i * 128, 128), :] = b[:128]
        dyp_ref[pl.ds(half + i * 128, 128), :] = b[128:]
    exits[3].start()
    for cp in kv_copies + exits:
        cp.wait()
    for i in range(4):
        keeps[i].wait()
        sends[4 + i].wait_recv()
    for cp in sends:
        cp.wait_send()


class Line:
    F_AT = (8, 9, 10, 12)
    D_AT = (11, 13, 14, 15)

    def __init__(self, n, chunk, pbuf, rbuf, obuf, sems):
        self.n, self.chunk, self.per = n, chunk, RUN // 2 // chunk
        self.count = 16 * self.per
        self.pbuf, self.rbuf, self.obuf = pbuf, rbuf, obuf
        self.rs, self.rr, self.bs, self.br = sems
        self.ticks = 32 // chunk
        self.hop = 3
        self.turn = 2 * (n - 1) * self.hop
        self.slots = self.count + self.turn

    def pieces(self, h, i):
        n, chunk = self.n, self.chunk
        z = lax.axis_index("tensor")
        job = i // self.per
        late = jnp.where((job == 11) | (job > 12), 1, 0)
        row = jnp.where(job < 8, lax.rem(job, 4), jnp.where(late == 1, jnp.maximum(job - 12, 0), jnp.minimum(job - 8, 3)))
        part = jnp.where(job < 8, job // 4, 2 - late)
        off = row * RUN + h * (RUN // 2) + lax.rem(i, self.per) * chunk
        rows = pl.ds(pl.multiple_of(off, chunk), chunk)
        orows = pl.ds(pl.multiple_of(part * (4 * RUN) + off, chunk), chunk)
        place = z if h == 0 else n - 1 - z
        up, down = jnp.minimum(z + 1, n - 1), jnp.maximum(z - 1, 0)
        ahead = {"tensor": up if h == 0 else down}
        back = {"tensor": down if h == 0 else up}
        fwd = remote(self.pbuf.at[rows], self.rbuf.at[rows], self.rs.at[h, i], self.rr.at[h, i], ahead)
        ret = remote(self.obuf.at[orows], self.obuf.at[orows], self.bs.at[h, i], self.br.at[h, i], back)
        return rows, orows, place, fwd, ret

    def reduce_step(self, h, i):
        rows, orows, place, fwd, ret = self.pieces(h, i)
        n = self.n

        @pl.when(place == 0)
        def _():
            fwd.start()

        @pl.when(place > 0)
        def _():
            fwd.wait_recv()
            total = (self.rbuf[rows, :].astype(F32) + self.pbuf[rows, :].astype(F32)).astype(BF)

            @pl.when(place < n - 1)
            def _():
                self.pbuf[rows, :] = total
                fwd.start()

            @pl.when(place == n - 1)
            def _():
                self.obuf[orows, :] = total
                ret.start()

    def spread_step(self, h, i):
        rows, orows, place, fwd, ret = self.pieces(h, i)

        @pl.when(place < self.n - 1)
        def _():
            ret.wait_recv()

        @pl.when((place < self.n - 1) & (place > 0))
        def _():
            ret.start()

    def serve(self, t):
        n = self.n
        z = lax.axis_index("tensor")
        for h in range(2):
            place = z if h == 0 else n - 1 - z
            i = t - place * self.hop

            @pl.when((i >= 0) & (i < self.count))
            def _():
                self.reduce_step(h, i)

            j = t - (2 * (n - 1) - place) * self.hop

            @pl.when((j >= 0) & (j < self.count))
            def _():
                self.spread_step(h, j)

    def sent(self, job, fwd=True, ret=False):
        def step(i, _):
            for h in range(2):
                rows, orows, place, f, r = self.pieces(h, job * self.per + i)
                if fwd:

                    @pl.when(place < self.n - 1)
                    def _():
                        f.wait_send()

                if ret:

                    @pl.when(place > 0)
                    def _():
                        r.wait_send()

            return 0

        lax.fori_loop(0, self.per, step, 0)


def run_items(items, serve):
    total = max(e for spans, _ in items for _, e in spans)

    def step(k, _):
        for spans, body in items:
            hit = functools.reduce(jnp.logical_or, [(k >= lo) & (k < hi) for lo, hi in spans])
            pl.when(hit)(functools.partial(body, k))
        serve(k)
        return 0

    lax.fori_loop(0, total, step, 0)


class Square:
    def __init__(self, rows, cols, src, mine, theirs, spare, out, credit, shard_send, shard_recv, send, recv, store):
        self.src, self.mine, self.theirs, self.res, self.out = src, mine, theirs, theirs, out
        self.r1, self.r2 = [spare[0:2], spare[2:4]], spare[4:6]
        self.credit, self.shard_sems, self.shard_recv, self.send, self.recv, self.store_sem = credit, shard_send, shard_recv, send, recv, store
        self.rows, self.qr, self.cols = rows, rows // 4, cols
        c = lax.axis_index("context")
        self.cy, self.cx = c // 2, lax.rem(c, 2)

    def at(self, y, x, half):
        w = self.cols // 2
        return (pl.ds(pl.multiple_of((2 * y + x) * self.qr, self.qr), self.qr), pl.ds(half * w, w))

    def peer(self, half, first):
        if (half == 0) == first:
            return {"context": 2 * self.cy + 1 - self.cx}
        return {"context": 2 * (1 - self.cy) + self.cx}

    def shard_copy(self):
        return remote(self.src, self.theirs, self.shard_sems, self.shard_recv, {"shard": 1 - lax.axis_index("shard")})

    def outer(self, half):
        if half == 0:
            return [(y, 1 - self.cx) for y in range(2)], [(y, self.cx) for y in range(2)]
        return [(1 - self.cy, x) for x in range(2)], [(self.cy, x) for x in range(2)]

    def p1(self, half, j):
        return remote(self.mine.at[self.at(*self.outer(half)[0][j], half)], self.r1[half][j],
                      self.send.at[0, half, j], self.recv.at[0, half, j], self.peer(half, True))

    def p2(self, half):
        q = (1 - self.cy, self.cx) if half == 0 else (self.cy, 1 - self.cx)
        return remote(self.mine.at[self.at(*q, half)], self.r2[half],
                      self.send.at[1, half, 0], self.recv.at[1, half, 0], self.peer(half, False))

    def p3(self, half):
        at = self.at(self.cy, self.cx, half)
        return remote(self.res.at[at], self.res.at[at], self.send.at[1, half, 1], self.recv.at[1, half, 1], self.peer(half, False))

    def p4(self, half, j):
        at = self.at(*self.outer(half)[1][j], half)
        return remote(self.res.at[at], self.res.at[at], self.send.at[2, half, j], self.recv.at[2, half, j], self.peer(half, True))

    def free(self):
        for t in ({"shard": 1 - lax.axis_index("shard")}, self.peer(0, True), self.peer(0, False)):
            pl.semaphore_signal(self.credit, inc=1, device_id=t, device_id_type=MESH)

    def e0(self):
        pl.semaphore_wait(self.credit, 3)
        self.shard_copy().start()

    def e1(self):
        self.shard_copy().wait_recv()
        step = self.qr

        def add(i, _):
            rows = pl.ds(pl.multiple_of(i * step, step), step)
            self.mine[rows, :] = (self.mine[rows, :].astype(F32) + self.theirs[rows, :].astype(F32)).astype(BF)
            return 0

        lax.fori_loop(0, self.rows // step, add, 0)
        for j in range(2):
            for half in range(2):
                self.p1(half, j).start()

    def e2(self):
        for half in range(2):
            for j in range(2):
                self.p1(half, j).wait_recv()
                at = self.at(*self.outer(half)[1][j], half)
                self.mine[at] = (self.mine[at].astype(F32) + self.r1[half][j][...].astype(F32)).astype(BF)
            self.p2(half).start()

    def e3(self):
        for half in range(2):
            self.p2(half).wait_recv()
            at = self.at(self.cy, self.cx, half)
            self.res[at] = (self.mine[at].astype(F32) + self.r2[half][...].astype(F32)).astype(BF)
            self.p3(half).start()

    def e4(self):
        for half in range(2):
            self.p3(half).wait_recv()
            for j in range(2):
                self.p4(half, j).start()

    def e5(self):
        for half in range(2):
            for j in range(2):
                self.p4(half, j).wait_recv()

    def store(self):
        return pltpu.make_async_copy(self.res, self.out, self.store_sem)

    def done(self):
        self.shard_copy().wait_send()
        for half in range(2):
            for j in range(2):
                self.p1(half, j).wait_send()
                self.p4(half, j).wait_send()
            self.p2(half).wait_send()
            self.p3(half).wait_send()


def line_barrier(n, peers=()):
    z = lax.axis_index("tensor")
    bar = pltpu.get_barrier_semaphore()
    for t in peers:
        pl.semaphore_signal(bar, inc=1, device_id=t, device_id_type=MESH)

    @pl.when(z > 0)
    def _():
        pl.semaphore_signal(bar, inc=1, device_id={"tensor": jnp.maximum(z - 1, 0)}, device_id_type=MESH)

    @pl.when(z < n - 1)
    def _():
        pl.semaphore_signal(bar, inc=1, device_id={"tensor": jnp.minimum(z + 1, n - 1)}, device_id_type=MESH)

    pl.semaphore_wait(bar, len(peers) + jnp.minimum(z, 1) + jnp.minimum(n - 1 - z, 1))


def main_kernel(n, nc, chunk, seg_ref, pos_ref, cb_ref, sb_ref, cj_ref, sj_ref, gf_ref, q_ref, kvc_ref, wo_ref,
                kvp_h, xp_h, dyp_h, wg_h, wu_h, wd_h, n1_h, wp_h,
                out_h, tg_h, gg_h, gu_h, gd_h, go_h, gw_h, dm_h, gds_h, fp_h, gains_ref,
                k_s, v_s, s_s, o_v, op_v, lse_v, xs, ys, pbuf, rbuf, obuf, wd, n2, wg, wu, hid, dg, du, gt,
                dk_s, dv_s, do_v, dq_s, delta_s, dqp, dkv_s, go_v, st_o, st_t, st_p, gpart, grecv,
                lsem, ksem, osem, fsem, msem, nsem, qsend, qrecv, gs, gr, rs, rr, bs, br, credits, shard_send, shard_recv, send, recv, store):
    s = lax.axis_index("shard")
    c = lax.axis_index("context")
    rows_here, d = xs.shape
    runs = rows_here // RUN
    per = runs // 2
    half = rows_here // 2
    hk = k_s.shape[0]
    hq = q_ref.shape[1] // PAD
    rep = hq // hk
    blocks = k_s.shape[1] // RUN
    ff = wg.shape[1]
    dh = d // 2
    nq, nk = hq * PAD, hk * PAD
    score = 1.0 / math.sqrt(HEAD_SIZE)
    scale = LOG2E * score
    own = pl.ds(pl.multiple_of(s * dh, dh), dh)
    yours = pl.ds(pl.multiple_of((1 - s) * dh, dh), dh)
    wide = 2 * hk * HEAD_SIZE

    def at(i, size=RUN):
        return pl.ds(pl.multiple_of(i * size, size), size)

    def limit(run):
        return jnp.where(run < per, first_of(pos_ref, run, per), first_of(seg_ref, run, per) * CLEN - 1)

    kv_in = [dg.at[pl.ds((b % 4) * RUN, RUN), pl.ds(b // 4 * wide, wide)] for b in range(blocks)]
    key_loads = [pltpu.make_async_copy(kvp_h.at[pl.ds(b * RUN, RUN)], kv_in[b], ksem.at[b]) for b in range(blocks)]
    for cp in key_loads:
        cp.start()
    pairs = [(xp_h, xs), (wg_h, wg), (wu_h, wu), (dyp_h, ys), (wd_h, wd)]
    loads = [pltpu.make_async_copy(a, b, lsem.at[i]) for i, (a, b) in enumerate(pairs)]
    for cp in loads:
        cp.start()
    peers = [{"shard": lax.rem(s + i // nc, 2), "context": lax.rem(c + lax.rem(i, nc), nc)} for i in range(1, 2 * nc)]
    line_barrier(n, peers)
    line = Line(n, chunk, pbuf, rbuf, obuf, (rs, rr, bs, br))
    a_of = lambda job: at(job)
    b_of = lambda job: at(runs + job)
    lane = iota((RUN, PAD), 1)
    for b in range(blocks):
        key_loads[b].wait()
        kv = mm(kv_in[b][...], pad_matrix(2 * hk))
        rows = pl.ds(b * RUN, RUN)
        for g in range(hk):
            k_s[g, rows, :] = kv[:, g * PAD : (g + 1) * PAD].astype(BF)
            v_s[g, rows, :] = jnp.where(lane == 48, 1.0, kv[:, (hk + g) * PAD : (hk + g + 1) * PAD]).astype(BF)
    dk_s[...] = jnp.zeros_like(dk_s)
    dv_s[...] = jnp.zeros_like(dv_s)
    gpart[...] = jnp.zeros_like(gpart)

    def across(total, width, body):
        def step(i, _):
            body(at(i, width))
            return 0

        lax.fori_loop(0, total // width, step, 0)

    def down_rows(start, count, size, body):
        def step(i, _):
            body(pl.ds(pl.multiple_of(start + i * size, size), size), pl.ds(pl.multiple_of(i * size, size), size))
            return 0

        lax.fori_loop(0, count // size, step, 0)

    def head(k, mixed):
        job, h = k // hq, lax.rem(k, hq)
        run = job + per if mixed else job - per
        diff = iota((RUN, RUN), 1) - iota((RUN, RUN), 0)
        rows, cols = at(run), at(h, PAD)
        g = h // rep
        q = q_ref[rows, cols]
        lim = limit(run)
        top = None
        for b in range(blocks):
            t = mm_nt(q, k_s[g, pl.ds(b * RUN, RUN), :]) * scale
            room = lim - pos_ref[0, 2 * RUN * b]
            if mixed:
                t = t + jnp.where(room >= 0, 0.0, NEG)
            else:
                t = jnp.where(diff <= room, t, NEG)
            s_s[:, b * RUN : (b + 1) * RUN] = t
            top = t if top is None else jnp.maximum(top, t)
        if mixed:
            crow = at(run - per)
            kc = kvc_ref[crow, at(g, PAD)]
            vc = kvc_ref[crow, at(hk + g, PAD)]
            vc = jnp.where(lane == 48, 1.0, vc.astype(F32)).astype(BF)
            t = jnp.where(diff <= 0, mm_nt(q, kc) * scale, NEG)
            s_s[:, blocks * RUN :] = t
            top = jnp.maximum(top, t)
        m = jnp.max(top, axis=1, keepdims=True)
        acc = None
        for b in range(blocks):
            p = jnp.exp2(s_s[:, b * RUN : (b + 1) * RUN] - m).astype(BF)
            o = mm(p, v_s[g, pl.ds(b * RUN, RUN), :])
            acc = o if acc is None else acc + o
        if mixed:
            p = jnp.exp2(s_s[:, blocks * RUN :] - m).astype(BF)
            acc = acc + mm(p, vc)
        total = acc[:, 48:49]
        op_v[rows, cols] = (acc / total).astype(BF)
        lse = jnp.broadcast_to(m + jnp.log2(total), (RUN, PAD)).T
        lse_v[at(run * hq + h, 8), :] = lse[0:8, :]

        @pl.when(h == hq - 1)
        def _():
            o = mm_nt(op_v[rows, :], pad_matrix(hq)).astype(BF)
            o_v[rows, :] = o


            def out(cols):
                pbuf[at(job), cols] = mm(o, wo_ref[:, cols]).astype(BF)

            across(d, 512, out)

    first = runs * hq

    def ffn(k):
        job = (k - first) // 4
        part = lax.rem(k - first, 4)
        run = lax.rem(job + per, runs)
        rows = at(run)

        @pl.when(k == first)
        def _():
            for cp in loads:
                cp.wait()

        @pl.when(part == 0)
        def _():
            def norm(to, sub):
                srows = pl.ds(pl.multiple_of(job * RUN + sub.start, 32), 32)
                mid = xs[to, :].astype(F32) + obuf[srows, :].astype(F32)
                r = lax.rsqrt(jnp.mean(mid * mid, axis=-1, keepdims=True) + norm_eps)
                n2[to, :] = (mid * r * gf_ref[8:9, :]).astype(BF)

            down_rows(run * RUN, RUN, 32, norm)

            def gate(cols):
                s_s[:, cols] = mm(n2[rows, :], wg[:, cols])

            across(ff, 512, gate)

        @pl.when(part == 1)
        def _():
            def up(i, _):
                s_s[:, pl.ds(pl.multiple_of(ff + i * 512, 512), 512)] = mm(n2[rows, :], wu[:, at(i, 512)])
                return 0

            lax.fori_loop(0, ff // 512, up, 0)

        @pl.when(part == 2)
        def _():
            def gated(i, _):
                cols = at(i)
                dhid = mm_nt(ys[rows, :], wd[cols, :])
                gate, up = s_s[:, cols], s_s[:, pl.ds(pl.multiple_of(ff + i * RUN, RUN), RUN)]
                sig = jax.nn.sigmoid(gate)
                silu = gate * sig
                hid[rows, cols] = (silu * up).astype(BF)
                dg[rows, cols] = (dhid * up * sig * (1.0 + gate * (1.0 - sig))).astype(BF)
                du[rows, cols] = (dhid * silu).astype(BF)
                return 0

            lax.fori_loop(0, ff // RUN, gated, 0)

        @pl.when(part == 3)
        def _():
            line.sent(job)

            def normed_two(cols):
                pbuf[at(job), cols] = (mm_nt(dg[rows, :], wg[cols, :]) + mm_nt(du[rows, :], wu[cols, :])).astype(BF)

            across(d, 512, normed_two)
            cp = pltpu.make_async_copy(st_o, fp_h.at[at(job)], osem.at[0])

            @pl.when(job > 0)
            def _():
                cp.wait()

            def project(cols):
                st_o[:, cols] = mm(hid[rows, :], wd[:, cols]).astype(BF)

            across(d, 512, project)
            cp.start()

    second = first + 4 * runs

    def stage(st, sem, dst, value, busy=True):
        cp = pltpu.make_async_copy(st, dst, sem)
        if busy is True:
            cp.wait()
        else:
            pl.when(busy)(cp.wait)

        def fill(cols):
            st[:, cols] = value(cols)

        across(d, 512, fill)
        cp.start()

    def grads_down(k):
        i = k - second
        for j in range(2):
            cols = at(2 * i + j)
            ht = hid[:, cols].T
            stage(st_o, osem.at[0], gds_h.at[cols], lambda to: mm(ht, ys[:, to]).astype(BF))

    def grads_up(k):
        i = k - second - 2
        for j in range(2):
            cols = at(2 * i + j)
            nt = n2[:, cols].T


            def both(to):
                wg[cols, to] = mm(nt, dg[:, to]).astype(BF)
                wu[cols, to] = mm(nt, du[:, to]).astype(BF)

            across(ff, 512, both)

    back = second + 5

    def middle(k):
        job = (k - back) // 5
        run = lax.rem(job + per, runs)
        rows = at(run)
        cp = pltpu.make_async_copy(s_s.at[:, pl.ds(0, d)], dm_h.at[rows], osem.at[1])

        @pl.when(job > 0)
        def _():
            cp.wait()

        def one(to, sub):
            def there(base):
                return pl.ds(pl.multiple_of(base + sub.start, 32), 32)

            mid = xs[to, :].astype(F32) + obuf[there(job * RUN), :].astype(F32)
            r = lax.rsqrt(jnp.mean(mid * mid, axis=-1, keepdims=True) + norm_eps)
            dn = obuf[there((runs + job) * RUN), :].astype(F32)
            w = gf_ref[8:9, :] * dn
            inner = jnp.mean(w * mid, axis=-1, keepdims=True)
            dm = ys[to, :].astype(F32) + r * w - mid * (r * r * r) * inner
            s_s[sub, 0:d] = dm
            gpart[8:16, :] += jnp.sum((dn * mid * r).reshape(4, 8, d), axis=0)
            ys[to, :] = dm.astype(BF)

        down_rows(run * RUN, RUN, 32, one)
        cp.start()
        do = mm_nt(ys[rows, :], wo_ref[...]).astype(BF)
        do_v[rows, :] = mm(do, pad_matrix(hq)).astype(BF)

    width = rep * RUN

    def pair(k, mixed):
        job = (k - back) // 5
        idx = lax.rem(k - back, 5) - 1
        g, part = idx // 2, lax.rem(idx, 2)
        run = lax.rem(job + per, runs)
        rows = at(run)
        diff = iota((RUN, width), 0) - (iota((RUN, width), 1) & (RUN - 1))

        def stack(ref):
            return jnp.concatenate([ref[rows, at(g * rep + j, PAD)] for j in range(rep)], axis=0)

        q, do = stack(q_ref), stack(do_v)

        @pl.when(part == 0)
        def _():
            op = stack(op_v)
            delta_s[0:1, :] = jnp.sum((do.astype(F32) * op.astype(F32)).T, axis=0, keepdims=True)
            dq_s[...] = jnp.zeros_like(dq_s)

        delta = delta_s[0:1, :]
        lse = jnp.concatenate(
            [lse_v[pl.ds(pl.multiple_of((run * hq + g * rep + j) * 8, 8), 1), :] for j in range(rep)], axis=1
        )
        lim = limit(run)

        def tile(kk, vv, hide):
            p = jnp.exp2(hide(mm_nt(kk, q) * scale - lse))
            ds = (p * (mm_nt(vv, do) - delta)).astype(BF)
            return mm(ds, q), mm(p.astype(BF), do), mm_tn(ds, kk)

        dq = dq_s[...]
        for bb in range(blocks // 2):
            b = part * (blocks // 2) + bb
            room = lim - pos_ref[0, 2 * RUN * b]
            if mixed:
                hide = lambda t: t + jnp.where(room >= 0, 0.0, NEG)
            else:
                hide = lambda t: jnp.where(diff <= room, t, NEG)
            dk, dv, dd = tile(k_s[g, at(b), :], v_s[g, at(b), :], hide)
            dk_s[g, at(b), :] += dk
            dv_s[g, at(b), :] += dv
            dq = dq + dd
        dq_s[...] = dq

        @pl.when(part == 1)
        def _():
            total = dq_s[...]
            ct, st = rope_tables(run, per, pos_ref, cb_ref, sb_ref, cj_ref, sj_ref)
            if mixed:
                crow = at(run - per)
                dk, dv, dd = tile(kvc_ref[crow, at(g, PAD)], kvc_ref[crow, at(hk + g, PAD)], lambda t: jnp.where(diff <= 0, t, NEG))
                total = total + dd
                dkv_s[rows, at(g, PAD)] = rope_back(dk * score, ct, st).astype(BF)
                dkv_s[rows, at(hk + g, PAD)] = dv.astype(BF)
            for j in range(rep):
                dqp[rows, at(g * rep + j, PAD)] = rope_back(total[j * RUN : (j + 1) * RUN] * score, ct, st).astype(BF)

    def spare(ref, r0, c0, rows, cols, across, count):
        return [ref.at[pl.ds(r0 + i // across * rows, rows), pl.ds(c0 + i % across * cols, cols)] for i in range(count)]

    def square(i, rows, cols, src, mine, theirs, views, out):
        return Square(rows, cols, src, mine, theirs, views, out, credits.at[i], shard_send.at[i], shard_recv.at[i], send.at[i], recv.at[i], store.at[i])

    q4, w4 = dh // 4, ff // 2
    sq_g = square(0, dh, ff, wg.at[yours], wg.at[own], dg.at[pl.ds(0, dh)], spare(n2, 0, 0, q4, w4, 2, 6), gg_h)
    left = spare(n2, 0, 2 * w4, q4, w4, 1, 3) + spare(n2, 3 * q4, 0, q4, w4, 3, 3)
    sq_u = square(1, dh, ff, wu.at[yours], wu.at[own], du.at[pl.ds(0, dh)], left, gu_h)
    f4, d4 = ff // 4, dh // 2
    sq_d = square(2, ff, dh, gds_h.at[:, yours], hid.at[:, pl.ds(0, dh)], gt,
                  spare(n2, dh, 0, f4, d4, 4, 4) + spare(dg, dh, 0, f4, d4, 2, 2), gd_h)
    dq_cols = hq * HEAD_SIZE
    sq_o = square(3, dq_cols, dh, go_v.at[1 - s], go_v.at[s], wg.at[pl.ds(0, dq_cols), pl.ds(0, dh)],
                  spare(wg, dq_cols, 0, dq_cols // 4, d4, 2, 6), go_h)
    gw_cols = dq_cols + wide
    sq_w = square(4, dh, gw_cols, wu.at[yours, pl.ds(0, gw_cols)], wu.at[own, pl.ds(0, gw_cols)], hid.at[pl.ds(0, dh), pl.ds(0, gw_cols)],
                  spare(gt, 0, 0, q4, gw_cols // 2, 2, 6), gw_h)
    down_load = pltpu.make_async_copy(gds_h.at[:, own], hid.at[:, pl.ds(0, dh)], lsem.at[5])
    wp_load = pltpu.make_async_copy(wp_h, wd, lsem.at[6])

    def f_load(job):
        return pltpu.make_async_copy(fp_h.at[at(job)], pbuf.at[at(job)], fsem.at[job])

    def f_start(job):
        line.sent(4 + job)
        f_load(job).start()

    def key_piece(b):
        return ys.at[pl.ds(pl.multiple_of(lax.rem(b, 4) * RUN, RUN), RUN), pl.ds(pl.multiple_of(b // 4 * wide, wide), wide)]

    def key_recv(i, run):
        m = (i - 1) * per + run
        return ys.at[pl.ds(m % 4 * RUN, RUN), pl.ds(dh + m // 4 * wide, wide)]

    def key_copy(i, run):
        to = lax.rem(c + i, nc)
        return remote(key_piece(to * per + run), key_recv(i, run), qsend.at[i, run], qrecv.at[i, run], {"context": to})

    def grad_out(j):
        ot = o_v[...].T

        def part(cols):
            go_v[j, :, cols] = mm(ot, ys[:, pl.ds(pl.multiple_of(j * dh + cols.start, RUN), RUN)]).astype(BF)

        across(dh, RUN, part)

    def pack():
        for i in range(1, nc):
            pl.semaphore_signal(credits.at[5], inc=1, device_id={"context": lax.rem(c + i, nc)}, device_id_type=MESH)

        def one(b, _):
            rows = at(b)
            parts = [(dk_s[g, rows, :] * score).astype(BF) for g in range(hk)]
            parts += [dv_s[g, rows, :].astype(BF) for g in range(hk)]
            value = mm_nt(jnp.concatenate(parts, axis=1), pad_matrix(2 * hk)).astype(BF)
            key_piece(b)[...] = value
            return 0

        lax.fori_loop(0, blocks, one, 0)
        pl.semaphore_wait(credits.at[5], nc - 1)
        for run in range(per):
            for i in range(1, nc):
                key_copy(i, run).start()

    def normed(job):
        rows = at(lax.rem(job + per, runs))
        line.sent(8 + job + jnp.where(job == 3, 1, 0))
        line.sent(4 + job, fwd=False, ret=True)

        def part(cols):
            dn = mm(dqp[rows, :], wd[0:nq, cols]) + mm(dkv_s[rows, :], wd[nq:, cols])
            pbuf[at(job), cols] = dn.astype(BF)

        across(d, 512, part)

    def keys(run):
        for i in range(1, nc):
            key_copy(i, run).wait_recv()
        selkv = pad_matrix(2 * hk)
        rows = pl.ds(run * RUN, RUN)
        total = mm(key_piece(c * per + run)[...], selkv)
        for i in range(1, nc):
            total = total + mm(key_recv(i, run)[...], selkv)
        ct, st = rope_tables(run, per, pos_ref, cb_ref, sb_ref, cj_ref, sj_ref)
        for g in range(hk):
            dkv_s[rows, g * PAD : (g + 1) * PAD] = rope_back(total[:, g * PAD : (g + 1) * PAD], ct, st).astype(BF)
        dkv_s[rows, hk * PAD :] = total[:, hk * PAD :].astype(BF)

    tile_v = hid.at[:, pl.ds(dh, RUN)]

    def tile_load(i):
        return pltpu.make_async_copy(n1_h.at[:, at(i)], tile_v, nsem)

    def grads_in(k):
        i = k - into

        @pl.when(i == 0)
        def _():
            def pack_rows(to, sub):
                du[to, 0:dq_cols] = mm_nt(dqp[to, :], pad_matrix(hq)).astype(BF)
                du[to, dq_cols:gw_cols] = mm_nt(dkv_s[to, :], pad_matrix(2 * hk)).astype(BF)

            down_rows(0, rows_here, RUN, pack_rows)

        for j in range(2):
            tile_load(2 * i + j).wait()
            nt = tile_v[...].T


            def part(cols, j=j):
                wu[at(2 * i + j), cols] = mm(nt, du[:, cols]).astype(BF)

            across(gw_cols, gw_cols // 2, part)

            @pl.when(2 * i + j + 1 < d // RUN)
            def _():
                tile_load(2 * i + j + 1).start()

    def halves(i, body):
        for j in range(2):

            def step(m, _, j=j):
                natural = pl.ds(pl.multiple_of(j * half + i * 128 + m * 32, 32), 32)
                by_job = lambda part: pl.ds(pl.multiple_of(part * rows_here + (1 - j) * half + i * 128 + m * 32, 32), 32)
                body(natural, by_job, pl.ds(pl.multiple_of(j * 128 + m * 32, 32), 32))
                return 0

            lax.fori_loop(0, 4, step, 0)

    def output(k):
        i = k - outs

        def one(natural, by_job, to):
            total = xs[natural, :].astype(F32) + obuf[by_job(0), :].astype(F32)
            st_p[to, :] = (total + obuf[by_job(2), :].astype(F32)).astype(BF)

        halves(i, one)
        stage(st_o, osem.at[0], out_h.at[at(i)], lambda cols: mm(merge_matrix(), st_p[:, cols]).astype(BF), i > 0)

    def m_load(i, j):
        src = dm_h.at[pl.ds(pl.multiple_of(j * half + i * 128, 128), 128)]
        return pltpu.make_async_copy(src, s_s.at[pl.ds(j * 128, 128), pl.ds(0, d)], msem.at[j])

    def finals(i):
        for j in range(2):
            m_load(i, j).wait()

        def one(natural, by_job, to):
            x = xs[natural, :].astype(F32)
            dn = obuf[by_job(1), :].astype(F32)
            r = lax.rsqrt(jnp.mean(x * x, axis=-1, keepdims=True) + norm_eps)
            w = gf_ref[0:1, :] * dn
            inner = jnp.mean(w * x, axis=-1, keepdims=True)
            st_p[to, :] = (s_s[to, 0:d] + (r * w - x * (r * r * r) * inner)).astype(BF)
            gpart[0:8, :] += jnp.sum((dn * x * r).reshape(4, 8, d), axis=0)

        halves(i, one)

        @pl.when(i + 1 < runs)
        def _():
            for j in range(2):
                m_load(i + 1, j).start()

        cp = pltpu.make_async_copy(st_t, tg_h.at[at(i)], osem.at[2])

        @pl.when(i > 0)
        def _():
            cp.wait()

        def fill(cols):
            st_t[:, cols] = mm(merge_matrix(), st_p[:, cols]).astype(BF)

        across(d, 512, fill)
        cp.start()

    packed = back + 5 * runs
    into = packed + 4
    outs = into + 4
    lag = hq - 1

    def due(job):
        return (line.per * (job + 1) - 1 + line.turn) // line.ticks + lag + 1

    begins = [back + 5 * job for job in range(runs)]
    items = [([(0, per * hq)], lambda k: head(k, True)), ([(per * hq, first)], lambda k: head(k, False)), ([(first, second)], ffn),
             ([(second, second + 2)], grads_down), ([(second + 2, back)], grads_up), ([(b, b + 1) for b in begins], middle),
             ([(b + 1, b + 5) for b in begins[:per]], lambda k: pair(k, True)),
             ([(b + 1, b + 5) for b in begins[per:]], lambda k: pair(k, False)),
             ([(into, into + 3)], grads_in), ([(outs, outs + runs)], output)]
    fin = due(Line.D_AT[per])

    def begin_down():
        pltpu.make_async_copy(st_o, gds_h.at[pl.ds(0, RUN)], osem.at[0]).wait()
        down_load.start()
        wp_load.start()

    def free_three():
        for sq in (sq_g, sq_u, sq_d):
            sq.free()
        for sq in (sq_d, sq_g, sq_u):
            sq.e0()

    def store_start(sq):
        def body():
            sq.e5()
            sq.store().start()

        return body

    def dm_begin():
        pltpu.make_async_copy(s_s.at[:, pl.ds(0, d)], dm_h.at[pl.ds(0, RUN)], osem.at[1]).wait()
        for j in range(2):
            m_load(0, j).start()

    def first_e1():
        down_load.wait()
        sq_d.e1()

    def give_o():
        sq_g.store().wait()
        sq_g.done()
        sq_o.free()

    def give_w():
        sq_d.store().wait()
        sq_d.done()
        sq_w.free()

    def release_u():
        sq_u.store().wait()
        sq_u.done()

    def number(k, steps):
        return sum(jnp.where(k >= step, 1, 0) for step in steps[1:])

    events = [(second + 2, begin_down), (second + 4, free_three)]
    at_f = [4 * Line.F_AT[job] + lag - 2 for job in range(runs)]
    events += [
        (38, first_e1), (40, sq_g.e1), (41, sq_d.e2), (42, sq_u.e1), (43, sq_g.e2), (44, sq_d.e3), (45, wp_load.wait), (46, sq_u.e2), (47, sq_g.e3),
        (48, sq_d.e4), (49, sq_u.e3), (50, sq_g.e4), (52, store_start(sq_d)), (53, sq_u.e4), (54, give_w), (55, store_start(sq_g)),
        (57, store_start(sq_u)), (57, give_o), (59, release_u),
        (53, lambda: grad_out(0)), (54, lambda: grad_out(1)), (packed, pack), (packed, lambda: tile_load(0).start()), (packed, dm_begin), (packed + 2, lambda: keys(0)), (packed + 2, sq_o.e0), (packed + 3, lambda: keys(1)),
        (61, sq_o.e1), (63, sq_o.e2), (64, sq_w.e0), (65, sq_w.e1), (65, sq_o.e3), (67, sq_w.e2), (67, sq_o.e4), (68, sq_w.e3),
        (69, store_start(sq_o)), (70, sq_w.e4), (73, store_start(sq_w)),
    ]
    items += [([(k, k + 1)], functools.partial(lambda e, k: e(), e)) for k, e in events]
    at_normed = (45, 50, packed + 2, packed + 4)
    items.append(([(k, k + 1) for k in at_f], lambda k: f_start(number(k, at_f))))
    items.append(([(k + 1, k + 2) for k in at_f], lambda k: f_load(number(k, at_f)).wait()))
    items.append(([(k, k + 1) for k in at_normed], lambda k: normed(number(k, at_normed))))
    end = -(-line.slots // line.ticks) + lag
    items.append(([(fin, fin + 2), (end, end + 2)], lambda k: finals(jnp.where(k < end, k - fin, k - end + 2))))

    def serve(k):
        def tick(j, _):
            line.serve(line.ticks * (k - lag) + j)
            return 0

        lax.fori_loop(0, line.ticks, tick, 0)

    run_items(items, serve)
    me = s * nc + c
    sums = jnp.concatenate(
        [jnp.broadcast_to(jnp.sum(gpart[k * 8 : (k + 1) * 8, :], axis=0, keepdims=True), (8, d)) for k in range(2)], axis=0
    )
    grecv[me] = sums
    gcopies = []
    for i, t in enumerate(peers):
        cp = remote(grecv.at[me], grecv.at[me], gs.at[i], gr.at[i], t)
        cp.start()
        gcopies.append(cp)

    def rest(job, _):
        line.sent(jnp.where(job < runs, job, job + runs), fwd=False, ret=True)
        return 0

    lax.fori_loop(0, 3 * runs, rest, 0)
    for job in Line.D_AT:
        line.sent(job)
    for sq in (sq_o, sq_w):
        sq.store().wait()
        sq.done()
    for i in range(1, nc):
        for run in range(per):
            key_copy(i, run).wait_send()
    pltpu.make_async_copy(st_o, out_h.at[pl.ds(0, RUN)], osem.at[0]).wait()
    pltpu.make_async_copy(st_t, tg_h.at[pl.ds(0, RUN)], osem.at[2]).wait()
    for cp in gcopies:
        cp.wait()
    total = grecv[0]
    for i in range(1, 2 * nc):
        total = total + grecv[i]
    gpart[...] = total
    gains_ref[...] = gpart[:, own]


def finish_kernel(out_h, tg_h, gw_h, go_h, gg_h, gu_h, gd_h, out_f, tg_f, gq_f, gk_f, gv_f, go_f, gg_f, gu_f, gd_f,
                  out_v, tg_v, gw_v, go_v, gg_v, gu_v, gd_v, q_v, kv_v, o_v, g_v, u_v, d_v, lsem, ssem):
    kw = gk_f.shape[0]
    nq = gw_h.shape[1] - 2 * kw
    pairs = [(gg_h, gg_v), (gu_h, gu_v), (gd_h, gd_v), (gw_h, gw_v), (go_h, go_v), (out_h, out_v), (tg_h, tg_v)]
    loads = [pltpu.make_async_copy(a, b, lsem.at[i]) for i, (a, b) in enumerate(pairs)]
    for cp in loads:
        cp.start()
    stores = [
        pltpu.make_async_copy(a, b, ssem.at[i])
        for i, (a, b) in enumerate([(g_v, gg_f), (u_v, gu_f), (d_v, gd_f), (q_v, gq_f), (kv_v.at[0:kw], gk_f), (kv_v.at[kw:], gv_f),
                                    (o_v, go_f), (out_v, out_f), (tg_v, tg_f)])
    ]

    def widen(src, dst, width):
        def step(i, _):
            rows = pl.ds(pl.multiple_of(i * 32, 32), 32)
            dst[rows, :] = src[rows, 0:width].astype(F32)
            return 0

        lax.fori_loop(0, src.shape[0] // 32, step, 0)

    for i, (src, dst) in enumerate([(gg_v, g_v), (gu_v, u_v), (gd_v, d_v)]):
        loads[i].wait()
        widen(src, dst, src.shape[1])
        stores[i].start()
    loads[5].wait()
    stores[7].start()
    loads[6].wait()
    stores[8].start()
    loads[3].wait()
    widen(gw_v, q_v, nq)
    stores[3].start()
    for i in range(gw_v.shape[0] // PAD):
        kv_v[:, i * PAD : (i + 1) * PAD] = gw_v[i * PAD : (i + 1) * PAD, nq:].astype(F32).T
    stores[4].start()
    stores[5].start()
    loads[4].wait()
    widen(go_v, o_v, go_v.shape[1])
    stores[6].start()
    for cp in stores:
        cp.wait()


def fast(
    tokens, w_query, key_weight, value_weight, w_out, w_gate, w_up, w_down, gain_attn, gain_ffn, segments, positions, cotangent, n, nc
):
    _, rows, d = tokens.shape
    half = rows // 2
    runs = rows // RUN
    per = runs // 2
    prompt = segments.shape[1] // 2
    blocks = prompt // RUN
    dq, dk = w_query.shape[1], key_weight.shape[1]
    hq, hk = dq // HEAD_SIZE, dk // HEAD_SIZE
    nq, nk = hq * PAD, hk * PAD
    ff = w_gate.shape[1]
    dh = d // 2
    x = tokens.reshape(rows, d)
    dy = cotangent.reshape(rows, d)
    freq = np.exp(np.arange(HEAD_SIZE // 2, dtype=np.float32) * np.float32(-2.0 * math.log(rope_base) / HEAD_SIZE)).astype(np.float32)
    lanes = np.zeros((PAD,), np.float32)
    lanes[0:48] = freq
    lanes[64:112] = freq
    sign = np.where(np.arange(PAD) < 64, -1.0, 1.0).astype(np.float32)
    inner = np.arange(RUN, dtype=np.float64)[:, None] * lanes[None, :].astype(np.float64)
    cj = jnp.asarray(np.cos(inner).astype(np.float32))
    sj = jnp.asarray((np.sin(inner) * sign).astype(np.float32))
    starts = np.arange(16, dtype=np.float64)[:, None] * RUN * lanes[None, :].astype(np.float64)
    cb = jnp.asarray(np.cos(starts).astype(np.float32))
    sb = jnp.asarray((np.sin(starts) * sign).astype(np.float32))
    gains = jnp.where(np.arange(2)[:, None] == 0, gain_attn[None, :], gain_ffn[None, :]).astype(F32)

    V = pl.BlockSpec(memory_space=pltpu.VMEM)
    S = pl.BlockSpec(memory_space=pltpu.SMEM)
    A = pl.BlockSpec(memory_space=pl.ANY)
    sds = jax.ShapeDtypeStruct
    DMA = pltpu.SemaphoreType.DMA

    def call(kernel, ins, outs, scratch, collective=None, flops=0):
        params = dict(vmem_limit_bytes=VLIM - 64 * 1024)
        if collective is not None:
            params.update(collective_id=collective, has_side_effects=True)
        args = [a for a, _ in ins]
        return pl.pallas_call(
            kernel,
            out_shape=[o for o, _ in outs],
            in_specs=[sp for _, sp in ins],
            out_specs=[sp for _, sp in outs],
            scratch_shapes=scratch,
            compiler_params=pltpu.CompilerParams(**params),
            cost_estimate=pl.CostEstimate(flops=flops, bytes_accessed=0, transcendentals=0),
        )(*args)

    rope_in = [(positions, S), (cb, V), (sb, V), (cj, V), (sj, V)]
    xp, dyp, n1, q, kvp, kvc, wp, gf, wo, wg, wu, wd = call(
        functools.partial(first_kernel, nc),
        [(x, V), (dy, A), (gains, V)] + rope_in + [(w_query, A), (key_weight.T, A), (value_weight.T, A), (w_out, A), (w_gate, A), (w_up, A), (w_down, A)],
        [
            (sds((rows, d), BF), A), (sds((rows, d), BF), A), (sds((rows, d), BF), A), (sds((rows, nq), BF), V),
            (sds((prompt, 2 * dk), BF), A), (sds((half, 2 * nk), BF), V), (sds((nq + 2 * nk, d), BF), A), (sds((16, d), F32), V),
            (sds((dq, d), BF), A), (sds((d, ff), BF), A), (sds((d, ff), BF), A), (sds((ff, d), BF), A),
        ],
        [
            pltpu.VMEM((rows, d), BF), pltpu.VMEM((rows, d), BF), pltpu.VMEM((rows, d), BF), pltpu.VMEM((nq + 2 * nk, d), BF),
            pltpu.VMEM((rows, d), BF), pltpu.VMEM((d, dq), BF), pltpu.VMEM((dk, d), BF), pltpu.VMEM((dk, d), BF), pltpu.VMEM((16, d), F32),
            pltpu.VMEM((dq, dh), BF), pltpu.VMEM((dh, ff), BF), pltpu.VMEM((dh, ff), BF), pltpu.VMEM((ff, dh), BF),
            pltpu.VMEM((half, 2 * dk), BF),
            DMA((9,)), DMA((8,)), DMA((8,)), DMA((4,)), DMA((per, nc)), DMA((per, nc)), DMA((4,)),
        ],
        collective=0, flops=60 * 10**9,
    )

    chunk = 16
    count = 16 * (RUN // 2 // chunk)
    U = pltpu.VMEM((rows, d), BF)
    W = pltpu.VMEM((d, ff), BF)
    H = pltpu.VMEM((rows, ff), BF)
    KV = pltpu.VMEM((hk, prompt, PAD), BF)
    KVF = pltpu.VMEM((hk, prompt, PAD), F32)
    width = hq // hk * RUN
    out, tg, gg, gu, gd, go, gw, _, _, _, gains_grad = call(
        functools.partial(main_kernel, n, nc, chunk),
        [(segments, S)] + rope_in
        + [(gf, V), (q, V), (kvc, V), (wo, V), (kvp, A), (xp, A), (dyp, A), (wg, A), (wu, A), (wd, A), (n1, A), (wp, A)],
        [(sds((rows, d), BF), A), (sds((rows, d), BF), A), (sds((dh, ff), BF), A), (sds((dh, ff), BF), A), (sds((ff, dh), BF), A),
         (sds((dq, dh), BF), A), (sds((dh, dq + 2 * dk), BF), A), (sds((rows, d), F32), A), (sds((ff, d), BF), A), (sds((rows, d), BF), A),
         (sds((16, dh), F32), V)],
        [KV, KV, pltpu.VMEM((RUN, prompt + RUN), F32), pltpu.VMEM((rows, dq), BF), pltpu.VMEM((rows, nq), BF), pltpu.VMEM((runs * hq * 8, RUN), F32),
         U, U, U, U, pltpu.VMEM((3 * rows, d), BF), pltpu.VMEM((ff, d), BF), U, W, W, H, H, H, pltpu.VMEM((ff, dh), BF),
         KVF, KVF, pltpu.VMEM((rows, nq), BF), pltpu.VMEM((width, PAD), F32), pltpu.VMEM((8, width), F32), pltpu.VMEM((rows, nq), BF),
         pltpu.VMEM((rows, 2 * nk), BF), pltpu.VMEM((2, dq, dh), BF), pltpu.VMEM((RUN, d), BF), pltpu.VMEM((RUN, d), BF), pltpu.VMEM((RUN, d), BF),
         pltpu.VMEM((16, d), F32), pltpu.VMEM((2 * nc, 16, d), F32),
         DMA((7,)), DMA((blocks,)), DMA((3,)), DMA((runs,)), DMA((2,)), DMA, DMA((nc, per)), DMA((nc, per)), DMA((2 * nc - 1,)), DMA((2 * nc - 1,))]
        + [DMA((2, count))] * 4
        + [pltpu.SemaphoreType.REGULAR((6,)), DMA((5,)), DMA((5,)), DMA((5, 3, 2, 2)), DMA((5, 3, 2, 2)), DMA((5,))],
        collective=1, flops=300 * 10**9,
    )
    shapes = [(rows, d), (rows, d), (dh, dq + 2 * dk), (dq, dh), (dh, ff), (dh, ff), (ff, dh)]
    wide = [(dh, dq), (2 * dk, dh), (dq, dh), (dh, ff), (dh, ff), (ff, dh)]
    finals = [(dh, dq), (dk, dh), (dk, dh), (dq, dh), (dh, ff), (dh, ff), (ff, dh)]
    out, tg, gq, gk, gv, go, gg, gu, gd = call(
        finish_kernel,
        [(a, A) for a in (out, tg, gw, go, gg, gu, gd)],
        [(sds((rows, d), BF), A), (sds((rows, d), BF), A)] + [(sds(shape, F32), A) for shape in finals],
        [pltpu.VMEM(shape, BF) for shape in shapes] + [pltpu.VMEM(shape, F32) for shape in wide] + [DMA((7,)), DMA((9,))],
    )
    return out[None], tg[None], gq, gk.T, gv.T, go, gg, gu, gd, gains_grad[0], gains_grad[8]


def body(mesh, *args):
    tokens, w_query, segments = args[0], args[1], args[10]
    n, nc = mesh.shape["tensor"], mesh.shape["context"]
    rows = tokens.shape[1]
    if (tokens.shape[0] == 1 and rows % (4 * CLEN) == 0 and n == 4 and nc == 4 and mesh.shape["shard"] == 2
            and segments.shape[1] == rows * nc):
        return fast(*args, n, nc)
    return general(*args)


def solution(mesh):
    in_specs = (
        P("shard", "context", None),
        P("shard", "tensor"),
        P("shard", "tensor"),
        P("shard", "tensor"),
        P("tensor", "shard"),
        P("shard", "tensor"),
        P("shard", "tensor"),
        P("tensor", "shard"),
        P("shard"),
        P("shard"),
        P("shard", None),
        P("shard", None),
        P("shard", "context", None),
    )
    out_specs = (
        P("shard", "context", None),
        P("shard", "context", None),
        P("shard", "tensor"),
        P("shard", "tensor"),
        P("shard", "tensor"),
        P("tensor", "shard"),
        P("shard", "tensor"),
        P("shard", "tensor"),
        P("tensor", "shard"),
        P("shard"),
        P("shard"),
    )
    return jax.shard_map(functools.partial(body, mesh), mesh=mesh, in_specs=in_specs, out_specs=out_specs, check_vma=False)
```

```python
import functools
import math

import jax
import jax.numpy as jnp
import numpy as np
from jax import lax
from jax.experimental import pallas as pl
from jax.experimental.pallas import tpu as pltpu
from jax.sharding import PartitionSpec as P

HEAD_SIZE = 96
CLEN = 256


rope_base = 100000.0
norm_eps = 1e-05


def tables(positions):
    half_width = HEAD_SIZE // 2
    frequency = jnp.exp(
        jnp.arange(half_width, dtype=jnp.float32) * (-2.0 * math.log(rope_base) / HEAD_SIZE)
    )
    angles = positions.astype(jnp.float32)[:, None] * frequency[None, :]
    return (jnp.cos(angles)[:, None, :], jnp.sin(angles)[:, None, :])


def rotary_apply(heads, cosine_table, sine_values):
    half_width = HEAD_SIZE // 2
    front_half = heads[..., :half_width]
    back_half = heads[..., half_width:]
    return jnp.concatenate(
        [
            front_half * cosine_table - back_half * sine_values,
            back_half * cosine_table + front_half * sine_values,
        ],
        axis=-1,
    )


def rotate_back(heads, cosine_table, sine_values):
    half_width = HEAD_SIZE // 2
    front_half = heads[..., :half_width]
    back_half = heads[..., half_width:]
    return jnp.concatenate(
        [
            front_half * cosine_table + back_half * sine_values,
            back_half * cosine_table - front_half * sine_values,
        ],
        axis=-1,
    )


def contract_rows(left, right):
    return lax.dot_general(
        left, right, (((0,), (0,)), ((), ())), preferred_element_type=jnp.float32
    )


def contract_cols(left, right):
    return lax.dot_general(
        left, right, (((1,), (1,)), ((), ())), preferred_element_type=jnp.float32
    )


def norm_back(tok_rows, norm_scale, gain, grad_normed):
    weighted = gain * grad_normed
    inner = jnp.mean(weighted * tok_rows, axis=-1, keepdims=True)
    grad_rows = norm_scale * weighted - tok_rows * (norm_scale * norm_scale * norm_scale) * inner
    grad_gain = jnp.sum(grad_normed * tok_rows * norm_scale, axis=0)
    return (grad_rows, grad_gain)


def visible(seg_query, pos_query, seg_keys, pos_keys):
    own = (seg_keys[None, :] == seg_query[:, None]) & (pos_keys[None, :] <= pos_query[:, None])
    branch = (
        (seg_keys[None, :] == 0)
        & (seg_query[:, None] > 0)
        & (pos_keys[None, :] < seg_query[:, None] * CLEN)
    )
    return own | branch


def general(
    tokens,
    w_query,
    key_weight,
    value_weight,
    w_out,
    w_gate,
    w_up,
    w_down,
    gain_attn,
    gain_ffn,
    segments,
    positions,
    cotangent,
):
    groups, tok_local, model_width = tokens.shape
    token_count = groups * tok_local
    heads_here = w_query.shape[1] // HEAD_SIZE
    kv_here = key_weight.shape[1] // HEAD_SIZE
    per_kv = heads_here // kv_here
    kv_width = kv_here * HEAD_SIZE
    score_scale = 1.0 / math.sqrt(HEAD_SIZE)
    context_index = lax.axis_index("context")
    first_row = context_index * tok_local
    seg_here = lax.dynamic_slice_in_dim(segments, first_row, tok_local, 1)
    pos_here = lax.dynamic_slice_in_dim(positions, first_row, tok_local, 1)
    w_query, key_weight, value_weight, w_gate, w_up, gain_attn, gain_ffn = (
        lax.all_gather(w_query, "shard", axis=0, tiled=True),
        lax.all_gather(key_weight, "shard", axis=0, tiled=True),
        lax.all_gather(value_weight, "shard", axis=0, tiled=True),
        lax.all_gather(w_gate, "shard", axis=0, tiled=True),
        lax.all_gather(w_up, "shard", axis=0, tiled=True),
        lax.all_gather(gain_attn, "shard", axis=0, tiled=True),
        lax.all_gather(gain_ffn, "shard", axis=0, tiled=True),
    )
    w_out, w_down = (
        lax.all_gather(w_out, "shard", axis=1, tiled=True),
        lax.all_gather(w_down, "shard", axis=1, tiled=True),
    )
    gain_one = gain_attn.astype(jnp.float32)
    gain_two = gain_ffn.astype(jnp.float32)
    tok_rows = tokens.reshape(token_count, model_width).astype(jnp.float32)
    scale_one = lax.rsqrt(jnp.mean(tok_rows * tok_rows, axis=-1, keepdims=True) + norm_eps)
    normed_input = (tok_rows * scale_one * gain_one).astype(jnp.bfloat16)
    cosine_table, sine_values = tables(pos_here.reshape(token_count))
    query_heads_rows = rotary_apply(
        jnp.dot(normed_input, w_query, preferred_element_type=jnp.float32).reshape(
            token_count, heads_here, HEAD_SIZE
        ),
        cosine_table,
        sine_values,
    )
    query_heads_rows = query_heads_rows.astype(jnp.bfloat16).reshape(
        groups, tok_local, heads_here * HEAD_SIZE
    )
    key_rows = rotary_apply(
        jnp.dot(normed_input, key_weight, preferred_element_type=jnp.float32).reshape(
            token_count, kv_here, HEAD_SIZE
        ),
        cosine_table,
        sine_values,
    )
    key_rows = key_rows.astype(jnp.bfloat16).reshape(token_count, kv_width)
    value_rows = jnp.dot(normed_input, value_weight, preferred_element_type=jnp.float32).astype(
        jnp.bfloat16
    )
    keyval = jnp.concatenate([key_rows, value_rows], axis=-1).reshape(
        groups, tok_local, 2 * kv_width
    )
    gathered = lax.all_gather(keyval, "context", axis=1, tiled=True)

    def scores_of(group_queries, group_keyval, seg_query, pos_query, seg_keys, pos_keys):
        grouped_heads = group_queries.reshape(tok_local, kv_here, per_kv, HEAD_SIZE)
        key_head_rows = group_keyval[:, :kv_width].reshape(-1, kv_here, HEAD_SIZE)
        scores = (
            jnp.einsum(
                "bhgd,khd->hgbk", grouped_heads, key_head_rows, preferred_element_type=jnp.float32
            )
            * score_scale
        )
        allowed = visible(seg_query, pos_query, seg_keys, pos_keys)
        return (jnp.where(allowed[None, None], scores, -1e30), grouped_heads, key_head_rows)

    def attend_group(inputs):
        group_queries, group_keyval, seg_query, pos_query, seg_keys, pos_keys = inputs
        scores, grouped_heads, key_head_rows = scores_of(
            group_queries, group_keyval, seg_query, pos_query, seg_keys, pos_keys
        )
        top_score = jnp.max(scores, axis=-1, keepdims=True)
        exponent = jnp.exp(scores - top_score)
        totals = jnp.sum(exponent, axis=-1, keepdims=True)
        soft_weights = (exponent / totals).astype(jnp.bfloat16)
        value_head_rows = group_keyval[:, kv_width:].reshape(-1, kv_here, HEAD_SIZE)
        attended_output = jnp.einsum(
            "hgbk,khd->bhgd", soft_weights, value_head_rows, preferred_element_type=jnp.float32
        )
        return (
            attended_output.reshape(tok_local, heads_here * HEAD_SIZE),
            (top_score + jnp.log(totals))[..., 0],
        )

    attended_output, log_total = lax.map(
        attend_group, (query_heads_rows, gathered, seg_here, pos_here, segments, positions)
    )
    attended_low = attended_output.reshape(token_count, heads_here * HEAD_SIZE).astype(jnp.bfloat16)
    attn_sum = lax.psum(jnp.dot(attended_low, w_out, preferred_element_type=jnp.float32), "tensor")
    middle = tok_rows + attn_sum
    scale_two = lax.rsqrt(jnp.mean(middle * middle, axis=-1, keepdims=True) + norm_eps)
    normed_two = (middle * scale_two * gain_two).astype(jnp.bfloat16)
    gate_proj = jnp.dot(normed_two, w_gate, preferred_element_type=jnp.float32)
    up_proj = jnp.dot(normed_two, w_up, preferred_element_type=jnp.float32)
    sigmoid_gate = jax.nn.sigmoid(gate_proj)
    silu_gate = gate_proj * sigmoid_gate
    hidden = (silu_gate * up_proj).astype(jnp.bfloat16)
    ffn_sum = lax.psum(
        jnp.dot(hidden, w_down, preferred_element_type=jnp.float32).astype(jnp.bfloat16), "tensor"
    ).astype(jnp.float32)
    output = (middle + ffn_sum).astype(jnp.bfloat16).reshape(groups, tok_local, model_width)
    grad_low = cotangent.reshape(token_count, model_width)
    grad_out = grad_low.astype(jnp.float32)
    grad_hidden = contract_cols(grad_low, w_down)
    grad_w_down_t = contract_rows(grad_low, hidden)
    grad_gate = (
        grad_hidden * up_proj * sigmoid_gate * (1.0 + gate_proj * (1.0 - sigmoid_gate))
    ).astype(jnp.bfloat16)
    grad_up = (grad_hidden * silu_gate).astype(jnp.bfloat16)
    grad_w_gate = contract_rows(normed_two, grad_gate)
    grad_w_up = contract_rows(normed_two, grad_up)
    grad_normed_two = lax.psum(
        contract_cols(grad_gate, w_gate) + contract_cols(grad_up, w_up), "tensor"
    )
    back_two, grad_gain_two = norm_back(middle, scale_two, gain_two, grad_normed_two)
    grad_middle = grad_out + back_two
    grad_mid_low = grad_middle.astype(jnp.bfloat16)
    grad_w_out_t = contract_rows(grad_mid_low, attended_low)
    grad_attended = (
        contract_cols(grad_mid_low, w_out)
        .astype(jnp.bfloat16)
        .reshape(groups, tok_local, heads_here * HEAD_SIZE)
    )

    def attend_back(inputs):
        (
            group_queries,
            group_keyval,
            group_grad,
            group_total,
            seg_query,
            pos_query,
            seg_keys,
            pos_keys,
        ) = inputs
        scores, grouped_heads, key_head_rows = scores_of(
            group_queries, group_keyval, seg_query, pos_query, seg_keys, pos_keys
        )
        soft_weights = jnp.exp(scores - group_total[..., None])
        value_head_rows = group_keyval[:, kv_width:].reshape(-1, kv_here, HEAD_SIZE)
        grad_grouped = group_grad.reshape(tok_local, kv_here, per_kv, HEAD_SIZE)
        grad_weights = jnp.einsum(
            "bhgd,khd->hgbk", grad_grouped, value_head_rows, preferred_element_type=jnp.float32
        )
        inner = jnp.sum(soft_weights * grad_weights, axis=-1, keepdims=True)
        grad_scores = (soft_weights * (grad_weights - inner)).astype(jnp.bfloat16)
        grad_queries = (
            jnp.einsum(
                "hgbk,khd->bhgd", grad_scores, key_head_rows, preferred_element_type=jnp.float32
            )
            * score_scale
        )
        grad_keys = (
            jnp.einsum(
                "hgbk,bhgd->khd", grad_scores, grouped_heads, preferred_element_type=jnp.float32
            )
            * score_scale
        )
        grad_values = jnp.einsum(
            "hgbk,bhgd->khd",
            soft_weights.astype(jnp.bfloat16),
            grad_grouped,
            preferred_element_type=jnp.float32,
        )
        grad_keyval = jnp.concatenate(
            [grad_keys.reshape(-1, kv_width), grad_values.reshape(-1, kv_width)], axis=-1
        )
        return (grad_queries.reshape(tok_local, heads_here * HEAD_SIZE), grad_keyval)

    grad_queries, grad_keyval = lax.map(
        attend_back,
        (
            query_heads_rows,
            gathered,
            grad_attended,
            log_total,
            seg_here,
            pos_here,
            segments,
            positions,
        ),
    )
    grad_keyval = lax.psum_scatter(grad_keyval, "context", scatter_dimension=1, tiled=True)
    grad_query_rows = rotate_back(
        grad_queries.reshape(token_count, heads_here, HEAD_SIZE), cosine_table, sine_values
    )
    grad_query_rows = grad_query_rows.astype(jnp.bfloat16).reshape(
        token_count, heads_here * HEAD_SIZE
    )
    grad_key_rows = rotate_back(
        grad_keyval[..., :kv_width].reshape(token_count, kv_here, HEAD_SIZE),
        cosine_table,
        sine_values,
    )
    grad_key_rows = grad_key_rows.astype(jnp.bfloat16).reshape(token_count, kv_width)
    grad_value_rows = (
        grad_keyval[..., kv_width:].reshape(token_count, kv_width).astype(jnp.bfloat16)
    )
    grad_w_query = contract_rows(normed_input, grad_query_rows)
    grad_w_key = contract_rows(normed_input, grad_key_rows)
    grad_w_value = contract_rows(normed_input, grad_value_rows)
    partial_one = (
        contract_cols(grad_query_rows, w_query)
        + contract_cols(grad_key_rows, key_weight)
        + contract_cols(grad_value_rows, value_weight)
    )
    grad_normed = lax.psum(partial_one, "tensor")
    back_one, grad_gain_one = norm_back(tok_rows, scale_one, gain_one, grad_normed)
    tokens_grad = (
        (grad_middle + back_one).astype(jnp.bfloat16).reshape(groups, tok_local, model_width)
    )
    summed = (
        lax.psum_scatter(grad_w_query, ("shard", "context"), scatter_dimension=0, tiled=True),
        lax.psum_scatter(grad_w_key, ("shard", "context"), scatter_dimension=0, tiled=True),
        lax.psum_scatter(grad_w_value, ("shard", "context"), scatter_dimension=0, tiled=True),
        lax.psum_scatter(grad_w_out_t, ("shard", "context"), scatter_dimension=0, tiled=True),
        lax.psum_scatter(grad_w_gate, ("shard", "context"), scatter_dimension=0, tiled=True),
        lax.psum_scatter(grad_w_up, ("shard", "context"), scatter_dimension=0, tiled=True),
        lax.psum_scatter(grad_w_down_t, ("shard", "context"), scatter_dimension=0, tiled=True),
        lax.psum_scatter(grad_gain_one, ("shard", "context"), scatter_dimension=0, tiled=True),
        lax.psum_scatter(grad_gain_two, ("shard", "context"), scatter_dimension=0, tiled=True),
    )
    summed = (
        lax.all_gather(summed[0].astype(jnp.bfloat16), "context", axis=0, tiled=True).astype(
            jnp.float32
        ),
        lax.all_gather(summed[1].astype(jnp.bfloat16), "context", axis=0, tiled=True).astype(
            jnp.float32
        ),
        lax.all_gather(summed[2].astype(jnp.bfloat16), "context", axis=0, tiled=True).astype(
            jnp.float32
        ),
        lax.all_gather(summed[3].astype(jnp.bfloat16), "context", axis=0, tiled=True).astype(
            jnp.float32
        ),
        lax.all_gather(summed[4].astype(jnp.bfloat16), "context", axis=0, tiled=True).astype(
            jnp.float32
        ),
        lax.all_gather(summed[5].astype(jnp.bfloat16), "context", axis=0, tiled=True).astype(
            jnp.float32
        ),
        lax.all_gather(summed[6].astype(jnp.bfloat16), "context", axis=0, tiled=True).astype(
            jnp.float32
        ),
        lax.all_gather(summed[7].astype(jnp.bfloat16), "context", axis=0, tiled=True).astype(
            jnp.float32
        ),
        lax.all_gather(summed[8].astype(jnp.bfloat16), "context", axis=0, tiled=True).astype(
            jnp.float32
        ),
    )
    return (
        output,
        tokens_grad,
        summed[0],
        summed[1],
        summed[2],
        summed[3].T,
        summed[4],
        summed[5],
        summed[6].T,
        summed[7],
        summed[8],
    )


MESH = pl.DeviceIdType.MESH
RUN = 256
PAD = 128
NEG = -1e30
LOG2E = 1.4426950408889634
BF = jnp.bfloat16
F32 = jnp.float32
VLIM = 64 * 1024 * 1024


def mm(a, b):
    return lax.dot_general(a, b, (((1,), (0,)), ((), ())), preferred_element_type=F32)


def mm_nt(a, b):
    return lax.dot_general(a, b, (((1,), (1,)), ((), ())), preferred_element_type=F32)


def mm_tn(a, b):
    return lax.dot_general(a, b, (((0,), (0,)), ((), ())), preferred_element_type=F32)


def iota(shape, axis):
    return lax.broadcasted_iota(jnp.int32, shape, axis)


def one_hot(hit):
    return jnp.where(hit, 1.0, 0.0).astype(BF)


def pad_matrix(heads, flip=False):
    shape = (heads * HEAD_SIZE, heads * PAD)
    if flip:
        row, col = iota(shape[::-1], 1), iota(shape[::-1], 0)
    else:
        row, col = iota(shape, 0), iota(shape, 1)
    lane = col & 127
    part = jnp.where(lane < 64, lane, lane - 16)
    return one_hot((row == (col >> 7) * HEAD_SIZE + part) & ((lane & 63) < 48))


def split_matrix():
    row, col = iota((RUN, RUN), 0), iota((RUN, RUN), 1)
    return one_hot(col == jnp.where(row < 128, 2 * row, 2 * row - 255))


def merge_matrix():
    row, col = iota((RUN, RUN), 0), iota((RUN, RUN), 1)
    return one_hot(col == (row >> 1) + (row & 1) * 128)


def first_of(ref, run, per):
    start = lax.axis_index("context") * (2 * per * RUN)
    return ref[0, start + run % per * (2 * RUN) + run // per]


def rope_tables(run, per, pos_ref, cb_ref, sb_ref, cj_ref, sj_ref):
    base = first_of(pos_ref, run, per) // RUN
    cb, sb = cb_ref[pl.ds(base, 1), :], sb_ref[pl.ds(base, 1), :]
    cj, sj = cj_ref[...], sj_ref[...]
    return cb * cj - sb * sj, sb * cj + cb * sj


def rope(u, c, s):
    return u * c + pltpu.roll(u, 64, 1) * s


def rope_back(u, c, s):
    return u * c - pltpu.roll(u, 64, 1) * s


def vmem(*shape_dtype):
    return pl.BlockSpec(memory_space=pltpu.VMEM)


def entry_barrier(targets):
    bar = pltpu.get_barrier_semaphore()
    for t in targets:
        pl.semaphore_signal(bar, inc=1, device_id=t, device_id_type=MESH)
    pl.semaphore_wait(bar, len(targets))


def remote(src, dst, send, recv, target):
    return pltpu.make_async_remote_copy(
        src_ref=src, dst_ref=dst, send_sem=send, recv_sem=recv, device_id=target, device_id_type=MESH
    )


def first_kernel(nc, x_ref, dy_h, g_ref, pos_ref, cb_ref, sb_ref, cj_ref, sj_ref, wq_h, wk_h, wv_h, wo_h, wg_h, wu_h, wd_h,
                 xp_h, dyp_h, n1_h, q_ref, kvp_ref, kvc_ref, wp_h, gf_ref, wo_f, wg_f, wu_f, wd_f,
                 xp_ref, dyp_ref, n1_ref, wp_ref, dy_v, wq_s, wk_s, wv_s, g_s, wo_v, wg_v, wu_v, wd_v, kv_send,
                 lsem, ssem, rsem, osem, csem, crem, esem):
    s = lax.axis_index("shard")
    c = lax.axis_index("context")
    dh = g_s.shape[1] // 2
    own = pl.ds(pl.multiple_of(s * dh, dh), dh)
    other = {"shard": 1 - s}
    loads = [
        pltpu.make_async_copy(wq_h, wq_s.at[own], lsem.at[0]),
        pltpu.make_async_copy(wk_h, wk_s.at[:, own], lsem.at[1]),
        pltpu.make_async_copy(wv_h, wv_s.at[:, own], lsem.at[2]),
        None,
        pltpu.make_async_copy(wo_h, wo_v, lsem.at[4]),
        pltpu.make_async_copy(wg_h, wg_v, lsem.at[5]),
        pltpu.make_async_copy(wu_h, wu_v, lsem.at[6]),
        pltpu.make_async_copy(wd_h, wd_v, lsem.at[7]),
        pltpu.make_async_copy(dy_h, dy_v, lsem.at[8]),
    ]
    for cp in loads[:3] + loads[4:]:
        cp.start()
    for i in range(2):
        g_s[8 * i : 8 * i + 8, own] = jnp.broadcast_to(g_ref[i : i + 1, :], (8, dh))
    entry_barrier([other] + [{"context": lax.rem(c + i, nc)} for i in range(1, nc)])
    sends = [
        remote(wq_s.at[own], wq_s.at[own], ssem.at[0], rsem.at[0], other),
        remote(wk_s.at[:, own], wk_s.at[:, own], ssem.at[1], rsem.at[1], other),
        remote(wv_s.at[:, own], wv_s.at[:, own], ssem.at[2], rsem.at[2], other),
        remote(g_s.at[:, own], g_s.at[:, own], ssem.at[3], rsem.at[3], other),
        remote(wo_v, wo_f.at[:, own], ssem.at[4], rsem.at[4], other),
        remote(wg_v, wg_f.at[own], ssem.at[5], rsem.at[5], other),
        remote(wu_v, wu_f.at[own], ssem.at[6], rsem.at[6], other),
        remote(wd_v, wd_f.at[:, own], ssem.at[7], rsem.at[7], other),
    ]
    keeps = [
        pltpu.make_async_copy(wo_v, wo_f.at[:, own], osem.at[0]),
        pltpu.make_async_copy(wg_v, wg_f.at[own], osem.at[1]),
        pltpu.make_async_copy(wu_v, wu_f.at[own], osem.at[2]),
        pltpu.make_async_copy(wd_v, wd_f.at[:, own], osem.at[3]),
    ]
    for i in (3, 0, 1, 2):
        if i != 3:
            loads[i].wait()
        sends[i].start()
    half = x_ref.shape[0] // 2
    split = split_matrix()
    for i in range(x_ref.shape[0] // RUN):
        xb = mm(split, x_ref[pl.ds(i * RUN, RUN), :])
        xp_ref[pl.ds(i * 128, 128), :] = xb[:128].astype(BF)
        xp_ref[pl.ds(half + i * 128, 128), :] = xb[128:].astype(BF)
        if i == 0:
            sends[3].wait_recv()
        r = lax.rsqrt(jnp.mean(xb * xb, axis=-1, keepdims=True) + norm_eps)
        nb = (xb * r * g_s[0:1, :]).astype(BF)
        n1_ref[pl.ds(i * 128, 128), :] = nb[:128]
        n1_ref[pl.ds(half + i * 128, 128), :] = nb[128:]
    gf_ref[...] = g_s[...]
    exits = [pltpu.make_async_copy(a, b, esem.at[i]) for i, (a, b) in enumerate([(xp_ref, xp_h), (n1_ref, n1_h), (wp_ref, wp_h), (dyp_ref, dyp_h)])]
    exits[0].start()
    exits[1].start()
    hq, hk = wq_s.shape[1] // HEAD_SIZE, wk_s.shape[0] // HEAD_SIZE
    selq, selk = pad_matrix(hq, True), pad_matrix(hk, True)
    nq, nk = hq * PAD, hk * PAD
    for i in range(3):
        sends[i].wait_recv()
    wp_ref[0:nq, :] = mm_nt(selq, wq_s[...]).astype(BF)
    wp_ref[nq : nq + nk, :] = mm(selk, wk_s[...]).astype(BF)
    wp_ref[nq + nk :, :] = mm(selk, wv_s[...]).astype(BF)
    exits[2].start()
    for i in range(4, 8):
        loads[i].wait()
        sends[i].start()
        keeps[i - 4].start()
    selkv = pad_matrix(2 * hk)
    runs = x_ref.shape[0] // RUN
    per = runs // 2
    kv_copies = []
    for run in range(runs):
        rows = pl.ds(run * RUN, RUN)
        y = mm_nt(n1_ref[rows, :], wp_ref[nq:, :])
        ct, st = rope_tables(run, per, pos_ref, cb_ref, sb_ref, cj_ref, sj_ref)
        kv = [rope(y[:, h * PAD : (h + 1) * PAD], ct, st).astype(BF) for h in range(hk)]
        kv = jnp.concatenate(kv + [y[:, nk:].astype(BF)], axis=1)
        if run < per:
            kv_send[pl.ds(run * RUN, RUN), :] = mm_nt(kv, selkv).astype(BF)
            mine = pl.ds(pl.multiple_of((c * per + run) * RUN, RUN), RUN)
            for i in range(1, nc):
                cp = remote(kv_send.at[pl.ds(run * RUN, RUN)], kvp_ref.at[mine], csem.at[run, i], crem.at[run, i],
                            {"context": lax.rem(c + i, nc)})
                cp.start()
                kv_copies.append(cp)
            cp = pltpu.make_async_copy(kv_send.at[pl.ds(run * RUN, RUN)], kvp_ref.at[mine], csem.at[run, 0])
            cp.start()
            kv_copies.append(cp)
        else:
            kvc_ref[pl.ds((run - per) * RUN, RUN), :] = kv
    for run in range(runs):
        rows = pl.ds(run * RUN, RUN)
        y = mm_nt(n1_ref[rows, :], wp_ref[0:nq, :])
        ct, st = rope_tables(run, per, pos_ref, cb_ref, sb_ref, cj_ref, sj_ref)
        for h in range(hq):
            q_ref[rows, h * PAD : (h + 1) * PAD] = rope(y[:, h * PAD : (h + 1) * PAD], ct, st).astype(BF)
    loads[8].wait()
    for i in range(x_ref.shape[0] // RUN):
        b = mm(split, dy_v[pl.ds(i * RUN, RUN), :]).astype(BF)
        dyp_ref[pl.ds(i * 128, 128), :] = b[:128]
        dyp_ref[pl.ds(half + i * 128, 128), :] = b[128:]
    exits[3].start()
    for cp in kv_copies + exits:
        cp.wait()
    for i in range(4):
        keeps[i].wait()
        sends[4 + i].wait_recv()
    for cp in sends:
        cp.wait_send()


class Line:
    F_AT = (8, 9, 10, 12)
    D_AT = (11, 13, 14, 15)

    def __init__(self, n, chunk, pbuf, rbuf, obuf, sems):
        self.n, self.chunk, self.per = n, chunk, RUN // 2 // chunk
        self.count = 16 * self.per
        self.pbuf, self.rbuf, self.obuf = pbuf, rbuf, obuf
        self.rs, self.rr, self.bs, self.br = sems
        self.ticks = 32 // chunk
        self.hop = 3
        self.turn = 2 * (n - 1) * self.hop
        self.slots = self.count + self.turn

    def pieces(self, h, i):
        n, chunk = self.n, self.chunk
        z = lax.axis_index("tensor")
        job = i // self.per
        late = jnp.where((job == 11) | (job > 12), 1, 0)
        row = jnp.where(job < 8, lax.rem(job, 4), jnp.where(late == 1, jnp.maximum(job - 12, 0), jnp.minimum(job - 8, 3)))
        part = jnp.where(job < 8, job // 4, 2 - late)
        off = row * RUN + h * (RUN // 2) + lax.rem(i, self.per) * chunk
        rows = pl.ds(pl.multiple_of(off, chunk), chunk)
        orows = pl.ds(pl.multiple_of(part * (4 * RUN) + off, chunk), chunk)
        place = z if h == 0 else n - 1 - z
        up, down = jnp.minimum(z + 1, n - 1), jnp.maximum(z - 1, 0)
        ahead = {"tensor": up if h == 0 else down}
        back = {"tensor": down if h == 0 else up}
        fwd = remote(self.pbuf.at[rows], self.rbuf.at[rows], self.rs.at[h, i], self.rr.at[h, i], ahead)
        ret = remote(self.obuf.at[orows], self.obuf.at[orows], self.bs.at[h, i], self.br.at[h, i], back)
        return rows, orows, place, fwd, ret

    def reduce_step(self, h, i):
        rows, orows, place, fwd, ret = self.pieces(h, i)
        n = self.n

        @pl.when(place == 0)
        def _():
            fwd.start()

        @pl.when(place > 0)
        def _():
            fwd.wait_recv()
            total = (self.rbuf[rows, :].astype(F32) + self.pbuf[rows, :].astype(F32)).astype(BF)

            @pl.when(place < n - 1)
            def _():
                self.pbuf[rows, :] = total
                fwd.start()

            @pl.when(place == n - 1)
            def _():
                self.obuf[orows, :] = total
                ret.start()

    def spread_step(self, h, i):
        rows, orows, place, fwd, ret = self.pieces(h, i)

        @pl.when(place < self.n - 1)
        def _():
            ret.wait_recv()

        @pl.when((place < self.n - 1) & (place > 0))
        def _():
            ret.start()

    def serve(self, t):
        n = self.n
        z = lax.axis_index("tensor")
        for h in range(2):
            place = z if h == 0 else n - 1 - z
            i = t - place * self.hop

            @pl.when((i >= 0) & (i < self.count))
            def _():
                self.reduce_step(h, i)

            j = t - (2 * (n - 1) - place) * self.hop

            @pl.when((j >= 0) & (j < self.count))
            def _():
                self.spread_step(h, j)

    def sent(self, job, fwd=True, ret=False):
        def step(i, _):
            for h in range(2):
                rows, orows, place, f, r = self.pieces(h, job * self.per + i)
                if fwd:

                    @pl.when(place < self.n - 1)
                    def _():
                        f.wait_send()

                if ret:

                    @pl.when(place > 0)
                    def _():
                        r.wait_send()

            return 0

        lax.fori_loop(0, self.per, step, 0)


def run_items(items, serve):
    total = max(e for spans, _ in items for _, e in spans)

    def step(k, _):
        for spans, body in items:
            hit = functools.reduce(jnp.logical_or, [(k >= lo) & (k < hi) for lo, hi in spans])
            pl.when(hit)(functools.partial(body, k))
        serve(k)
        return 0

    lax.fori_loop(0, total, step, 0)


class Square:
    def __init__(self, rows, cols, src, mine, theirs, spare, out, credit, shard_send, shard_recv, send, recv, store):
        self.src, self.mine, self.theirs, self.res, self.out = src, mine, theirs, theirs, out
        self.r1, self.r2 = [spare[0:2], spare[2:4]], spare[4:6]
        self.credit, self.shard_sems, self.shard_recv, self.send, self.recv, self.store_sem = credit, shard_send, shard_recv, send, recv, store
        self.rows, self.qr, self.cols = rows, rows // 4, cols
        c = lax.axis_index("context")
        self.cy, self.cx = c // 2, lax.rem(c, 2)

    def at(self, y, x, half):
        w = self.cols // 2
        return (pl.ds(pl.multiple_of((2 * y + x) * self.qr, self.qr), self.qr), pl.ds(half * w, w))

    def peer(self, half, first):
        if (half == 0) == first:
            return {"context": 2 * self.cy + 1 - self.cx}
        return {"context": 2 * (1 - self.cy) + self.cx}

    def shard_copy(self):
        return remote(self.src, self.theirs, self.shard_sems, self.shard_recv, {"shard": 1 - lax.axis_index("shard")})

    def outer(self, half):
        if half == 0:
            return [(y, 1 - self.cx) for y in range(2)], [(y, self.cx) for y in range(2)]
        return [(1 - self.cy, x) for x in range(2)], [(self.cy, x) for x in range(2)]

    def p1(self, half, j):
        return remote(self.mine.at[self.at(*self.outer(half)[0][j], half)], self.r1[half][j],
                      self.send.at[0, half, j], self.recv.at[0, half, j], self.peer(half, True))

    def p2(self, half):
        q = (1 - self.cy, self.cx) if half == 0 else (self.cy, 1 - self.cx)
        return remote(self.mine.at[self.at(*q, half)], self.r2[half],
                      self.send.at[1, half, 0], self.recv.at[1, half, 0], self.peer(half, False))

    def p3(self, half):
        at = self.at(self.cy, self.cx, half)
        return remote(self.res.at[at], self.res.at[at], self.send.at[1, half, 1], self.recv.at[1, half, 1], self.peer(half, False))

    def p4(self, half, j):
        at = self.at(*self.outer(half)[1][j], half)
        return remote(self.res.at[at], self.res.at[at], self.send.at[2, half, j], self.recv.at[2, half, j], self.peer(half, True))

    def free(self):
        for t in ({"shard": 1 - lax.axis_index("shard")}, self.peer(0, True), self.peer(0, False)):
            pl.semaphore_signal(self.credit, inc=1, device_id=t, device_id_type=MESH)

    def e0(self):
        pl.semaphore_wait(self.credit, 3)
        self.shard_copy().start()

    def e1(self):
        self.shard_copy().wait_recv()
        step = self.qr

        def add(i, _):
            rows = pl.ds(pl.multiple_of(i * step, step), step)
            self.mine[rows, :] = (self.mine[rows, :].astype(F32) + self.theirs[rows, :].astype(F32)).astype(BF)
            return 0

        lax.fori_loop(0, self.rows // step, add, 0)
        for j in range(2):
            for half in range(2):
                self.p1(half, j).start()

    def e2(self):
        for half in range(2):
            for j in range(2):
                self.p1(half, j).wait_recv()
                at = self.at(*self.outer(half)[1][j], half)
                self.mine[at] = (self.mine[at].astype(F32) + self.r1[half][j][...].astype(F32)).astype(BF)
            self.p2(half).start()

    def e3(self):
        for half in range(2):
            self.p2(half).wait_recv()
            at = self.at(self.cy, self.cx, half)
            self.res[at] = (self.mine[at].astype(F32) + self.r2[half][...].astype(F32)).astype(BF)
            self.p3(half).start()

    def e4(self):
        for half in range(2):
            self.p3(half).wait_recv()
            for j in range(2):
                self.p4(half, j).start()

    def e5(self):
        for half in range(2):
            for j in range(2):
                self.p4(half, j).wait_recv()

    def store(self):
        return pltpu.make_async_copy(self.res, self.out, self.store_sem)

    def done(self):
        self.shard_copy().wait_send()
        for half in range(2):
            for j in range(2):
                self.p1(half, j).wait_send()
                self.p4(half, j).wait_send()
            self.p2(half).wait_send()
            self.p3(half).wait_send()


def line_barrier(n, peers=()):
    z = lax.axis_index("tensor")
    bar = pltpu.get_barrier_semaphore()
    for t in peers:
        pl.semaphore_signal(bar, inc=1, device_id=t, device_id_type=MESH)

    @pl.when(z > 0)
    def _():
        pl.semaphore_signal(bar, inc=1, device_id={"tensor": jnp.maximum(z - 1, 0)}, device_id_type=MESH)

    @pl.when(z < n - 1)
    def _():
        pl.semaphore_signal(bar, inc=1, device_id={"tensor": jnp.minimum(z + 1, n - 1)}, device_id_type=MESH)

    pl.semaphore_wait(bar, len(peers) + jnp.minimum(z, 1) + jnp.minimum(n - 1 - z, 1))


def main_kernel(n, nc, chunk, seg_ref, pos_ref, cb_ref, sb_ref, cj_ref, sj_ref, gf_ref, q_ref, kvc_ref, wo_ref,
                kvp_h, xp_h, dyp_h, wg_h, wu_h, wd_h, n1_h, wp_h,
                out_h, tg_h, gg_h, gu_h, gd_h, go_h, gw_h, dm_h, gds_h, fp_h, gains_ref,
                k_s, v_s, s_s, o_v, op_v, lse_v, xs, ys, pbuf, rbuf, obuf, wd, n2, wg, wu, hid, dg, du, gt,
                dk_s, dv_s, do_v, dq_s, delta_s, dqp, dkv_s, go_v, st_o, st_t, st_p, gpart, grecv,
                lsem, ksem, osem, fsem, msem, nsem, qsend, qrecv, gs, gr, rs, rr, bs, br, credits, shard_send, shard_recv, send, recv, store):
    s = lax.axis_index("shard")
    c = lax.axis_index("context")
    rows_here, d = xs.shape
    runs = rows_here // RUN
    per = runs // 2
    half = rows_here // 2
    hk = k_s.shape[0]
    hq = q_ref.shape[1] // PAD
    rep = hq // hk
    blocks = k_s.shape[1] // RUN
    ff = wg.shape[1]
    dh = d // 2
    nq, nk = hq * PAD, hk * PAD
    score = 1.0 / math.sqrt(HEAD_SIZE)
    scale = LOG2E * score
    own = pl.ds(pl.multiple_of(s * dh, dh), dh)
    yours = pl.ds(pl.multiple_of((1 - s) * dh, dh), dh)
    wide = 2 * hk * HEAD_SIZE

    def at(i, size=RUN):
        return pl.ds(pl.multiple_of(i * size, size), size)

    def limit(run):
        return jnp.where(run < per, first_of(pos_ref, run, per), first_of(seg_ref, run, per) * CLEN - 1)

    kv_in = [dg.at[pl.ds((b % 4) * RUN, RUN), pl.ds(b // 4 * wide, wide)] for b in range(blocks)]
    key_loads = [pltpu.make_async_copy(kvp_h.at[pl.ds(b * RUN, RUN)], kv_in[b], ksem.at[b]) for b in range(blocks)]
    for cp in key_loads:
        cp.start()
    pairs = [(xp_h, xs), (wg_h, wg), (wu_h, wu), (dyp_h, ys), (wd_h, wd)]
    loads = [pltpu.make_async_copy(a, b, lsem.at[i]) for i, (a, b) in enumerate(pairs)]
    for cp in loads:
        cp.start()
    peers = [{"shard": lax.rem(s + i // nc, 2), "context": lax.rem(c + lax.rem(i, nc), nc)} for i in range(1, 2 * nc)]
    line_barrier(n, peers)
    line = Line(n, chunk, pbuf, rbuf, obuf, (rs, rr, bs, br))
    a_of = lambda job: at(job)
    b_of = lambda job: at(runs + job)
    lane = iota((RUN, PAD), 1)
    for b in range(blocks):
        key_loads[b].wait()
        kv = mm(kv_in[b][...], pad_matrix(2 * hk))
        rows = pl.ds(b * RUN, RUN)
        for g in range(hk):
            k_s[g, rows, :] = kv[:, g * PAD : (g + 1) * PAD].astype(BF)
            v_s[g, rows, :] = jnp.where(lane == 48, 1.0, kv[:, (hk + g) * PAD : (hk + g + 1) * PAD]).astype(BF)
    dk_s[...] = jnp.zeros_like(dk_s)
    dv_s[...] = jnp.zeros_like(dv_s)
    gpart[...] = jnp.zeros_like(gpart)

    def across(total, width, body):
        def step(i, _):
            body(at(i, width))
            return 0

        lax.fori_loop(0, total // width, step, 0)

    def down_rows(start, count, size, body):
        def step(i, _):
            body(pl.ds(pl.multiple_of(start + i * size, size), size), pl.ds(pl.multiple_of(i * size, size), size))
            return 0

        lax.fori_loop(0, count // size, step, 0)

    def head(k, mixed):
        job, h = k // hq, lax.rem(k, hq)
        run = job + per if mixed else job - per
        diff = iota((RUN, RUN), 1) - iota((RUN, RUN), 0)
        rows, cols = at(run), at(h, PAD)
        g = h // rep
        q = q_ref[rows, cols]
        lim = limit(run)
        top = None
        for b in range(blocks):
            t = mm_nt(q, k_s[g, pl.ds(b * RUN, RUN), :]) * scale
            room = lim - pos_ref[0, 2 * RUN * b]
            if mixed:
                t = t + jnp.where(room >= 0, 0.0, NEG)
            else:
                t = jnp.where(diff <= room, t, NEG)
            s_s[:, b * RUN : (b + 1) * RUN] = t
            top = t if top is None else jnp.maximum(top, t)
        if mixed:
            crow = at(run - per)
            kc = kvc_ref[crow, at(g, PAD)]
            vc = kvc_ref[crow, at(hk + g, PAD)]
            vc = jnp.where(lane == 48, 1.0, vc.astype(F32)).astype(BF)
            t = jnp.where(diff <= 0, mm_nt(q, kc) * scale, NEG)
            s_s[:, blocks * RUN :] = t
            top = jnp.maximum(top, t)
        m = jnp.max(top, axis=1, keepdims=True)
        acc = None
        for b in range(blocks):
            p = jnp.exp2(s_s[:, b * RUN : (b + 1) * RUN] - m).astype(BF)
            o = mm(p, v_s[g, pl.ds(b * RUN, RUN), :])
            acc = o if acc is None else acc + o
        if mixed:
            p = jnp.exp2(s_s[:, blocks * RUN :] - m).astype(BF)
            acc = acc + mm(p, vc)
        total = acc[:, 48:49]
        op_v[rows, cols] = (acc / total).astype(BF)
        lse = jnp.broadcast_to(m + jnp.log2(total), (RUN, PAD)).T
        lse_v[at(run * hq + h, 8), :] = lse[0:8, :]

        @pl.when(h == hq - 1)
        def _():
            o = mm_nt(op_v[rows, :], pad_matrix(hq)).astype(BF)
            o_v[rows, :] = o


            def out(cols):
                pbuf[at(job), cols] = mm(o, wo_ref[:, cols]).astype(BF)

            across(d, 512, out)

    first = runs * hq

    def ffn(k):
        job = (k - first) // 4
        part = lax.rem(k - first, 4)
        run = lax.rem(job + per, runs)
        rows = at(run)

        @pl.when(k == first)
        def _():
            for cp in loads:
                cp.wait()

        @pl.when(part == 0)
        def _():
            def norm(to, sub):
                srows = pl.ds(pl.multiple_of(job * RUN + sub.start, 32), 32)
                mid = xs[to, :].astype(F32) + obuf[srows, :].astype(F32)
                r = lax.rsqrt(jnp.mean(mid * mid, axis=-1, keepdims=True) + norm_eps)
                n2[to, :] = (mid * r * gf_ref[8:9, :]).astype(BF)

            down_rows(run * RUN, RUN, 32, norm)

            def gate(cols):
                s_s[:, cols] = mm(n2[rows, :], wg[:, cols])

            across(ff, 512, gate)

        @pl.when(part == 1)
        def _():
            def up(i, _):
                s_s[:, pl.ds(pl.multiple_of(ff + i * 512, 512), 512)] = mm(n2[rows, :], wu[:, at(i, 512)])
                return 0

            lax.fori_loop(0, ff // 512, up, 0)

        @pl.when(part == 2)
        def _():
            def gated(i, _):
                cols = at(i)
                dhid = mm_nt(ys[rows, :], wd[cols, :])
                gate, up = s_s[:, cols], s_s[:, pl.ds(pl.multiple_of(ff + i * RUN, RUN), RUN)]
                sig = jax.nn.sigmoid(gate)
                silu = gate * sig
                hid[rows, cols] = (silu * up).astype(BF)
                dg[rows, cols] = (dhid * up * sig * (1.0 + gate * (1.0 - sig))).astype(BF)
                du[rows, cols] = (dhid * silu).astype(BF)
                return 0

            lax.fori_loop(0, ff // RUN, gated, 0)

        @pl.when(part == 3)
        def _():
            line.sent(job)

            def normed_two(cols):
                pbuf[at(job), cols] = (mm_nt(dg[rows, :], wg[cols, :]) + mm_nt(du[rows, :], wu[cols, :])).astype(BF)

            across(d, 512, normed_two)
            cp = pltpu.make_async_copy(st_o, fp_h.at[at(job)], osem.at[0])

            @pl.when(job > 0)
            def _():
                cp.wait()

            def project(cols):
                st_o[:, cols] = mm(hid[rows, :], wd[:, cols]).astype(BF)

            across(d, 512, project)
            cp.start()

    second = first + 4 * runs

    def stage(st, sem, dst, value, busy=True):
        cp = pltpu.make_async_copy(st, dst, sem)
        if busy is True:
            cp.wait()
        else:
            pl.when(busy)(cp.wait)

        def fill(cols):
            st[:, cols] = value(cols)

        across(d, 512, fill)
        cp.start()

    def grads_down(k):
        i = k - second
        for j in range(2):
            cols = at(2 * i + j)
            ht = hid[:, cols].T
            stage(st_o, osem.at[0], gds_h.at[cols], lambda to: mm(ht, ys[:, to]).astype(BF))

    def grads_up(k):
        i = k - second - 2
        for j in range(2):
            cols = at(2 * i + j)
            nt = n2[:, cols].T


            def both(to):
                wg[cols, to] = mm(nt, dg[:, to]).astype(BF)
                wu[cols, to] = mm(nt, du[:, to]).astype(BF)

            across(ff, 512, both)

    back = second + 5

    def middle(k):
        job = (k - back) // 5
        run = lax.rem(job + per, runs)
        rows = at(run)
        cp = pltpu.make_async_copy(s_s.at[:, pl.ds(0, d)], dm_h.at[rows], osem.at[1])

        @pl.when(job > 0)
        def _():
            cp.wait()

        def one(to, sub):
            def there(base):
                return pl.ds(pl.multiple_of(base + sub.start, 32), 32)

            mid = xs[to, :].astype(F32) + obuf[there(job * RUN), :].astype(F32)
            r = lax.rsqrt(jnp.mean(mid * mid, axis=-1, keepdims=True) + norm_eps)
            dn = obuf[there((runs + job) * RUN), :].astype(F32)
            w = gf_ref[8:9, :] * dn
            inner = jnp.mean(w * mid, axis=-1, keepdims=True)
            dm = ys[to, :].astype(F32) + r * w - mid * (r * r * r) * inner
            s_s[sub, 0:d] = dm
            gpart[8:16, :] += jnp.sum((dn * mid * r).reshape(4, 8, d), axis=0)
            ys[to, :] = dm.astype(BF)

        down_rows(run * RUN, RUN, 32, one)
        cp.start()
        do = mm_nt(ys[rows, :], wo_ref[...]).astype(BF)
        do_v[rows, :] = mm(do, pad_matrix(hq)).astype(BF)

    width = rep * RUN

    def pair(k, mixed):
        job = (k - back) // 5
        idx = lax.rem(k - back, 5) - 1
        g, part = idx // 2, lax.rem(idx, 2)
        run = lax.rem(job + per, runs)
        rows = at(run)
        diff = iota((RUN, width), 0) - (iota((RUN, width), 1) & (RUN - 1))

        def stack(ref):
            return jnp.concatenate([ref[rows, at(g * rep + j, PAD)] for j in range(rep)], axis=0)

        q, do = stack(q_ref), stack(do_v)

        @pl.when(part == 0)
        def _():
            op = stack(op_v)
            delta_s[0:1, :] = jnp.sum((do.astype(F32) * op.astype(F32)).T, axis=0, keepdims=True)
            dq_s[...] = jnp.zeros_like(dq_s)

        delta = delta_s[0:1, :]
        lse = jnp.concatenate(
            [lse_v[pl.ds(pl.multiple_of((run * hq + g * rep + j) * 8, 8), 1), :] for j in range(rep)], axis=1
        )
        lim = limit(run)

        def tile(kk, vv, hide):
            p = jnp.exp2(hide(mm_nt(kk, q) * scale - lse))
            ds = (p * (mm_nt(vv, do) - delta)).astype(BF)
            return mm(ds, q), mm(p.astype(BF), do), mm_tn(ds, kk)

        dq = dq_s[...]
        for bb in range(blocks // 2):
            b = part * (blocks // 2) + bb
            room = lim - pos_ref[0, 2 * RUN * b]
            if mixed:
                hide = lambda t: t + jnp.where(room >= 0, 0.0, NEG)
            else:
                hide = lambda t: jnp.where(diff <= room, t, NEG)
            dk, dv, dd = tile(k_s[g, at(b), :], v_s[g, at(b), :], hide)
            dk_s[g, at(b), :] += dk
            dv_s[g, at(b), :] += dv
            dq = dq + dd
        dq_s[...] = dq

        @pl.when(part == 1)
        def _():
            total = dq_s[...]
            ct, st = rope_tables(run, per, pos_ref, cb_ref, sb_ref, cj_ref, sj_ref)
            if mixed:
                crow = at(run - per)
                dk, dv, dd = tile(kvc_ref[crow, at(g, PAD)], kvc_ref[crow, at(hk + g, PAD)], lambda t: jnp.where(diff <= 0, t, NEG))
                total = total + dd
                dkv_s[rows, at(g, PAD)] = rope_back(dk * score, ct, st).astype(BF)
                dkv_s[rows, at(hk + g, PAD)] = dv.astype(BF)
            for j in range(rep):
                dqp[rows, at(g * rep + j, PAD)] = rope_back(total[j * RUN : (j + 1) * RUN] * score, ct, st).astype(BF)

    def spare(ref, r0, c0, rows, cols, across, count):
        return [ref.at[pl.ds(r0 + i // across * rows, rows), pl.ds(c0 + i % across * cols, cols)] for i in range(count)]

    def square(i, rows, cols, src, mine, theirs, views, out):
        return Square(rows, cols, src, mine, theirs, views, out, credits.at[i], shard_send.at[i], shard_recv.at[i], send.at[i], recv.at[i], store.at[i])

    q4, w4 = dh // 4, ff // 2
    sq_g = square(0, dh, ff, wg.at[yours], wg.at[own], dg.at[pl.ds(0, dh)], spare(n2, 0, 0, q4, w4, 2, 6), gg_h)
    left = spare(n2, 0, 2 * w4, q4, w4, 1, 3) + spare(n2, 3 * q4, 0, q4, w4, 3, 3)
    sq_u = square(1, dh, ff, wu.at[yours], wu.at[own], du.at[pl.ds(0, dh)], left, gu_h)
    f4, d4 = ff // 4, dh // 2
    sq_d = square(2, ff, dh, gds_h.at[:, yours], hid.at[:, pl.ds(0, dh)], gt,
                  spare(n2, dh, 0, f4, d4, 4, 4) + spare(dg, dh, 0, f4, d4, 2, 2), gd_h)
    dq_cols = hq * HEAD_SIZE
    sq_o = square(3, dq_cols, dh, go_v.at[1 - s], go_v.at[s], wg.at[pl.ds(0, dq_cols), pl.ds(0, dh)],
                  spare(wg, dq_cols, 0, dq_cols // 4, d4, 2, 6), go_h)
    gw_cols = dq_cols + wide
    sq_w = square(4, dh, gw_cols, wu.at[yours, pl.ds(0, gw_cols)], wu.at[own, pl.ds(0, gw_cols)], hid.at[pl.ds(0, dh), pl.ds(0, gw_cols)],
                  spare(gt, 0, 0, q4, gw_cols // 2, 2, 6), gw_h)
    down_load = pltpu.make_async_copy(gds_h.at[:, own], hid.at[:, pl.ds(0, dh)], lsem.at[5])
    wp_load = pltpu.make_async_copy(wp_h, wd, lsem.at[6])

    def f_load(job):
        return pltpu.make_async_copy(fp_h.at[at(job)], pbuf.at[at(job)], fsem.at[job])

    def f_start(job):
        line.sent(4 + job)
        f_load(job).start()

    def key_piece(b):
        return ys.at[pl.ds(pl.multiple_of(lax.rem(b, 4) * RUN, RUN), RUN), pl.ds(pl.multiple_of(b // 4 * wide, wide), wide)]

    def key_recv(i, run):
        m = (i - 1) * per + run
        return ys.at[pl.ds(m % 4 * RUN, RUN), pl.ds(dh + m // 4 * wide, wide)]

    def key_copy(i, run):
        to = lax.rem(c + i, nc)
        return remote(key_piece(to * per + run), key_recv(i, run), qsend.at[i, run], qrecv.at[i, run], {"context": to})

    def grad_out(j):
        ot = o_v[...].T

        def part(cols):
            go_v[j, :, cols] = mm(ot, ys[:, pl.ds(pl.multiple_of(j * dh + cols.start, RUN), RUN)]).astype(BF)

        across(dh, RUN, part)

    def pack():
        for i in range(1, nc):
            pl.semaphore_signal(credits.at[5], inc=1, device_id={"context": lax.rem(c + i, nc)}, device_id_type=MESH)

        def one(b, _):
            rows = at(b)
            parts = [(dk_s[g, rows, :] * score).astype(BF) for g in range(hk)]
            parts += [dv_s[g, rows, :].astype(BF) for g in range(hk)]
            value = mm_nt(jnp.concatenate(parts, axis=1), pad_matrix(2 * hk)).astype(BF)
            key_piece(b)[...] = value
            return 0

        lax.fori_loop(0, blocks, one, 0)
        pl.semaphore_wait(credits.at[5], nc - 1)
        for run in range(per):
            for i in range(1, nc):
                key_copy(i, run).start()

    def normed(job):
        rows = at(lax.rem(job + per, runs))
        line.sent(8 + job + jnp.where(job == 3, 1, 0))
        line.sent(4 + job, fwd=False, ret=True)

        def part(cols):
            dn = mm(dqp[rows, :], wd[0:nq, cols]) + mm(dkv_s[rows, :], wd[nq:, cols])
            pbuf[at(job), cols] = dn.astype(BF)

        across(d, 512, part)

    def keys(run):
        for i in range(1, nc):
            key_copy(i, run).wait_recv()
        selkv = pad_matrix(2 * hk)
        rows = pl.ds(run * RUN, RUN)
        total = mm(key_piece(c * per + run)[...], selkv)
        for i in range(1, nc):
            total = total + mm(key_recv(i, run)[...], selkv)
        ct, st = rope_tables(run, per, pos_ref, cb_ref, sb_ref, cj_ref, sj_ref)
        for g in range(hk):
            dkv_s[rows, g * PAD : (g + 1) * PAD] = rope_back(total[:, g * PAD : (g + 1) * PAD], ct, st).astype(BF)
        dkv_s[rows, hk * PAD :] = total[:, hk * PAD :].astype(BF)

    tile_v = hid.at[:, pl.ds(dh, RUN)]

    def tile_load(i):
        return pltpu.make_async_copy(n1_h.at[:, at(i)], tile_v, nsem)

    def grads_in(k):
        i = k - into

        @pl.when(i == 0)
        def _():
            def pack_rows(to, sub):
                du[to, 0:dq_cols] = mm_nt(dqp[to, :], pad_matrix(hq)).astype(BF)
                du[to, dq_cols:gw_cols] = mm_nt(dkv_s[to, :], pad_matrix(2 * hk)).astype(BF)

            down_rows(0, rows_here, RUN, pack_rows)

        for j in range(2):
            tile_load(2 * i + j).wait()
            nt = tile_v[...].T


            def part(cols, j=j):
                wu[at(2 * i + j), cols] = mm(nt, du[:, cols]).astype(BF)

            across(gw_cols, gw_cols // 2, part)

            @pl.when(2 * i + j + 1 < d // RUN)
            def _():
                tile_load(2 * i + j + 1).start()

    def halves(i, body):
        for j in range(2):

            def step(m, _, j=j):
                natural = pl.ds(pl.multiple_of(j * half + i * 128 + m * 32, 32), 32)
                by_job = lambda part: pl.ds(pl.multiple_of(part * rows_here + (1 - j) * half + i * 128 + m * 32, 32), 32)
                body(natural, by_job, pl.ds(pl.multiple_of(j * 128 + m * 32, 32), 32))
                return 0

            lax.fori_loop(0, 4, step, 0)

    def output(k):
        i = k - outs

        def one(natural, by_job, to):
            total = xs[natural, :].astype(F32) + obuf[by_job(0), :].astype(F32)
            st_p[to, :] = (total + obuf[by_job(2), :].astype(F32)).astype(BF)

        halves(i, one)
        stage(st_o, osem.at[0], out_h.at[at(i)], lambda cols: mm(merge_matrix(), st_p[:, cols]).astype(BF), i > 0)

    def m_load(i, j):
        src = dm_h.at[pl.ds(pl.multiple_of(j * half + i * 128, 128), 128)]
        return pltpu.make_async_copy(src, s_s.at[pl.ds(j * 128, 128), pl.ds(0, d)], msem.at[j])

    def finals(i):
        for j in range(2):
            m_load(i, j).wait()

        def one(natural, by_job, to):
            x = xs[natural, :].astype(F32)
            dn = obuf[by_job(1), :].astype(F32)
            r = lax.rsqrt(jnp.mean(x * x, axis=-1, keepdims=True) + norm_eps)
            w = gf_ref[0:1, :] * dn
            inner = jnp.mean(w * x, axis=-1, keepdims=True)
            st_p[to, :] = (s_s[to, 0:d] + (r * w - x * (r * r * r) * inner)).astype(BF)
            gpart[0:8, :] += jnp.sum((dn * x * r).reshape(4, 8, d), axis=0)

        halves(i, one)

        @pl.when(i + 1 < runs)
        def _():
            for j in range(2):
                m_load(i + 1, j).start()

        cp = pltpu.make_async_copy(st_t, tg_h.at[at(i)], osem.at[2])

        @pl.when(i > 0)
        def _():
            cp.wait()

        def fill(cols):
            st_t[:, cols] = mm(merge_matrix(), st_p[:, cols]).astype(BF)

        across(d, 512, fill)
        cp.start()

    packed = back + 5 * runs
    into = packed + 4
    outs = into + 4
    lag = hq - 1

    def due(job):
        return (line.per * (job + 1) - 1 + line.turn) // line.ticks + lag + 1

    begins = [back + 5 * job for job in range(runs)]
    items = [([(0, per * hq)], lambda k: head(k, True)), ([(per * hq, first)], lambda k: head(k, False)), ([(first, second)], ffn),
             ([(second, second + 2)], grads_down), ([(second + 2, back)], grads_up), ([(b, b + 1) for b in begins], middle),
             ([(b + 1, b + 5) for b in begins[:per]], lambda k: pair(k, True)),
             ([(b + 1, b + 5) for b in begins[per:]], lambda k: pair(k, False)),
             ([(into, into + 3)], grads_in), ([(outs, outs + runs)], output)]
    fin = due(Line.D_AT[per])

    def begin_down():
        pltpu.make_async_copy(st_o, gds_h.at[pl.ds(0, RUN)], osem.at[0]).wait()
        down_load.start()
        wp_load.start()

    def free_three():
        for sq in (sq_g, sq_u, sq_d):
            sq.free()
        for sq in (sq_d, sq_g, sq_u):
            sq.e0()

    def store_start(sq):
        def body():
            sq.e5()
            sq.store().start()

        return body

    def dm_begin():
        pltpu.make_async_copy(s_s.at[:, pl.ds(0, d)], dm_h.at[pl.ds(0, RUN)], osem.at[1]).wait()
        for j in range(2):
            m_load(0, j).start()

    def first_e1():
        down_load.wait()
        sq_d.e1()

    def give_o():
        sq_g.store().wait()
        sq_g.done()
        sq_o.free()

    def give_w():
        sq_d.store().wait()
        sq_d.done()
        sq_w.free()

    def release_u():
        sq_u.store().wait()
        sq_u.done()

    def number(k, steps):
        return sum(jnp.where(k >= step, 1, 0) for step in steps[1:])

    events = [(second + 2, begin_down), (second + 4, free_three)]
    at_f = [4 * Line.F_AT[job] + lag - 2 for job in range(runs)]
    events += [
        (38, first_e1), (40, sq_g.e1), (41, sq_d.e2), (42, sq_u.e1), (43, sq_g.e2), (44, sq_d.e3), (45, wp_load.wait), (46, sq_u.e2), (47, sq_g.e3),
        (48, sq_d.e4), (49, sq_u.e3), (50, sq_g.e4), (52, store_start(sq_d)), (53, sq_u.e4), (54, give_w), (55, store_start(sq_g)),
        (57, store_start(sq_u)), (57, give_o), (59, release_u),
        (53, lambda: grad_out(0)), (54, lambda: grad_out(1)), (packed, pack), (packed, lambda: tile_load(0).start()), (packed, dm_begin), (packed + 2, lambda: keys(0)), (packed + 2, sq_o.e0), (packed + 3, lambda: keys(1)),
        (61, sq_o.e1), (63, sq_o.e2), (64, sq_w.e0), (65, sq_w.e1), (65, sq_o.e3), (67, sq_w.e2), (67, sq_o.e4), (68, sq_w.e3),
        (69, store_start(sq_o)), (70, sq_w.e4), (73, store_start(sq_w)),
    ]
    items += [([(k, k + 1)], functools.partial(lambda e, k: e(), e)) for k, e in events]
    at_normed = (45, 50, packed + 2, packed + 4)
    items.append(([(k, k + 1) for k in at_f], lambda k: f_start(number(k, at_f))))
    items.append(([(k + 1, k + 2) for k in at_f], lambda k: f_load(number(k, at_f)).wait()))
    items.append(([(k, k + 1) for k in at_normed], lambda k: normed(number(k, at_normed))))
    end = -(-line.slots // line.ticks) + lag
    items.append(([(fin, fin + 2), (end, end + 2)], lambda k: finals(jnp.where(k < end, k - fin, k - end + 2))))

    def serve(k):
        def tick(j, _):
            line.serve(line.ticks * (k - lag) + j)
            return 0

        lax.fori_loop(0, line.ticks, tick, 0)

    run_items(items, serve)
    me = s * nc + c
    sums = jnp.concatenate(
        [jnp.broadcast_to(jnp.sum(gpart[k * 8 : (k + 1) * 8, :], axis=0, keepdims=True), (8, d)) for k in range(2)], axis=0
    )
    grecv[me] = sums
    gcopies = []
    for i, t in enumerate(peers):
        cp = remote(grecv.at[me], grecv.at[me], gs.at[i], gr.at[i], t)
        cp.start()
        gcopies.append(cp)

    def rest(job, _):
        line.sent(jnp.where(job < runs, job, job + runs), fwd=False, ret=True)
        return 0

    lax.fori_loop(0, 3 * runs, rest, 0)
    for job in Line.D_AT:
        line.sent(job)
    for sq in (sq_o, sq_w):
        sq.store().wait()
        sq.done()
    for i in range(1, nc):
        for run in range(per):
            key_copy(i, run).wait_send()
    pltpu.make_async_copy(st_o, out_h.at[pl.ds(0, RUN)], osem.at[0]).wait()
    pltpu.make_async_copy(st_t, tg_h.at[pl.ds(0, RUN)], osem.at[2]).wait()
    for cp in gcopies:
        cp.wait()
    total = grecv[0]
    for i in range(1, 2 * nc):
        total = total + grecv[i]
    gpart[...] = total
    gains_ref[...] = gpart[:, own]


def finish_kernel(gains_ref, out_h, tg_h, gw_h, go_h, gg_h, gu_h, gd_h, one_ref, two_ref, out_f, tg_f, gq_f, gk_f, gv_f, go_f, gg_f, gu_f, gd_f,
                  out_v, tg_v, gw_v, go_v, gg_v, gu_v, gd_v, q_v, kv_v, o_v, g_v, u_v, d_v, lsem, ssem):
    one_ref[...] = gains_ref[0]
    two_ref[...] = gains_ref[8]
    kw = gk_f.shape[0]
    nq = gw_h.shape[1] - 2 * kw
    pairs = [(gg_h, gg_v), (gu_h, gu_v), (gd_h, gd_v), (gw_h, gw_v), (go_h, go_v), (out_h, out_v), (tg_h, tg_v)]
    loads = [pltpu.make_async_copy(a, b, lsem.at[i]) for i, (a, b) in enumerate(pairs)]
    for cp in loads:
        cp.start()
    stores = [
        pltpu.make_async_copy(a, b, ssem.at[i])
        for i, (a, b) in enumerate([(g_v, gg_f), (u_v, gu_f), (d_v, gd_f), (q_v, gq_f), (kv_v.at[0:kw], gk_f), (kv_v.at[kw:], gv_f),
                                    (o_v, go_f), (out_v, out_f), (tg_v, tg_f)])
    ]

    def widen(src, dst, width):
        def step(i, _):
            rows = pl.ds(pl.multiple_of(i * 32, 32), 32)
            dst[rows, :] = src[rows, 0:width].astype(F32)
            return 0

        lax.fori_loop(0, src.shape[0] // 32, step, 0)

    for i, (src, dst) in enumerate([(gg_v, g_v), (gu_v, u_v), (gd_v, d_v)]):
        loads[i].wait()
        widen(src, dst, src.shape[1])
        stores[i].start()
    loads[5].wait()
    stores[7].start()
    loads[6].wait()
    stores[8].start()
    loads[3].wait()
    widen(gw_v, q_v, nq)
    stores[3].start()
    for i in range(gw_v.shape[0] // PAD):
        kv_v[:, i * PAD : (i + 1) * PAD] = gw_v[i * PAD : (i + 1) * PAD, nq:].astype(F32).T
    stores[4].start()
    stores[5].start()
    loads[4].wait()
    widen(go_v, o_v, go_v.shape[1])
    stores[6].start()
    for cp in stores:
        cp.wait()


def fast(
    tokens, w_query, key_weight, value_weight, w_out, w_gate, w_up, w_down, gain_attn, gain_ffn, segments, positions, cotangent, n, nc
):
    _, rows, d = tokens.shape
    half = rows // 2
    runs = rows // RUN
    per = runs // 2
    prompt = segments.shape[1] // 2
    blocks = prompt // RUN
    dq, dk = w_query.shape[1], key_weight.shape[1]
    hq, hk = dq // HEAD_SIZE, dk // HEAD_SIZE
    nq, nk = hq * PAD, hk * PAD
    ff = w_gate.shape[1]
    dh = d // 2
    x = tokens.reshape(rows, d)
    dy = cotangent.reshape(rows, d)
    freq = np.exp(np.arange(HEAD_SIZE // 2, dtype=np.float32) * np.float32(-2.0 * math.log(rope_base) / HEAD_SIZE)).astype(np.float32)
    lanes = np.zeros((PAD,), np.float32)
    lanes[0:48] = freq
    lanes[64:112] = freq
    sign = np.where(np.arange(PAD) < 64, -1.0, 1.0).astype(np.float32)
    inner = np.arange(RUN, dtype=np.float64)[:, None] * lanes[None, :].astype(np.float64)
    cj = jnp.asarray(np.cos(inner).astype(np.float32))
    sj = jnp.asarray((np.sin(inner) * sign).astype(np.float32))
    starts = np.arange(16, dtype=np.float64)[:, None] * RUN * lanes[None, :].astype(np.float64)
    cb = jnp.asarray(np.cos(starts).astype(np.float32))
    sb = jnp.asarray((np.sin(starts) * sign).astype(np.float32))
    gains = jnp.where(np.arange(2)[:, None] == 0, gain_attn[None, :], gain_ffn[None, :]).astype(F32)

    V = pl.BlockSpec(memory_space=pltpu.VMEM)
    S = pl.BlockSpec(memory_space=pltpu.SMEM)
    A = pl.BlockSpec(memory_space=pl.ANY)
    sds = jax.ShapeDtypeStruct
    DMA = pltpu.SemaphoreType.DMA

    def call(kernel, ins, outs, scratch, collective=None, flops=0):
        params = dict(vmem_limit_bytes=VLIM - 64 * 1024)
        if collective is not None:
            params.update(collective_id=collective, has_side_effects=True)
        args = [a for a, _ in ins]
        return pl.pallas_call(
            kernel,
            out_shape=[o for o, _ in outs],
            in_specs=[sp for _, sp in ins],
            out_specs=[sp for _, sp in outs],
            scratch_shapes=scratch,
            compiler_params=pltpu.CompilerParams(**params),
            cost_estimate=pl.CostEstimate(flops=flops, bytes_accessed=0, transcendentals=0),
        )(*args)

    rope_in = [(positions, S), (cb, V), (sb, V), (cj, V), (sj, V)]
    xp, dyp, n1, q, kvp, kvc, wp, gf, wo, wg, wu, wd = call(
        functools.partial(first_kernel, nc),
        [(x, V), (dy, A), (gains, V)] + rope_in + [(w_query, A), (key_weight.T, A), (value_weight.T, A), (w_out, A), (w_gate, A), (w_up, A), (w_down, A)],
        [
            (sds((rows, d), BF), A), (sds((rows, d), BF), A), (sds((rows, d), BF), A), (sds((rows, nq), BF), V),
            (sds((prompt, 2 * dk), BF), A), (sds((half, 2 * nk), BF), V), (sds((nq + 2 * nk, d), BF), A), (sds((16, d), F32), V),
            (sds((dq, d), BF), A), (sds((d, ff), BF), A), (sds((d, ff), BF), A), (sds((ff, d), BF), A),
        ],
        [
            pltpu.VMEM((rows, d), BF), pltpu.VMEM((rows, d), BF), pltpu.VMEM((rows, d), BF), pltpu.VMEM((nq + 2 * nk, d), BF),
            pltpu.VMEM((rows, d), BF), pltpu.VMEM((d, dq), BF), pltpu.VMEM((dk, d), BF), pltpu.VMEM((dk, d), BF), pltpu.VMEM((16, d), F32),
            pltpu.VMEM((dq, dh), BF), pltpu.VMEM((dh, ff), BF), pltpu.VMEM((dh, ff), BF), pltpu.VMEM((ff, dh), BF),
            pltpu.VMEM((half, 2 * dk), BF),
            DMA((9,)), DMA((8,)), DMA((8,)), DMA((4,)), DMA((per, nc)), DMA((per, nc)), DMA((4,)),
        ],
        collective=0, flops=60 * 10**9,
    )

    chunk = 16
    count = 16 * (RUN // 2 // chunk)
    U = pltpu.VMEM((rows, d), BF)
    W = pltpu.VMEM((d, ff), BF)
    H = pltpu.VMEM((rows, ff), BF)
    KV = pltpu.VMEM((hk, prompt, PAD), BF)
    KVF = pltpu.VMEM((hk, prompt, PAD), F32)
    width = hq // hk * RUN
    out, tg, gg, gu, gd, go, gw, _, _, _, gains_grad = call(
        functools.partial(main_kernel, n, nc, chunk),
        [(segments, S)] + rope_in
        + [(gf, V), (q, V), (kvc, V), (wo, V), (kvp, A), (xp, A), (dyp, A), (wg, A), (wu, A), (wd, A), (n1, A), (wp, A)],
        [(sds((rows, d), BF), A), (sds((rows, d), BF), A), (sds((dh, ff), BF), A), (sds((dh, ff), BF), A), (sds((ff, dh), BF), A),
         (sds((dq, dh), BF), A), (sds((dh, dq + 2 * dk), BF), A), (sds((rows, d), F32), A), (sds((ff, d), BF), A), (sds((rows, d), BF), A),
         (sds((16, dh), F32), V)],
        [KV, KV, pltpu.VMEM((RUN, prompt + RUN), F32), pltpu.VMEM((rows, dq), BF), pltpu.VMEM((rows, nq), BF), pltpu.VMEM((runs * hq * 8, RUN), F32),
         U, U, U, U, pltpu.VMEM((3 * rows, d), BF), pltpu.VMEM((ff, d), BF), U, W, W, H, H, H, pltpu.VMEM((ff, dh), BF),
         KVF, KVF, pltpu.VMEM((rows, nq), BF), pltpu.VMEM((width, PAD), F32), pltpu.VMEM((8, width), F32), pltpu.VMEM((rows, nq), BF),
         pltpu.VMEM((rows, 2 * nk), BF), pltpu.VMEM((2, dq, dh), BF), pltpu.VMEM((RUN, d), BF), pltpu.VMEM((RUN, d), BF), pltpu.VMEM((RUN, d), BF),
         pltpu.VMEM((16, d), F32), pltpu.VMEM((2 * nc, 16, d), F32),
         DMA((7,)), DMA((blocks,)), DMA((3,)), DMA((runs,)), DMA((2,)), DMA, DMA((nc, per)), DMA((nc, per)), DMA((2 * nc - 1,)), DMA((2 * nc - 1,))]
        + [DMA((2, count))] * 4
        + [pltpu.SemaphoreType.REGULAR((6,)), DMA((5,)), DMA((5,)), DMA((5, 3, 2, 2)), DMA((5, 3, 2, 2)), DMA((5,))],
        collective=1, flops=300 * 10**9,
    )
    shapes = [(rows, d), (rows, d), (dh, dq + 2 * dk), (dq, dh), (dh, ff), (dh, ff), (ff, dh)]
    wide = [(dh, dq), (2 * dk, dh), (dq, dh), (dh, ff), (dh, ff), (ff, dh)]
    finals = [(dh, dq), (dk, dh), (dk, dh), (dq, dh), (dh, ff), (dh, ff), (ff, dh)]
    g1o, g2o, out, tg, gq, gk, gv, go, gg, gu, gd = call(
        finish_kernel,
        [(gains_grad, V)] + [(a, A) for a in (out, tg, gw, go, gg, gu, gd)],
        [(sds((dh,), F32), V), (sds((dh,), F32), V), (sds((rows, d), BF), A), (sds((rows, d), BF), A)] + [(sds(shape, F32), A) for shape in finals],
        [pltpu.VMEM(shape, BF) for shape in shapes] + [pltpu.VMEM(shape, F32) for shape in wide] + [DMA((7,)), DMA((9,))],
    )
    return out[None], tg[None], gq, gk.T, gv.T, go, gg, gu, gd, g1o, g2o


def body(mesh, *args):
    tokens, w_query, segments = args[0], args[1], args[10]
    n, nc = mesh.shape["tensor"], mesh.shape["context"]
    rows = tokens.shape[1]
    if (tokens.shape[0] == 1 and rows % (4 * CLEN) == 0 and n == 4 and nc == 4 and mesh.shape["shard"] == 2
            and segments.shape[1] == rows * nc):
        return fast(*args, n, nc)
    return general(*args)


def solution(mesh):
    in_specs = (
        P("shard", "context", None),
        P("shard", "tensor"),
        P("shard", "tensor"),
        P("shard", "tensor"),
        P("tensor", "shard"),
        P("shard", "tensor"),
        P("shard", "tensor"),
        P("tensor", "shard"),
        P("shard"),
        P("shard"),
        P("shard", None),
        P("shard", None),
        P("shard", "context", None),
    )
    out_specs = (
        P("shard", "context", None),
        P("shard", "context", None),
        P("shard", "tensor"),
        P("shard", "tensor"),
        P("shard", "tensor"),
        P("tensor", "shard"),
        P("shard", "tensor"),
        P("shard", "tensor"),
        P("tensor", "shard"),
        P("shard"),
        P("shard"),
    )
    return jax.shard_map(functools.partial(body, mesh), mesh=mesh, in_specs=in_specs, out_specs=out_specs, check_vma=False)
```
